128 devices in a mesh: expert: 32 (over y, z, core), tensor: 4 (over x).
Axes of the slice: x: 4, y: 4, z: 4, core: 2. Of those that a mesh axis runs over, the one named last changes fastest.
Arguments:
- tokens: bfloat16 [8192, 2048], P('expert', 'tensor'), may hold values from -6 to 6
- out_grad: bfloat16 [8192, 2048], P('expert', 'tensor'), may hold values from -6 to 6
- seq_lengths: int32 [32, 3], P('expert'), may hold values from 1 to 128, 256 in all within a row
- dest_index: int32 [8192], P('expert'), may hold values from 0 to 8191, as said below
- routes: int32 [8192, 8], P('expert'), may hold values from 0 to 63, all different within a row; in each aligned block of 256 rows (0 to 255, 256 to 511, ...) at most 48 rows name the same one
- pair_order: int32 [32, 2048], P('expert'), may hold values from 0 to 2047, each once within a row
- norm1_gain: bfloat16 [2048], replicated, may hold values from 0.25 to 1.75
- w_query: bfloat16 [2048, 2048], P(None, 'tensor'), may hold values from -0.125 to 0.125
- w_key: bfloat16 [2048, 2048], P(None, 'tensor'), may hold values from -0.125 to 0.125
- w_value: bfloat16 [2048, 2048], P(None, 'tensor'), may hold values from -0.125 to 0.125
- q_gain: bfloat16 [128], replicated, may hold values from 0.25 to 1.75
- k_gain: bfloat16 [128], replicated, may hold values from 0.25 to 1.75
- w_output: bfloat16 [2048, 2048], P('tensor'), may hold values from -1 to 1
- norm2_gain: bfloat16 [2048], replicated, may hold values from 0.25 to 1.75
- w_router: bfloat16 [2048, 64], replicated, may hold values from -0.0625 to 0.0625
- expert_w: bfloat16 [64, 2048, 3, 1024], P('expert', None, None, 'tensor'), may hold values from -3 to 3
Outputs:
- block_out: bfloat16 [8192, 2048], P('expert', 'tensor')
- grad_tokens: bfloat16 [8192, 2048], P('expert', 'tensor')
- grad_norm1: float32 [2048], replicated
- grad_query: float32 [2048, 2048], P(None, 'tensor')
- grad_key: float32 [2048, 2048], P(None, 'tensor')
- grad_value: float32 [2048, 2048], P(None, 'tensor')
- grad_qgain: float32 [128], replicated
- grad_kgain: float32 [128], replicated
- grad_output: float32 [2048, 2048], P('tensor')
- grad_norm2: float32 [2048], replicated
- grad_router: float32 [2048, 64], replicated
- grad_experts: float32 [64, 2048, 3, 1024], P('expert', None, None, 'tensor')
The draws below stay inside these ranges and needn't reach their ends.
Inputs may be any that keep to these rules, and one draw needn't show every extreme that they name: `dest_index`: a permutation of the balanced positions; the arriving rows of each group go to exactly 8 positions of every group's range of 256 positions. `routes`: each row names 8 different experts; within the rows of one group no expert is named more than 48 times. `pair_order`: each row is a permutation. `seq_lengths`: each row sums to 256 and its largest entry is 128.
All inputs are finite; a program needn't handle non-finite values.
Results may differ from the reference program's by a relative error of at most 0.035.
Values may be sent and summed in bfloat16 or wider, within the bound.
A program may use at most 256 MiB of HBM per device.

```python
import math
from functools import partial
import jax
import jax.numpy as jnp
import numpy as np
from jax import lax

D = 2048
HEADS = 16
HEAD = 128
EXPERTS = 64
FF = 1024
TOP = 8
TOK_DEV = 256
SEQS = 3
GROUPS = 32
TOKENS = 8192
LONGEST = 128
MOST = 48
CAP = 1280
N_TENSOR = 4


def shuffle_one(key_one):
    return jax.random.permutation(key_one, TOK_DEV).astype(jnp.int32)


def place_one(order_row, values_row):
    return jnp.zeros((TOK_DEV,), jnp.int32).at[order_row].set(values_row)


def draw_dest_index(key, part):
    move_rows = TOK_DEV // GROUPS
    key_source = jax.random.fold_in(key, 11)
    key_target = jax.random.fold_in(key, 23)
    source_perm = jax.vmap(shuffle_one)(jax.random.split(key_source, GROUPS))
    target_perm = jax.vmap(shuffle_one)(jax.random.split(key_target, GROUPS))
    layout = target_perm.reshape(GROUPS, GROUPS, move_rows)
    dest_grid = jnp.transpose(layout, (1, 0, 2)) + (jnp.arange(GROUPS, dtype=jnp.int32) * TOK_DEV)[None, :, None]
    dest_rows = dest_grid.reshape(GROUPS, TOK_DEV).astype(jnp.int32)
    placed = jax.vmap(place_one)(source_perm, dest_rows)
    return placed.reshape(TOKENS).astype(jnp.int32)


def draw_expert_w(key, part):
    base = jnp.clip(jax.random.normal(key, (EXPERTS, D, 3, FF), jnp.float32), -4.0, 4.0)
    scales = jnp.array([D ** (-0.5), D ** (-0.5), 4.0 * FF ** (-0.5)], jnp.float32)
    return (base * scales[None, None, :, None]).astype(jnp.bfloat16)


def shard_levels(stream_key, shape, cuts, smallest, top_value):
    def one(position, blocks):
        draws = jax.random.uniform(jax.random.fold_in(jax.random.fold_in(stream_key, 6), position), (blocks,), jnp.float32, smallest / len(cuts), top_value / len(cuts))
        return jnp.repeat(jnp.exp(draws), shape[position] // blocks).reshape((-1,) + (1,) * (len(shape) - position - 1))

    gain = one(*cuts[0])
    for cut in cuts[1:]:
        gain = gain * one(*cut)
    return gain


def split_up(number_of, total, most, lean):
    portions = [(1 << 20) // math.isqrt(standing ** lean) + 1 for standing in range(2, number_of + 1)]
    surplus, given = total - most - (number_of - 1), [1] * (number_of - 1)
    while surplus > 0:
        candidates = [i for i in range(number_of - 1) if given[i] < most]
        whole, budget = sum([portions[i] for i in candidates]), surplus
        for i in candidates:
            extra = min(most - given[i], max(1, budget * portions[i] // whole), surplus)
            given[i] = given[i] + extra
            surplus = surplus - extra
    return np.array([most] + given)


def ragged_sizes(own_key, amount, total, most, skew):
    if amount == 2:
        one = jax.random.randint(own_key, (), max(1, total - most), min(most, total - 1) + 1)
        return jnp.stack([one, total - one])
    lengths = jnp.asarray(split_up(amount, total, most, skew), jnp.int32)
    pairs = (amount - 1) // 2
    giver, sink = lengths[1:1 + 2 * pairs:2], lengths[2:2 + 2 * pairs:2]
    margin = jnp.minimum(giver - 1, most - sink)
    moved = jax.random.randint(jax.random.fold_in(own_key, 1), (pairs,), 0, 1 << 20) % (margin + 1)
    lengths = lengths.at[1:1 + 2 * pairs:2].set(giver - moved).at[2:2 + 2 * pairs:2].set(sink + moved)
    return lengths[jax.random.permutation(jax.random.fold_in(own_key, 2), amount)]


def shared_out(rng, own, number, rows, count, top, most, skew):
    sequence = jax.random.permutation(rng, count)
    packed, usual = shares(count, rows * top, most, skew, True), shares(count, rows * top, most, skew, False)
    places = jnp.arange(count)

    def named(sizes, rotation):
        used = int((sizes > 0).sum())
        fixed = max(1, used // 4)
        shifted = fixed + (places - fixed + rotation * (used - fixed)) % max(1, count - fixed)
        return jnp.zeros((count,), jnp.int32).at[sequence[jnp.where(places < fixed, places, shifted)]].set(jnp.asarray(sizes, jnp.int32))

    sizes = jnp.where(number % 4 == 0, named(packed, number // 4), named(usual, number - number // 4 - 1))
    mixed = jax.random.permutation(jax.random.fold_in(own, 3), count)
    source_of, sink = mixed[0:count // 2 * 2:2], mixed[1:count // 2 * 2:2]
    slack = jnp.minimum(sizes[source_of] - 1, most - sizes[sink]) // 2
    slack = jnp.where((source_of == sequence[0]) | (sink == sequence[0]) | (sizes[sink] == 0), 0, jnp.maximum(slack, 0))
    shifted = jax.random.randint(jax.random.fold_in(own, 4), (count // 2,), 0, 1 << 20) % (slack + 1)
    sizes = sizes.at[source_of].add(-shifted).at[sink].add(shifted)
    members = jnp.searchsorted(jnp.cumsum(sizes), jnp.arange(rows * top), side="right").astype(jnp.int32)
    grid = members.reshape(top, rows).T
    grid = grid[jax.random.permutation(jax.random.fold_in(own, 1), rows)]
    rotation = jax.random.randint(jax.random.fold_in(own, 2), (rows, 1), 0, top)
    return jnp.take_along_axis(grid, (jnp.arange(top)[None, :] + rotation) % top, axis=1)


def shares(amount, total, reach, lean, full):
    portions = [(1 << 20) // math.isqrt(grade ** lean) + 1 for grade in range(1, amount + 1)]
    largest = reach if full else min(reach, max(-(-total // amount), total * portions[0] // sum(portions)))
    least = 1 if total - largest >= amount - 1 else 0
    given, surplus = [largest] + [least] * (amount - 1), total - largest - least * (amount - 1)
    while surplus > 0:
        movable = [i for i in range(1, amount) if given[i] < largest] or [i for i in range(1, amount) if given[i] < reach]
        whole, left = sum([portions[i] for i in movable]), surplus
        for i in movable:
            addition = min(reach - given[i], max(1, left * portions[i] // whole), surplus)
            given[i] = given[i] + addition
            surplus = surplus - addition
    return np.array(given)


def gaussian(rng, shape, scale, limit, cuts=(), held_as=jnp.bfloat16):
    result = scale * jax.random.normal(rng, shape, jnp.float32)
    if cuts:
        result = result * shard_levels(rng, shape, cuts, -0.22, 0.18)
    return jnp.clip(result, -limit, limit).astype(held_as)


def setup_inputs(seed: int = 0) -> dict:
    keys = jax.random.split(jax.random.key(seed), 17)
    tokens = gaussian(keys[0], (TOKENS, D), 1.0, 6.0, ((0, 32), (1, 4)))
    out_grad = gaussian(keys[1], (TOKENS, D), 1.0, 6.0, ((0, 32), (1, 4)))
    seq_lengths = jax.vmap(lambda own: ragged_sizes(own, SEQS, TOK_DEV, LONGEST, 1))(jax.random.split(keys[2], GROUPS)).reshape((GROUPS, SEQS)).astype(jnp.int32)
    dest_index = draw_dest_index(jax.random.fold_in(keys[16], 71), 0)
    routes_keys = jax.random.split(jax.random.fold_in(keys[4], 1), TOKENS // TOK_DEV)
    routes_turns = jax.random.permutation(jax.random.fold_in(keys[4], 3), TOKENS // TOK_DEV)
    routes = jax.vmap(lambda own, number: shared_out(jax.random.fold_in(keys[4], 2), own, number, TOK_DEV, EXPERTS, TOP, MOST, 1))(routes_keys, routes_turns).reshape((TOKENS, TOP))
    pair_order = jax.vmap(lambda own: jax.random.permutation(own, TOK_DEV * TOP))(jax.random.split(keys[5], GROUPS)).reshape((GROUPS, TOK_DEV * TOP)).astype(jnp.int32)
    norm1_gain = jnp.clip(1.0 + 0.15 * jax.random.normal(keys[6], (D,), jnp.float32), 0.25, 1.75).astype(jnp.bfloat16)
    w_query = gaussian(keys[7], (D, HEADS * HEAD), D ** -0.5, 0.125, ((1, 4),))
    w_key = gaussian(keys[8], (D, HEADS * HEAD), D ** -0.5, 0.125, ((1, 4),))
    w_value = gaussian(keys[9], (D, HEADS * HEAD), D ** -0.5, 0.125, ((1, 4),))
    q_gain = jnp.clip(1.0 + 0.15 * jax.random.normal(keys[10], (HEAD,), jnp.float32), 0.25, 1.75).astype(jnp.bfloat16)
    k_gain = jnp.clip(1.0 + 0.15 * jax.random.normal(keys[11], (HEAD,), jnp.float32), 0.25, 1.75).astype(jnp.bfloat16)
    w_output = gaussian(keys[12], (HEADS * HEAD, D), (HEADS * HEAD // 64) ** -0.5, 1.0, ((0, 4),))
    norm2_gain = jnp.clip(1.0 + 0.15 * jax.random.normal(keys[13], (D,), jnp.float32), 0.25, 1.75).astype(jnp.bfloat16)
    w_router = gaussian(keys[14], (D, EXPERTS), (4 * D) ** -0.5, 0.0625)
    expert_w = draw_expert_w(jax.random.fold_in(keys[16], 71), 0)
    return dict(tokens=tokens, out_grad=out_grad, seq_lengths=seq_lengths, dest_index=dest_index, routes=routes, pair_order=pair_order, norm1_gain=norm1_gain, w_query=w_query, w_key=w_key, w_value=w_value, q_gain=q_gain, k_gain=k_gain, w_output=w_output, norm2_gain=norm2_gain, w_router=w_router, expert_w=expert_w)


@jax.custom_vjp
def low(v):
    return lax.optimization_barrier(v.astype(jnp.bfloat16)).astype(jnp.float32)

@jax.custom_vjp
def low_back(v):
    return v

def low_keep(v):
    return (low(v), None)

def low_pass(kept, grad):
    return (grad,)

def back_keep(v):
    return (v, None)

def back_low(kept, grad):
    return (low(grad),)
low.defvjp(low_keep, low_pass)
low_back.defvjp(back_keep, back_low)
norm_eps = 1e-06
rope_base = 10000.0
mask_fill = -1e+30

def matmul_high(left, right):
    return jnp.dot(left, right, precision=lax.Precision.HIGHEST)

def rms_apply(values, gain_vec):
    inverse = lax.rsqrt(lax.optimization_barrier(jnp.mean(values * values, axis=-1, keepdims=True)) + norm_eps)
    return values * inverse * gain_vec

def rope_tables(positions, width):
    half_width = width // 2
    steps_idx = jnp.arange(half_width, dtype=jnp.float32)
    freqs = jnp.exp(steps_idx * (-2.0 * math.log(rope_base) / width))
    angles = positions.astype(jnp.float32)[:, None] * freqs[None, :]
    return (jnp.cos(angles), jnp.sin(angles))

def head_prep(raw, gain_vec, cos_tab, sin_tab, heads):
    token_count = raw.shape[0]
    shaped = rms_apply(raw.reshape(token_count, heads, -1), gain_vec)
    half_width = shaped.shape[-1] // 2
    lower_half = shaped[..., :half_width]
    upper_half = shaped[..., half_width:]
    cos_rows = cos_tab[:, None, :]
    sin_rows = sin_tab[:, None, :]
    return jnp.concatenate([lower_half * cos_rows - upper_half * sin_rows, upper_half * cos_rows + lower_half * sin_rows], axis=-1)

def sequence_layout(lengths_row, count):
    seq_ends = jnp.cumsum(lengths_row).astype(jnp.int32)
    places = jnp.arange(count, dtype=jnp.int32)
    passed = (places[:, None] >= seq_ends[None, :]).astype(jnp.int32)
    seq_ids = lax.optimization_barrier(jnp.sum(passed, axis=1)).astype(jnp.int32)
    starts = lax.optimization_barrier(jnp.sum(passed * lengths_row[None, :], axis=1)).astype(jnp.int32)
    return (seq_ids, places - starts)

def pair_ranks(pair_expert, order_keys, expert_count):
    pair_total = pair_expert.shape[0]
    keyed = pair_expert * pair_total + order_keys
    sorter = jnp.argsort(keyed).astype(jnp.int32)
    sorted_ids = pair_expert[sorter]
    expert_axis = jnp.arange(expert_count, dtype=jnp.int32)
    counts = lax.optimization_barrier(jnp.sum((pair_expert[:, None] == expert_axis[None, :]).astype(jnp.int32), axis=0)).astype(jnp.int32)
    starts = (jnp.cumsum(counts) - counts).astype(jnp.int32)
    start_of = lax.optimization_barrier(jnp.sum(jnp.where(sorted_ids[:, None] == expert_axis[None, :], starts[None, :], 0), axis=1)).astype(jnp.int32)
    positions = jnp.arange(pair_total, dtype=jnp.int32) - start_of
    ranks = jnp.zeros((pair_total,), jnp.int32).at[sorter].set(positions)
    return (ranks, counts)

def reference(tokens, out_grad, seq_lengths, dest_index, routes, pair_order, norm1_gain, w_query, w_key, w_value, q_gain, k_gain, w_output, norm2_gain, w_router, expert_w):
    inverse = jnp.argsort(dest_index).astype(jnp.int32)
    tokens_bal = tokens[inverse].astype(jnp.float32)
    grad_bal = out_grad[inverse].astype(jnp.float32)
    pair_expert = routes.reshape(GROUPS, TOK_DEV * TOP).astype(jnp.int32)
    ranks, counts = jax.vmap(partial(pair_ranks, expert_count=EXPERTS))(pair_expert, pair_order)
    offsets = (jnp.cumsum(counts, axis=0) - counts).astype(jnp.int32)
    slot_global = (jnp.take_along_axis(offsets, pair_expert, axis=1) + ranks).astype(jnp.int32)
    kept = slot_global < CAP
    kept_flat = kept.reshape(-1)
    expert_flat = pair_expert.reshape(-1)
    slot_flat = slot_global.reshape(-1)
    pair_ids = jnp.arange(TOKENS * TOP, dtype=jnp.int32)
    target_expert = jnp.where(kept_flat, expert_flat, EXPERTS).astype(jnp.int32)
    slot_pair = jnp.full((EXPERTS, CAP), -1, jnp.int32).at[target_expert, jnp.minimum(slot_flat, CAP - 1)].set(pair_ids, mode='drop')
    keep_mask = kept_flat.reshape(TOKENS, TOP).astype(jnp.float32)
    seq_ids, positions = jax.vmap(partial(sequence_layout, count=TOK_DEV))(seq_lengths)
    token_all = (jnp.maximum(slot_pair, 0) // TOP).reshape(-1).astype(jnp.int32)
    scale_attn = 1.0 / math.sqrt(HEAD)
    quarter_width = FF // N_TENSOR

    def forward(x_in, gain_one, query_w, key_w, value_w, qgain_v, kgain_v, output_w, gain_two, router_w, experts_w):

        def attention_group(group_args):
            x_grp, ids_grp, pos_grp = group_args
            cos_tab, sin_tab = rope_tables(pos_grp, HEAD)
            normed = low(rms_apply(x_grp, gain_one))
            q_raw = low_back(matmul_high(normed, query_w))
            k_raw = low_back(matmul_high(normed, key_w))
            v_raw = low_back(matmul_high(normed, value_w))
            q_rot = low(head_prep(q_raw, qgain_v, cos_tab, sin_tab, HEADS))
            k_rot = low(head_prep(k_raw, kgain_v, cos_tab, sin_tab, HEADS))
            v_rot = low(v_raw).reshape(TOK_DEV, HEADS, HEAD)
            raw = jnp.einsum('qhd,khd->hqk', q_rot, k_rot, precision=lax.Precision.HIGHEST)
            scores = low_back(raw * scale_attn)
            same_seq = ids_grp[:, None] == ids_grp[None, :]
            scores = jnp.where(same_seq[None], scores, mask_fill)
            probs = low(jax.nn.softmax(scores, axis=-1))
            attended = jnp.einsum('hqk,khd->qhd', probs, v_rot, precision=lax.Precision.HIGHEST).reshape(TOK_DEV, HEADS * HEAD)
            attended = low_back(low(attended))
            attn_out = low_back(matmul_high(attended, output_w))
            return x_grp + attn_out
        resid = lax.map(jax.checkpoint(attention_group), (x_in.reshape(GROUPS, TOK_DEV, D), seq_ids, positions)).reshape(TOKENS, D)
        mixed = low(rms_apply(resid, gain_two))
        logits = low_back(matmul_high(mixed, router_w))
        chosen = jnp.take_along_axis(logits, routes, axis=1)
        gates = jax.nn.softmax(chosen, axis=-1)
        gate_flat = (gates * keep_mask).reshape(-1)

        def expert_rows(expert_args):
            weights, pair_slots = expert_args
            filled = (pair_slots >= 0).astype(jnp.float32)
            safe_pair = jnp.maximum(pair_slots, 0)
            token_ids = safe_pair // TOP
            rows_in = mixed[token_ids] * filled[:, None]
            slot_gate = gate_flat[safe_pair] * filled
            summed = jnp.zeros((CAP, D), jnp.float32)
            for quarter in range(N_TENSOR):
                low_col = quarter * quarter_width
                piece_w = weights[:, :, low_col:low_col + quarter_width]
                part_in = low_back(rows_in)
                gate_pre = low_back(matmul_high(part_in, piece_w[:, 0]))
                up_pre = low_back(matmul_high(part_in, piece_w[:, 1]))
                active = low(jax.nn.silu(gate_pre) * up_pre)
                part_out = low_back(low(matmul_high(active, piece_w[:, 2].T)))
                summed = summed + part_out
            return summed * slot_gate[:, None]
        expert_out = lax.map(jax.checkpoint(expert_rows), (experts_w, slot_pair))
        moe = jnp.zeros((TOKENS, D), jnp.float32).at[token_all].add(expert_out.reshape(-1, D))
        return resid + moe
    output_bal, pullback = jax.vjp(forward, tokens_bal, norm1_gain.astype(jnp.float32), w_query.astype(jnp.float32), w_key.astype(jnp.float32), w_value.astype(jnp.float32), q_gain.astype(jnp.float32), k_gain.astype(jnp.float32), w_output.astype(jnp.float32), norm2_gain.astype(jnp.float32), w_router.astype(jnp.float32), expert_w.astype(jnp.float32))
    grads = pullback(grad_bal)
    block_out = output_bal.astype(jnp.bfloat16)[dest_index]
    grad_tokens = grads[0].astype(jnp.bfloat16)[dest_index]
    return (block_out, grad_tokens, grads[1], grads[2], grads[3], grads[4], grads[5], grads[6], grads[7], grads[8], grads[9], grads[10])
```

```python
import functools
import math

import jax
import jax.numpy as jnp
from jax import lax
from jax.experimental import pallas as pl
from jax.experimental.pallas import tpu as pltpu
from jax.sharding import PartitionSpec as P

norm_eps = 1e-06
rope_base = 10000.0
mask_fill = -1e30


def rms_apply(values, gain_vec):
    inverse = lax.rsqrt(jnp.mean(values * values, axis=-1, keepdims=True) + norm_eps)
    return values * inverse * gain_vec


def rope_tables(positions, width):
    half_width = width // 2
    steps_idx = jnp.arange(half_width, dtype=jnp.float32)
    freqs = jnp.exp(steps_idx * (-2.0 * math.log(rope_base) / width))
    angles = positions.astype(jnp.float32)[:, None] * freqs[None, :]
    return (jnp.cos(angles), jnp.sin(angles))


def head_prep(raw, gain_vec, cos_tab, sin_tab, heads):
    token_count = raw.shape[0]
    shaped = rms_apply(raw.reshape(token_count, heads, -1), gain_vec)
    half_width = shaped.shape[-1] // 2
    lower_half = shaped[..., :half_width]
    upper_half = shaped[..., half_width:]
    cos_rows = cos_tab[:, None, :]
    sin_rows = sin_tab[:, None, :]
    return jnp.concatenate(
        [
            lower_half * cos_rows - upper_half * sin_rows,
            upper_half * cos_rows + lower_half * sin_rows,
        ],
        axis=-1,
    )


def sequence_layout(lengths_row, count):
    seq_ends = jnp.cumsum(lengths_row)
    places = jnp.arange(count, dtype=jnp.int32)
    passed = (places[:, None] >= seq_ends[None, :]).astype(jnp.int32)
    seq_ids = jnp.sum(passed, axis=1)
    starts = jnp.sum(passed * lengths_row[None, :], axis=1)
    return (seq_ids, places - starts)


BF = jnp.bfloat16
F32 = jnp.float32


def dot(left, right, left_dim=1, right_dim=0):
    return lax.dot_general(
        left, right, (((left_dim,), (right_dim,)), ((), ())), preferred_element_type=F32
    )


def expert_kernel(side, per, rows_ref, grads_ref, w_ref, *rest):
    if side:
        y_in, dx_in = rest[:2]
        rest = rest[2:]
    y_ref, dx_ref, grad_ref, rows, rows_t, dys, dys_t, y_acc, dx_acc = rest
    step = pl.program_id(0)
    count = rows.shape[0]
    both = rows_ref.shape[0]

    def selector(shape, row_dim):
        place = lax.broadcasted_iota(jnp.int32, shape, row_dim)
        source = lax.broadcasted_iota(jnp.int32, shape, 1 - row_dim)
        return (place + (place // per + side) * per == source).astype(F32).astype(BF)

    @pl.when(step == 0)
    def _():
        pick = selector((count, both), 0)
        rows[...] = dot(pick, rows_ref[...]).astype(BF)
        dys[...] = dot(pick, grads_ref[...]).astype(BF)
        rows_t[...] = rows[...].T
        dys_t[...] = dys[...].T
        y_acc[...] = jnp.zeros_like(y_acc)
        dx_acc[...] = jnp.zeros_like(dx_acc)

    w_gate, w_up, w_down = w_ref[0, 0], w_ref[0, 1], w_ref[0, 2]
    gate = dot(rows[...], w_gate)
    up = dot(rows[...], w_up)
    d_act = dot(dys[...], w_down)
    sig = 1.0 / (1.0 + jnp.exp(-gate))
    silu = gate * sig
    act = (silu * up).astype(BF)
    d_gate = (d_act * up * sig * (1.0 + gate * (1.0 - sig))).astype(BF)
    d_up = (d_act * silu).astype(BF)
    y_acc[...] += dot(act, w_down, 1, 1)
    dx_acc[...] += dot(d_gate, w_gate, 1, 1) + dot(d_up, w_up, 1, 1)
    grad_ref[0, 0] = dot(rows_t[...], d_gate).astype(BF)
    grad_ref[0, 1] = dot(rows_t[...], d_up).astype(BF)
    grad_ref[0, 2] = dot(dys_t[...], act).astype(BF)

    @pl.when(step == pl.num_programs(0) - 1)
    def _():
        spread = selector((both, count), 1)
        y_all = dot(spread, y_acc[...].astype(BF)).astype(BF)
        dx_all = dot(spread, dx_acc[...].astype(BF)).astype(BF)
        if side:
            y_all = y_all + y_in[...]
            dx_all = dx_all + dx_in[...]
        y_ref[...] = y_all
        dx_ref[...] = dx_all


def expert_call(side, per, rows, grads, weights, earlier):
    quarters, _, width, hidden = weights.shape
    both = rows.shape[0]
    count = both // 2
    whole = pl.BlockSpec((both, width), lambda q: (0, 0), pipeline_mode=pl.Buffered(1))
    block = pl.BlockSpec((1, 3, width, hidden), lambda q: (q, 0, 0, 0))
    flops = 2 * 9 * count * width * hidden * quarters
    moved = 2 * (2 * weights.size + 4 * rows.size)
    return pl.pallas_call(
        functools.partial(expert_kernel, side, per),
        grid=(quarters,),
        out_shape=(
            jax.ShapeDtypeStruct((both, width), BF),
            jax.ShapeDtypeStruct((both, width), BF),
            jax.ShapeDtypeStruct(weights.shape, BF),
        ),
        in_specs=[whole, whole, block] + [whole] * len(earlier),
        out_specs=(whole, whole, block),
        scratch_shapes=[
            pltpu.VMEM((count, width), BF),
            pltpu.VMEM((width, count), BF),
            pltpu.VMEM((count, width), BF),
            pltpu.VMEM((width, count), BF),
            pltpu.VMEM((count, width), F32),
            pltpu.VMEM((count, width), F32),
        ],
        compiler_params=pltpu.CompilerParams(vmem_limit_bytes=60 * 1024 * 1024),
        cost_estimate=pl.CostEstimate(
            flops=flops, bytes_accessed=moved, transcendentals=count * hidden * quarters
        ),
        name=f"expert{side}",
    )(rows, grads, weights, *earlier)


def exchange(value, axis):
    return lax.all_to_all(value, axis, split_axis=0, concat_axis=0, tiled=True)


def gather_blocks(value, axis):
    return exchange(jnp.broadcast_to(value[None], (lax.axis_size(axis),) + value.shape), axis)


def side_by_side(blocks):
    return jnp.concatenate([blocks[t] for t in range(blocks.shape[0])], axis=1)


def column_blocks(value, count):
    return jnp.stack(jnp.split(value, count, axis=1))


def body(
    tokens,
    out_grad,
    seq_lengths,
    dest_index,
    routes,
    pair_order,
    norm1_gain,
    w_query,
    w_key,
    w_value,
    q_gain,
    k_gain,
    w_output,
    norm2_gain,
    w_router,
    expert_w,
):
    groups = lax.axis_size("expert")
    tensor_count = lax.axis_size("tensor")
    group_id = lax.axis_index("expert")
    tensor_id = lax.axis_index("tensor")
    tok_count, col_count = tokens.shape
    width = col_count * tensor_count
    move_rows = tok_count // groups
    expert_count = w_router.shape[1]
    top_count = routes.shape[1]
    local_experts = expert_w.shape[0]

    w_stored = jnp.transpose(expert_w, (0, 2, 1, 3))
    w_all = [lax.all_gather(w_stored[e], "tensor", axis=0) for e in range(local_experts)]

    routes_t = routes.T
    order_t = pair_order[0].reshape(tok_count, top_count).T
    pair_expert = routes_t.reshape(-1)
    pair_total = tok_count * top_count
    base = pair_expert * pair_total
    keyed = base + order_t.reshape(-1)
    before = (keyed[None, :] < keyed[:, None]) & (keyed[None, :] >= base[:, None])
    ranks = jnp.sum(before.astype(jnp.int32), axis=1).reshape(top_count, tok_count)
    expert_axis = jnp.arange(expert_count, dtype=jnp.int32)
    route_hot = routes_t[:, None, :] == expert_axis[None, :, None]
    counts = jnp.sum(route_hot.astype(F32), axis=(0, 2))

    places = jnp.arange(tok_count, dtype=jnp.int32)
    arrival_rank = jnp.sum((dest_index[None, :] < dest_index[:, None]).astype(jnp.int32), axis=1)
    by_rank = (arrival_rank[None, :] == places[:, None]).astype(BF)
    inner = jnp.broadcast_to((dest_index % tok_count).astype(BF)[:, None], (tok_count, 64))
    facts = jnp.broadcast_to(counts.astype(BF)[None, :], (tok_count, expert_count))
    outgoing = dot(by_rank, jnp.concatenate([tokens, out_grad, inner, facts], axis=1)).astype(BF)
    got = exchange(outgoing.reshape(groups, move_rows, -1), "expert")
    all_counts = got[:, 0, 2 * col_count + 64 :].astype(jnp.int32)
    lower = jnp.arange(groups, dtype=jnp.int32) < group_id
    offsets = jnp.sum(jnp.where(lower[:, None], all_counts, 0), axis=0)
    mine = got[:, :, 2 * col_count].astype(jnp.int32).reshape(-1)
    put = (mine[None, :] == places[:, None]).astype(BF)
    local = dot(put, got.reshape(tok_count, -1)[:, : 2 * col_count]).astype(BF)
    blocks = gather_blocks(local, "tensor")
    full_x = side_by_side(blocks[:, :, :col_count])
    full_dy = side_by_side(blocks[:, :, col_count:])
    x_float = full_x.astype(jnp.float32)
    dy_float = full_dy.astype(jnp.float32)
    seq_ids, positions = sequence_layout(seq_lengths[0], tok_count)
    same_seq = seq_ids[:, None] == seq_ids[None, :]
    head_dim = q_gain.shape[0]
    heads_local = w_query.shape[1] // head_dim
    scale_attn = 1.0 / math.sqrt(head_dim)
    cos_tab, sin_tab = rope_tables(positions, head_dim)
    gain_one = norm1_gain.astype(jnp.float32)
    normed_float, norm_one_back = jax.vjp(rms_apply, x_float, gain_one)
    normed = normed_float.astype(jnp.bfloat16)
    q_raw = jnp.dot(normed, w_query, preferred_element_type=jnp.float32)
    k_raw = jnp.dot(normed, w_key, preferred_element_type=jnp.float32)
    v_raw = jnp.dot(normed, w_value, preferred_element_type=jnp.float32)

    def prep_pair(query_in, key_in, qgain_in, kgain_in):
        return (
            head_prep(query_in, qgain_in, cos_tab, sin_tab, heads_local),
            head_prep(key_in, kgain_in, cos_tab, sin_tab, heads_local),
        )

    rotated, prep_back = jax.vjp(
        prep_pair, q_raw, k_raw, q_gain.astype(jnp.float32), k_gain.astype(jnp.float32)
    )
    query_b = rotated[0].astype(jnp.bfloat16)
    key_b = rotated[1].astype(jnp.bfloat16)
    value_b = v_raw.reshape(tok_count, heads_local, head_dim).astype(jnp.bfloat16)
    scores = (
        jnp.einsum("qhd,khd->hqk", query_b, key_b, preferred_element_type=jnp.float32) * scale_attn
    )
    scores = jnp.where(same_seq[None], scores, mask_fill)
    peak = jnp.max(scores, axis=-1, keepdims=True)
    log_total = peak + jnp.log(jnp.sum(jnp.exp(scores - peak), axis=-1, keepdims=True))
    probs_b = jnp.exp(scores - log_total).astype(jnp.bfloat16)
    attended = (
        jnp.einsum("hqk,khd->qhd", probs_b, value_b, preferred_element_type=jnp.float32)
        .reshape(tok_count, heads_local * head_dim)
        .astype(jnp.bfloat16)
    )
    attn_part = jnp.dot(attended, w_output, preferred_element_type=jnp.float32)
    attn_got = exchange(column_blocks(attn_part.astype(BF), tensor_count), "tensor")
    attn_sum = jnp.sum(attn_got.astype(F32), axis=0).astype(BF)
    attn_full = side_by_side(gather_blocks(attn_sum, "tensor")).astype(F32)
    resid = x_float + attn_full
    gain_two = norm2_gain.astype(jnp.float32)
    mixed_float, norm_two_back = jax.vjp(rms_apply, resid, gain_two)
    mixed_b = mixed_float.astype(jnp.bfloat16)
    logits_t = dot(w_router, mixed_b, 0, 1)
    chosen = jnp.sum(jnp.where(route_hot, logits_t[None], 0.0), axis=1)
    chosen_exp = jnp.exp(chosen - jnp.max(chosen, axis=0, keepdims=True))
    gates = chosen_exp / jnp.sum(chosen_exp, axis=0, keepdims=True)
    capacity = 5 * tok_count * groups * top_count // (4 * expert_count)
    most_rows = 3 * tok_count * top_count // (2 * expert_count)
    per = most_rows // tensor_count
    slot_global = jnp.sum(jnp.where(route_hot, offsets[None, :, None], 0), axis=1) + ranks
    kept = slot_global < capacity
    keep_mask = kept.astype(F32)
    gate_eff = gates * keep_mask

    slots = expert_count * per
    here = kept & (ranks % tensor_count == tensor_id)
    slot_of = jnp.where(here, routes_t * per + ranks // tensor_count, -1)
    slot_axis = jnp.arange(slots, dtype=jnp.int32)
    slot_hot = slot_of[:, None, :] == slot_axis[None, :, None]
    slot_pick = jnp.sum(slot_hot.astype(F32), axis=0).astype(BF)
    slot_weight = jnp.sum(jnp.where(slot_hot, gate_eff[:, None, :], 0.0), axis=0)
    slot_gate = jnp.sum(slot_weight, axis=1)
    send_rows = dot(slot_pick, mixed_b).astype(BF)
    slot_dy = dot(slot_pick, full_dy)
    send_grads = (slot_gate[:, None] * slot_dy).astype(BF)
    recv_rows, recv_grads = (
        exchange(value.reshape(groups, -1, width), "expert").reshape(slots, width)
        for value in (send_rows, send_grads)
    )
    earlier = ()
    expert_grads = []
    for e in range(local_experts):
        *earlier, partial = expert_call(e, per, recv_rows, recv_grads, w_all[e], earlier)
        expert_grads.append(lax.psum_scatter(partial, "tensor", scatter_dimension=0, tiled=False))
    ret_rows = exchange(earlier[1].reshape(groups, -1, width), "expert").reshape(slots, width)
    ret_out = exchange(earlier[0].reshape(groups, -1, width), "expert").reshape(slots, width)
    mixed_part = dot(slot_pick, ret_rows, 0, 0)
    weight_hi = slot_weight.astype(BF)
    weight_lo = (slot_weight - weight_hi.astype(F32)).astype(BF)
    moe_part = dot(weight_hi, ret_out, 0, 0) + dot(weight_lo, ret_out, 0, 0)
    dgate_slot = jnp.sum(slot_dy * ret_out.astype(F32), axis=1)
    dgate_part = jnp.sum(jnp.where(slot_hot, dgate_slot[None, :, None], 0.0), axis=1)
    dgate_block = jnp.pad(dgate_part.T.astype(BF), ((0, 0), (0, 128 - top_count)))
    leaving = jnp.concatenate(
        [
            column_blocks(moe_part.astype(BF), tensor_count),
            column_blocks(mixed_part.astype(BF), tensor_count),
            jnp.broadcast_to(dgate_block[None], (tensor_count,) + dgate_block.shape),
        ],
        axis=2,
    )
    summed_t = jnp.sum(exchange(leaving, "tensor").astype(F32), axis=0)
    moe_slice = summed_t[:, :col_count]
    mixed_slice = summed_t[:, col_count : 2 * col_count].astype(BF)
    dgate_full = summed_t[:, 2 * col_count : 2 * col_count + top_count].T
    mixed_experts = side_by_side(gather_blocks(mixed_slice, "tensor")).astype(F32)
    resid_slice = lax.dynamic_slice_in_dim(resid, tensor_id * col_count, col_count, 1)
    out_slice = (resid_slice + moe_slice).astype(BF)
    d_gates = dgate_full * keep_mask
    d_chosen = gates * (d_gates - jnp.sum(gates * d_gates, axis=0, keepdims=True))
    d_logits = jnp.sum(jnp.where(route_hot, d_chosen[:, None, :], 0.0), axis=0).astype(BF)
    router_grad = dot(mixed_b, d_logits, 0, 1)
    d_mixed = mixed_experts + dot(d_logits, w_router, 0, 1)
    d_resid_norm, gain_two_grad = norm_two_back(d_mixed)
    d_resid = dy_float + d_resid_norm
    d_resid_b = d_resid.astype(jnp.bfloat16)
    out_proj_grad = jnp.einsum("pa,pd->ad", attended, d_resid_b, preferred_element_type=jnp.float32)
    d_att = (
        jnp.einsum("pd,ad->pa", d_resid_b, w_output, preferred_element_type=jnp.float32)
        .astype(jnp.bfloat16)
        .reshape(tok_count, heads_local, head_dim)
    )
    scores_again = (
        jnp.einsum("qhd,khd->hqk", query_b, key_b, preferred_element_type=jnp.float32) * scale_attn
    )
    scores_again = jnp.where(same_seq[None], scores_again, mask_fill)
    probs_again = jnp.exp(scores_again - log_total)
    probs_again_b = probs_again.astype(jnp.bfloat16)
    d_probs = jnp.einsum("qhd,khd->hqk", d_att, value_b, preferred_element_type=jnp.float32)
    delta = jnp.sum(probs_again * d_probs, axis=-1, keepdims=True)
    d_scores = (probs_again * (d_probs - delta)).astype(jnp.bfloat16)
    d_query = (
        jnp.einsum("hqk,khd->qhd", d_scores, key_b, preferred_element_type=jnp.float32) * scale_attn
    )
    d_key = (
        jnp.einsum("hqk,qhd->khd", d_scores, query_b, preferred_element_type=jnp.float32)
        * scale_attn
    )
    d_value = (
        jnp.einsum("hqk,qhd->khd", probs_again_b, d_att, preferred_element_type=jnp.float32)
        .reshape(tok_count, -1)
        .astype(jnp.bfloat16)
    )
    d_qraw, d_kraw, qgain_part, kgain_part = prep_back((d_query, d_key))
    d_qraw_b = d_qraw.astype(jnp.bfloat16)
    d_kraw_b = d_kraw.astype(jnp.bfloat16)
    d_normed = jnp.einsum("pa,da->pd", d_qraw_b, w_query, preferred_element_type=jnp.float32)
    d_normed = d_normed + jnp.einsum(
        "pa,da->pd", d_kraw_b, w_key, preferred_element_type=jnp.float32
    )
    d_normed = d_normed + jnp.einsum(
        "pa,da->pd", d_value, w_value, preferred_element_type=jnp.float32
    )
    query_grad = jnp.einsum("pd,pa->da", normed, d_qraw_b, preferred_element_type=jnp.float32)
    key_grad = jnp.einsum("pd,pa->da", normed, d_kraw_b, preferred_element_type=jnp.float32)
    value_grad = jnp.einsum("pd,pa->da", normed, d_value, preferred_element_type=jnp.float32)
    normed_got = exchange(column_blocks(d_normed.astype(BF), tensor_count), "tensor")
    normed_sum = jnp.sum(normed_got.astype(F32), axis=0).astype(BF)
    d_normed_full = side_by_side(gather_blocks(normed_sum, "tensor")).astype(F32)
    d_x_norm, gain_one_grad = norm_one_back(d_normed_full)
    d_tokens = d_resid + d_x_norm
    summed = tuple(
        lax.psum(value.astype(BF), axes).astype(F32)
        for value, axes in (
            (query_grad, "expert"),
            (key_grad, "expert"),
            (value_grad, "expert"),
            (out_proj_grad, "expert"),
            (router_grad, "expert"),
            (gain_one_grad, "expert"),
            (gain_two_grad, "expert"),
            (qgain_part, ("expert", "tensor")),
            (kgain_part, ("expert", "tensor")),
        )
    )
    dx_slice = lax.dynamic_slice_in_dim(d_tokens, tensor_id * col_count, col_count, 1).astype(BF)
    going = dot(put, jnp.concatenate([out_slice, dx_slice], axis=1), 0, 0).astype(BF)
    back = exchange(going.reshape(groups, move_rows, -1), "expert").reshape(tok_count, -1)
    back = dot(by_rank, back, 0, 0).astype(BF)
    block_out = back[:, :col_count]
    grad_tokens = back[:, col_count:]
    expert_grad = jnp.transpose(jnp.stack(expert_grads).astype(F32), (0, 2, 1, 3))
    return (
        block_out,
        grad_tokens,
        summed[5],
        summed[0],
        summed[1],
        summed[2],
        summed[7],
        summed[8],
        summed[3],
        summed[6],
        summed[4],
        expert_grad,
    )


def solution(mesh):
    in_specs = (
        P("expert", "tensor"),
        P("expert", "tensor"),
        P("expert", None),
        P("expert"),
        P("expert", None),
        P("expert", None),
        P(),
        P(None, "tensor"),
        P(None, "tensor"),
        P(None, "tensor"),
        P(),
        P(),
        P("tensor", None),
        P(),
        P(),
        P("expert", None, None, "tensor"),
    )
    out_specs = (
        P("expert", "tensor"),
        P("expert", "tensor"),
        P(),
        P(None, "tensor"),
        P(None, "tensor"),
        P(None, "tensor"),
        P(),
        P(),
        P("tensor", None),
        P(),
        P(),
        P("expert", None, None, "tensor"),
    )
    return jax.shard_map(body, mesh=mesh, in_specs=in_specs, out_specs=out_specs, check_vma=False)
```

```python
import functools
import math

import jax
import jax.numpy as jnp
from jax import lax
from jax.experimental import pallas as pl
from jax.experimental.pallas import tpu as pltpu
from jax.sharding import PartitionSpec as P

norm_eps = 1e-06
rope_base = 10000.0
mask_fill = -1e30


def rope_tables(positions, width):
    half_width = width // 2
    steps_idx = jnp.arange(half_width, dtype=jnp.float32)
    freqs = jnp.exp(steps_idx * (-2.0 * math.log(rope_base) / width))
    angles = positions.astype(jnp.float32)[:, None] * freqs[None, :]
    return (jnp.cos(angles), jnp.sin(angles))


def sequence_layout(lengths_row, count):
    seq_ends = jnp.cumsum(lengths_row)
    places = jnp.arange(count, dtype=jnp.int32)
    passed = (places[:, None] >= seq_ends[None, :]).astype(jnp.int32)
    seq_ids = jnp.sum(passed, axis=1)
    starts = jnp.sum(passed * lengths_row[None, :], axis=1)
    return (seq_ids, places - starts)


BF = jnp.bfloat16
F32 = jnp.float32


def dot(left, right, left_dim=1, right_dim=0):
    return lax.dot_general(
        left, right, (((left_dim,), (right_dim,)), ((), ())), preferred_element_type=F32
    )


def exchange(value, axis):
    return lax.all_to_all(value, axis, split_axis=0, concat_axis=0, tiled=True)


def gather_blocks(value, axis):
    return exchange(jnp.broadcast_to(value[None], (lax.axis_size(axis),) + value.shape), axis)


def column_blocks(value, count):
    return jnp.stack(jnp.split(value, count, axis=1))


MESH = pl.DeviceIdType.MESH


def tensor_peers():
    me = lax.axis_index("tensor")
    count = lax.axis_size("tensor")
    return me, [(me + d) % count for d in range(1, count)]


def greet(axis, peers):
    barrier = pltpu.get_barrier_semaphore()
    for peer in peers:
        pl.semaphore_signal(barrier, inc=1, device_id={axis: peer}, device_id_type=MESH)
    return lambda: pl.semaphore_wait(barrier, len(peers))


class Post:
    def __init__(self, axis, send_sem, recv_sem):
        self.axis, self.send_sem, self.recv_sem = axis, send_sem, recv_sem
        self.started = []
        self.used = 0

    def push(self, source, target, peer):
        slot = self.used
        self.used += 1
        copy = pltpu.make_async_remote_copy(
            src_ref=source,
            dst_ref=target,
            send_sem=self.send_sem.at[slot],
            recv_sem=self.recv_sem.at[slot],
            device_id={self.axis: peer},
            device_id_type=MESH,
        )
        copy.start()
        self.started.append(copy)
        return copy

    def finish(self):
        for copy in self.started:
            copy.wait_send()
        self.started = []


def arrive(copies):
    for copy in copies:
        copy.wait_recv()


def fetch(pairs, sem):
    copies = [
        pltpu.make_async_copy(source, target, sem.at[n]) for n, (source, target) in enumerate(pairs)
    ]
    for copy in copies:
        copy.start()
    return copies


def turn(value, cos_rows, sin_rows):
    return value * cos_rows + pltpu.roll(value, value.shape[-1] // 2, 1) * sin_rows


def inverse_rms(total, width):
    return lax.rsqrt(total * (1.0 / width) + norm_eps)


def row_sum(value):
    return jnp.sum(value, axis=1, keepdims=True)


def softmax_rows(query, key, bias, scale):
    scores = dot(query, key, 1, 1) * scale + bias
    grown = jnp.exp(scores - jnp.max(scores, axis=1, keepdims=True))
    return grown / row_sum(grown)


def front_kernel(
    local, bias, cos_rows, sin_rows, gain1, gain2, q_gain, k_gain, router_t, routes, slot_of, keep,
    wq_hbm, wk_hbm, wv_hbm, wo_hbm,
    x_out, dy_out, an_out, resid_out, mixed_out, q_out, k_out, qh_out, kh_out, vh_out, ob_out,
    gates_out, send_out, send_dy_out, pick_out,
    wq, wk, wv, wo, x_all, dy_all, parts, box, total, load_sem, send_sem, recv_sem,
):
    me, peers = tensor_peers()
    ready = greet("tensor", peers)
    loads = fetch([(wq_hbm, wq), (wk_hbm, wk), (wv_hbm, wv), (wo_hbm, wo)], load_sem)
    blocks, tok, col = x_all.shape
    width = blocks * col
    x_all[me] = local[:, :col]
    dy_all[me] = local[:, col:]
    ready()
    post = Post("tensor", send_sem, recv_sem)
    x_in = [post.push(x_all.at[me], x_all.at[me], peer) for peer in peers]
    dy_in = [post.push(dy_all.at[me], dy_all.at[me], peer) for peer in peers]
    arrive(x_in)
    square = jnp.zeros((tok, 1), F32)
    for t in range(blocks):
        value = x_all[t].astype(F32)
        square = square + row_sum(value * value)
    r1 = inverse_rms(square, width)
    for t in range(blocks):
        an_out[t] = (x_all[t].astype(F32) * r1 * gain1[t : t + 1, :]).astype(BF)
    x_out[...] = x_all[...]

    for copy in loads:
        copy.wait()

    def project(weight):
        value = dot(an_out[0], weight[0:col, :])
        for t in range(1, blocks):
            value = value + dot(an_out[t], weight[t * col : (t + 1) * col, :])
        return value

    q_out[...] = project(wq)
    k_out[...] = project(wk)
    vh_out[...] = project(wv).astype(BF)
    head = q_gain.shape[1]
    scale = 1.0 / math.sqrt(head)
    for h in range(col // head):
        lanes = slice(h * head, (h + 1) * head)
        for raw, gain, rotated in ((q_out, q_gain, qh_out), (k_out, k_gain, kh_out)):
            value = raw[:, lanes]
            value = value * inverse_rms(row_sum(value * value), head) * gain[...]
            rotated[:, lanes] = turn(value, cos_rows[...], sin_rows[...]).astype(BF)
        probs = softmax_rows(qh_out[:, lanes], kh_out[:, lanes], bias[...], scale).astype(BF)
        ob_out[:, lanes] = dot(probs, vh_out[:, lanes]).astype(BF)
    for t in range(blocks):
        parts[t] = dot(ob_out[...], wo[:, t * col : (t + 1) * col]).astype(BF)
    arrive([post.push(parts.at[peer], box.at[d], peer) for d, peer in enumerate(peers)])
    summed = parts[me].astype(F32)
    for d in range(blocks - 1):
        summed = summed + box[d].astype(F32)
    total[me] = summed.astype(BF)
    arrive([post.push(total.at[me], total.at[me], peer) for peer in peers])
    square = jnp.zeros((tok, 1), F32)
    for t in range(blocks):
        value = x_all[t].astype(F32) + total[t].astype(F32)
        resid_out[t] = value
        square = square + row_sum(value * value)
    r2 = inverse_rms(square, width)
    logits = jnp.zeros((router_t.shape[0], tok), F32)
    for t in range(blocks):
        mixed_out[t] = (resid_out[t] * r2 * gain2[t : t + 1, :]).astype(BF)
        logits = logits + dot(router_t[:, t * col : (t + 1) * col], mixed_out[t], 1, 1)
    expert = lax.broadcasted_iota(jnp.int32, logits.shape, 0)
    top = routes.shape[0]
    chosen = [
        jnp.sum(jnp.where(routes[k : k + 1, :] == expert, logits, 0.0), axis=0, keepdims=True)
        for k in range(top)
    ]
    peak = functools.reduce(jnp.maximum, chosen)
    grown = [jnp.exp(value - peak) for value in chosen]
    whole = functools.reduce(jnp.add, grown)
    slots = send_out.shape[0]
    slot = lax.broadcasted_iota(jnp.int32, (slots, tok), 0)
    pick = jnp.zeros((slots, tok), F32)
    weight = jnp.zeros((slots, tok), F32)
    for k in range(top):
        gate = grown[k] / whole
        gates_out[k : k + 1, :] = gate
        hot = slot_of[k : k + 1, :] == slot
        pick = jnp.where(hot, 1.0, pick)
        weight = jnp.where(hot, gate * keep[k : k + 1, :], weight)
    pick_out[...] = pick.T.astype(BF)
    pick = pick.astype(BF)
    for t in range(blocks):
        send_out[:, t * col : (t + 1) * col] = dot(pick, mixed_out[t]).astype(BF)
    gate = row_sum(weight)
    first = gate.astype(BF)
    second = (gate - first.astype(F32)).astype(BF)
    third = (gate - first.astype(F32) - second.astype(F32)).astype(BF)
    lane = lax.broadcasted_iota(jnp.int32, (slots, 128), 1)
    facts = jnp.zeros((slots, 128), F32)
    for n, piece in enumerate((first, second, third)):
        facts = jnp.where(lane == n, piece.astype(F32), facts)
    send_out[:, width:] = facts.astype(BF)
    arrive(dy_in)
    dy_out[...] = dy_all[...]
    for t in range(blocks):
        send_dy_out[:, t * col : (t + 1) * col] = dot(pick, dy_all[t]).astype(BF)
    post.finish()


def front_call(local, bias, cos_rows, sin_rows, gain1, gain2, q_gain, k_gain, router_t, routes,
               slot_of, keep, weights, slots):
    tok, both = local.shape
    col = both // 2
    blocks = gain1.shape[0]
    width = col * blocks
    shape = jax.ShapeDtypeStruct
    vmem = pl.BlockSpec(memory_space=pltpu.VMEM)
    tiles = (blocks, tok, col)
    top = routes.shape[0]
    return pl.pallas_call(
        front_kernel,
        out_shape=(
            shape(tiles, BF), shape(tiles, BF), shape(tiles, BF), shape(tiles, F32),
            shape(tiles, BF), shape((tok, col), F32), shape((tok, col), F32),
            shape((tok, col), BF), shape((tok, col), BF), shape((tok, col), BF),
            shape((tok, col), BF), shape((top, tok), F32), shape((slots, width + 128), BF),
            shape((slots, width), BF), shape((tok, slots), BF),
        ),
        in_specs=[vmem] * 12 + [pl.BlockSpec(memory_space=pl.ANY)] * 4,
        out_specs=(vmem,) * 15,
        scratch_shapes=[
            pltpu.VMEM((width, col), BF), pltpu.VMEM((width, col), BF), pltpu.VMEM((width, col), BF),
            pltpu.VMEM((col, width), BF),
            pltpu.VMEM(tiles, BF), pltpu.VMEM(tiles, BF), pltpu.VMEM(tiles, BF),
            pltpu.VMEM((blocks - 1, tok, col), BF), pltpu.VMEM(tiles, BF),
            pltpu.SemaphoreType.DMA((4,)),
            pltpu.SemaphoreType.DMA((12,)), pltpu.SemaphoreType.DMA((12,)),
        ],
        compiler_params=pltpu.CompilerParams(
            collective_id=1, has_side_effects=True, vmem_limit_bytes=56 * 1024 * 1024
        ),
        name="front",
    )(local, bias, cos_rows, sin_rows, gain1, gain2, q_gain, k_gain, router_t, routes, slot_of,
      keep, *weights)


def back_kernel(
    pick_t, ret, slot_of, keep, gates, routes, bias, cos_rows, sin_rows, gain1, gain2, q_gain,
    k_gain, router, resid, dy_all, x_all, mixed, qh, kh, vh, ob,
    q_hbm, k_hbm, an_hbm, wq_hbm, wk_hbm, wv_hbm, wo_hbm,
    grads, dx_out, small_out,
    q_raw, k_raw, an, wq, wk, wv, wo, parts, box, total, dm, dr, d_qkv, d_att,
    dg_mine, dg_box, note, load_sem, send_sem, recv_sem,
):
    me, peers = tensor_peers()
    ready = greet("tensor", peers)
    loads = fetch(
        [(wo_hbm, wo), (q_hbm, q_raw), (k_hbm, k_raw), (wq_hbm, wq), (wk_hbm, wk), (wv_hbm, wv),
         (an_hbm, an)],
        load_sem,
    )
    blocks, tok, col = parts.shape
    width = blocks * col
    post = Post("tensor", send_sem, recv_sem)
    for t in range(blocks):
        parts[t] = dot(pick_t[...], ret[:, t * col : (t + 1) * col]).astype(BF)
    ready()
    part_in = [post.push(parts.at[peer], box.at[d], peer) for d, peer in enumerate(peers)]
    slots = ret.shape[0]
    dgate = row_sum(ret[:, width : width + 128].astype(F32))
    slot = lax.broadcasted_iota(jnp.int32, (slots, tok), 0)
    top = routes.shape[0]
    for k in range(top):
        hot = slot_of[k : k + 1, :] == slot
        dg_mine[k : k + 1, :] = jnp.sum(jnp.where(hot, dgate, 0.0), axis=0, keepdims=True)
    dg_in = [post.push(dg_mine, dg_box.at[d], peer) for d, peer in enumerate(peers)]
    arrive(part_in)
    summed = parts[me].astype(F32)
    for d in range(blocks - 1):
        summed = summed + box[d].astype(F32)
    total[me] = summed.astype(BF)
    total_in = [post.push(total.at[me], total.at[me], peer) for peer in peers]

    arrive(dg_in)
    d_gates = dg_mine[...]
    for d in range(blocks - 1):
        d_gates = d_gates + dg_box[d]
    d_gates = d_gates * keep[...]
    gate = gates[...]
    d_chosen = gate * (d_gates - jnp.sum(gate * d_gates, axis=0, keepdims=True))
    expert = lax.broadcasted_iota(jnp.int32, (router.shape[1], tok), 0)
    d_logits_t = jnp.zeros(expert.shape, F32)
    for k in range(top):
        hot = routes[k : k + 1, :] == expert
        d_logits_t = jnp.where(hot, d_chosen[k : k + 1, :], d_logits_t)
    d_logits = d_logits_t.T.astype(BF)
    square = jnp.zeros((tok, 1), F32)
    for t in range(blocks):
        rows = slice(t * col, (t + 1) * col)
        grads[rows, 4 * col :] = dot(mixed[t].T, d_logits).astype(BF)
        dm[t] = dot(d_logits, router[rows, :], 1, 1)
        square = square + row_sum(resid[t] * resid[t])
    r2 = inverse_rms(square, width)
    arrive(total_in)
    cross = jnp.zeros((tok, 1), F32)
    for t in range(blocks):
        dm[t] = dm[t] + total[t].astype(F32)
        cross = cross + row_sum(resid[t] * gain2[t : t + 1, :] * dm[t])
    cross = cross * (1.0 / width) * r2 * r2 * r2
    for t in range(blocks):
        d_mixed = dm[t]
        small_out[4 + t : 5 + t, :] = jnp.sum(d_mixed * resid[t] * r2, axis=0, keepdims=True)
        d_resid = dy_all[t].astype(F32) + r2 * gain2[t : t + 1, :] * d_mixed - resid[t] * cross
        dm[t] = d_resid
        dr[t] = d_resid.astype(BF)
    for copy in loads:
        copy.wait()
    value = dot(dr[0], wo[:, 0:col], 1, 1)
    for t in range(1, blocks):
        value = value + dot(dr[t], wo[:, t * col : (t + 1) * col], 1, 1)
    d_att[...] = value.astype(BF)

    head = q_gain.shape[1]
    scale = 1.0 / math.sqrt(head)
    q_part = jnp.zeros((1, head), F32)
    k_part = jnp.zeros((1, head), F32)

    def unturn(grown, raw, gain):
        d_unit = grown * cos_rows[...] - pltpu.roll(grown, head // 2, 1) * sin_rows[...]
        inverse = inverse_rms(row_sum(raw * raw), head)
        unit = raw * inverse
        gain_part = jnp.sum(d_unit * unit, axis=0, keepdims=True)
        d_unit = d_unit * gain[...]
        d_raw = inverse * (d_unit - unit * (row_sum(unit * d_unit) * (1.0 / head)))
        return d_raw.astype(BF), gain_part

    for h in range(col // head):
        lanes = slice(h * head, (h + 1) * head)
        probs = softmax_rows(qh[:, lanes], kh[:, lanes], bias[...], scale)
        d_head = d_att[:, lanes]
        d_probs = dot(d_head, vh[:, lanes], 1, 1)
        d_scores = probs * (d_probs - row_sum(probs * d_probs))
        d_qkv[:, 2 * col + h * head : 2 * col + (h + 1) * head] = dot(
            probs.T.astype(BF), d_head
        ).astype(BF)
        d_q, part = unturn(dot(d_scores.astype(BF), kh[:, lanes]) * scale, q_raw[:, lanes], q_gain)
        q_part = q_part + part
        d_qkv[:, lanes] = d_q
        d_k, part = unturn(dot(d_scores.T.astype(BF), qh[:, lanes]) * scale, k_raw[:, lanes], k_gain)
        k_part = k_part + part
        d_qkv[:, col + h * head : col + (h + 1) * head] = d_k
    post.finish()
    for t in range(blocks):
        rows = slice(t * col, (t + 1) * col)
        parts[t] = (
            dot(d_qkv[:, 0:col], wq[rows, :], 1, 1)
            + dot(d_qkv[:, col : 2 * col], wk[rows, :], 1, 1)
            + dot(d_qkv[:, 2 * col : 3 * col], wv[rows, :], 1, 1)
        ).astype(BF)
    again = [post.push(parts.at[peer], box.at[blocks - 1 + d], peer) for d, peer in enumerate(peers)]
    for t in range(blocks):
        rows = slice(t * col, (t + 1) * col)
        grads[rows, : 3 * col] = dot(an[t].T, d_qkv[...]).astype(BF)
        grads[rows, 3 * col : 4 * col] = dot(dr[t].T, ob[...]).astype(BF)
    square = jnp.zeros((tok, 1), F32)
    for t in range(blocks):
        value = x_all[t].astype(F32)
        square = square + row_sum(value * value)
    r1 = inverse_rms(square, width)
    arrive(again)
    d_an = parts[me].astype(F32)
    for d in range(blocks - 1):
        d_an = d_an + box[blocks - 1 + d].astype(F32)
    x_mine = x_all[me].astype(F32)
    grown = gain1[pl.ds(me, 1), :] * d_an
    mean_part = row_sum(x_mine * grown)
    note[me, 0:8, :] = jnp.broadcast_to(
        jnp.sum(d_an * x_mine * r1, axis=0, keepdims=True), (8, col)
    )
    note[me, 8:16, 0:tok] = jnp.broadcast_to(mean_part, (tok, 128)).T[0:8, :]
    note[me, 8:16, tok : tok + head] = jnp.broadcast_to(q_part, (8, head))
    note[me, 8:16, tok + head : tok + 2 * head] = jnp.broadcast_to(k_part, (8, head))
    arrive([post.push(note.at[me], note.at[me], peer) for peer in peers])
    facts = note[0, 8:16, :]
    for t in range(1, blocks):
        facts = facts + note[t, 8:16, :]
    for t in range(blocks):
        small_out[t : t + 1, :] = note[t, 0:1, :]
    small_out[8:16, :] = facts
    mean = jnp.broadcast_to(facts[0:1, 0:tok], (128, tok)).T[:, 0:1] * (1.0 / width)
    dx_out[...] = (dm[me] + r1 * grown - x_mine * (r1 * r1 * r1 * mean)).astype(BF)
    post.finish()


def back_call(pick_t, ret, slot_of, keep, gates, routes, bias, cos_rows, sin_rows, gain1, gain2,
              q_gain, k_gain, router, resid, dy_all, x_all, mixed, qh, kh, vh, ob, q_raw, k_raw,
              an, weights):
    blocks, tok, col = x_all.shape
    width = blocks * col
    tiles = (blocks, tok, col)
    shape = jax.ShapeDtypeStruct
    vmem = pl.BlockSpec(memory_space=pltpu.VMEM)
    top = routes.shape[0]
    count = 5 * (blocks - 1)
    return pl.pallas_call(
        back_kernel,
        out_shape=(
            shape((width, 4 * col + 128), BF), shape((tok, col), BF), shape((16, col), F32),
        ),
        in_specs=[vmem] * 22 + [pl.BlockSpec(memory_space=pl.ANY)] * 7,
        out_specs=(vmem,) * 3,
        scratch_shapes=[
            pltpu.VMEM((tok, col), F32), pltpu.VMEM((tok, col), F32), pltpu.VMEM(tiles, BF),
            pltpu.VMEM((width, col), BF), pltpu.VMEM((width, col), BF), pltpu.VMEM((width, col), BF),
            pltpu.VMEM((col, width), BF),
            pltpu.VMEM(tiles, BF), pltpu.VMEM((2 * (blocks - 1), tok, col), BF),
            pltpu.VMEM(tiles, BF), pltpu.VMEM(tiles, F32), pltpu.VMEM(tiles, BF),
            pltpu.VMEM((tok, 3 * col), BF), pltpu.VMEM((tok, col), BF),
            pltpu.VMEM((top, tok), F32), pltpu.VMEM((blocks - 1, top, tok), F32),
            pltpu.VMEM((blocks, 16, col), F32),
            pltpu.SemaphoreType.DMA((7,)),
            pltpu.SemaphoreType.DMA((count,)), pltpu.SemaphoreType.DMA((count,)),
        ],
        compiler_params=pltpu.CompilerParams(
            collective_id=2, has_side_effects=True, vmem_limit_bytes=60 * 1024 * 1024
        ),
        name="back",
    )(pick_t, ret, slot_of, keep, gates, routes, bias, cos_rows, sin_rows, gain1, gain2, q_gain,
      k_gain, router, resid, dy_all, x_all, mixed, qh, kh, vh, ob, q_raw, k_raw, an, *weights)


def expert_kernel(side, per, rows_ref, grads_ref, w_ref, *rest):
    if side:
        y_in, dx_in = rest[:2]
        rest = rest[2:]
    y_ref, dx_ref, grad_ref, rows, rows_t, dys, dys_t, y_acc, dx_acc, gate_of, dgate = rest
    step = pl.program_id(0)
    count = rows.shape[0]
    both = rows_ref.shape[0]

    def selector(shape, row_dim):
        place = lax.broadcasted_iota(jnp.int32, shape, row_dim)
        source = lax.broadcasted_iota(jnp.int32, shape, 1 - row_dim)
        return (place + (place // per + side) * per == source).astype(F32).astype(BF)

    @pl.when(step == 0)
    def _():
        pick = selector((count, both), 0)
        width = rows.shape[1]
        rows[...] = dot(pick, rows_ref[:, :width]).astype(BF)
        gate_of[...] = row_sum(dot(pick, rows_ref[:, width:]))
        dy_rows = dot(pick, grads_ref[...])
        dys[...] = dy_rows.astype(BF)
        rows_t[...] = rows[...].T
        dys_t[...] = (dy_rows * gate_of[...]).astype(BF).T
        dgate[...] = jnp.zeros_like(dgate)
        y_acc[...] = jnp.zeros_like(y_acc)
        dx_acc[...] = jnp.zeros_like(dx_acc)

    w_gate, w_up, w_down = w_ref[0, 0], w_ref[0, 1], w_ref[0, 2]
    gate = dot(rows[...], w_gate)
    up = dot(rows[...], w_up)
    d_raw = dot(dys[...], w_down)
    d_act = d_raw * gate_of[...]
    sig = 1.0 / (1.0 + jnp.exp(-gate))
    silu = gate * sig
    act = (silu * up).astype(BF)
    dgate[...] += row_sum(act.astype(F32) * d_raw)
    d_gate = (d_act * up * sig * (1.0 + gate * (1.0 - sig))).astype(BF)
    d_up = (d_act * silu).astype(BF)
    y_acc[...] += dot(act, w_down, 1, 1)
    dx_acc[...] += dot(d_gate, w_gate, 1, 1) + dot(d_up, w_up, 1, 1)
    grad_ref[0, 0] = dot(rows_t[...], d_gate).astype(BF)
    grad_ref[0, 1] = dot(rows_t[...], d_up).astype(BF)
    grad_ref[0, 2] = dot(dys_t[...], act).astype(BF)

    @pl.when(step == pl.num_programs(0) - 1)
    def _():
        spread = selector((both, count), 1)
        width = rows.shape[1]
        first = dgate[...].astype(BF).astype(F32)
        lane = lax.broadcasted_iota(jnp.int32, (count, 128), 1)
        facts = jnp.where(lane == 0, first, jnp.where(lane == 1, dgate[...] - first, 0.0))
        y_all = dot(spread, (y_acc[...] * gate_of[...]).astype(BF)).astype(BF)
        dx_all = dot(spread, dx_acc[...].astype(BF)).astype(BF)
        facts = dot(spread, facts.astype(BF)).astype(BF)
        if side:
            y_all = y_all + y_in[...]
            dx_all = dx_all + dx_in[:, :width]
            facts = facts + dx_in[:, width:]
        y_ref[...] = y_all
        dx_ref[:, :width] = dx_all
        dx_ref[:, width:] = facts


def expert_call(side, per, rows, grads, weights, earlier):
    quarters, _, width, hidden = weights.shape
    both = rows.shape[0]
    count = both // 2
    whole = pl.BlockSpec((both, width), lambda q: (0, 0), pipeline_mode=pl.Buffered(1))
    wider = pl.BlockSpec((both, width + 128), lambda q: (0, 0), pipeline_mode=pl.Buffered(1))
    block = pl.BlockSpec((1, 3, width, hidden), lambda q: (q, 0, 0, 0))
    flops = 2 * 9 * count * width * hidden * quarters
    moved = 2 * (2 * weights.size + 4 * rows.size)
    return pl.pallas_call(
        functools.partial(expert_kernel, side, per),
        grid=(quarters,),
        out_shape=(
            jax.ShapeDtypeStruct((both, width), BF),
            jax.ShapeDtypeStruct((both, width + 128), BF),
            jax.ShapeDtypeStruct(weights.shape, BF),
        ),
        in_specs=[wider, whole, block] + [whole, wider][: len(earlier)],
        out_specs=(whole, wider, block),
        scratch_shapes=[
            pltpu.VMEM((count, width), BF),
            pltpu.VMEM((width, count), BF),
            pltpu.VMEM((count, width), BF),
            pltpu.VMEM((width, count), BF),
            pltpu.VMEM((count, width), F32),
            pltpu.VMEM((count, width), F32),
            pltpu.VMEM((count, 1), F32),
            pltpu.VMEM((count, 1), F32),
        ],
        compiler_params=pltpu.CompilerParams(vmem_limit_bytes=60 * 1024 * 1024),
        cost_estimate=pl.CostEstimate(
            flops=flops, bytes_accessed=moved, transcendentals=count * hidden * quarters
        ),
        name=f"expert{side}",
    )(rows, grads, weights, *earlier)


def plane():
    me = lax.axis_index("expert")
    core, z, y = me % 2, (me // 2) % 4, me // 8
    return [
        (core, me + 1 - 2 * core),
        ((y + y // 2) % 2, me + 8 * (1 - 2 * (y % 2))),
        (y // 2, me + 8 * (3 - 2 * y)),
        ((z + z // 2) % 2, me + 2 * (1 - 2 * (z % 2))),
        (z // 2, me + 2 * (3 - 2 * z)),
    ]

ORDERS = ((1, 3, 2, 4), (3, 2, 4, 1), (2, 4, 1, 3), (4, 1, 3, 2))

def reduce_kernel(part, out, buf, box, got, load_sem, out_sem, send_sem, recv_sem):
    dims = plane()
    barrier = pltpu.get_barrier_semaphore()
    for _, partner in dims:
        pl.semaphore_signal(barrier, inc=1, device_id={"expert": partner}, device_id_type=MESH)
    load = pltpu.make_async_copy(part, buf, load_sem)
    load.start()
    pl.semaphore_wait(barrier, len(dims))
    load.wait()
    core = dims[0][0]
    sends = []

    def push(slot, source, target, partner):
        copy = pltpu.make_async_remote_copy(
            src_ref=source, dst_ref=target, send_sem=send_sem.at[slot], recv_sem=recv_sem.at[slot],
            device_id={"expert": partner}, device_id_type=MESH)
        copy.start()
        sends.append(copy)
        return copy

    def add(target, target_at, place, first, count):
        def one(i, _):
            total = buf[place + i].astype(F32) + box[first + i].astype(F32)
            target[target_at + i] = total.astype(BF)
            return 0
        lax.fori_loop(0, count, one, 0)

    copies = []
    for s in range(4):
        copies.append(push(s, buf.at[pl.ds((1 - core) * 64 + s * 16, 16)], box.at[pl.ds(31 * s, 16)], dims[0][1]))
    place = [core * 64 + s * 16 for s in range(4)]
    for s in range(4):
        copies[s].wait_recv()
        add(buf, place[s], place[s], 31 * s, 16)
        bit, partner = dims[ORDERS[s][0]]
        copies[s] = push(4 + s, buf.at[pl.ds(place[s] + (1 - bit) * 8, 8)], box.at[pl.ds(31 * s + 16, 8)], partner)
        place[s] = place[s] + bit * 8
    size, first = 8, 16
    for k in range(1, 5):
        for s in range(4):
            copies[s].wait_recv()
            if k < 4:
                add(buf, place[s], place[s], 31 * s + first, size)
                bit, partner = dims[ORDERS[s][k]]
                half = size // 2
                copies[s] = push(4 * (k + 1) + s, buf.at[pl.ds(place[s] + (1 - bit) * half, half)],
                                 box.at[pl.ds(31 * s + first + size, half)], partner)
                place[s] = place[s] + bit * half
            else:
                add(got, place[s], place[s], 31 * s + first, 1)
                bit, partner = dims[ORDERS[s][3]]
                here = got.at[pl.ds(place[s], 1)]
                copies[s] = push(20 + s, here, here, partner)
        first, size = first + size, size // 2
    size = 1
    for k in range(3, -1, -1):
        for s in range(4):
            copies[s].wait_recv()
            bit, _ = dims[ORDERS[s][k]]
            place[s] = place[s] - bit * size
            if k:
                _, partner = dims[ORDERS[s][k - 1]]
            else:
                partner = dims[0][1]
            here = got.at[pl.ds(place[s], 2 * size)]
            copies[s] = push(20 + 4 * (4 - k) + s, here, here, partner)
        size *= 2
    for s in range(4):
        copies[s].wait_recv()
    store = pltpu.make_async_copy(got, out, out_sem)
    store.start()
    for copy in sends:
        copy.wait_send()
    store.wait()

def reduce_call(part):
    chunks, rows, cols = part.shape
    return pl.pallas_call(
        reduce_kernel,
        out_shape=jax.ShapeDtypeStruct(part.shape, BF),
        in_specs=[pl.BlockSpec(memory_space=pl.ANY)],
        out_specs=pl.BlockSpec(memory_space=pl.ANY),
        scratch_shapes=[
            pltpu.VMEM(part.shape, BF),
            pltpu.VMEM((124, rows, cols), BF),
            pltpu.VMEM(part.shape, BF),
            pltpu.SemaphoreType.DMA, pltpu.SemaphoreType.DMA,
            pltpu.SemaphoreType.DMA((40,)), pltpu.SemaphoreType.DMA((40,)),
        ],
        compiler_params=pltpu.CompilerParams(collective_id=3, has_side_effects=True, vmem_limit_bytes=48*1024*1024),
        name="reduce",
    )(part)


def body(
    tokens,
    out_grad,
    seq_lengths,
    dest_index,
    routes,
    pair_order,
    norm1_gain,
    w_query,
    w_key,
    w_value,
    q_gain,
    k_gain,
    w_output,
    norm2_gain,
    w_router,
    expert_w,
):
    groups = lax.axis_size("expert")
    tensor_count = lax.axis_size("tensor")
    group_id = lax.axis_index("expert")
    tensor_id = lax.axis_index("tensor")
    tok_count, col_count = tokens.shape
    width = col_count * tensor_count
    move_rows = tok_count // groups
    expert_count = w_router.shape[1]
    top_count = routes.shape[1]
    local_experts = expert_w.shape[0]

    w_stored = jnp.transpose(expert_w, (0, 2, 1, 3))
    w_all = [lax.all_gather(w_stored[e], "tensor", axis=0) for e in range(local_experts)]

    routes_t = routes.T
    order_t = pair_order[0].reshape(tok_count, top_count).T
    pair_expert = routes_t.reshape(-1)
    pair_total = tok_count * top_count
    base = pair_expert * pair_total
    keyed = base + order_t.reshape(-1)
    before = (keyed[None, :] < keyed[:, None]) & (keyed[None, :] >= base[:, None])
    ranks = jnp.sum(before.astype(jnp.int32), axis=1).reshape(top_count, tok_count)
    expert_axis = jnp.arange(expert_count, dtype=jnp.int32)
    route_hot = routes_t[:, None, :] == expert_axis[None, :, None]
    counts = jnp.sum(route_hot.astype(F32), axis=(0, 2))

    places = jnp.arange(tok_count, dtype=jnp.int32)
    arrival_rank = jnp.sum((dest_index[None, :] < dest_index[:, None]).astype(jnp.int32), axis=1)
    by_rank = (arrival_rank[None, :] == places[:, None]).astype(BF)
    inner = jnp.broadcast_to((dest_index % tok_count).astype(BF)[:, None], (tok_count, 64))
    facts = jnp.broadcast_to(counts.astype(BF)[None, :], (tok_count, expert_count))
    outgoing = dot(by_rank, jnp.concatenate([tokens, out_grad, inner, facts], axis=1)).astype(BF)
    got = exchange(outgoing.reshape(groups, move_rows, -1), "expert")
    all_counts = got[:, 0, 2 * col_count + 64 :].astype(jnp.int32)
    lower = jnp.arange(groups, dtype=jnp.int32) < group_id
    offsets = jnp.sum(jnp.where(lower[:, None], all_counts, 0), axis=0)
    mine = got[:, :, 2 * col_count].astype(jnp.int32).reshape(-1)
    put = (mine[None, :] == places[:, None]).astype(BF)
    local = dot(put, got.reshape(tok_count, -1)[:, : 2 * col_count]).astype(BF)
    capacity = 5 * tok_count * groups * top_count // (4 * expert_count)
    most_rows = 3 * tok_count * top_count // (2 * expert_count)
    per = most_rows // tensor_count
    slots = expert_count * per
    slot_global = jnp.sum(jnp.where(route_hot, offsets[None, :, None], 0), axis=1) + ranks
    kept = slot_global < capacity
    keep_mask = kept.astype(F32)
    here = kept & (ranks % tensor_count == tensor_id)
    slot_of = jnp.where(here, routes_t * per + ranks // tensor_count, -1)

    seq_ids, positions = sequence_layout(seq_lengths[0], tok_count)
    bias = jnp.where(seq_ids[:, None] == seq_ids[None, :], 0.0, mask_fill)
    cos_tab, sin_tab = rope_tables(positions, q_gain.shape[0])
    cos_rows = jnp.concatenate([cos_tab, cos_tab], axis=1)
    sin_rows = jnp.concatenate([-sin_tab, sin_tab], axis=1)
    gain1 = norm1_gain.astype(F32).reshape(tensor_count, col_count)
    gain2 = norm2_gain.astype(F32).reshape(tensor_count, col_count)
    head_gains = (q_gain.astype(F32)[None], k_gain.astype(F32)[None])
    router = jnp.pad(w_router, ((0, 0), (0, 128 - expert_count)))
    weights = (w_query, w_key, w_value, w_output)
    (
        x_all, dy_all, normed, resid, mixed, q_raw, k_raw, qh, kh, vh, attended, gates, send_rows,
        send_dy, pick_t,
    ) = front_call(
        local, bias, cos_rows, sin_rows, gain1, gain2, *head_gains, router.T, routes_t, slot_of,
        keep_mask, weights, slots,
    )
    recv_rows = exchange(send_rows.reshape(groups, -1, width + 128), "expert")
    recv_dy = exchange(send_dy.reshape(groups, -1, width), "expert")
    earlier = ()
    expert_grads = []
    for e in range(local_experts):
        *earlier, partial = expert_call(
            e, per, recv_rows.reshape(slots, -1), recv_dy.reshape(slots, -1), w_all[e], earlier
        )
        expert_grads.append(lax.psum_scatter(partial, "tensor", scatter_dimension=0, tiled=False))
    out_rows, d_rows = earlier
    ret_rows = exchange(d_rows.reshape(groups, -1, width + 128), "expert")
    ret_rows, out_rows = lax.optimization_barrier((ret_rows, out_rows))
    ret_out = exchange(out_rows.reshape(groups, -1, width), "expert")
    grads, dx_slice, small = back_call(
        pick_t, ret_rows.reshape(slots, -1), slot_of, keep_mask, gates, routes_t, bias, cos_rows,
        sin_rows, gain1, gain2, *head_gains, router, resid, dy_all, x_all, mixed, qh, kh, vh,
        attended, q_raw, k_raw, normed, weights,
    )
    moe_part = dot(pick_t, ret_out.reshape(slots, -1)).astype(BF)
    moe_got = exchange(column_blocks(moe_part, tensor_count), "tensor")
    moe_slice = jnp.sum(moe_got.astype(F32), axis=0)
    resid_slice = lax.dynamic_index_in_dim(resid, tensor_id, 0, False)
    out_slice = (resid_slice + moe_slice).astype(BF)
    summed = reduce_call(grads.reshape(4 * groups, -1, grads.shape[1])).reshape(grads.shape)

    going = dot(put, jnp.concatenate([out_slice, dx_slice], axis=1), 0, 0).astype(BF)
    small = small[:9].astype(BF).reshape(move_rows, -1)
    small = jnp.pad(small, ((0, 0), (0, -small.shape[1] % 128)))
    small = jnp.broadcast_to(small[None], (groups,) + small.shape)
    back = exchange(jnp.concatenate([going.reshape(groups, move_rows, -1), small], axis=2), "expert")
    small = jnp.sum(back[:, :, 2 * col_count :].astype(F32), axis=0)[:, : 9 * col_count // move_rows]
    small = small.reshape(-1)
    back = dot(by_rank, back.reshape(tok_count, -1)[:, : 2 * col_count], 0, 0).astype(BF)
    expert_grad = jnp.transpose(jnp.stack(expert_grads).astype(F32), (0, 2, 1, 3))
    wide = [summed[:, n * col_count : (n + 1) * col_count] for n in range(4)]
    gain_at = 2 * width + tok_count
    head = q_gain.shape[0]
    return (
        back[:, :col_count],
        back[:, col_count:],
        small[:width],
        wide[0].astype(F32),
        wide[1].astype(F32),
        wide[2].astype(F32),
        small[gain_at : gain_at + head],
        small[gain_at + head : gain_at + 2 * head],
        wide[3].T.astype(F32),
        small[width : 2 * width],
        summed[:, width : width + expert_count].astype(F32),
        expert_grad,
    )


def solution(mesh):
    in_specs = (
        P("expert", "tensor"),
        P("expert", "tensor"),
        P("expert", None),
        P("expert"),
        P("expert", None),
        P("expert", None),
        P(),
        P(None, "tensor"),
        P(None, "tensor"),
        P(None, "tensor"),
        P(),
        P(),
        P("tensor", None),
        P(),
        P(),
        P("expert", None, None, "tensor"),
    )
    out_specs = (
        P("expert", "tensor"),
        P("expert", "tensor"),
        P(),
        P(None, "tensor"),
        P(None, "tensor"),
        P(None, "tensor"),
        P(),
        P(),
        P("tensor", None),
        P(),
        P(),
        P("expert", None, None, "tensor"),
    )
    return jax.shard_map(body, mesh=mesh, in_specs=in_specs, out_specs=out_specs, check_vma=False)
```

```python
import functools
import math

import jax
import jax.numpy as jnp
from jax import lax
from jax.experimental import pallas as pl
from jax.experimental.pallas import tpu as pltpu
from jax.sharding import PartitionSpec as P

norm_eps = 1e-06
rope_base = 10000.0
mask_fill = -1e30


def rope_tables(positions, width):
    half_width = width // 2
    steps_idx = jnp.arange(half_width, dtype=jnp.float32)
    freqs = jnp.exp(steps_idx * (-2.0 * math.log(rope_base) / width))
    angles = positions.astype(jnp.float32)[:, None] * freqs[None, :]
    return (jnp.cos(angles), jnp.sin(angles))


def sequence_layout(lengths_row, count):
    seq_ends = jnp.cumsum(lengths_row)
    places = jnp.arange(count, dtype=jnp.int32)
    passed = (places[:, None] >= seq_ends[None, :]).astype(jnp.int32)
    seq_ids = jnp.sum(passed, axis=1)
    starts = jnp.sum(passed * lengths_row[None, :], axis=1)
    return (seq_ids, places - starts)


BF = jnp.bfloat16
F32 = jnp.float32
COSTE = pl.CostEstimate(flops=20000000000, bytes_accessed=1, transcendentals=0)
COST = pl.CostEstimate(flops=1, bytes_accessed=1, transcendentals=0)


def dot(left, right, left_dim=1, right_dim=0):
    return lax.dot_general(
        left, right, (((left_dim,), (right_dim,)), ((), ())), preferred_element_type=F32
    )


def exchange(value, axis):
    return lax.all_to_all(value, axis, split_axis=0, concat_axis=0, tiled=True)


def gather_blocks(value, axis):
    return exchange(jnp.broadcast_to(value[None], (lax.axis_size(axis),) + value.shape), axis)


def column_blocks(value, count):
    return jnp.stack(jnp.split(value, count, axis=1))


MESH = pl.DeviceIdType.MESH


def tensor_peers():
    me = lax.axis_index("tensor")
    count = lax.axis_size("tensor")
    return me, [(me + d) % count for d in range(1, count)]


def greet(axis, peers):
    barrier = pltpu.get_barrier_semaphore()
    for peer in peers:
        pl.semaphore_signal(barrier, inc=1, device_id={axis: peer}, device_id_type=MESH)
    return lambda: pl.semaphore_wait(barrier, len(peers))


class Post:
    def __init__(self, axis, send_sem, recv_sem):
        self.axis, self.send_sem, self.recv_sem = axis, send_sem, recv_sem
        self.started = []
        self.used = 0

    def push(self, source, target, peer):
        slot = self.used
        self.used += 1
        copy = pltpu.make_async_remote_copy(
            src_ref=source,
            dst_ref=target,
            send_sem=self.send_sem.at[slot],
            recv_sem=self.recv_sem.at[slot],
            device_id={self.axis: peer},
            device_id_type=MESH,
        )
        copy.start()
        self.started.append(copy)
        return copy

    def finish(self):
        for copy in self.started:
            copy.wait_send()
        self.started = []


def arrive(copies):
    for copy in copies:
        copy.wait_recv()


def ring(me):
    count = lax.axis_size("tensor")
    return (me + 1) % count, (me + count - 1) % count


def gather_start(post, ref, me):
    right, left = ring(me)
    return [post.push(ref.at[me], ref.at[me], peer) for peer in (right, left)]


def gather_relay(post, ref, me, first):
    right, left = ring(me)
    half = ref.shape[1] // 2
    first[0].wait_recv()
    here = ref.at[left, pl.ds(0, half)]
    one = post.push(here, here, right)
    first[1].wait_recv()
    here = ref.at[right, pl.ds(half, half)]
    return [one, post.push(here, here, left)]


def scatter_start(post, parts, halves, me):
    right, left = ring(me)
    far = ring(right)[0]
    half = parts.shape[1] // 2
    return [
        post.push(parts.at[far, pl.ds(0, half)], halves.at[0], right),
        post.push(parts.at[far, pl.ds(half, half)], halves.at[1], left),
    ]


def scatter_relay(post, parts, halves, box, me, first):
    right, left = ring(me)
    half = parts.shape[1] // 2
    copies = []
    for n, (peer, rows) in enumerate(((right, pl.ds(0, half)), (left, pl.ds(half, half)))):
        first[n].wait_recv()
        parts[peer, rows, :] = (parts[peer, rows, :].astype(F32) + halves[n].astype(F32)).astype(BF)
        copies.append(post.push(parts.at[peer], box.at[n], peer))
    return copies


def scatter_total(parts, box, me, copies):
    arrive(copies)
    return parts[me].astype(F32) + box[0].astype(F32) + box[1].astype(F32)


def fetch(pairs, sem):
    copies = [
        pltpu.make_async_copy(source, target, sem.at[n]) for n, (source, target) in enumerate(pairs)
    ]
    for copy in copies:
        copy.start()
    return copies


def turn(value, cos_rows, sin_rows):
    return value * cos_rows + pltpu.roll(value, value.shape[-1] // 2, 1) * sin_rows


def inverse_rms(total, width):
    return lax.rsqrt(total * (1.0 / width) + norm_eps)


def row_sum(value):
    return jnp.sum(value, axis=1, keepdims=True)


def softmax_rows(query, key, bias, scale):
    scores = dot(query, key, 1, 1) * scale + bias
    grown = jnp.exp(scores - jnp.max(scores, axis=1, keepdims=True))
    return grown / row_sum(grown)


def front_kernel(
    local, bias, cos_rows, sin_rows, gain1, gain2, q_gain, k_gain, router_t, routes, slot_of, slot_back, keep,
    wq_hbm, wk_hbm, wv_hbm, wo_hbm,
    x_out, dy_out, an_out, resid_out, mixed_out, q_out, k_out, qh_out, kh_out, vh_out, ob_out,
    gates_out, send_out, send_dy_out, pick_out,
    wq, wk, wv, wo, x_all, dy_all, parts, halves, box, total, load_sem, send_sem, recv_sem,
):
    me = lax.axis_index("tensor")
    ready = greet("tensor", ring(me))
    loads = fetch([(wq_hbm, wq), (wk_hbm, wk), (wv_hbm, wv), (wo_hbm, wo)], load_sem)
    blocks, tok, col = x_all.shape
    width = blocks * col
    x_all[me] = local[:, :col]
    dy_all[me] = local[:, col:]
    ready()
    post = Post("tensor", send_sem, recv_sem)
    x_in = gather_relay(post, x_all, me, gather_start(post, x_all, me))
    dy_in = gather_start(post, dy_all, me)
    arrive(x_in)
    square = jnp.zeros((tok, 1), F32)
    for t in range(blocks):
        value = x_all[t].astype(F32)
        square = square + row_sum(value * value)
    r1 = inverse_rms(square, width)
    for t in range(blocks):
        an_out[t] = (x_all[t].astype(F32) * r1 * gain1[t : t + 1, :]).astype(BF)
    x_out[...] = x_all[...]

    for copy in loads:
        copy.wait()

    def project(weight):
        value = dot(an_out[0], weight[0:col, :])
        for t in range(1, blocks):
            value = value + dot(an_out[t], weight[t * col : (t + 1) * col, :])
        return value

    q_out[...] = project(wq)
    k_out[...] = project(wk)
    vh_out[...] = project(wv).astype(BF)
    dy_in = gather_relay(post, dy_all, me, dy_in)
    head = q_gain.shape[1]
    scale = 1.0 / math.sqrt(head)
    for h in range(col // head):
        lanes = slice(h * head, (h + 1) * head)
        for raw, gain, rotated in ((q_out, q_gain, qh_out), (k_out, k_gain, kh_out)):
            value = raw[:, lanes]
            value = value * inverse_rms(row_sum(value * value), head) * gain[...]
            rotated[:, lanes] = turn(value, cos_rows[...], sin_rows[...]).astype(BF)
        probs = softmax_rows(qh_out[:, lanes], kh_out[:, lanes], bias[...], scale).astype(BF)
        ob_out[:, lanes] = dot(probs, vh_out[:, lanes]).astype(BF)
    for t in range(blocks):
        parts[t] = dot(ob_out[...], wo[:, t * col : (t + 1) * col]).astype(BF)
    first = scatter_start(post, parts, halves, me)
    moved = scatter_relay(post, parts, halves, box, me, first)
    total[me] = scatter_total(parts, box, me, moved).astype(BF)
    arrive(gather_relay(post, total, me, gather_start(post, total, me)))
    square = jnp.zeros((tok, 1), F32)
    for t in range(blocks):
        value = x_all[t].astype(F32) + total[t].astype(F32)
        resid_out[t] = value
        square = square + row_sum(value * value)
    r2 = inverse_rms(square, width)
    logits = jnp.zeros((router_t.shape[0], tok), F32)
    for t in range(blocks):
        mixed_out[t] = (resid_out[t] * r2 * gain2[t : t + 1, :]).astype(BF)
        logits = logits + dot(router_t[:, t * col : (t + 1) * col], mixed_out[t], 1, 1)
    expert = lax.broadcasted_iota(jnp.int32, logits.shape, 0)
    top = routes.shape[0]
    chosen = [
        jnp.sum(jnp.where(routes[k : k + 1, :] == expert, logits, 0.0), axis=0, keepdims=True)
        for k in range(top)
    ]
    peak = functools.reduce(jnp.maximum, chosen)
    grown = [jnp.exp(value - peak) for value in chosen]
    whole = functools.reduce(jnp.add, grown)
    slots = send_out.shape[0]
    slot = lax.broadcasted_iota(jnp.int32, (slots, tok), 0)
    pick = jnp.zeros((slots, tok), F32)
    pick_back = jnp.zeros((slots, tok), F32)
    weight = jnp.zeros((slots, tok), F32)
    for k in range(top):
        gate = grown[k] / whole
        gates_out[k : k + 1, :] = gate
        hot = slot_of[k : k + 1, :] == slot
        pick = jnp.where(hot, 1.0, pick)
        pick_back = jnp.where(slot_back[k : k + 1, :] == slot, 1.0, pick_back)
        weight = jnp.where(hot, gate * keep[k : k + 1, :], weight)
    pick_out[...] = pick_back.T.astype(BF)
    pick = pick.astype(BF)
    for t in range(blocks):
        send_out[:, t * col : (t + 1) * col] = dot(pick, mixed_out[t]).astype(BF)
    gate = row_sum(weight)
    first = gate.astype(BF)
    second = (gate - first.astype(F32)).astype(BF)
    third = (gate - first.astype(F32) - second.astype(F32)).astype(BF)
    lane = lax.broadcasted_iota(jnp.int32, (slots, 128), 1)
    facts = jnp.zeros((slots, 128), F32)
    for n, piece in enumerate((first, second, third)):
        facts = jnp.where(lane == n, piece.astype(F32), facts)
    send_out[:, width:] = facts.astype(BF)
    arrive(dy_in)
    dy_out[...] = dy_all[...]
    for t in range(blocks):
        send_dy_out[:, t * col : (t + 1) * col] = dot(pick, dy_all[t]).astype(BF)
    post.finish()


def front_call(local, bias, cos_rows, sin_rows, gain1, gain2, q_gain, k_gain, router_t, routes,
               slot_of, slot_back, keep, weights, slots):
    tok, both = local.shape
    col = both // 2
    blocks = gain1.shape[0]
    width = col * blocks
    shape = jax.ShapeDtypeStruct
    vmem = pl.BlockSpec(memory_space=pltpu.VMEM)
    tiles = (blocks, tok, col)
    top = routes.shape[0]
    return pl.pallas_call(
        front_kernel,
        out_shape=(
            shape(tiles, BF), shape(tiles, BF), shape(tiles, BF), shape(tiles, F32),
            shape(tiles, BF), shape((tok, col), F32), shape((tok, col), F32),
            shape((tok, col), BF), shape((tok, col), BF), shape((tok, col), BF),
            shape((tok, col), BF), shape((top, tok), F32), shape((slots, width + 128), BF),
            shape((slots, width), BF), shape((tok, slots), BF),
        ),
        in_specs=[vmem] * 13 + [pl.BlockSpec(memory_space=pl.ANY)] * 4,
        out_specs=(vmem,) * 15,
        scratch_shapes=[
            pltpu.VMEM((width, col), BF), pltpu.VMEM((width, col), BF), pltpu.VMEM((width, col), BF),
            pltpu.VMEM((col, width), BF),
            pltpu.VMEM(tiles, BF), pltpu.VMEM(tiles, BF), pltpu.VMEM(tiles, BF),
            pltpu.VMEM((2, tok // 2, col), BF), pltpu.VMEM((2, tok, col), BF), pltpu.VMEM(tiles, BF),
            pltpu.SemaphoreType.DMA((4,)),
            pltpu.SemaphoreType.DMA((16,)), pltpu.SemaphoreType.DMA((16,)),
        ],
        compiler_params=pltpu.CompilerParams(
            collective_id=1, has_side_effects=True, vmem_limit_bytes=56 * 1024 * 1024
        ),
        name="front",
    )(local, bias, cos_rows, sin_rows, gain1, gain2, q_gain, k_gain, router_t, routes, slot_of,
      slot_back, keep, *weights)


def back_kernel(
    pick_t, ret_early, ret_late, slot_of, keep, gates, routes, bias, cos_rows, sin_rows, gain1, gain2, q_gain,
    k_gain, router, resid, dy_all, x_all, mixed, qh, kh, vh, ob,
    q_hbm, k_hbm, an_hbm, wq_hbm, wk_hbm, wv_hbm, wo_hbm,
    grads, dx_out, small_out,
    q_raw, k_raw, an, wq, wk, wv, wo, parts, box, total, dm, dr, d_qkv, d_att,
    halves, dg_mine, dg_box, note, load_sem, send_sem, recv_sem,
):
    me, peers = tensor_peers()
    ready = greet("tensor", peers)
    loads = fetch(
        [(wo_hbm, wo), (q_hbm, q_raw), (k_hbm, k_raw), (wq_hbm, wq), (wk_hbm, wk), (wv_hbm, wv),
         (an_hbm, an)],
        load_sem,
    )
    blocks, tok, col = parts.shape
    width = blocks * col
    post = Post("tensor", send_sem, recv_sem)
    early = ret_early.shape[0]
    for t in range(blocks):
        lanes = slice(t * col, (t + 1) * col)
        parts[t] = (
            dot(pick_t[:, :early], ret_early[:, lanes]) + dot(pick_t[:, early:], ret_late[:, lanes])
        ).astype(BF)
    ready()
    first = scatter_start(post, parts, halves.at[pl.ds(0, 2)], me)
    top = routes.shape[0]
    for n, (ret, base) in enumerate(((ret_early, 0), (ret_late, early))):
        dgate = row_sum(ret[:, width : width + 128].astype(F32))
        slot = lax.broadcasted_iota(jnp.int32, (ret.shape[0], tok), 0) + base
        for k in range(top):
            hot = slot_of[k : k + 1, :] == slot
            found = jnp.sum(jnp.where(hot, dgate, 0.0), axis=0, keepdims=True)
            dg_mine[k : k + 1, :] = dg_mine[k : k + 1, :] + found if n else found
    dg_in = [post.push(dg_mine, dg_box.at[d], peer) for d, peer in enumerate(peers)]
    moved = scatter_relay(post, parts, halves.at[pl.ds(0, 2)], box.at[pl.ds(0, 2)], me, first)
    total[me] = scatter_total(parts, box.at[pl.ds(0, 2)], me, moved).astype(BF)
    total_first = gather_start(post, total, me)

    arrive(dg_in)
    d_gates = dg_mine[...]
    for d in range(blocks - 1):
        d_gates = d_gates + dg_box[d]
    d_gates = d_gates * keep[...]
    gate = gates[...]
    d_chosen = gate * (d_gates - jnp.sum(gate * d_gates, axis=0, keepdims=True))
    expert = lax.broadcasted_iota(jnp.int32, (router.shape[1], tok), 0)
    d_logits_t = jnp.zeros(expert.shape, F32)
    for k in range(top):
        hot = routes[k : k + 1, :] == expert
        d_logits_t = jnp.where(hot, d_chosen[k : k + 1, :], d_logits_t)
    d_logits = d_logits_t.T.astype(BF)
    square = jnp.zeros((tok, 1), F32)
    for t in range(blocks):
        rows = slice(t * col, (t + 1) * col)
        grads[rows, 4 * col :] = dot(mixed[t].T, d_logits).astype(BF)
        dm[t] = dot(d_logits, router[rows, :], 1, 1)
        square = square + row_sum(resid[t] * resid[t])
    r2 = inverse_rms(square, width)
    arrive(gather_relay(post, total, me, total_first))
    cross = jnp.zeros((tok, 1), F32)
    for t in range(blocks):
        dm[t] = dm[t] + total[t].astype(F32)
        cross = cross + row_sum(resid[t] * gain2[t : t + 1, :] * dm[t])
    cross = cross * (1.0 / width) * r2 * r2 * r2
    for t in range(blocks):
        d_mixed = dm[t]
        small_out[4 + t : 5 + t, :] = jnp.sum(d_mixed * resid[t] * r2, axis=0, keepdims=True)
        d_resid = dy_all[t].astype(F32) + r2 * gain2[t : t + 1, :] * d_mixed - resid[t] * cross
        dm[t] = d_resid
        dr[t] = d_resid.astype(BF)
    for copy in loads:
        copy.wait()
    value = dot(dr[0], wo[:, 0:col], 1, 1)
    for t in range(1, blocks):
        value = value + dot(dr[t], wo[:, t * col : (t + 1) * col], 1, 1)
    d_att[...] = value.astype(BF)

    head = q_gain.shape[1]
    scale = 1.0 / math.sqrt(head)
    q_part = jnp.zeros((1, head), F32)
    k_part = jnp.zeros((1, head), F32)

    def unturn(grown, raw, gain):
        d_unit = grown * cos_rows[...] - pltpu.roll(grown, head // 2, 1) * sin_rows[...]
        inverse = inverse_rms(row_sum(raw * raw), head)
        unit = raw * inverse
        gain_part = jnp.sum(d_unit * unit, axis=0, keepdims=True)
        d_unit = d_unit * gain[...]
        d_raw = inverse * (d_unit - unit * (row_sum(unit * d_unit) * (1.0 / head)))
        return d_raw.astype(BF), gain_part

    for h in range(col // head):
        lanes = slice(h * head, (h + 1) * head)
        probs = softmax_rows(qh[:, lanes], kh[:, lanes], bias[...], scale)
        d_head = d_att[:, lanes]
        d_probs = dot(d_head, vh[:, lanes], 1, 1)
        d_scores = probs * (d_probs - row_sum(probs * d_probs))
        d_qkv[:, 2 * col + h * head : 2 * col + (h + 1) * head] = dot(
            probs.T.astype(BF), d_head
        ).astype(BF)
        d_q, part = unturn(dot(d_scores.astype(BF), kh[:, lanes]) * scale, q_raw[:, lanes], q_gain)
        q_part = q_part + part
        d_qkv[:, lanes] = d_q
        d_k, part = unturn(dot(d_scores.T.astype(BF), qh[:, lanes]) * scale, k_raw[:, lanes], k_gain)
        k_part = k_part + part
        d_qkv[:, col + h * head : col + (h + 1) * head] = d_k
    post.finish()
    for t in range(blocks):
        rows = slice(t * col, (t + 1) * col)
        parts[t] = (
            dot(d_qkv[:, 0:col], wq[rows, :], 1, 1)
            + dot(d_qkv[:, col : 2 * col], wk[rows, :], 1, 1)
            + dot(d_qkv[:, 2 * col : 3 * col], wv[rows, :], 1, 1)
        ).astype(BF)
    halves_again, box_again = halves.at[pl.ds(2, 2)], box.at[pl.ds(2, 2)]
    first = scatter_start(post, parts, halves_again, me)
    for t in range(blocks):
        rows = slice(t * col, (t + 1) * col)
        grads[rows, : 3 * col] = dot(an[t].T, d_qkv[...]).astype(BF)
        if t == 1:
            moved = scatter_relay(post, parts, halves_again, box_again, me, first)
    for t in range(blocks):
        rows = slice(t * col, (t + 1) * col)
        grads[rows, 3 * col : 4 * col] = dot(dr[t].T, ob[...]).astype(BF)
    square = jnp.zeros((tok, 1), F32)
    for t in range(blocks):
        value = x_all[t].astype(F32)
        square = square + row_sum(value * value)
    r1 = inverse_rms(square, width)
    d_an = scatter_total(parts, box_again, me, moved)
    x_mine = x_all[me].astype(F32)
    grown = gain1[pl.ds(me, 1), :] * d_an
    mean_part = row_sum(x_mine * grown)
    note[me, 0:8, :] = jnp.broadcast_to(
        jnp.sum(d_an * x_mine * r1, axis=0, keepdims=True), (8, col)
    )
    note[me, 8:16, 0:tok] = jnp.broadcast_to(mean_part, (tok, 128)).T[0:8, :]
    note[me, 8:16, tok : tok + head] = jnp.broadcast_to(q_part, (8, head))
    note[me, 8:16, tok + head : tok + 2 * head] = jnp.broadcast_to(k_part, (8, head))
    arrive([post.push(note.at[me], note.at[me], peer) for peer in peers])
    facts = note[0, 8:16, :]
    for t in range(1, blocks):
        facts = facts + note[t, 8:16, :]
    for t in range(blocks):
        small_out[t : t + 1, :] = note[t, 0:1, :]
    small_out[8:16, :] = facts
    mean = jnp.broadcast_to(facts[0:1, 0:tok], (128, tok)).T[:, 0:1] * (1.0 / width)
    dx_out[...] = (dm[me] + r1 * grown - x_mine * (r1 * r1 * r1 * mean)).astype(BF)
    post.finish()


def back_call(pick_t, ret_early, ret_late, slot_of, keep, gates, routes, bias, cos_rows, sin_rows, gain1, gain2,
              q_gain, k_gain, router, resid, dy_all, x_all, mixed, qh, kh, vh, ob, q_raw, k_raw,
              an, weights):
    blocks, tok, col = x_all.shape
    width = blocks * col
    tiles = (blocks, tok, col)
    shape = jax.ShapeDtypeStruct
    vmem = pl.BlockSpec(memory_space=pltpu.VMEM)
    top = routes.shape[0]
    count = 12 + 2 * (blocks - 1)
    return pl.pallas_call(
        back_kernel,
        out_shape=(
            shape((width, 4 * col + 128), BF), shape((tok, col), BF), shape((16, col), F32),
        ),
        in_specs=[vmem] * 23 + [pl.BlockSpec(memory_space=pl.ANY)] * 7,
        out_specs=(vmem,) * 3,
        scratch_shapes=[
            pltpu.VMEM((tok, col), F32), pltpu.VMEM((tok, col), F32), pltpu.VMEM(tiles, BF),
            pltpu.VMEM((width, col), BF), pltpu.VMEM((width, col), BF), pltpu.VMEM((width, col), BF),
            pltpu.VMEM((col, width), BF),
            pltpu.VMEM(tiles, BF), pltpu.VMEM((4, tok, col), BF),
            pltpu.VMEM(tiles, BF), pltpu.VMEM(tiles, F32), pltpu.VMEM(tiles, BF),
            pltpu.VMEM((tok, 3 * col), BF), pltpu.VMEM((tok, col), BF),
            pltpu.VMEM((4, tok // 2, col), BF),
            pltpu.VMEM((top, tok), F32), pltpu.VMEM((blocks - 1, top, tok), F32),
            pltpu.VMEM((blocks, 16, col), F32),
            pltpu.SemaphoreType.DMA((7,)),
            pltpu.SemaphoreType.DMA((count,)), pltpu.SemaphoreType.DMA((count,)),
        ],
        compiler_params=pltpu.CompilerParams(
            collective_id=2, has_side_effects=True, vmem_limit_bytes=60 * 1024 * 1024
        ),
        cost_estimate=pl.CostEstimate(
            flops=20000000000, bytes_accessed=1, transcendentals=0
        ),
        name="back",
    )(pick_t, ret_early, ret_late, slot_of, keep, gates, routes, bias, cos_rows, sin_rows, gain1, gain2, q_gain,
      k_gain, router, resid, dy_all, x_all, mixed, qh, kh, vh, ob, q_raw, k_raw, an, *weights)


def expert_kernel(side, per, early, rows_ref, grads_ref, w_ref, *rest):
    if side:
        y_rest, dx_rest, *rest = rest
        y_ref, dx_ref, *rest = rest
    else:
        y_ref, dx_ref, y_rest, dx_rest, *rest = rest
    grad_ref, rows, rows_t, dys, dys_t, y_acc, dx_acc, gate_of, dgate = rest
    step = pl.program_id(0)
    count, width = rows.shape
    both = rows_ref.shape[0]
    late = per - early

    def selector(shape, source_of):
        place = lax.broadcasted_iota(jnp.int32, shape, 0)
        source = lax.broadcasted_iota(jnp.int32, shape, 1)
        return (source_of(place) == source).astype(F32).astype(BF)

    @pl.when(step == 0)
    def _():
        pick = selector((count, both), lambda p: p + (p // per + side) * per)
        rows[...] = dot(pick, rows_ref[:, :width]).astype(BF)
        gate_of[...] = row_sum(dot(pick, rows_ref[:, width:]))
        dy_rows = dot(pick, grads_ref[...])
        dys[...] = dy_rows.astype(BF)
        rows_t[...] = rows[...].T
        dys_t[...] = (dy_rows * gate_of[...]).astype(BF).T
        dgate[...] = jnp.zeros_like(dgate)
        y_acc[...] = jnp.zeros_like(y_acc)
        dx_acc[...] = jnp.zeros_like(dx_acc)

    w_gate, w_up, w_down = w_ref[0, 0], w_ref[0, 1], w_ref[0, 2]
    gate = dot(rows[...], w_gate)
    up = dot(rows[...], w_up)
    d_raw = dot(dys[...], w_down)
    d_act = d_raw * gate_of[...]
    sig = 1.0 / (1.0 + jnp.exp(-gate))
    silu = gate * sig
    act = (silu * up).astype(BF)
    dgate[...] += row_sum(act.astype(F32) * d_raw)
    d_gate = (d_act * up * sig * (1.0 + gate * (1.0 - sig))).astype(BF)
    d_up = (d_act * silu).astype(BF)
    y_acc[...] += dot(act, w_down, 1, 1)
    dx_acc[...] += dot(d_gate, w_gate, 1, 1) + dot(d_up, w_up, 1, 1)
    grad_ref[0, 0] = dot(rows_t[...], d_gate).astype(BF)
    grad_ref[0, 1] = dot(rows_t[...], d_up).astype(BF)
    grad_ref[0, 2] = dot(dys_t[...], act).astype(BF)

    @pl.when(step == pl.num_programs(0) - 1)
    def _():
        first = dgate[...].astype(BF).astype(F32)
        lane = lax.broadcasted_iota(jnp.int32, (count, 128), 1)
        facts = jnp.where(lane == 0, first, jnp.where(lane == 1, dgate[...] - first, 0.0))
        facts = facts.astype(BF)
        y_rows = (y_acc[...] * gate_of[...]).astype(BF)
        dx_rows = dx_acc[...].astype(BF)
        if side:
            chunk = per + late
            here = selector(
                (y_ref.shape[0], count),
                lambda p: jnp.where(p % chunk < late, -1, p // chunk * per + p % chunk - late),
            )
            there = selector(
                (y_ref.shape[0], y_rest.shape[0]),
                lambda p: jnp.where(p % chunk < late, p // chunk * late + p % chunk, -1),
            )
            y_ref[...] = (dot(here, y_rows) + dot(there, y_rest[...])).astype(BF)
            dx_ref[:, :width] = (dot(here, dx_rows) + dot(there, dx_rest[:, :width])).astype(BF)
            dx_ref[:, width:] = (dot(here, facts) + dot(there, dx_rest[:, width:])).astype(BF)
        else:
            soon = selector((y_ref.shape[0], count), lambda p: p // early * per + p % early)
            later = selector(
                (y_rest.shape[0], count), lambda p: p // late * per + early + p % late
            )
            for pick, y_out, dx_out in ((soon, y_ref, dx_ref), (later, y_rest, dx_rest)):
                y_out[...] = dot(pick, y_rows).astype(BF)
                dx_out[:, :width] = dot(pick, dx_rows).astype(BF)
                dx_out[:, width:] = dot(pick, facts).astype(BF)


def expert_call(side, per, early, rows, grads, weights, rest):
    quarters, _, width, hidden = weights.shape
    both = rows.shape[0]
    count = both // 2
    groups = count // per
    shape = jax.ShapeDtypeStruct

    def whole(value):
        return pl.BlockSpec(value.shape, lambda q: (0, 0), pipeline_mode=pl.Buffered(1))

    def pair(size):
        return [shape((groups * size, width), BF), shape((groups * size, width + 128), BF)]

    block = pl.BlockSpec((1, 3, width, hidden), lambda q: (q, 0, 0, 0))
    outs = pair(2 * per - early) if side else pair(early) + pair(per - early)
    return pl.pallas_call(
        functools.partial(expert_kernel, side, per, early),
        grid=(quarters,),
        out_shape=tuple(outs) + (shape(weights.shape, BF),),
        in_specs=[whole(rows), whole(grads), block] + [whole(value) for value in rest],
        out_specs=tuple(whole(value) for value in outs) + (block,),
        scratch_shapes=[
            pltpu.VMEM((count, width), BF),
            pltpu.VMEM((width, count), BF),
            pltpu.VMEM((count, width), BF),
            pltpu.VMEM((width, count), BF),
            pltpu.VMEM((count, width), F32),
            pltpu.VMEM((count, width), F32),
            pltpu.VMEM((count, 1), F32),
            pltpu.VMEM((count, 1), F32),
        ],
        compiler_params=pltpu.CompilerParams(vmem_limit_bytes=60 * 1024 * 1024),
        cost_estimate=COSTE if side else COST,
        name=f"expert{side}",
    )(rows, grads, weights, *rest)


def plane():
    me = lax.axis_index("expert")
    core, z, y = me % 2, (me // 2) % 4, me // 8
    return [
        (core, me + 1 - 2 * core),
        ((y + y // 2) % 2, me + 8 * (1 - 2 * (y % 2))),
        (y // 2, me + 8 * (3 - 2 * y)),
        ((z + z // 2) % 2, me + 2 * (1 - 2 * (z % 2))),
        (z // 2, me + 2 * (3 - 2 * z)),
    ]

ORDERS = ((1, 3, 2, 4), (3, 2, 4, 1), (2, 4, 1, 3), (4, 1, 3, 2))

def reduce_kernel(part, out, buf, box, got, load_sem, out_sem, send_sem, recv_sem):
    dims = plane()
    barrier = pltpu.get_barrier_semaphore()
    for _, partner in dims:
        pl.semaphore_signal(barrier, inc=1, device_id={"expert": partner}, device_id_type=MESH)
    load = pltpu.make_async_copy(part, buf, load_sem)
    load.start()
    pl.semaphore_wait(barrier, len(dims))
    load.wait()
    core = dims[0][0]
    sends = []

    def push(slot, source, target, partner):
        copy = pltpu.make_async_remote_copy(
            src_ref=source, dst_ref=target, send_sem=send_sem.at[slot], recv_sem=recv_sem.at[slot],
            device_id={"expert": partner}, device_id_type=MESH)
        copy.start()
        sends.append(copy)
        return copy

    def add(target, target_at, place, first, count):
        def one(i, _):
            total = buf[place + i].astype(F32) + box[first + i].astype(F32)
            target[target_at + i] = total.astype(BF)
            return 0
        lax.fori_loop(0, count, one, 0)

    copies = []
    for s in range(4):
        copies.append(push(s, buf.at[pl.ds((1 - core) * 64 + s * 16, 16)], box.at[pl.ds(31 * s, 16)], dims[0][1]))
    place = [core * 64 + s * 16 for s in range(4)]
    for s in range(4):
        copies[s].wait_recv()
        add(buf, place[s], place[s], 31 * s, 16)
        bit, partner = dims[ORDERS[s][0]]
        copies[s] = push(4 + s, buf.at[pl.ds(place[s] + (1 - bit) * 8, 8)], box.at[pl.ds(31 * s + 16, 8)], partner)
        place[s] = place[s] + bit * 8
    size, first = 8, 16
    for k in range(1, 5):
        for s in range(4):
            copies[s].wait_recv()
            if k < 4:
                add(buf, place[s], place[s], 31 * s + first, size)
                bit, partner = dims[ORDERS[s][k]]
                half = size // 2
                copies[s] = push(4 * (k + 1) + s, buf.at[pl.ds(place[s] + (1 - bit) * half, half)],
                                 box.at[pl.ds(31 * s + first + size, half)], partner)
                place[s] = place[s] + bit * half
            else:
                add(got, place[s], place[s], 31 * s + first, 1)
                bit, partner = dims[ORDERS[s][3]]
                here = got.at[pl.ds(place[s], 1)]
                copies[s] = push(20 + s, here, here, partner)
        first, size = first + size, size // 2
    size = 1
    for k in range(3, -1, -1):
        for s in range(4):
            copies[s].wait_recv()
            bit, _ = dims[ORDERS[s][k]]
            place[s] = place[s] - bit * size
            if k:
                _, partner = dims[ORDERS[s][k - 1]]
            else:
                partner = dims[0][1]
            here = got.at[pl.ds(place[s], 2 * size)]
            copies[s] = push(20 + 4 * (4 - k) + s, here, here, partner)
        size *= 2
    for s in range(4):
        copies[s].wait_recv()
    store = pltpu.make_async_copy(got, out, out_sem)
    store.start()
    for copy in sends:
        copy.wait_send()
    store.wait()

def reduce_call(part):
    chunks, rows, cols = part.shape
    return pl.pallas_call(
        reduce_kernel,
        out_shape=jax.ShapeDtypeStruct(part.shape, BF),
        in_specs=[pl.BlockSpec(memory_space=pl.ANY)],
        out_specs=pl.BlockSpec(memory_space=pl.ANY),
        scratch_shapes=[
            pltpu.VMEM(part.shape, BF),
            pltpu.VMEM((124, rows, cols), BF),
            pltpu.VMEM(part.shape, BF),
            pltpu.SemaphoreType.DMA, pltpu.SemaphoreType.DMA,
            pltpu.SemaphoreType.DMA((40,)), pltpu.SemaphoreType.DMA((40,)),
        ],
        compiler_params=pltpu.CompilerParams(collective_id=3, has_side_effects=True, vmem_limit_bytes=48*1024*1024),
        name="reduce",
    )(part)


def body(
    tokens,
    out_grad,
    seq_lengths,
    dest_index,
    routes,
    pair_order,
    norm1_gain,
    w_query,
    w_key,
    w_value,
    q_gain,
    k_gain,
    w_output,
    norm2_gain,
    w_router,
    expert_w,
):
    groups = lax.axis_size("expert")
    tensor_count = lax.axis_size("tensor")
    group_id = lax.axis_index("expert")
    tensor_id = lax.axis_index("tensor")
    tok_count, col_count = tokens.shape
    width = col_count * tensor_count
    move_rows = tok_count // groups
    expert_count = w_router.shape[1]
    top_count = routes.shape[1]
    local_experts = expert_w.shape[0]

    w_stored = jnp.transpose(expert_w, (0, 2, 1, 3))
    w_all = [lax.all_gather(w_stored[e], "tensor", axis=0) for e in range(local_experts)]

    routes_t = routes.T
    order_t = pair_order[0].reshape(tok_count, top_count).T
    pair_expert = routes_t.reshape(-1)
    pair_total = tok_count * top_count
    base = pair_expert * pair_total
    keyed = base + order_t.reshape(-1)
    before = (keyed[None, :] < keyed[:, None]) & (keyed[None, :] >= base[:, None])
    ranks = jnp.sum(before.astype(jnp.int32), axis=1).reshape(top_count, tok_count)
    expert_axis = jnp.arange(expert_count, dtype=jnp.int32)
    route_hot = routes_t[:, None, :] == expert_axis[None, :, None]
    counts = jnp.sum(route_hot.astype(F32), axis=(0, 2))

    places = jnp.arange(tok_count, dtype=jnp.int32)
    arrival_rank = jnp.sum((dest_index[None, :] < dest_index[:, None]).astype(jnp.int32), axis=1)
    by_rank = (arrival_rank[None, :] == places[:, None]).astype(BF)
    inner = jnp.broadcast_to((dest_index % tok_count).astype(BF)[:, None], (tok_count, 64))
    facts = jnp.broadcast_to(counts.astype(BF)[None, :], (tok_count, expert_count))
    outgoing = dot(by_rank, jnp.concatenate([tokens, out_grad, inner, facts], axis=1)).astype(BF)
    got = exchange(outgoing.reshape(groups, move_rows, -1), "expert")
    all_counts = got[:, 0, 2 * col_count + 64 :].astype(jnp.int32)
    lower = jnp.arange(groups, dtype=jnp.int32) < group_id
    offsets = jnp.sum(jnp.where(lower[:, None], all_counts, 0), axis=0)
    mine = got[:, :, 2 * col_count].astype(jnp.int32).reshape(-1)
    put = (mine[None, :] == places[:, None]).astype(BF)
    local = dot(put, got.reshape(tok_count, -1)[:, : 2 * col_count]).astype(BF)
    capacity = 5 * tok_count * groups * top_count // (4 * expert_count)
    most_rows = 3 * tok_count * top_count // (2 * expert_count)
    per = most_rows // tensor_count
    slots = expert_count * per
    slot_global = jnp.sum(jnp.where(route_hot, offsets[None, :, None], 0), axis=1) + ranks
    kept = slot_global < capacity
    keep_mask = kept.astype(F32)
    here = kept & (ranks % tensor_count == tensor_id)
    place = ranks // tensor_count
    slot_of = jnp.where(here, routes_t * per + place, -1)
    early = per // 8 * 8
    side, owner = routes_t % local_experts, routes_t // local_experts
    ahead = owner * early + place
    behind = groups * early + owner * (2 * per - early)
    behind = behind + jnp.where(side == 0, place - early, per - early + place)
    slot_back = jnp.where(here, jnp.where((side == 0) & (place < early), ahead, behind), -1)

    seq_ids, positions = sequence_layout(seq_lengths[0], tok_count)
    bias = jnp.where(seq_ids[:, None] == seq_ids[None, :], 0.0, mask_fill)
    cos_tab, sin_tab = rope_tables(positions, q_gain.shape[0])
    cos_rows = jnp.concatenate([cos_tab, cos_tab], axis=1)
    sin_rows = jnp.concatenate([-sin_tab, sin_tab], axis=1)
    gain1 = norm1_gain.astype(F32).reshape(tensor_count, col_count)
    gain2 = norm2_gain.astype(F32).reshape(tensor_count, col_count)
    head_gains = (q_gain.astype(F32)[None], k_gain.astype(F32)[None])
    router = jnp.pad(w_router, ((0, 0), (0, 128 - expert_count)))
    weights = (w_query, w_key, w_value, w_output)
    (
        x_all, dy_all, normed, resid, mixed, q_raw, k_raw, qh, kh, vh, attended, gates, send_rows,
        send_dy, pick_t,
    ) = front_call(
        local, bias, cos_rows, sin_rows, gain1, gain2, *head_gains, router.T, routes_t, slot_of,
        slot_back, keep_mask, weights, slots,
    )
    recv_rows = exchange(send_rows.reshape(groups, -1, width + 128), "expert")
    recv_dy = exchange(send_dy.reshape(groups, -1, width), "expert")
    recv_rows = recv_rows.reshape(slots, -1)
    recv_dy = recv_dy.reshape(slots, -1)
    def homeward(value):
        return exchange(value.reshape(groups, -1, value.shape[1]), "expert").reshape(value.shape)

    y_early, d_early, *rest, partial = expert_call(0, per, early, recv_rows, recv_dy, w_all[0], ())
    grad_first = lax.psum_scatter(partial, "tensor", scatter_dimension=0, tiled=False)
    ret_early = homeward(d_early)
    ret_early, y_early, later_rows = lax.optimization_barrier((ret_early, y_early, recv_rows))
    out_early = homeward(y_early)
    y_late, d_late, partial = expert_call(1, per, early, later_rows, recv_dy, w_all[1], rest)
    grad_second = lax.psum_scatter(partial, "tensor", scatter_dimension=0, tiled=False)

    ret_late = homeward(d_late)
    ret_late, y_late = lax.optimization_barrier((ret_late, y_late))
    out_late = homeward(y_late)
    grads, dx_slice, small = back_call(
        pick_t, ret_early, ret_late, slot_back, keep_mask, gates, routes_t, bias, cos_rows,
        sin_rows, gain1, gain2, *head_gains, router, resid, dy_all, x_all, mixed, qh, kh, vh,
        attended, q_raw, k_raw, normed, weights,
    )
    out_late, small = lax.optimization_barrier((out_late, small))
    moe_part = dot(pick_t[:, : out_early.shape[0]], out_early)
    moe_part = (moe_part + dot(pick_t[:, out_early.shape[0] :], out_late)).astype(BF)
    moe_got = exchange(column_blocks(moe_part, tensor_count), "tensor")
    moe_slice = jnp.sum(moe_got.astype(F32), axis=0)
    resid_slice = lax.dynamic_index_in_dim(resid, tensor_id, 0, False)
    out_slice = (resid_slice + moe_slice).astype(BF)
    summed = reduce_call(grads.reshape(4 * groups, -1, grads.shape[1])).reshape(grads.shape)

    going = dot(put, jnp.concatenate([out_slice, dx_slice], axis=1), 0, 0).astype(BF)
    small = small[:9].astype(BF).reshape(move_rows, -1)
    small = jnp.pad(small, ((0, 0), (0, -small.shape[1] % 128)))
    small = jnp.broadcast_to(small[None], (groups,) + small.shape)
    back = exchange(jnp.concatenate([going.reshape(groups, move_rows, -1), small], axis=2), "expert")
    small = jnp.sum(back[:, :, 2 * col_count :].astype(F32), axis=0)[:, : 9 * col_count // move_rows]
    small = small.reshape(-1)
    back = dot(by_rank, back.reshape(tok_count, -1)[:, : 2 * col_count], 0, 0).astype(BF)
    expert_grad = jnp.transpose(jnp.stack([grad_first, grad_second]).astype(F32), (0, 2, 1, 3))
    wide = [summed[:, n * col_count : (n + 1) * col_count] for n in range(4)]
    gain_at = 2 * width + tok_count
    head = q_gain.shape[0]
    return (
        back[:, :col_count],
        back[:, col_count:],
        small[:width],
        wide[0].astype(F32),
        wide[1].astype(F32),
        wide[2].astype(F32),
        small[gain_at : gain_at + head],
        small[gain_at + head : gain_at + 2 * head],
        wide[3].T.astype(F32),
        small[width : 2 * width],
        summed[:, width : width + expert_count].astype(F32),
        expert_grad,
    )


def solution(mesh):
    in_specs = (
        P("expert", "tensor"),
        P("expert", "tensor"),
        P("expert", None),
        P("expert"),
        P("expert", None),
        P("expert", None),
        P(),
        P(None, "tensor"),
        P(None, "tensor"),
        P(None, "tensor"),
        P(),
        P(),
        P("tensor", None),
        P(),
        P(),
        P("expert", None, None, "tensor"),
    )
    out_specs = (
        P("expert", "tensor"),
        P("expert", "tensor"),
        P(),
        P(None, "tensor"),
        P(None, "tensor"),
        P(None, "tensor"),
        P(),
        P(),
        P("tensor", None),
        P(),
        P(),
        P("expert", None, None, "tensor"),
    )
    return jax.shard_map(body, mesh=mesh, in_specs=in_specs, out_specs=out_specs, check_vma=False)
```

```python
import functools
import math

import jax
import jax.numpy as jnp
from jax import lax
from jax.experimental import pallas as pl
from jax.experimental.pallas import tpu as pltpu
from jax.sharding import PartitionSpec as P

norm_eps = 1e-06
rope_base = 10000.0
mask_fill = -1e30


def rope_tables(positions, width):
    half_width = width // 2
    steps_idx = jnp.arange(half_width, dtype=jnp.float32)
    freqs = jnp.exp(steps_idx * (-2.0 * math.log(rope_base) / width))
    angles = positions.astype(jnp.float32)[:, None] * freqs[None, :]
    return (jnp.cos(angles), jnp.sin(angles))


def sequence_layout(lengths_row, count):
    seq_ends = jnp.cumsum(lengths_row)
    places = jnp.arange(count, dtype=jnp.int32)
    passed = (places[:, None] >= seq_ends[None, :]).astype(jnp.int32)
    seq_ids = jnp.sum(passed, axis=1)
    starts = jnp.sum(passed * lengths_row[None, :], axis=1)
    return (seq_ids, places - starts)


BF = jnp.bfloat16
F32 = jnp.float32
COST = pl.CostEstimate(flops=1, bytes_accessed=1, transcendentals=0)


def dot(left, right, left_dim=1, right_dim=0):
    return lax.dot_general(
        left, right, (((left_dim,), (right_dim,)), ((), ())), preferred_element_type=F32
    )


def exchange(value, axis):
    return lax.all_to_all(value, axis, split_axis=0, concat_axis=0, tiled=True)


def gather_blocks(value, axis):
    return exchange(jnp.broadcast_to(value[None], (lax.axis_size(axis),) + value.shape), axis)


def column_blocks(value, count):
    return jnp.stack(jnp.split(value, count, axis=1))


MESH = pl.DeviceIdType.MESH


def tensor_peers():
    me = lax.axis_index("tensor")
    count = lax.axis_size("tensor")
    return me, [(me + d) % count for d in range(1, count)]


def greet(axis, peers):
    barrier = pltpu.get_barrier_semaphore()
    for peer in peers:
        pl.semaphore_signal(barrier, inc=1, device_id={axis: peer}, device_id_type=MESH)
    return lambda: pl.semaphore_wait(barrier, len(peers))


class Post:
    def __init__(self, axis, send_sem, recv_sem):
        self.axis, self.send_sem, self.recv_sem = axis, send_sem, recv_sem
        self.started = []
        self.used = 0

    def push(self, source, target, peer):
        slot = self.used
        self.used += 1
        copy = pltpu.make_async_remote_copy(
            src_ref=source,
            dst_ref=target,
            send_sem=self.send_sem.at[slot],
            recv_sem=self.recv_sem.at[slot],
            device_id={self.axis: peer},
            device_id_type=MESH,
        )
        copy.start()
        self.started.append(copy)
        return copy

    def finish(self):
        for copy in self.started:
            copy.wait_send()
        self.started = []


def arrive(copies):
    for copy in copies:
        copy.wait_recv()


def ring(me):
    count = lax.axis_size("tensor")
    return (me + 1) % count, (me + count - 1) % count


def gather_start(post, ref, me):
    right, left = ring(me)
    return [post.push(ref.at[me], ref.at[me], peer) for peer in (right, left)]


def gather_relay(post, ref, me, first):
    right, left = ring(me)
    half = ref.shape[1] // 2
    first[0].wait_recv()
    here = ref.at[left, pl.ds(0, half)]
    one = post.push(here, here, right)
    first[1].wait_recv()
    here = ref.at[right, pl.ds(half, half)]
    return [one, post.push(here, here, left)]


def scatter_start(post, parts, halves, me):
    right, left = ring(me)
    far = ring(right)[0]
    half = parts.shape[1] // 2
    return [
        post.push(parts.at[far, pl.ds(0, half)], halves.at[0], right),
        post.push(parts.at[far, pl.ds(half, half)], halves.at[1], left),
    ]


def scatter_relay(post, parts, halves, box, me, first):
    right, left = ring(me)
    half = parts.shape[1] // 2
    copies = []
    for n, (peer, rows) in enumerate(((right, pl.ds(0, half)), (left, pl.ds(half, half)))):
        first[n].wait_recv()
        parts[peer, rows, :] = (parts[peer, rows, :].astype(F32) + halves[n].astype(F32)).astype(BF)
        copies.append(post.push(parts.at[peer], box.at[n], peer))
    return copies


def scatter_total(parts, box, me, copies):
    arrive(copies)
    return parts[me].astype(F32) + box[0].astype(F32) + box[1].astype(F32)


def fetch(pairs, sem):
    copies = [
        pltpu.make_async_copy(source, target, sem.at[n]) for n, (source, target) in enumerate(pairs)
    ]
    for copy in copies:
        copy.start()
    return copies


def turn(value, cos_rows, sin_rows):
    return value * cos_rows + pltpu.roll(value, value.shape[-1] // 2, 1) * sin_rows


def inverse_rms(total, width):
    return lax.rsqrt(total * (1.0 / width) + norm_eps)


def row_sum(value):
    return jnp.sum(value, axis=1, keepdims=True)


def softmax_rows(query, key, bias, scale):
    scores = dot(query, key, 1, 1) * scale + bias
    grown = jnp.exp(scores - jnp.max(scores, axis=1, keepdims=True))
    return grown / row_sum(grown)


def front_kernel(
    local, bias, cos_rows, sin_rows, gain1, gain2, q_gain, k_gain, router_t, routes, slot_of, slot_back, keep,
    wq_hbm, wk_hbm, wv_hbm, wo_hbm,
    x_out, dy_out, resid_out, mixed_out, q_out, k_out, qh_out, kh_out, vh_out, ob_out,
    gates_out, send_out, send_dy_out, pick_out, pick_y_out,
    wq, wk, wv, wo, x_all, dy_all, an, parts, halves, box, total, load_sem, send_sem, recv_sem,
):
    me = lax.axis_index("tensor")
    ready = greet("tensor", ring(me))
    loads = fetch([(wq_hbm, wq), (wk_hbm, wk), (wv_hbm, wv), (wo_hbm, wo)], load_sem)
    blocks, tok, col = x_all.shape
    width = blocks * col
    x_all[me] = local[:, :col]
    dy_all[me] = local[:, col:]
    ready()
    post = Post("tensor", send_sem, recv_sem)
    x_in = gather_relay(post, x_all, me, gather_start(post, x_all, me))
    dy_in = gather_start(post, dy_all, me)
    arrive(x_in)
    square = jnp.zeros((tok, 1), F32)
    for t in range(blocks):
        value = x_all[t].astype(F32)
        square = square + row_sum(value * value)
    r1 = inverse_rms(square, width)
    for t in range(blocks):
        an[t] = (x_all[t].astype(F32) * r1 * gain1[t : t + 1, :]).astype(BF)
    x_out[...] = x_all[...]

    for copy in loads:
        copy.wait()

    def project(weight):
        value = dot(an[0], weight[0:col, :])
        for t in range(1, blocks):
            value = value + dot(an[t], weight[t * col : (t + 1) * col, :])
        return value

    q_out[...] = project(wq)
    k_out[...] = project(wk)
    vh_out[...] = project(wv).astype(BF)
    dy_in = gather_relay(post, dy_all, me, dy_in)
    head = q_gain.shape[1]
    scale = 1.0 / math.sqrt(head)
    for h in range(col // head):
        lanes = slice(h * head, (h + 1) * head)
        for raw, gain, rotated in ((q_out, q_gain, qh_out), (k_out, k_gain, kh_out)):
            value = raw[:, lanes]
            value = value * inverse_rms(row_sum(value * value), head) * gain[...]
            rotated[:, lanes] = turn(value, cos_rows[...], sin_rows[...]).astype(BF)
        probs = softmax_rows(qh_out[:, lanes], kh_out[:, lanes], bias[...], scale).astype(BF)
        ob_out[:, lanes] = dot(probs, vh_out[:, lanes]).astype(BF)
    for t in range(blocks):
        parts[t] = dot(ob_out[...], wo[:, t * col : (t + 1) * col]).astype(BF)
    first = scatter_start(post, parts, halves, me)
    moved = scatter_relay(post, parts, halves, box, me, first)
    total[me] = scatter_total(parts, box, me, moved).astype(BF)
    arrive(gather_relay(post, total, me, gather_start(post, total, me)))
    square = jnp.zeros((tok, 1), F32)
    for t in range(blocks):
        value = x_all[t].astype(F32) + total[t].astype(F32)
        resid_out[t] = value
        square = square + row_sum(value * value)
    r2 = inverse_rms(square, width)
    logits = jnp.zeros((router_t.shape[0], tok), F32)
    for t in range(blocks):
        mixed_out[t] = (resid_out[t] * r2 * gain2[t : t + 1, :]).astype(BF)
        logits = logits + dot(router_t[:, t * col : (t + 1) * col], mixed_out[t], 1, 1)
    expert = lax.broadcasted_iota(jnp.int32, logits.shape, 0)
    top = routes.shape[0]
    chosen = [
        jnp.sum(jnp.where(routes[k : k + 1, :] == expert, logits, 0.0), axis=0, keepdims=True)
        for k in range(top)
    ]
    peak = functools.reduce(jnp.maximum, chosen)
    grown = [jnp.exp(value - peak) for value in chosen]
    whole = functools.reduce(jnp.add, grown)
    slots = send_out.shape[0]
    slot = lax.broadcasted_iota(jnp.int32, (slots, tok), 0)
    pick = jnp.zeros((slots, tok), F32)
    pick_back = jnp.zeros((slots, tok), F32)
    weight = jnp.zeros((slots, tok), F32)
    for k in range(top):
        gate = grown[k] / whole
        gates_out[k : k + 1, :] = gate
        hot = slot_of[k : k + 1, :] == slot
        pick = jnp.where(hot, 1.0, pick)
        pick_back = jnp.where(slot_back[k : k + 1, :] == slot, 1.0, pick_back)
        weight = jnp.where(hot, gate * keep[k : k + 1, :], weight)
    pick_out[...] = pick_back.T.astype(BF)
    pick_y_out[...] = pick.T.astype(BF)
    pick = pick.astype(BF)
    for t in range(blocks):
        send_out[:, t * col : (t + 1) * col] = dot(pick, mixed_out[t]).astype(BF)
    gate = row_sum(weight)
    first = gate.astype(BF)
    second = (gate - first.astype(F32)).astype(BF)
    third = (gate - first.astype(F32) - second.astype(F32)).astype(BF)
    lane = lax.broadcasted_iota(jnp.int32, (slots, 128), 1)
    facts = jnp.zeros((slots, 128), F32)
    for n, piece in enumerate((first, second, third)):
        facts = jnp.where(lane == n, piece.astype(F32), facts)
    send_out[:, width:] = facts.astype(BF)
    arrive(dy_in)
    dy_out[...] = dy_all[...]
    for t in range(blocks):
        send_dy_out[:, t * col : (t + 1) * col] = dot(pick, dy_all[t]).astype(BF)
    post.finish()


def front_call(local, bias, cos_rows, sin_rows, gain1, gain2, q_gain, k_gain, router_t, routes,
               slot_of, slot_back, keep, weights, slots):
    tok, both = local.shape
    col = both // 2
    blocks = gain1.shape[0]
    width = col * blocks
    shape = jax.ShapeDtypeStruct
    vmem = pl.BlockSpec(memory_space=pltpu.VMEM)
    tiles = (blocks, tok, col)
    top = routes.shape[0]
    return pl.pallas_call(
        front_kernel,
        out_shape=(
            shape(tiles, BF), shape(tiles, BF), shape(tiles, F32),
            shape(tiles, BF), shape((tok, col), F32), shape((tok, col), F32),
            shape((tok, col), BF), shape((tok, col), BF), shape((tok, col), BF),
            shape((tok, col), BF), shape((top, tok), F32), shape((slots, width + 128), BF),
            shape((slots, width), BF), shape((tok, slots), BF), shape((tok, slots), BF),
        ),
        in_specs=[vmem] * 13 + [pl.BlockSpec(memory_space=pl.ANY)] * 4,
        out_specs=(vmem,) * 15,
        scratch_shapes=[
            pltpu.VMEM((width, col), BF), pltpu.VMEM((width, col), BF), pltpu.VMEM((width, col), BF),
            pltpu.VMEM((col, width), BF),
            pltpu.VMEM(tiles, BF), pltpu.VMEM(tiles, BF), pltpu.VMEM(tiles, BF), pltpu.VMEM(tiles, BF),
            pltpu.VMEM((2, tok // 2, col), BF), pltpu.VMEM((2, tok, col), BF), pltpu.VMEM(tiles, BF),
            pltpu.SemaphoreType.DMA((4,)),
            pltpu.SemaphoreType.DMA((16,)), pltpu.SemaphoreType.DMA((16,)),
        ],
        compiler_params=pltpu.CompilerParams(
            collective_id=1, has_side_effects=True, vmem_limit_bytes=56 * 1024 * 1024
        ),
        name="front",
    )(local, bias, cos_rows, sin_rows, gain1, gain2, q_gain, k_gain, router_t, routes, slot_of,
      slot_back, keep, *weights)


def back_kernel(
    pick_t, ret_early, ret_late, slot_of, keep, gates, routes, bias, cos_rows, sin_rows, gain2,
    q_gain, k_gain, router, resid, dy_all, mixed, qh, kh, vh,
    q_hbm, k_hbm, wo_hbm,
    d_qkv, dr, d_mine, router_out, small_out,
    q_raw, k_raw, wo, parts, halves, box, total, dm, d_att, dg_mine, dg_box,
    load_sem, send_sem, recv_sem,
):
    me, peers = tensor_peers()
    ready = greet("tensor", peers)
    loads = fetch([(wo_hbm, wo), (q_hbm, q_raw), (k_hbm, k_raw)], load_sem)
    blocks, tok, col = parts.shape
    width = blocks * col
    post = Post("tensor", send_sem, recv_sem)
    early = ret_early.shape[0]
    for t in range(blocks):
        lanes = slice(t * col, (t + 1) * col)
        parts[t] = (
            dot(pick_t[:, :early], ret_early[:, lanes]) + dot(pick_t[:, early:], ret_late[:, lanes])
        ).astype(BF)
    ready()
    first = scatter_start(post, parts, halves, me)
    top = routes.shape[0]
    for n, (ret, base) in enumerate(((ret_early, 0), (ret_late, early))):
        dgate = row_sum(ret[:, width : width + 128].astype(F32))
        slot = lax.broadcasted_iota(jnp.int32, (ret.shape[0], tok), 0) + base
        for k in range(top):
            hot = slot_of[k : k + 1, :] == slot
            found = jnp.sum(jnp.where(hot, dgate, 0.0), axis=0, keepdims=True)
            dg_mine[k : k + 1, :] = dg_mine[k : k + 1, :] + found if n else found
    dg_in = [post.push(dg_mine, dg_box.at[d], peer) for d, peer in enumerate(peers)]
    moved = scatter_relay(post, parts, halves, box, me, first)
    total[me] = scatter_total(parts, box, me, moved).astype(BF)
    total_first = gather_start(post, total, me)

    arrive(dg_in)
    d_gates = dg_mine[...]
    for d in range(blocks - 1):
        d_gates = d_gates + dg_box[d]
    d_gates = d_gates * keep[...]
    gate = gates[...]
    d_chosen = gate * (d_gates - jnp.sum(gate * d_gates, axis=0, keepdims=True))
    expert = lax.broadcasted_iota(jnp.int32, (router.shape[1], tok), 0)
    d_logits_t = jnp.zeros(expert.shape, F32)
    for k in range(top):
        hot = routes[k : k + 1, :] == expert
        d_logits_t = jnp.where(hot, d_chosen[k : k + 1, :], d_logits_t)
    d_logits = d_logits_t.T.astype(BF)
    square = jnp.zeros((tok, 1), F32)
    for t in range(blocks):
        rows = slice(t * col, (t + 1) * col)
        dm[t] = dot(d_logits, router[rows, :], 1, 1)
        square = square + row_sum(resid[t] * resid[t])
    r2 = inverse_rms(square, width)
    total_moved = gather_relay(post, total, me, total_first)
    for t in range(blocks):
        rows = slice(t * col, (t + 1) * col)
        router_out[rows, :] = dot(mixed[t].T, d_logits).astype(BF)
    arrive(total_moved)
    cross = jnp.zeros((tok, 1), F32)
    for t in range(blocks):
        dm[t] = dm[t] + total[t].astype(F32)
        cross = cross + row_sum(resid[t] * gain2[t : t + 1, :] * dm[t])
    cross = cross * (1.0 / width) * r2 * r2 * r2
    small_out[...] = jnp.zeros_like(small_out)
    for t in range(blocks):
        d_mixed = dm[t]
        small_out[t : t + 1, :] = jnp.sum(d_mixed * resid[t] * r2, axis=0, keepdims=True)
        d_resid = dy_all[t].astype(F32) + r2 * gain2[t : t + 1, :] * d_mixed - resid[t] * cross
        dm[t] = d_resid
        dr[t] = d_resid.astype(BF)
    d_mine[...] = dm[me]
    for copy in loads:
        copy.wait()
    value = dot(dr[0], wo[:, 0:col], 1, 1)
    for t in range(1, blocks):
        value = value + dot(dr[t], wo[:, t * col : (t + 1) * col], 1, 1)
    d_att[...] = value.astype(BF)

    head = q_gain.shape[1]
    scale = 1.0 / math.sqrt(head)
    q_part = jnp.zeros((1, head), F32)
    k_part = jnp.zeros((1, head), F32)

    def unturn(grown, raw, gain):
        d_unit = grown * cos_rows[...] - pltpu.roll(grown, head // 2, 1) * sin_rows[...]
        inverse = inverse_rms(row_sum(raw * raw), head)
        unit = raw * inverse
        gain_part = jnp.sum(d_unit * unit, axis=0, keepdims=True)
        d_unit = d_unit * gain[...]
        d_raw = inverse * (d_unit - unit * (row_sum(unit * d_unit) * (1.0 / head)))
        return d_raw.astype(BF), gain_part

    for h in range(col // head):
        lanes = slice(h * head, (h + 1) * head)
        probs = softmax_rows(qh[:, lanes], kh[:, lanes], bias[...], scale)
        d_head = d_att[:, lanes]
        d_probs = dot(d_head, vh[:, lanes], 1, 1)
        d_scores = probs * (d_probs - row_sum(probs * d_probs))
        d_qkv[:, 2 * col + h * head : 2 * col + (h + 1) * head] = dot(
            probs.T.astype(BF), d_head
        ).astype(BF)
        d_q, part = unturn(dot(d_scores.astype(BF), kh[:, lanes]) * scale, q_raw[:, lanes], q_gain)
        q_part = q_part + part
        d_qkv[:, lanes] = d_q
        d_k, part = unturn(dot(d_scores.T.astype(BF), qh[:, lanes]) * scale, k_raw[:, lanes], k_gain)
        k_part = k_part + part
        d_qkv[:, col + h * head : col + (h + 1) * head] = d_k
    small_out[blocks : blocks + 1, :head] = q_part
    small_out[blocks : blocks + 1, head : 2 * head] = k_part
    post.finish()


def back_call(pick_t, ret_early, ret_late, slot_of, keep, gates, routes, bias, cos_rows, sin_rows,
              gain2, q_gain, k_gain, router, resid, dy_all, mixed, qh, kh, vh, q_raw, k_raw, wo):
    blocks, tok, col = dy_all.shape
    width = blocks * col
    tiles = (blocks, tok, col)
    shape = jax.ShapeDtypeStruct
    vmem = pl.BlockSpec(memory_space=pltpu.VMEM)
    top = routes.shape[0]
    count = 8 + blocks - 1
    return pl.pallas_call(
        back_kernel,
        out_shape=(
            shape((tok, 3 * col), BF), shape(tiles, BF), shape((tok, col), F32),
            shape((width, 128), BF), shape((8, col), F32),
        ),
        in_specs=[vmem] * 20 + [pl.BlockSpec(memory_space=pl.ANY)] * 3,
        out_specs=(vmem,) * 5,
        scratch_shapes=[
            pltpu.VMEM((tok, col), F32), pltpu.VMEM((tok, col), F32), pltpu.VMEM((col, width), BF),
            pltpu.VMEM(tiles, BF), pltpu.VMEM((2, tok // 2, col), BF), pltpu.VMEM((2, tok, col), BF),
            pltpu.VMEM(tiles, BF), pltpu.VMEM(tiles, F32), pltpu.VMEM((tok, col), BF),
            pltpu.VMEM((top, tok), F32), pltpu.VMEM((blocks - 1, top, tok), F32),
            pltpu.SemaphoreType.DMA((3,)),
            pltpu.SemaphoreType.DMA((count,)), pltpu.SemaphoreType.DMA((count,)),
        ],
        compiler_params=pltpu.CompilerParams(
            collective_id=2, has_side_effects=True, vmem_limit_bytes=48 * 1024 * 1024
        ),
        cost_estimate=pl.CostEstimate(
            flops=20_000_000_000, bytes_accessed=1, transcendentals=0
        ),
        name="back",
    )(pick_t, ret_early, ret_late, slot_of, keep, gates, routes, bias, cos_rows, sin_rows, gain2,
      q_gain, k_gain, router, resid, dy_all, mixed, qh, kh, vh, q_raw, k_raw, wo)


def expert_kernel(side, per, early, rows_ref, grads_ref, w_ref, *rest):
    if side:
        y_rest, dx_rest, *rest = rest
        y_ref, dx_ref, *rest = rest
    else:
        dx_ref, y_rest, dx_rest, *rest = rest
    grad_ref, rows, rows_t, dys, dys_t, y_acc, dx_acc, gate_of, dgate = rest
    step = pl.program_id(0)
    count, width = rows.shape
    both = rows_ref.shape[0]
    late = per - early

    def selector(shape, source_of):
        place = lax.broadcasted_iota(jnp.int32, shape, 0)
        source = lax.broadcasted_iota(jnp.int32, shape, 1)
        return (source_of(place) == source).astype(F32).astype(BF)

    @pl.when(step == 0)
    def _():
        pick = selector((count, both), lambda p: p + (p // per + side) * per)
        rows[...] = dot(pick, rows_ref[:, :width]).astype(BF)
        gate_of[...] = row_sum(dot(pick, rows_ref[:, width:]))
        dy_rows = dot(pick, grads_ref[...])
        dys[...] = dy_rows.astype(BF)
        rows_t[...] = rows[...].T
        dys_t[...] = (dy_rows * gate_of[...]).astype(BF).T
        dgate[...] = jnp.zeros_like(dgate)
        y_acc[...] = jnp.zeros_like(y_acc)
        dx_acc[...] = jnp.zeros_like(dx_acc)

    w_gate, w_up, w_down = w_ref[0, 0], w_ref[0, 1], w_ref[0, 2]
    gate = dot(rows[...], w_gate)
    up = dot(rows[...], w_up)
    d_raw = dot(dys[...], w_down)
    d_act = d_raw * gate_of[...]
    sig = 1.0 / (1.0 + jnp.exp(-gate))
    silu = gate * sig
    act = (silu * up).astype(BF)
    dgate[...] += row_sum(act.astype(F32) * d_raw)
    d_gate = (d_act * up * sig * (1.0 + gate * (1.0 - sig))).astype(BF)
    d_up = (d_act * silu).astype(BF)
    y_acc[...] += dot(act, w_down, 1, 1)
    dx_acc[...] += dot(d_gate, w_gate, 1, 1) + dot(d_up, w_up, 1, 1)
    grad_ref[0, 0] = dot(rows_t[...], d_gate).astype(BF)
    grad_ref[0, 1] = dot(rows_t[...], d_up).astype(BF)
    grad_ref[0, 2] = dot(dys_t[...], act).astype(BF)

    @pl.when(step == pl.num_programs(0) - 1)
    def _():
        first = dgate[...].astype(BF).astype(F32)
        lane = lax.broadcasted_iota(jnp.int32, (count, 128), 1)
        facts = jnp.where(lane == 0, first, jnp.where(lane == 1, dgate[...] - first, 0.0))
        facts = facts.astype(BF)
        y_rows = (y_acc[...] * gate_of[...]).astype(BF)
        dx_rows = dx_acc[...].astype(BF)
        if side:
            here = selector(
                (y_ref.shape[0], count),
                lambda p: jnp.where(p % (2 * per) < per, -1, p // (2 * per) * per + p % (2 * per) - per),
            )
            there = selector(
                (y_ref.shape[0], count),
                lambda p: jnp.where(p % (2 * per) < per, p // (2 * per) * per + p % (2 * per), -1),
            )
            y_ref[...] = (dot(here, y_rows) + dot(there, y_rest[...])).astype(BF)
            chunk = per + late
            here = selector(
                (dx_ref.shape[0], count),
                lambda p: jnp.where(p % chunk < late, -1, p // chunk * per + p % chunk - late),
            )
            there = selector(
                (dx_ref.shape[0], dx_rest.shape[0]),
                lambda p: jnp.where(p % chunk < late, p // chunk * late + p % chunk, -1),
            )
            dx_ref[:, :width] = (dot(here, dx_rows) + dot(there, dx_rest[:, :width])).astype(BF)
            dx_ref[:, width:] = (dot(here, facts) + dot(there, dx_rest[:, width:])).astype(BF)
        else:
            y_rest[...] = y_rows
            soon = selector((dx_ref.shape[0], count), lambda p: p // early * per + p % early)
            later = selector(
                (dx_rest.shape[0], count), lambda p: p // late * per + early + p % late
            )
            for pick, dx_out in ((soon, dx_ref), (later, dx_rest)):
                dx_out[:, :width] = dot(pick, dx_rows).astype(BF)
                dx_out[:, width:] = dot(pick, facts).astype(BF)


def expert_call(side, per, early, rows, grads, weights, rest):
    quarters, _, width, hidden = weights.shape
    both = rows.shape[0]
    count = both // 2
    groups = count // per
    shape = jax.ShapeDtypeStruct

    def whole(value):
        return pl.BlockSpec(value.shape, lambda q: (0, 0), pipeline_mode=pl.Buffered(1))

    def plain(size):
        return shape((groups * size, width), BF)

    def wider(size):
        return shape((groups * size, width + 128), BF)

    block = pl.BlockSpec((1, 3, width, hidden), lambda q: (q, 0, 0, 0))
    if side:
        outs = [plain(2 * per), wider(2 * per - early)]
    else:
        outs = [wider(early), plain(per), wider(per - early)]
    return pl.pallas_call(
        functools.partial(expert_kernel, side, per, early),
        grid=(quarters,),
        out_shape=tuple(outs) + (shape(weights.shape, BF),),
        in_specs=[whole(rows), whole(grads), block] + [whole(value) for value in rest],
        out_specs=tuple(whole(value) for value in outs) + (block,),
        scratch_shapes=[
            pltpu.VMEM((count, width), BF),
            pltpu.VMEM((width, count), BF),
            pltpu.VMEM((count, width), BF),
            pltpu.VMEM((width, count), BF),
            pltpu.VMEM((count, width), F32),
            pltpu.VMEM((count, width), F32),
            pltpu.VMEM((count, 1), F32),
            pltpu.VMEM((count, 1), F32),
        ],
        compiler_params=pltpu.CompilerParams(vmem_limit_bytes=60 * 1024 * 1024),
        cost_estimate=COST,
        name=f"expert{side}",
    )(rows, grads, weights, *rest)


def plane():
    me = lax.axis_index("expert")
    core, z, y = me % 2, (me // 2) % 4, me // 8
    return [
        (core, me + 1 - 2 * core),
        ((y + y // 2) % 2, me + 8 * (1 - 2 * (y % 2))),
        (y // 2, me + 8 * (3 - 2 * y)),
        ((z + z // 2) % 2, me + 2 * (1 - 2 * (z % 2))),
        (z // 2, me + 2 * (3 - 2 * z)),
    ]

ORDERS = ((1, 3, 2, 4), (3, 2, 4, 1), (2, 4, 1, 3), (4, 1, 3, 2))

def reduce_kernel(
    d_qkv, dr, d_mine, router_part, small_in, x_all, gain1, ob, pick_y, ret_y,
    resid_hbm, wq_hbm, wk_hbm, wv_hbm,
    wide_out, dx_out, out_out, small_out,
    wq, wk, wv, resid, parts, y_parts, halves, box_x, note, buf, box, got,
    load_sem, out_sem, x_send, x_recv, send_sem, recv_sem,
):
    me, peers = tensor_peers()
    dims = plane()
    barrier = pltpu.get_barrier_semaphore()
    for axis, others in (("tensor", peers), ("expert", [partner for _, partner in dims])):
        for other in others:
            pl.semaphore_signal(barrier, inc=1, device_id={axis: other}, device_id_type=MESH)
    loads = fetch(
        [(wq_hbm, wq), (wk_hbm, wk), (wv_hbm, wv), (resid_hbm.at[me], resid)], load_sem
    )
    blocks, tok, col = x_all.shape
    width = blocks * col
    head = col // blocks
    core = dims[0][0]
    square = jnp.zeros((tok, 1), F32)
    for t in range(blocks):
        value = x_all[t].astype(F32)
        square = square + row_sum(value * value)
    r1 = inverse_rms(square, width)
    for copy in loads:
        copy.wait()
    for t in range(blocks):
        rows = slice(t * col, (t + 1) * col)
        parts[t] = (
            dot(d_qkv[:, 0:col], wq[rows, :], 1, 1)
            + dot(d_qkv[:, col : 2 * col], wk[rows, :], 1, 1)
            + dot(d_qkv[:, 2 * col : 3 * col], wv[rows, :], 1, 1)
        ).astype(BF)
    pl.semaphore_wait(barrier, len(peers) + len(dims))
    post_x = Post("tensor", x_send, x_recv)
    post = Post("expert", send_sem, recv_sem)
    x_halves, x_box = halves.at[pl.ds(0, 2)], box_x.at[pl.ds(0, 2)]
    y_halves, y_box = halves.at[pl.ds(2, 2)], box_x.at[pl.ds(2, 2)]
    x_first = scatter_start(post_x, parts, x_halves, me)

    chunks = buf.shape[0] // blocks
    rows_chunk = buf.shape[1]

    def products(t):
        here = pl.ds(t * chunks, chunks)
        normed = (x_all[t].astype(F32) * r1 * gain1[pl.ds(t, 1), :]).T.astype(BF)
        for n in range(3):
            lanes = slice(n * col, (n + 1) * col)
            value = dot(normed, d_qkv[:, lanes]).astype(BF)
            buf[here, :, lanes] = value.reshape(chunks, rows_chunk, col)
        value = dot(dr[t].T, ob[...]).astype(BF)
        buf[here, :, 3 * col : 4 * col] = value.reshape(chunks, rows_chunk, col)
        value = router_part[pl.ds(t * col, col), :]
        buf[here, :, 4 * col :] = value.reshape(chunks, rows_chunk, value.shape[1])

    def add(target, place, first, count):
        def one(i, _):
            total = buf[place + i].astype(F32) + box[first + i].astype(F32)
            target[place + i] = total.astype(BF)
            return 0

        lax.fori_loop(0, count, one, 0)

    copies = []
    for n in range(2):
        products(2 * (1 - core) + n)
        for s in range(2 * n, 2 * n + 2):
            source = buf.at[pl.ds((1 - core) * 64 + s * 16, 16)]
            copies.append(post.push(source, box.at[pl.ds(31 * s, 16)], dims[0][1]))
    x_moved = scatter_relay(post_x, parts, x_halves, x_box, me, x_first)
    for n in range(2):
        products(2 * core + n)
    place = [core * 64 + s * 16 for s in range(4)]
    size, first = 16, 0

    def halve(k):
        for s in range(4):
            copies[s].wait_recv()
            add(buf, place[s], 31 * s + first, size)
            bit, partner = dims[ORDERS[s][k]]
            half = size // 2
            copies[s] = post.push(
                buf.at[pl.ds(place[s] + (1 - bit) * half, half)],
                box.at[pl.ds(31 * s + first + size, half)],
                partner,
            )
            place[s] = place[s] + bit * half

    halve(0)
    first, size = first + size, size // 2

    for t in range(blocks):
        y_parts[t] = dot(pick_y[...], ret_y[:, t * col : (t + 1) * col]).astype(BF)
    y_first = scatter_start(post_x, y_parts, y_halves, me)
    d_an = scatter_total(parts, x_box, me, x_moved)
    x_mine = x_all[me].astype(F32)
    grown = gain1[pl.ds(me, 1), :] * d_an
    mean_part = row_sum(x_mine * grown)
    note[me, 0:8, :] = jnp.broadcast_to(
        jnp.sum(d_an * x_mine * r1, axis=0, keepdims=True), (8, col)
    )
    note[me, 8:16, 0:tok] = jnp.broadcast_to(mean_part, (tok, 128)).T[0:8, :]
    note[me, 8:16, tok:] = jnp.broadcast_to(small_in[blocks : blocks + 1, : 2 * head], (8, 2 * head))
    note_in = [post_x.push(note.at[me], note.at[me], peer) for peer in peers]

    halve(1)
    first, size = first + size, size // 2
    y_moved = scatter_relay(post_x, y_parts, y_halves, y_box, me, y_first)
    halve(2)
    first, size = first + size, size // 2
    halve(3)
    first, size = first + size, size // 2
    for s in range(4):
        copies[s].wait_recv()
        add(got, place[s], 31 * s + first, 1)
        here = got.at[pl.ds(place[s], 1)]
        copies[s] = post.push(here, here, dims[ORDERS[s][3]][1])

    arrive(note_in)
    facts = note[0, 8:16, :]
    for t in range(1, blocks):
        facts = facts + note[t, 8:16, :]
    for t in range(blocks):
        small_out[t : t + 1, :] = note[t, 0:1, :]
        small_out[blocks + t : blocks + t + 1, :] = small_in[t : t + 1, :]
    small_out[2 * blocks :, :] = facts
    mean = jnp.broadcast_to(facts[0:1, 0:tok], (128, tok)).T[:, 0:1] * (1.0 / width)
    dx_out[...] = (d_mine[...] + r1 * grown - x_mine * (r1 * r1 * r1 * mean)).astype(BF)

    size = 1
    stores = []
    for k in range(3, -1, -1):
        for s in range(4):
            copies[s].wait_recv()
            bit, _ = dims[ORDERS[s][k]]
            place[s] = place[s] - bit * size
            partner = dims[ORDERS[s][k - 1]][1] if k else dims[0][1]
            here = got.at[pl.ds(place[s], 2 * size)]
            copies[s] = post.push(here, here, partner)
            if not k:
                stores.append(
                    pltpu.make_async_copy(here, wide_out.at[pl.ds(place[s], 16)], out_sem.at[s])
                )
                stores[-1].start()
        size *= 2
        if k == 2:
            out_out[...] = (resid[...] + scatter_total(y_parts, y_box, me, y_moved)).astype(BF)
    for s in range(4):
        copies[s].wait_recv()
        there = pl.ds((1 - core) * 64 + s * 16, 16)
        stores.append(pltpu.make_async_copy(got.at[there], wide_out.at[there], out_sem.at[4 + s]))
        stores[-1].start()
    post.finish()
    post_x.finish()
    for store in stores:
        store.wait()


def reduce_call(d_qkv, dr, d_mine, router_part, small, x_all, gain1, ob, pick_y, ret_y, resid,
                weights):
    blocks, tok, col = x_all.shape
    width = blocks * col
    tiles = (blocks, tok, col)
    wide = (128, 16, 4 * col + 128)
    shape = jax.ShapeDtypeStruct
    vmem = pl.BlockSpec(memory_space=pltpu.VMEM)
    hbm = pl.BlockSpec(memory_space=pl.ANY)
    count = 8 + blocks - 1
    return pl.pallas_call(
        reduce_kernel,
        out_shape=(
            shape(wide, BF), shape((tok, col), BF), shape((tok, col), BF), shape((16, col), F32),
        ),
        in_specs=[vmem] * 10 + [hbm] * 4,
        out_specs=(hbm, vmem, vmem, vmem),
        scratch_shapes=[
            pltpu.VMEM((width, col), BF), pltpu.VMEM((width, col), BF), pltpu.VMEM((width, col), BF),
            pltpu.VMEM((tok, col), F32), pltpu.VMEM(tiles, BF), pltpu.VMEM(tiles, BF),
            pltpu.VMEM((4, tok // 2, col), BF), pltpu.VMEM((4, tok, col), BF),
            pltpu.VMEM((blocks, 16, col), F32),
            pltpu.VMEM(wide, BF), pltpu.VMEM((124,) + wide[1:], BF), pltpu.VMEM(wide, BF),
            pltpu.SemaphoreType.DMA((4,)), pltpu.SemaphoreType.DMA((8,)),
            pltpu.SemaphoreType.DMA((count,)), pltpu.SemaphoreType.DMA((count,)),
            pltpu.SemaphoreType.DMA((40,)), pltpu.SemaphoreType.DMA((40,)),
        ],
        compiler_params=pltpu.CompilerParams(
            collective_id=3, has_side_effects=True, vmem_limit_bytes=60 * 1024 * 1024
        ),
        cost_estimate=COST,
        name="reduce",
    )(d_qkv, dr, d_mine, router_part, small, x_all, gain1, ob, pick_y, ret_y, resid, *weights)


def body(
    tokens,
    out_grad,
    seq_lengths,
    dest_index,
    routes,
    pair_order,
    norm1_gain,
    w_query,
    w_key,
    w_value,
    q_gain,
    k_gain,
    w_output,
    norm2_gain,
    w_router,
    expert_w,
):
    groups = lax.axis_size("expert")
    tensor_count = lax.axis_size("tensor")
    group_id = lax.axis_index("expert")
    tensor_id = lax.axis_index("tensor")
    tok_count, col_count = tokens.shape
    width = col_count * tensor_count
    move_rows = tok_count // groups
    expert_count = w_router.shape[1]
    top_count = routes.shape[1]
    local_experts = expert_w.shape[0]

    w_stored = jnp.transpose(expert_w, (0, 2, 1, 3))
    w_first = lax.all_gather(w_stored[0], "tensor", axis=0)

    routes_t = routes.T
    order_t = pair_order[0].reshape(tok_count, top_count).T
    pair_expert = routes_t.reshape(-1)
    pair_total = tok_count * top_count
    base = pair_expert * pair_total
    keyed = base + order_t.reshape(-1)
    before = (keyed[None, :] < keyed[:, None]) & (keyed[None, :] >= base[:, None])
    ranks = jnp.sum(before.astype(jnp.int32), axis=1).reshape(top_count, tok_count)
    expert_axis = jnp.arange(expert_count, dtype=jnp.int32)
    route_hot = routes_t[:, None, :] == expert_axis[None, :, None]
    counts = jnp.sum(route_hot.astype(F32), axis=(0, 2))

    places = jnp.arange(tok_count, dtype=jnp.int32)
    arrival_rank = jnp.sum((dest_index[None, :] < dest_index[:, None]).astype(jnp.int32), axis=1)
    by_rank = (arrival_rank[None, :] == places[:, None]).astype(BF)
    inner = jnp.broadcast_to((dest_index % tok_count).astype(BF)[:, None], (tok_count, 64))
    facts = jnp.broadcast_to(counts.astype(BF)[None, :], (tok_count, expert_count))
    outgoing = dot(by_rank, jnp.concatenate([tokens, out_grad, inner, facts], axis=1)).astype(BF)
    outgoing, w_stored = lax.optimization_barrier((outgoing, w_stored))
    w_second = lax.all_gather(w_stored[1], "tensor", axis=0)
    got = exchange(outgoing.reshape(groups, move_rows, -1), "expert")
    all_counts = got[:, 0, 2 * col_count + 64 :].astype(jnp.int32)
    lower = jnp.arange(groups, dtype=jnp.int32) < group_id
    offsets = jnp.sum(jnp.where(lower[:, None], all_counts, 0), axis=0)
    mine = got[:, :, 2 * col_count].astype(jnp.int32).reshape(-1)
    put = (mine[None, :] == places[:, None]).astype(BF)
    local = dot(put, got.reshape(tok_count, -1)[:, : 2 * col_count]).astype(BF)
    capacity = 5 * tok_count * groups * top_count // (4 * expert_count)
    most_rows = 3 * tok_count * top_count // (2 * expert_count)
    per = most_rows // tensor_count
    slots = expert_count * per
    slot_global = jnp.sum(jnp.where(route_hot, offsets[None, :, None], 0), axis=1) + ranks
    kept = slot_global < capacity
    keep_mask = kept.astype(F32)
    here = kept & (ranks % tensor_count == tensor_id)
    place = ranks // tensor_count
    slot_of = jnp.where(here, routes_t * per + place, -1)
    early = per // 8 * 8
    side, owner = routes_t % local_experts, routes_t // local_experts
    ahead = owner * early + place
    behind = groups * early + owner * (2 * per - early)
    behind = behind + jnp.where(side == 0, place - early, per - early + place)
    slot_back = jnp.where(here, jnp.where((side == 0) & (place < early), ahead, behind), -1)

    seq_ids, positions = sequence_layout(seq_lengths[0], tok_count)
    bias = jnp.where(seq_ids[:, None] == seq_ids[None, :], 0.0, mask_fill)
    cos_tab, sin_tab = rope_tables(positions, q_gain.shape[0])
    cos_rows = jnp.concatenate([cos_tab, cos_tab], axis=1)
    sin_rows = jnp.concatenate([-sin_tab, sin_tab], axis=1)
    gain1 = norm1_gain.astype(F32).reshape(tensor_count, col_count)
    gain2 = norm2_gain.astype(F32).reshape(tensor_count, col_count)
    head_gains = (q_gain.astype(F32)[None], k_gain.astype(F32)[None])
    router = jnp.pad(w_router, ((0, 0), (0, 128 - expert_count)))
    weights = (w_query, w_key, w_value, w_output)
    (
        x_all, dy_all, resid, mixed, q_raw, k_raw, qh, kh, vh, attended, gates, send_rows,
        send_dy, pick_t, pick_y,
    ) = front_call(
        local, bias, cos_rows, sin_rows, gain1, gain2, *head_gains, router.T, routes_t, slot_of,
        slot_back, keep_mask, weights, slots,
    )
    recv_rows = exchange(send_rows.reshape(groups, -1, width + 128), "expert")
    recv_dy = exchange(send_dy.reshape(groups, -1, width), "expert")
    recv_rows = recv_rows.reshape(slots, -1)
    recv_dy = recv_dy.reshape(slots, -1)
    def homeward(value):
        return exchange(value.reshape(groups, -1, value.shape[1]), "expert").reshape(value.shape)

    d_early, *rest, partial = expert_call(0, per, early, recv_rows, recv_dy, w_first, ())
    grad_first = lax.psum_scatter(partial, "tensor", scatter_dimension=0, tiled=False)
    ret_early = homeward(d_early)
    ret_early, later_rows = lax.optimization_barrier((ret_early, recv_rows))
    y_rows, d_late, partial = expert_call(1, per, early, later_rows, recv_dy, w_second, rest)
    grad_second = lax.psum_scatter(partial, "tensor", scatter_dimension=0, tiled=False)
    ret_late = homeward(d_late)
    ret_late, y_rows = lax.optimization_barrier((ret_late, y_rows))
    ret_y = homeward(y_rows)
    d_qkv, dr, d_mine, router_part, small = back_call(
        pick_t, ret_early, ret_late, slot_back, keep_mask, gates, routes_t, bias, cos_rows,
        sin_rows, gain2, *head_gains, router, resid, dy_all, mixed, qh, kh, vh, q_raw, k_raw,
        w_output,
    )
    summed, dx_slice, out_slice, small = reduce_call(
        d_qkv, dr, d_mine, router_part, small, x_all, gain1, attended, pick_y, ret_y, resid,
        weights[:3],
    )
    summed = summed.reshape(width, -1)

    going = dot(put, jnp.concatenate([out_slice, dx_slice], axis=1), 0, 0).astype(BF)
    small = small[:9].astype(BF).reshape(move_rows, -1)
    small = jnp.pad(small, ((0, 0), (0, -small.shape[1] % 128)))
    small = jnp.broadcast_to(small[None], (groups,) + small.shape)
    back = exchange(jnp.concatenate([going.reshape(groups, move_rows, -1), small], axis=2), "expert")
    small = jnp.sum(back[:, :, 2 * col_count :].astype(F32), axis=0)[:, : 9 * col_count // move_rows]
    small = small.reshape(-1)
    back = dot(by_rank, back.reshape(tok_count, -1)[:, : 2 * col_count], 0, 0).astype(BF)
    expert_grad = jnp.transpose(jnp.stack([grad_first, grad_second]).astype(F32), (0, 2, 1, 3))
    wide = [summed[:, n * col_count : (n + 1) * col_count] for n in range(4)]
    gain_at = 2 * width + tok_count
    head = q_gain.shape[0]
    return (
        back[:, :col_count],
        back[:, col_count:],
        small[:width],
        wide[0].astype(F32),
        wide[1].astype(F32),
        wide[2].astype(F32),
        small[gain_at : gain_at + head],
        small[gain_at + head : gain_at + 2 * head],
        wide[3].T.astype(F32),
        small[width : 2 * width],
        summed[:, width : width + expert_count].astype(F32),
        expert_grad,
    )


def solution(mesh):
    in_specs = (
        P("expert", "tensor"),
        P("expert", "tensor"),
        P("expert", None),
        P("expert"),
        P("expert", None),
        P("expert", None),
        P(),
        P(None, "tensor"),
        P(None, "tensor"),
        P(None, "tensor"),
        P(),
        P(),
        P("tensor", None),
        P(),
        P(),
        P("expert", None, None, "tensor"),
    )
    out_specs = (
        P("expert", "tensor"),
        P("expert", "tensor"),
        P(),
        P(None, "tensor"),
        P(None, "tensor"),
        P(None, "tensor"),
        P(),
        P(),
        P("tensor", None),
        P(),
        P(),
        P("expert", None, None, "tensor"),
    )
    return jax.shard_map(body, mesh=mesh, in_specs=in_specs, out_specs=out_specs, check_vma=False)
```

```python
import functools
import math

import jax
import jax.numpy as jnp
from jax import lax
from jax.experimental import pallas as pl
from jax.experimental.pallas import tpu as pltpu
from jax.sharding import PartitionSpec as P

norm_eps = 1e-06
rope_base = 10000.0
mask_fill = -1e30


def rope_tables(positions, width):
    half_width = width // 2
    steps_idx = jnp.arange(half_width, dtype=jnp.float32)
    freqs = jnp.exp(steps_idx * (-2.0 * math.log(rope_base) / width))
    angles = positions.astype(jnp.float32)[:, None] * freqs[None, :]
    return (jnp.cos(angles), jnp.sin(angles))


def sequence_layout(lengths_row, count):
    seq_ends = jnp.cumsum(lengths_row)
    places = jnp.arange(count, dtype=jnp.int32)
    passed = (places[:, None] >= seq_ends[None, :]).astype(jnp.int32)
    seq_ids = jnp.sum(passed, axis=1)
    starts = jnp.sum(passed * lengths_row[None, :], axis=1)
    return (seq_ids, places - starts)


BF = jnp.bfloat16
F32 = jnp.float32
SHADOW = pl.CostEstimate(flops=40_000_000_000, bytes_accessed=1, transcendentals=0)
COST = pl.CostEstimate(flops=1, bytes_accessed=1, transcendentals=0)


def dot(left, right, left_dim=1, right_dim=0):
    return lax.dot_general(
        left, right, (((left_dim,), (right_dim,)), ((), ())), preferred_element_type=F32
    )


def exchange(value, axis):
    return lax.all_to_all(value, axis, split_axis=0, concat_axis=0, tiled=True)


def gather_blocks(value, axis):
    return exchange(jnp.broadcast_to(value[None], (lax.axis_size(axis),) + value.shape), axis)


def column_blocks(value, count):
    return jnp.stack(jnp.split(value, count, axis=1))


MESH = pl.DeviceIdType.MESH


def tensor_peers():
    me = lax.axis_index("tensor")
    count = lax.axis_size("tensor")
    return me, [(me + d) % count for d in range(1, count)]


def greet(axis, peers):
    barrier = pltpu.get_barrier_semaphore()
    for peer in peers:
        pl.semaphore_signal(barrier, inc=1, device_id={axis: peer}, device_id_type=MESH)
    return lambda: pl.semaphore_wait(barrier, len(peers))


class Post:
    def __init__(self, axis, send_sem, recv_sem):
        self.axis, self.send_sem, self.recv_sem = axis, send_sem, recv_sem
        self.started = []
        self.used = 0

    def push(self, source, target, peer):
        slot = self.used
        self.used += 1
        copy = pltpu.make_async_remote_copy(
            src_ref=source,
            dst_ref=target,
            send_sem=self.send_sem.at[slot],
            recv_sem=self.recv_sem.at[slot],
            device_id={self.axis: peer},
            device_id_type=MESH,
        )
        copy.start()
        self.started.append(copy)
        return copy

    def finish(self):
        for copy in self.started:
            copy.wait_send()
        self.started = []


def arrive(copies):
    for copy in copies:
        copy.wait_recv()


def ring(me):
    count = lax.axis_size("tensor")
    return (me + 1) % count, (me + count - 1) % count


def gather_start(post, ref, me):
    right, left = ring(me)
    return [post.push(ref.at[me], ref.at[me], peer) for peer in (right, left)]


def gather_relay(post, ref, me, first):
    right, left = ring(me)
    half = ref.shape[1] // 2
    first[0].wait_recv()
    here = ref.at[left, pl.ds(0, half)]
    one = post.push(here, here, right)
    first[1].wait_recv()
    here = ref.at[right, pl.ds(half, half)]
    return [one, post.push(here, here, left)]


def scatter_start(post, parts, halves, me):
    right, left = ring(me)
    far = ring(right)[0]
    half = parts.shape[1] // 2
    return [
        post.push(parts.at[far, pl.ds(0, half)], halves.at[0], right),
        post.push(parts.at[far, pl.ds(half, half)], halves.at[1], left),
    ]


def scatter_relay(post, parts, halves, box, me, first):
    right, left = ring(me)
    half = parts.shape[1] // 2
    copies = []
    for n, (peer, rows) in enumerate(((right, pl.ds(0, half)), (left, pl.ds(half, half)))):
        first[n].wait_recv()
        parts[peer, rows, :] = (parts[peer, rows, :].astype(F32) + halves[n].astype(F32)).astype(BF)
        copies.append(post.push(parts.at[peer], box.at[n], peer))
    return copies


def scatter_total(parts, box, me, copies):
    arrive(copies)
    return parts[me].astype(F32) + box[0].astype(F32) + box[1].astype(F32)


def fetch(pairs, sem):
    copies = [
        pltpu.make_async_copy(source, target, sem.at[n]) for n, (source, target) in enumerate(pairs)
    ]
    for copy in copies:
        copy.start()
    return copies


def turn(value, cos_rows, sin_rows):
    return value * cos_rows + pltpu.roll(value, value.shape[-1] // 2, 1) * sin_rows


def inverse_rms(total, width):
    return lax.rsqrt(total * (1.0 / width) + norm_eps)


def row_sum(value):
    return jnp.sum(value, axis=1, keepdims=True)


def softmax_rows(query, key, bias, scale):
    scores = dot(query, key, 1, 1) * scale + bias
    grown = jnp.exp(scores - jnp.max(scores, axis=1, keepdims=True))
    return grown / row_sum(grown)


def front_kernel(
    local, bias, cos_rows, sin_rows, gain1, gain2, q_gain, k_gain, router_t, routes, slot_of, keep,
    wq_hbm, wk_hbm, wv_hbm, wo_hbm,
    x_out, dy_out, resid_out, mixed_out, q_out, k_out, qh_out, kh_out, vh_out, ob_out,
    gates_out, send_out, pick_out,
    wq, wk, wv, wo, x_all, dy_all, an, parts, halves, box, total, load_sem, send_sem, recv_sem,
):
    me = lax.axis_index("tensor")
    ready = greet("tensor", ring(me))
    loads = fetch([(wq_hbm, wq), (wk_hbm, wk), (wv_hbm, wv), (wo_hbm, wo)], load_sem)
    blocks, tok, col = x_all.shape
    width = blocks * col
    x_all[me] = local[:, :col]
    dy_all[me] = local[:, col:]
    ready()
    post = Post("tensor", send_sem, recv_sem)
    x_in = gather_relay(post, x_all, me, gather_start(post, x_all, me))
    dy_in = gather_start(post, dy_all, me)
    arrive(x_in)
    square = jnp.zeros((tok, 1), F32)
    for t in range(blocks):
        value = x_all[t].astype(F32)
        square = square + row_sum(value * value)
    r1 = inverse_rms(square, width)
    for t in range(blocks):
        an[t] = (x_all[t].astype(F32) * r1 * gain1[t : t + 1, :]).astype(BF)
    x_out[...] = x_all[...]

    for copy in loads:
        copy.wait()

    def project(weight):
        value = dot(an[0], weight[0:col, :])
        for t in range(1, blocks):
            value = value + dot(an[t], weight[t * col : (t + 1) * col, :])
        return value

    q_out[...] = project(wq)
    k_out[...] = project(wk)
    vh_out[...] = project(wv).astype(BF)
    dy_in = gather_relay(post, dy_all, me, dy_in)
    head = q_gain.shape[1]
    scale = 1.0 / math.sqrt(head)
    for h in range(col // head):
        lanes = slice(h * head, (h + 1) * head)
        for raw, gain, rotated in ((q_out, q_gain, qh_out), (k_out, k_gain, kh_out)):
            value = raw[:, lanes]
            value = value * inverse_rms(row_sum(value * value), head) * gain[...]
            rotated[:, lanes] = turn(value, cos_rows[...], sin_rows[...]).astype(BF)
        probs = softmax_rows(qh_out[:, lanes], kh_out[:, lanes], bias[...], scale).astype(BF)
        ob_out[:, lanes] = dot(probs, vh_out[:, lanes]).astype(BF)
    for t in range(blocks):
        parts[t] = dot(ob_out[...], wo[:, t * col : (t + 1) * col]).astype(BF)
    first = scatter_start(post, parts, halves, me)
    moved = scatter_relay(post, parts, halves, box, me, first)
    total[me] = scatter_total(parts, box, me, moved).astype(BF)
    arrive(gather_relay(post, total, me, gather_start(post, total, me)))
    square = jnp.zeros((tok, 1), F32)
    for t in range(blocks):
        value = x_all[t].astype(F32) + total[t].astype(F32)
        resid_out[t] = value
        square = square + row_sum(value * value)
    r2 = inverse_rms(square, width)
    logits = jnp.zeros((router_t.shape[0], tok), F32)
    for t in range(blocks):
        mixed_out[t] = (resid_out[t] * r2 * gain2[t : t + 1, :]).astype(BF)
        logits = logits + dot(router_t[:, t * col : (t + 1) * col], mixed_out[t], 1, 1)
    expert = lax.broadcasted_iota(jnp.int32, logits.shape, 0)
    top = routes.shape[0]
    chosen = [
        jnp.sum(jnp.where(routes[k : k + 1, :] == expert, logits, 0.0), axis=0, keepdims=True)
        for k in range(top)
    ]
    peak = functools.reduce(jnp.maximum, chosen)
    grown = [jnp.exp(value - peak) for value in chosen]
    whole = functools.reduce(jnp.add, grown)
    slots = send_out.shape[0]
    slot = lax.broadcasted_iota(jnp.int32, (slots, tok), 0)
    pick = jnp.zeros((slots, tok), F32)
    weight = jnp.zeros((slots, tok), F32)
    for k in range(top):
        gate = grown[k] / whole
        gates_out[k : k + 1, :] = gate
        hot = slot_of[k : k + 1, :] == slot
        pick = jnp.where(hot, 1.0, pick)
        weight = jnp.where(hot, gate * keep[k : k + 1, :], weight)
    pick_out[...] = pick.T.astype(BF)
    pick = pick.astype(BF)
    for t in range(blocks):
        send_out[:, t * col : (t + 1) * col] = dot(pick, mixed_out[t]).astype(BF)
    gate = row_sum(weight)
    first = gate.astype(BF)
    second = (gate - first.astype(F32)).astype(BF)
    third = (gate - first.astype(F32) - second.astype(F32)).astype(BF)
    lane = lax.broadcasted_iota(jnp.int32, (slots, 128), 1)
    facts = jnp.zeros((slots, 128), F32)
    for n, piece in enumerate((first, second, third)):
        facts = jnp.where(lane == n, piece.astype(F32), facts)
    send_out[:, width : width + 128] = facts.astype(BF)
    arrive(dy_in)
    dy_out[...] = dy_all[...]
    for t in range(blocks):
        lanes = slice(width + 128 + t * col, width + 128 + (t + 1) * col)
        send_out[:, lanes] = dot(pick, dy_all[t]).astype(BF)
    post.finish()


def front_call(local, bias, cos_rows, sin_rows, gain1, gain2, q_gain, k_gain, router_t, routes,
               slot_of, keep, weights, slots):
    tok, both = local.shape
    col = both // 2
    blocks = gain1.shape[0]
    width = col * blocks
    shape = jax.ShapeDtypeStruct
    vmem = pl.BlockSpec(memory_space=pltpu.VMEM)
    tiles = (blocks, tok, col)
    top = routes.shape[0]
    return pl.pallas_call(
        front_kernel,
        out_shape=(
            shape(tiles, BF), shape(tiles, BF), shape(tiles, F32),
            shape(tiles, BF), shape((tok, col), F32), shape((tok, col), F32),
            shape((tok, col), BF), shape((tok, col), BF), shape((tok, col), BF),
            shape((tok, col), BF), shape((top, tok), F32), shape((slots, 2 * width + 128), BF),
            shape((tok, slots), BF),
        ),
        in_specs=[vmem] * 12 + [pl.BlockSpec(memory_space=pl.ANY)] * 4,
        out_specs=(vmem,) * 13,
        scratch_shapes=[
            pltpu.VMEM((width, col), BF), pltpu.VMEM((width, col), BF), pltpu.VMEM((width, col), BF),
            pltpu.VMEM((col, width), BF),
            pltpu.VMEM(tiles, BF), pltpu.VMEM(tiles, BF), pltpu.VMEM(tiles, BF), pltpu.VMEM(tiles, BF),
            pltpu.VMEM((2, tok // 2, col), BF), pltpu.VMEM((2, tok, col), BF), pltpu.VMEM(tiles, BF),
            pltpu.SemaphoreType.DMA((4,)),
            pltpu.SemaphoreType.DMA((16,)), pltpu.SemaphoreType.DMA((16,)),
        ],
        compiler_params=pltpu.CompilerParams(
            collective_id=1, has_side_effects=True, vmem_limit_bytes=56 * 1024 * 1024
        ),
        name="front",
    )(local, bias, cos_rows, sin_rows, gain1, gain2, q_gain, k_gain, router_t, routes, slot_of,
      keep, *weights)


def back_kernel(
    pick_t, ret, slot_of, keep, gates, routes, bias, cos_rows, sin_rows, gain2,
    q_gain, k_gain, router, resid, dy_all, mixed, qh, kh, vh,
    q_hbm, k_hbm, wo_hbm,
    d_qkv, dr, d_mine, router_out, small_out,
    q_raw, k_raw, wo, parts, halves, box, total, dm, d_att, dg_mine, dg_box,
    load_sem, send_sem, recv_sem,
):
    me, peers = tensor_peers()
    ready = greet("tensor", peers)
    loads = fetch([(wo_hbm, wo), (q_hbm, q_raw), (k_hbm, k_raw)], load_sem)
    blocks, tok, col = parts.shape
    width = blocks * col
    post = Post("tensor", send_sem, recv_sem)
    for t in range(blocks):
        parts[t] = dot(pick_t[...], ret[:, t * col : (t + 1) * col]).astype(BF)
    ready()
    first = scatter_start(post, parts, halves, me)
    top = routes.shape[0]
    dgate = row_sum(ret[:, width:].astype(F32))
    slot = lax.broadcasted_iota(jnp.int32, (ret.shape[0], tok), 0)
    for k in range(top):
        hot = slot_of[k : k + 1, :] == slot
        dg_mine[k : k + 1, :] = jnp.sum(jnp.where(hot, dgate, 0.0), axis=0, keepdims=True)
    dg_in = [post.push(dg_mine, dg_box.at[d], peer) for d, peer in enumerate(peers)]
    moved = scatter_relay(post, parts, halves, box, me, first)
    total[me] = scatter_total(parts, box, me, moved).astype(BF)
    total_first = gather_start(post, total, me)

    arrive(dg_in)
    d_gates = dg_mine[...]
    for d in range(blocks - 1):
        d_gates = d_gates + dg_box[d]
    d_gates = d_gates * keep[...]
    gate = gates[...]
    d_chosen = gate * (d_gates - jnp.sum(gate * d_gates, axis=0, keepdims=True))
    expert = lax.broadcasted_iota(jnp.int32, (router.shape[1], tok), 0)
    d_logits_t = jnp.zeros(expert.shape, F32)
    for k in range(top):
        hot = routes[k : k + 1, :] == expert
        d_logits_t = jnp.where(hot, d_chosen[k : k + 1, :], d_logits_t)
    d_logits = d_logits_t.T.astype(BF)
    square = jnp.zeros((tok, 1), F32)
    for t in range(blocks):
        rows = slice(t * col, (t + 1) * col)
        dm[t] = dot(d_logits, router[rows, :], 1, 1)
        square = square + row_sum(resid[t] * resid[t])
    r2 = inverse_rms(square, width)
    total_moved = gather_relay(post, total, me, total_first)
    for t in range(blocks):
        rows = slice(t * col, (t + 1) * col)
        router_out[rows, :] = dot(mixed[t].T, d_logits).astype(BF)
    arrive(total_moved)
    cross = jnp.zeros((tok, 1), F32)
    for t in range(blocks):
        dm[t] = dm[t] + total[t].astype(F32)
        cross = cross + row_sum(resid[t] * gain2[t : t + 1, :] * dm[t])
    cross = cross * (1.0 / width) * r2 * r2 * r2
    small_out[...] = jnp.zeros_like(small_out)
    for t in range(blocks):
        d_mixed = dm[t]
        small_out[t : t + 1, :] = jnp.sum(d_mixed * resid[t] * r2, axis=0, keepdims=True)
        d_resid = dy_all[t].astype(F32) + r2 * gain2[t : t + 1, :] * d_mixed - resid[t] * cross
        dm[t] = d_resid
        dr[t] = d_resid.astype(BF)
    d_mine[...] = dm[me]
    for copy in loads:
        copy.wait()
    value = dot(dr[0], wo[:, 0:col], 1, 1)
    for t in range(1, blocks):
        value = value + dot(dr[t], wo[:, t * col : (t + 1) * col], 1, 1)
    d_att[...] = value.astype(BF)

    head = q_gain.shape[1]
    scale = 1.0 / math.sqrt(head)
    q_part = jnp.zeros((1, head), F32)
    k_part = jnp.zeros((1, head), F32)

    def unturn(grown, raw, gain):
        d_unit = grown * cos_rows[...] - pltpu.roll(grown, head // 2, 1) * sin_rows[...]
        inverse = inverse_rms(row_sum(raw * raw), head)
        unit = raw * inverse
        gain_part = jnp.sum(d_unit * unit, axis=0, keepdims=True)
        d_unit = d_unit * gain[...]
        d_raw = inverse * (d_unit - unit * (row_sum(unit * d_unit) * (1.0 / head)))
        return d_raw.astype(BF), gain_part

    for h in range(col // head):
        lanes = slice(h * head, (h + 1) * head)
        probs = softmax_rows(qh[:, lanes], kh[:, lanes], bias[...], scale)
        d_head = d_att[:, lanes]
        d_probs = dot(d_head, vh[:, lanes], 1, 1)
        d_scores = probs * (d_probs - row_sum(probs * d_probs))
        d_qkv[:, 2 * col + h * head : 2 * col + (h + 1) * head] = dot(
            probs.T.astype(BF), d_head
        ).astype(BF)
        d_q, part = unturn(dot(d_scores.astype(BF), kh[:, lanes]) * scale, q_raw[:, lanes], q_gain)
        q_part = q_part + part
        d_qkv[:, lanes] = d_q
        d_k, part = unturn(dot(d_scores.T.astype(BF), qh[:, lanes]) * scale, k_raw[:, lanes], k_gain)
        k_part = k_part + part
        d_qkv[:, col + h * head : col + (h + 1) * head] = d_k
    small_out[blocks : blocks + 1, :head] = q_part
    small_out[blocks : blocks + 1, head : 2 * head] = k_part
    post.finish()


def back_call(pick_t, ret, slot_of, keep, gates, routes, bias, cos_rows, sin_rows,
              gain2, q_gain, k_gain, router, resid, dy_all, mixed, qh, kh, vh, q_raw, k_raw, wo):
    blocks, tok, col = dy_all.shape
    width = blocks * col
    tiles = (blocks, tok, col)
    shape = jax.ShapeDtypeStruct
    vmem = pl.BlockSpec(memory_space=pltpu.VMEM)
    top = routes.shape[0]
    count = 8 + blocks - 1
    return pl.pallas_call(
        back_kernel,
        out_shape=(
            shape((tok, 3 * col), BF), shape(tiles, BF), shape((tok, col), F32),
            shape((width, 128), BF), shape((8, col), F32),
        ),
        in_specs=[vmem] * 19 + [pl.BlockSpec(memory_space=pl.ANY)] * 3,
        out_specs=(vmem,) * 5,
        scratch_shapes=[
            pltpu.VMEM((tok, col), F32), pltpu.VMEM((tok, col), F32), pltpu.VMEM((col, width), BF),
            pltpu.VMEM(tiles, BF), pltpu.VMEM((2, tok // 2, col), BF), pltpu.VMEM((2, tok, col), BF),
            pltpu.VMEM(tiles, BF), pltpu.VMEM(tiles, F32), pltpu.VMEM((tok, col), BF),
            pltpu.VMEM((top, tok), F32), pltpu.VMEM((blocks - 1, top, tok), F32),
            pltpu.SemaphoreType.DMA((3,)),
            pltpu.SemaphoreType.DMA((count,)), pltpu.SemaphoreType.DMA((count,)),
        ],
        compiler_params=pltpu.CompilerParams(
            collective_id=2, has_side_effects=True, vmem_limit_bytes=48 * 1024 * 1024
        ),
        cost_estimate=pl.CostEstimate(
            flops=20_000_000_000, bytes_accessed=1, transcendentals=0
        ),
        name="back",
    )(pick_t, ret, slot_of, keep, gates, routes, bias, cos_rows, sin_rows, gain2,
      q_gain, k_gain, router, resid, dy_all, mixed, qh, kh, vh, q_raw, k_raw, wo)


def octet():
    me = lax.axis_index("expert")
    core = me % 2
    return me - core, core, lax.axis_index("tensor")


def octet_others(base, core, rank):
    count = lax.axis_size("tensor")
    others = [{"expert": base + core, "tensor": (rank + d) % count} for d in range(1, count)]
    return others + [
        {"expert": base + 1 - core, "tensor": (rank + d) % count} for d in range(count)
    ]


def meet(others):
    barrier = pltpu.get_barrier_semaphore()
    for other in others:
        pl.semaphore_signal(barrier, inc=1, device_id=other, device_id_type=MESH)
    return lambda: pl.semaphore_wait(barrier, len(others))


def remote(source, target, send_sem, recv_sem, device):
    return pltpu.make_async_remote_copy(
        src_ref=source, dst_ref=target, send_sem=send_sem, recv_sem=recv_sem, device_id=device,
        device_id_type=MESH,
    )


def weights_kernel(w, out, local_sem, send_sem, recv_sem, pass_send, pass_recv):
    base, core, rank = octet()
    ready = meet(octet_others(base, core, rank))
    ranks = out.shape[0]
    half = out.shape[2] // 2
    sibling = {"expert": base + 1 - core, "tensor": rank}

    def part(ref, index, side):
        return ref.at[index, :, pl.ds(side * half, half), :]

    ready()
    sends = []
    for s in range(2):
        for k in range(2):
            target = 2 * core + s
            here = (target == rank) & (core == k)
            source, place = part(w, s, k), part(out, rank, k)
            local = pltpu.make_async_copy(source, place, local_sem)
            away = remote(
                source, place, send_sem.at[2 * s + k], recv_sem.at[rank],
                {"expert": base + k, "tensor": target},
            )
            pl.when(here)(local.start)
            pl.when(jnp.logical_not(here))(away.start)
            sends.append((here, away))
    passed = []
    for d in (0, 1, 3, 2):
        quarter = (rank + d) % ranks
        mine = part(out, quarter, core)
        arrival = remote(mine, mine, send_sem.at[0], recv_sem.at[quarter], sibling)
        here = (rank // 2 == core) & (d == 0)
        pl.when(here)(pltpu.make_async_copy(part(w, 0, 0), mine, local_sem).wait)
        pl.when(jnp.logical_not(here))(arrival.wait_recv)
        passed.append(remote(mine, mine, pass_send.at[d], pass_recv.at[d], sibling))
        passed[-1].start()
    for copy in passed:
        copy.wait()
    for here, away in sends:
        pl.when(jnp.logical_not(here))(away.wait_send)


def weights_call(w):
    _, three, width, hidden = w.shape
    hbm = pl.BlockSpec(memory_space=pl.ANY)
    sems = pltpu.SemaphoreType.DMA((4,))
    return pl.pallas_call(
        weights_kernel,
        out_shape=jax.ShapeDtypeStruct((4, three, width, hidden), BF),
        in_specs=[hbm],
        out_specs=hbm,
        scratch_shapes=[pltpu.SemaphoreType.DMA, sems, sems, sems, sems],
        compiler_params=pltpu.CompilerParams(collective_id=4, has_side_effects=True),
        cost_estimate=SHADOW,
        name="weights",
    )(w)


def home_kernel(grads, out, far_out, own, got, load_sem, local_sem, swap_send, swap_recv, send_sem, recv_sem):
    base, core, rank = octet()
    ready = meet(octet_others(base, core, rank))
    ranks, three, half, hidden = own.shape
    sibling = {"expert": base + 1 - core, "tensor": rank}
    order = (1, 3, 0, 2)
    loads, swaps = [], []
    for d in order:
        quarter = (rank + d) % ranks
        source = grads.at[quarter, :, pl.ds(core * half, half), :]
        loads.append(pltpu.make_async_copy(source, own.at[d], load_sem.at[d]))
        loads[-1].start()
    ready()
    for d in order:
        quarter = (rank + d) % ranks
        source = grads.at[quarter, :, pl.ds((1 - core) * half, half), :]
        swaps.append(remote(source, got.at[d], swap_send.at[d], swap_recv.at[d], sibling))
        swaps[-1].start()
    owner = rank // 2
    side = rank - 2 * owner
    rows = 64
    place = out.at[side, :, pl.ds(core * half, half), :]
    stays = owner == core
    sends = []
    for n, d in enumerate(order):
        loads[n].wait()
        swaps[n].wait_recv()

        def one(i, _, d=d):
            c, at = i // (half // rows), i % (half // rows) * rows
            here = pl.ds(pl.multiple_of(at, rows), rows)
            value = own[d, c, here, :].astype(F32) + got[d, c, here, :].astype(F32)
            own[d, c, here, :] = value.astype(BF)
            return 0

        lax.fori_loop(0, three * (half // rows), one, 0)
        if d == 2:
            far = pltpu.make_async_copy(own.at[d], far_out, load_sem.at[d])
            far.start()
            continue
        away = remote(
            own.at[d], place, send_sem.at[d], recv_sem.at[2 * side + core],
            {"expert": base + owner, "tensor": (rank + d) % ranks},
        )
        if d:
            away.start()
        else:
            kept = pltpu.make_async_copy(own.at[d], place, local_sem)
            pl.when(stays)(kept.start)
            pl.when(jnp.logical_not(stays))(away.start)
        sends.append((d, away))
    for s in range(2):
        for k in range(2):
            off = (2 * core + s - rank) % ranks
            mine = out.at[s, :, pl.ds(k * half, half), :]
            arrival = remote(own.at[0], mine, send_sem.at[0], recv_sem.at[2 * s + k], sibling)
            own_chip = off == 0
            comes = (off != 2) & jnp.logical_not(own_chip & (core == k))
            pl.when(comes)(arrival.wait_recv)
    pl.when(stays)(kept.wait)
    for d, away in sends:
        if d:
            away.wait_send()
        else:
            pl.when(jnp.logical_not(stays))(away.wait_send)
    for swap in swaps:
        swap.wait_send()
    far.wait()


def home_call(grads):
    ranks, three, width, hidden = grads.shape
    hbm = pl.BlockSpec(memory_space=pl.ANY)
    sems = pltpu.SemaphoreType.DMA((4,))
    halves = pltpu.VMEM((ranks, three, width // 2, hidden), BF)
    shape = jax.ShapeDtypeStruct
    return pl.pallas_call(
        home_kernel,
        out_shape=(
            shape((2, three, width, hidden), BF), shape((three, width // 2, hidden), BF),
        ),
        in_specs=[hbm],
        out_specs=(hbm, hbm),
        scratch_shapes=[
            halves, halves, sems, pltpu.SemaphoreType.DMA, sems, sems, sems, sems,
        ],
        compiler_params=pltpu.CompilerParams(
            collective_id=5, has_side_effects=True, vmem_limit_bytes=24 * 1024 * 1024
        ),
        cost_estimate=SHADOW,
        name="home",
    )(grads)


def expert_kernel(rows_ref, w_ref, y_ref, dx_ref, grad_ref, rows_t, dys_t, y_acc, dx_acc, gate_of, dgate):
    step = pl.program_id(0)
    width = y_acc.shape[1]
    rows = rows_ref.at[:, :width]
    dys = rows_ref.at[:, width + 128 :]

    @pl.when(step == 0)
    def _():
        gate_of[...] = row_sum(rows_ref[:, width : width + 128].astype(F32))
        rows_t[...] = rows[...].T
        dys_t[...] = (dys[...].astype(F32) * gate_of[...]).astype(BF).T
        dgate[...] = jnp.zeros_like(dgate)
        y_acc[...] = jnp.zeros_like(y_acc)
        dx_acc[...] = jnp.zeros_like(dx_acc)

    w_gate, w_up, w_down = w_ref[0, 0], w_ref[0, 1], w_ref[0, 2]
    gate = dot(rows[...], w_gate)
    up = dot(rows[...], w_up)
    d_raw = dot(dys[...], w_down)
    d_act = d_raw * gate_of[...]
    sig = 1.0 / (1.0 + jnp.exp(-gate))
    silu = gate * sig
    act = (silu * up).astype(BF)
    dgate[...] += row_sum(act.astype(F32) * d_raw)
    d_gate = (d_act * up * sig * (1.0 + gate * (1.0 - sig))).astype(BF)
    d_up = (d_act * silu).astype(BF)
    y_acc[...] += dot(act, w_down, 1, 1)
    dx_acc[...] += dot(d_gate, w_gate, 1, 1) + dot(d_up, w_up, 1, 1)
    grad_ref[0, 0] = dot(rows_t[...], d_gate).astype(BF)
    grad_ref[0, 1] = dot(rows_t[...], d_up).astype(BF)
    grad_ref[0, 2] = dot(dys_t[...], act).astype(BF)

    @pl.when(step == pl.num_programs(0) - 1)
    def _():
        first = dgate[...].astype(BF).astype(F32)
        lane = lax.broadcasted_iota(jnp.int32, (y_ref.shape[0], 128), 1)
        facts = jnp.where(lane == 0, first, jnp.where(lane == 1, dgate[...] - first, 0.0))
        y_ref[...] = (y_acc[...] * gate_of[...]).astype(BF)
        dx_ref[:, :width] = dx_acc[...].astype(BF)
        dx_ref[:, width:] = facts.astype(BF)


def expert_call(rows, weights):
    quarters, _, width, hidden = weights.shape
    count = rows.shape[0]
    shape = jax.ShapeDtypeStruct

    def whole(value):
        return pl.BlockSpec(value.shape, lambda q: (0, 0), pipeline_mode=pl.Buffered(1))

    block = pl.BlockSpec((1, 3, width, hidden), lambda q: (q, 0, 0, 0))
    outs = [shape((count, width), BF), shape((count, width + 128), BF)]
    return pl.pallas_call(
        expert_kernel,
        grid=(quarters,),
        out_shape=tuple(outs) + (shape(weights.shape, BF),),
        in_specs=[whole(rows), block],
        out_specs=tuple(whole(value) for value in outs) + (block,),
        scratch_shapes=[
            pltpu.VMEM((width, count), BF),
            pltpu.VMEM((width, count), BF),
            pltpu.VMEM((count, width), F32),
            pltpu.VMEM((count, width), F32),
            pltpu.VMEM((count, 1), F32),
            pltpu.VMEM((count, 1), F32),
        ],
        compiler_params=pltpu.CompilerParams(vmem_limit_bytes=62 * 1024 * 1024),
        cost_estimate=COST,
        name="expert",
    )(rows, weights)


def plane():
    me = lax.axis_index("expert")
    core, z, y = me % 2, (me // 2) % 4, me // 8
    return [
        (core, me + 1 - 2 * core),
        ((y + y // 2) % 2, me + 8 * (1 - 2 * (y % 2))),
        (y // 2, me + 8 * (3 - 2 * y)),
        ((z + z // 2) % 2, me + 2 * (1 - 2 * (z % 2))),
        (z // 2, me + 2 * (3 - 2 * z)),
    ]

ORDERS = ((1, 3, 2, 4), (3, 2, 4, 1), (2, 4, 1, 3), (4, 1, 3, 2))

def reduce_kernel(
    d_qkv, dr, d_mine, router_part, small_in, x_all, gain1, ob, pick_y, ret_y,
    far_hbm, resid_hbm, wq_hbm, wk_hbm, wv_hbm,
    wide_out, dx_out, out_out, small_out, far_out,
    wq, wk, wv, resid, parts, y_parts, halves, box_x, note, buf, box, got,
    load_sem, out_sem, x_send, x_recv, send_sem, recv_sem, far_send, far_recv,
):
    me, peers = tensor_peers()
    dims = plane()
    base, core, _ = octet()
    ready = meet(octet_others(base, core, me) + [{"expert": partner} for _, partner in dims[1:]])
    loads = fetch(
        [(wq_hbm, wq), (wk_hbm, wk), (wv_hbm, wv), (resid_hbm.at[me], resid)], load_sem
    )
    blocks, tok, col = x_all.shape
    width = blocks * col
    head = col // blocks
    square = jnp.zeros((tok, 1), F32)
    for t in range(blocks):
        value = x_all[t].astype(F32)
        square = square + row_sum(value * value)
    r1 = inverse_rms(square, width)
    for copy in loads:
        copy.wait()
    for t in range(blocks):
        rows = slice(t * col, (t + 1) * col)
        parts[t] = (
            dot(d_qkv[:, 0:col], wq[rows, :], 1, 1)
            + dot(d_qkv[:, col : 2 * col], wk[rows, :], 1, 1)
            + dot(d_qkv[:, 2 * col : 3 * col], wv[rows, :], 1, 1)
        ).astype(BF)
    ready()
    post_x = Post("tensor", x_send, x_recv)
    post = Post("expert", send_sem, recv_sem)
    x_halves, x_box = halves.at[pl.ds(0, 2)], box_x.at[pl.ds(0, 2)]
    y_halves, y_box = halves.at[pl.ds(2, 2)], box_x.at[pl.ds(2, 2)]
    x_first = scatter_start(post_x, parts, x_halves, me)

    half = far_hbm.shape[1]
    owner = me // 2

    def far_copy(n, side, device):
        return remote(
            far_hbm.at[n], far_out.at[n, pl.ds(side * half, half), :],
            far_send.at[n], far_recv.at[n, side], device,
        )

    far_copies = [
        far_copy(n, core, {"expert": base + owner, "tensor": (me + 2) % blocks}) for n in range(3)
    ]
    far_copies[0].start()

    chunks = buf.shape[0] // blocks
    rows_chunk = buf.shape[1]

    def products(t):
        here = pl.ds(t * chunks, chunks)
        normed = (x_all[t].astype(F32) * r1 * gain1[pl.ds(t, 1), :]).T.astype(BF)
        for n in range(3):
            lanes = slice(n * col, (n + 1) * col)
            value = dot(normed, d_qkv[:, lanes]).astype(BF)
            buf[here, :, lanes] = value.reshape(chunks, rows_chunk, col)
        value = dot(dr[t].T, ob[...]).astype(BF)
        buf[here, :, 3 * col : 4 * col] = value.reshape(chunks, rows_chunk, col)
        value = router_part[pl.ds(t * col, col), :]
        buf[here, :, 4 * col :] = value.reshape(chunks, rows_chunk, value.shape[1])

    def add(target, place, first, count):
        def one(i, _):
            total = buf[place + i].astype(F32) + box[first + i].astype(F32)
            target[place + i] = total.astype(BF)
            return 0

        lax.fori_loop(0, count, one, 0)

    copies = []
    for n in range(2):
        products(2 * (1 - core) + n)
        for s in range(2 * n, 2 * n + 2):
            source = buf.at[pl.ds((1 - core) * 64 + s * 16, 16)]
            copies.append(post.push(source, box.at[pl.ds(31 * s, 16)], dims[0][1]))
    x_moved = scatter_relay(post_x, parts, x_halves, x_box, me, x_first)
    far_copies[1].start()
    for n in range(2):
        products(2 * core + n)
    place = [core * 64 + s * 16 for s in range(4)]
    size, first = 16, 0

    def halve(k):
        for s in range(4):
            copies[s].wait_recv()
            add(buf, place[s], 31 * s + first, size)
            bit, partner = dims[ORDERS[s][k]]
            half = size // 2
            copies[s] = post.push(
                buf.at[pl.ds(place[s] + (1 - bit) * half, half)],
                box.at[pl.ds(31 * s + first + size, half)],
                partner,
            )
            place[s] = place[s] + bit * half

    halve(0)
    first, size = first + size, size // 2

    for t in range(blocks):
        y_parts[t] = dot(pick_y[...], ret_y[:, t * col : (t + 1) * col]).astype(BF)
    y_first = scatter_start(post_x, y_parts, y_halves, me)
    d_an = scatter_total(parts, x_box, me, x_moved)
    x_mine = x_all[me].astype(F32)
    grown = gain1[pl.ds(me, 1), :] * d_an
    mean_part = row_sum(x_mine * grown)
    note[me, 0:8, :] = jnp.broadcast_to(
        jnp.sum(d_an * x_mine * r1, axis=0, keepdims=True), (8, col)
    )
    note[me, 8:16, 0:tok] = jnp.broadcast_to(mean_part, (tok, 128)).T[0:8, :]
    note[me, 8:16, tok:] = jnp.broadcast_to(small_in[blocks : blocks + 1, : 2 * head], (8, 2 * head))
    note_in = [post_x.push(note.at[me], note.at[me], peer) for peer in peers]

    halve(1)
    first, size = first + size, size // 2
    y_moved = scatter_relay(post_x, y_parts, y_halves, y_box, me, y_first)
    far_copies[2].start()
    halve(2)
    first, size = first + size, size // 2
    halve(3)
    first, size = first + size, size // 2
    for s in range(4):
        copies[s].wait_recv()
        add(got, place[s], 31 * s + first, 1)
        here = got.at[pl.ds(place[s], 1)]
        copies[s] = post.push(here, here, dims[ORDERS[s][3]][1])

    arrive(note_in)
    facts = note[0, 8:16, :]
    for t in range(1, blocks):
        facts = facts + note[t, 8:16, :]
    for t in range(blocks):
        small_out[t : t + 1, :] = note[t, 0:1, :]
        small_out[blocks + t : blocks + t + 1, :] = small_in[t : t + 1, :]
    small_out[2 * blocks :, :] = facts
    mean = jnp.broadcast_to(facts[0:1, 0:tok], (128, tok)).T[:, 0:1] * (1.0 / width)
    dx_out[...] = (d_mine[...] + r1 * grown - x_mine * (r1 * r1 * r1 * mean)).astype(BF)

    size = 1
    stores = []
    for k in range(3, -1, -1):
        for s in range(4):
            copies[s].wait_recv()
            bit, _ = dims[ORDERS[s][k]]
            place[s] = place[s] - bit * size
            partner = dims[ORDERS[s][k - 1]][1] if k else dims[0][1]
            here = got.at[pl.ds(place[s], 2 * size)]
            copies[s] = post.push(here, here, partner)
            if not k:
                stores.append(
                    pltpu.make_async_copy(here, wide_out.at[pl.ds(place[s], 16)], out_sem.at[s])
                )
                stores[-1].start()
        size *= 2
        if k == 2:
            out_out[...] = (resid[...] + scatter_total(y_parts, y_box, me, y_moved)).astype(BF)
    for s in range(4):
        copies[s].wait_recv()
        there = pl.ds((1 - core) * 64 + s * 16, 16)
        stores.append(pltpu.make_async_copy(got.at[there], wide_out.at[there], out_sem.at[4 + s]))
        stores[-1].start()
    post.finish()
    post_x.finish()
    for store in stores:
        store.wait()
    comes = (me + 2) % blocks // 2 == core
    for n in range(3):
        for side in range(2):
            pl.when(comes)(far_copy(n, side, {"expert": base + core, "tensor": (me + 2) % blocks}).wait_recv)
        far_copies[n].wait_send()


def reduce_call(d_qkv, dr, d_mine, router_part, small, x_all, gain1, ob, pick_y, ret_y, far, resid,
                weights):
    blocks, tok, col = x_all.shape
    width = blocks * col
    tiles = (blocks, tok, col)
    wide = (128, 16, 4 * col + 128)
    shape = jax.ShapeDtypeStruct
    vmem = pl.BlockSpec(memory_space=pltpu.VMEM)
    hbm = pl.BlockSpec(memory_space=pl.ANY)
    count = 8 + blocks - 1
    return pl.pallas_call(
        reduce_kernel,
        out_shape=(
            shape(wide, BF), shape((tok, col), BF), shape((tok, col), BF), shape((16, col), F32),
            shape((far.shape[0], 2 * far.shape[1], far.shape[2]), BF),
        ),
        in_specs=[vmem] * 10 + [hbm] * 5,
        out_specs=(hbm, vmem, vmem, vmem, hbm),
        scratch_shapes=[
            pltpu.VMEM((width, col), BF), pltpu.VMEM((width, col), BF), pltpu.VMEM((width, col), BF),
            pltpu.VMEM((tok, col), F32), pltpu.VMEM(tiles, BF), pltpu.VMEM(tiles, BF),
            pltpu.VMEM((4, tok // 2, col), BF), pltpu.VMEM((4, tok, col), BF),
            pltpu.VMEM((blocks, 16, col), F32),
            pltpu.VMEM(wide, BF), pltpu.VMEM((124,) + wide[1:], BF), pltpu.VMEM(wide, BF),
            pltpu.SemaphoreType.DMA((4,)), pltpu.SemaphoreType.DMA((8,)),
            pltpu.SemaphoreType.DMA((count,)), pltpu.SemaphoreType.DMA((count,)),
            pltpu.SemaphoreType.DMA((40,)), pltpu.SemaphoreType.DMA((40,)),
            pltpu.SemaphoreType.DMA((3,)), pltpu.SemaphoreType.DMA((3, 2)),
        ],
        compiler_params=pltpu.CompilerParams(
            collective_id=3, has_side_effects=True, vmem_limit_bytes=60 * 1024 * 1024
        ),
        cost_estimate=COST,
        name="reduce",
    )(d_qkv, dr, d_mine, router_part, small, x_all, gain1, ob, pick_y, ret_y, far, resid, *weights)


def body(
    tokens,
    out_grad,
    seq_lengths,
    dest_index,
    routes,
    pair_order,
    norm1_gain,
    w_query,
    w_key,
    w_value,
    q_gain,
    k_gain,
    w_output,
    norm2_gain,
    w_router,
    expert_w,
):
    groups = lax.axis_size("expert")
    tensor_count = lax.axis_size("tensor")
    group_id = lax.axis_index("expert")
    tensor_id = lax.axis_index("tensor")
    tok_count, col_count = tokens.shape
    width = col_count * tensor_count
    move_rows = tok_count // groups
    expert_count = w_router.shape[1]
    top_count = routes.shape[1]
    local_experts = expert_w.shape[0]

    w_stored = jnp.transpose(expert_w, (0, 2, 1, 3))

    routes_t = routes.T
    order_t = pair_order[0].reshape(tok_count, top_count).T
    pair_expert = routes_t.reshape(-1)
    pair_total = tok_count * top_count
    base = pair_expert * pair_total
    keyed = base + order_t.reshape(-1)
    before = (keyed[None, :] < keyed[:, None]) & (keyed[None, :] >= base[:, None])
    ranks = jnp.sum(before.astype(jnp.int32), axis=1).reshape(top_count, tok_count)
    expert_axis = jnp.arange(expert_count, dtype=jnp.int32)
    route_hot = routes_t[:, None, :] == expert_axis[None, :, None]
    counts = jnp.sum(route_hot.astype(F32), axis=(0, 2))

    places = jnp.arange(tok_count, dtype=jnp.int32)
    arrival_rank = jnp.sum((dest_index[None, :] < dest_index[:, None]).astype(jnp.int32), axis=1)
    by_rank = (arrival_rank[None, :] == places[:, None]).astype(BF)
    inner = jnp.broadcast_to((dest_index % tok_count).astype(BF)[:, None], (tok_count, 64))
    facts = jnp.broadcast_to(counts.astype(BF)[None, :], (tok_count, expert_count))
    outgoing = dot(by_rank, jnp.concatenate([tokens, out_grad, inner, facts], axis=1)).astype(BF)
    got = exchange(outgoing.reshape(groups, move_rows, -1), "expert")
    all_counts = got[:, 0, 2 * col_count + 64 :].astype(jnp.int32)
    lower = jnp.arange(groups, dtype=jnp.int32) < group_id
    offsets = jnp.sum(jnp.where(lower[:, None], all_counts, 0), axis=0)
    mine = got[:, :, 2 * col_count].astype(jnp.int32).reshape(-1)
    put = (mine[None, :] == places[:, None]).astype(BF)
    local = dot(put, got.reshape(tok_count, -1)[:, : 2 * col_count]).astype(BF)
    capacity = 5 * tok_count * groups * top_count // (4 * expert_count)
    most_rows = 3 * tok_count * top_count // (2 * expert_count)
    per = most_rows // 2
    slots = groups * per
    slot_global = jnp.sum(jnp.where(route_hot, offsets[None, :, None], 0), axis=1) + ranks
    kept = slot_global < capacity
    keep_mask = kept.astype(F32)
    here = kept & (routes_t % tensor_count == tensor_id)
    owner = routes_t // tensor_count * 2 + ranks % 2
    slot_of = jnp.where(here, owner * per + ranks // 2, -1)

    seq_ids, positions = sequence_layout(seq_lengths[0], tok_count)
    bias = jnp.where(seq_ids[:, None] == seq_ids[None, :], 0.0, mask_fill)
    cos_tab, sin_tab = rope_tables(positions, q_gain.shape[0])
    cos_rows = jnp.concatenate([cos_tab, cos_tab], axis=1)
    sin_rows = jnp.concatenate([-sin_tab, sin_tab], axis=1)
    gain1 = norm1_gain.astype(F32).reshape(tensor_count, col_count)
    gain2 = norm2_gain.astype(F32).reshape(tensor_count, col_count)
    head_gains = (q_gain.astype(F32)[None], k_gain.astype(F32)[None])
    router = jnp.pad(w_router, ((0, 0), (0, 128 - expert_count)))
    weights = (w_query, w_key, w_value, w_output)
    (
        x_all, dy_all, resid, mixed, q_raw, k_raw, qh, kh, vh, attended, gates, send_rows, pick_t,
    ) = front_call(
        local, bias, cos_rows, sin_rows, gain1, gain2, *head_gains, router.T, routes_t, slot_of,
        keep_mask, weights, slots,
    )
    def homeward(value):
        return exchange(value.reshape(groups, -1, value.shape[1]), "expert").reshape(value.shape)

    send_rows, w_stored = lax.optimization_barrier((send_rows, w_stored))
    recv_rows = homeward(send_rows)
    y_rows, d_rows, partial = expert_call(recv_rows, weights_call(w_stored))
    ret_rows = homeward(d_rows)
    near, far = home_call(partial)
    ret_rows, near, far, y_rows = lax.optimization_barrier((ret_rows, near, far, y_rows))
    ret_y = homeward(y_rows)
    d_qkv, dr, d_mine, router_part, small = back_call(
        pick_t, ret_rows, slot_of, keep_mask, gates, routes_t, bias, cos_rows,
        sin_rows, gain2, *head_gains, router, resid, dy_all, mixed, qh, kh, vh, q_raw, k_raw,
        w_output,
    )
    summed, dx_slice, out_slice, small, far = reduce_call(
        d_qkv, dr, d_mine, router_part, small, x_all, gain1, attended, pick_t, ret_y, far, resid,
        weights[:3],
    )
    summed = summed.reshape(width, -1)

    going = dot(put, jnp.concatenate([out_slice, dx_slice], axis=1), 0, 0).astype(BF)
    small = small[:9].astype(BF).reshape(move_rows, -1)
    small = jnp.pad(small, ((0, 0), (0, -small.shape[1] % 128)))
    small = jnp.broadcast_to(small[None], (groups,) + small.shape)
    back = exchange(jnp.concatenate([going.reshape(groups, move_rows, -1), small], axis=2), "expert")
    small = jnp.sum(back[:, :, 2 * col_count :].astype(F32), axis=0)[:, : 9 * col_count // move_rows]
    small = small.reshape(-1)
    back = dot(by_rank, back.reshape(tok_count, -1)[:, : 2 * col_count], 0, 0).astype(BF)
    opposite = (tensor_id + 2) % tensor_count - 2 * (group_id % 2)
    is_far = jnp.arange(local_experts) == opposite
    expert_grad = jnp.where(is_far[:, None, None, None], far[None], near).astype(F32)
    expert_grad = jnp.transpose(expert_grad, (0, 2, 1, 3))
    wide = [summed[:, n * col_count : (n + 1) * col_count] for n in range(4)]
    gain_at = 2 * width + tok_count
    head = q_gain.shape[0]
    return (
        back[:, :col_count],
        back[:, col_count:],
        small[:width],
        wide[0].astype(F32),
        wide[1].astype(F32),
        wide[2].astype(F32),
        small[gain_at : gain_at + head],
        small[gain_at + head : gain_at + 2 * head],
        wide[3].T.astype(F32),
        small[width : 2 * width],
        summed[:, width : width + expert_count].astype(F32),
        expert_grad,
    )


def solution(mesh):
    in_specs = (
        P("expert", "tensor"),
        P("expert", "tensor"),
        P("expert", None),
        P("expert"),
        P("expert", None),
        P("expert", None),
        P(),
        P(None, "tensor"),
        P(None, "tensor"),
        P(None, "tensor"),
        P(),
        P(),
        P("tensor", None),
        P(),
        P(),
        P("expert", None, None, "tensor"),
    )
    out_specs = (
        P("expert", "tensor"),
        P("expert", "tensor"),
        P(),
        P(None, "tensor"),
        P(None, "tensor"),
        P(None, "tensor"),
        P(),
        P(),
        P("tensor", None),
        P(),
        P(),
        P("expert", None, None, "tensor"),
    )
    return jax.shard_map(body, mesh=mesh, in_specs=in_specs, out_specs=out_specs, check_vma=False)
```

```python
import functools
import math

import jax
import jax.numpy as jnp
from jax import lax
from jax.experimental import pallas as pl
from jax.experimental.pallas import tpu as pltpu
from jax.sharding import PartitionSpec as P

norm_eps = 1e-06
rope_base = 10000.0
mask_fill = -1e30


def rope_tables(positions, width):
    half_width = width // 2
    steps_idx = jnp.arange(half_width, dtype=jnp.float32)
    freqs = jnp.exp(steps_idx * (-2.0 * math.log(rope_base) / width))
    angles = positions.astype(jnp.float32)[:, None] * freqs[None, :]
    return (jnp.cos(angles), jnp.sin(angles))


def sequence_layout(lengths_row, count):
    seq_ends = jnp.cumsum(lengths_row)
    places = jnp.arange(count, dtype=jnp.int32)
    passed = (places[:, None] >= seq_ends[None, :]).astype(jnp.int32)
    seq_ids = jnp.sum(passed, axis=1)
    starts = jnp.sum(passed * lengths_row[None, :], axis=1)
    return (seq_ids, places - starts)


BF = jnp.bfloat16
F32 = jnp.float32
SHADOW = pl.CostEstimate(flops=40_000_000_000, bytes_accessed=1, transcendentals=0)
COST = pl.CostEstimate(flops=1, bytes_accessed=1, transcendentals=0)


def dot(left, right, left_dim=1, right_dim=0):
    return lax.dot_general(
        left, right, (((left_dim,), (right_dim,)), ((), ())), preferred_element_type=F32
    )


def exchange(value, axis):
    return lax.all_to_all(value, axis, split_axis=0, concat_axis=0, tiled=True)


def gather_blocks(value, axis):
    return exchange(jnp.broadcast_to(value[None], (lax.axis_size(axis),) + value.shape), axis)


def column_blocks(value, count):
    return jnp.stack(jnp.split(value, count, axis=1))


MESH = pl.DeviceIdType.MESH


def tensor_peers():
    me = lax.axis_index("tensor")
    count = lax.axis_size("tensor")
    return me, [(me + d) % count for d in range(1, count)]


def greet(axis, peers):
    barrier = pltpu.get_barrier_semaphore()
    for peer in peers:
        pl.semaphore_signal(barrier, inc=1, device_id={axis: peer}, device_id_type=MESH)
    return lambda: pl.semaphore_wait(barrier, len(peers))


class Post:
    def __init__(self, axis, send_sem, recv_sem):
        self.axis, self.send_sem, self.recv_sem = axis, send_sem, recv_sem
        self.started = []
        self.used = 0

    def push(self, source, target, peer):
        slot = self.used
        self.used += 1
        copy = pltpu.make_async_remote_copy(
            src_ref=source,
            dst_ref=target,
            send_sem=self.send_sem.at[slot],
            recv_sem=self.recv_sem.at[slot],
            device_id={self.axis: peer},
            device_id_type=MESH,
        )
        copy.start()
        self.started.append(copy)
        return copy

    def finish(self):
        for copy in self.started:
            copy.wait_send()
        self.started = []


def arrive(copies):
    for copy in copies:
        copy.wait_recv()


def ring(me):
    count = lax.axis_size("tensor")
    return (me + 1) % count, (me + count - 1) % count


def gather_start(post, ref, me):
    right, left = ring(me)
    return [post.push(ref.at[me], ref.at[me], peer) for peer in (right, left)]


def gather_relay(post, ref, me, first):
    right, left = ring(me)
    half = ref.shape[1] // 2
    first[0].wait_recv()
    here = ref.at[left, pl.ds(0, half)]
    one = post.push(here, here, right)
    first[1].wait_recv()
    here = ref.at[right, pl.ds(half, half)]
    return [one, post.push(here, here, left)]


def scatter_start(post, parts, halves, me):
    right, left = ring(me)
    far = ring(right)[0]
    half = parts.shape[1] // 2
    return [
        post.push(parts.at[far, pl.ds(0, half)], halves.at[0], right),
        post.push(parts.at[far, pl.ds(half, half)], halves.at[1], left),
    ]


def scatter_relay(post, parts, halves, box, me, first):
    right, left = ring(me)
    half = parts.shape[1] // 2
    copies = []
    for n, (peer, rows) in enumerate(((right, pl.ds(0, half)), (left, pl.ds(half, half)))):
        first[n].wait_recv()
        parts[peer, rows, :] = (parts[peer, rows, :].astype(F32) + halves[n].astype(F32)).astype(BF)
        copies.append(post.push(parts.at[peer], box.at[n], peer))
    return copies


def scatter_total(parts, box, me, copies):
    arrive(copies)
    return parts[me].astype(F32) + box[0].astype(F32) + box[1].astype(F32)


def fetch(pairs, sem):
    copies = [
        pltpu.make_async_copy(source, target, sem.at[n]) for n, (source, target) in enumerate(pairs)
    ]
    for copy in copies:
        copy.start()
    return copies


def turn(value, cos_rows, sin_rows):
    return value * cos_rows + pltpu.roll(value, value.shape[-1] // 2, 1) * sin_rows


def inverse_rms(total, width):
    return lax.rsqrt(total * (1.0 / width) + norm_eps)


def row_sum(value):
    return jnp.sum(value, axis=1, keepdims=True)


def softmax_rows(query, key, bias, scale):
    scores = dot(query, key, 1, 1) * scale + bias
    grown = jnp.exp(scores - jnp.max(scores, axis=1, keepdims=True))
    return grown / row_sum(grown)


def select_slots(slot_of, slots):
    top, tok = slot_of.shape
    slot = lax.broadcasted_iota(jnp.int32, (slots, tok), 0)
    pick = jnp.zeros((slots, tok), F32)
    for k in range(top):
        pick = jnp.where(slot_of[k : k + 1, :] == slot, 1.0, pick)
    return pick


def pre_kernel(local, slot_of, x_out, dy_out, send_out, x_all, dy_all, send_sem, recv_sem):
    me = lax.axis_index("tensor")
    ready = greet("tensor", ring(me))
    blocks, _, col = x_all.shape
    x_all[me] = local[:, :col]
    dy_all[me] = local[:, col:]
    ready()
    post = Post("tensor", send_sem, recv_sem)
    dy_in = gather_start(post, dy_all, me)
    x_in = gather_start(post, x_all, me)
    pick = select_slots(slot_of, send_out.shape[0]).astype(BF)
    dy_in = gather_relay(post, dy_all, me, dy_in)
    x_in = gather_relay(post, x_all, me, x_in)
    arrive(dy_in)
    dy_out[...] = dy_all[...]
    for t in range(blocks):
        send_out[:, t * col : (t + 1) * col] = dot(pick, dy_all[t]).astype(BF)
    arrive(x_in)
    x_out[...] = x_all[...]
    post.finish()


def pre_call(local, slot_of, blocks, slots):
    tok, both = local.shape
    col = both // 2
    tiles = (blocks, tok, col)
    shape = jax.ShapeDtypeStruct
    vmem = pl.BlockSpec(memory_space=pltpu.VMEM)
    return pl.pallas_call(
        pre_kernel,
        out_shape=(shape(tiles, BF), shape(tiles, BF), shape((slots, col * blocks), BF)),
        in_specs=[vmem] * 2,
        out_specs=(vmem,) * 3,
        scratch_shapes=[
            pltpu.VMEM(tiles, BF), pltpu.VMEM(tiles, BF),
            pltpu.SemaphoreType.DMA((8,)), pltpu.SemaphoreType.DMA((8,)),
        ],
        compiler_params=pltpu.CompilerParams(
            collective_id=6, has_side_effects=True, vmem_limit_bytes=48 * 1024 * 1024
        ),
        cost_estimate=COST,
        name="pre",
    )(local, slot_of)


def front_kernel(
    x_all, bias, cos_rows, sin_rows, gain1, gain2, q_gain, k_gain, router_t, routes, slot_of, keep,
    wq_hbm, wk_hbm, wv_hbm, wo_hbm,
    resid_out, mixed_out, q_out, k_out, qh_out, kh_out, vh_out, ob_out,
    gates_out, send_out, pick_out,
    wq, wk, wv, wo, an, parts, halves, box, total, load_sem, send_sem, recv_sem,
):
    me = lax.axis_index("tensor")
    ready = greet("tensor", ring(me))
    loads = fetch([(wq_hbm, wq), (wk_hbm, wk), (wv_hbm, wv), (wo_hbm, wo)], load_sem)
    blocks, tok, col = x_all.shape
    width = blocks * col
    post = Post("tensor", send_sem, recv_sem)
    square = jnp.zeros((tok, 1), F32)
    for t in range(blocks):
        value = x_all[t].astype(F32)
        square = square + row_sum(value * value)
    r1 = inverse_rms(square, width)
    for t in range(blocks):
        an[t] = (x_all[t].astype(F32) * r1 * gain1[t : t + 1, :]).astype(BF)

    for copy in loads:
        copy.wait()

    def project(weight):
        value = dot(an[0], weight[0:col, :])
        for t in range(1, blocks):
            value = value + dot(an[t], weight[t * col : (t + 1) * col, :])
        return value

    q_out[...] = project(wq)
    k_out[...] = project(wk)
    vh_out[...] = project(wv).astype(BF)
    head = q_gain.shape[1]
    scale = 1.0 / math.sqrt(head)
    for h in range(col // head):
        lanes = slice(h * head, (h + 1) * head)
        for raw, gain, rotated in ((q_out, q_gain, qh_out), (k_out, k_gain, kh_out)):
            value = raw[:, lanes]
            value = value * inverse_rms(row_sum(value * value), head) * gain[...]
            rotated[:, lanes] = turn(value, cos_rows[...], sin_rows[...]).astype(BF)
        probs = softmax_rows(qh_out[:, lanes], kh_out[:, lanes], bias[...], scale).astype(BF)
        ob_out[:, lanes] = dot(probs, vh_out[:, lanes]).astype(BF)
    for t in range(blocks):
        parts[t] = dot(ob_out[...], wo[:, t * col : (t + 1) * col]).astype(BF)
    ready()
    first = scatter_start(post, parts, halves, me)
    moved = scatter_relay(post, parts, halves, box, me, first)
    total[me] = scatter_total(parts, box, me, moved).astype(BF)
    arrive(gather_relay(post, total, me, gather_start(post, total, me)))
    square = jnp.zeros((tok, 1), F32)
    for t in range(blocks):
        value = x_all[t].astype(F32) + total[t].astype(F32)
        resid_out[t] = value
        square = square + row_sum(value * value)
    r2 = inverse_rms(square, width)
    logits = jnp.zeros((router_t.shape[0], tok), F32)
    for t in range(blocks):
        mixed_out[t] = (resid_out[t] * r2 * gain2[t : t + 1, :]).astype(BF)
        logits = logits + dot(router_t[:, t * col : (t + 1) * col], mixed_out[t], 1, 1)
    expert = lax.broadcasted_iota(jnp.int32, logits.shape, 0)
    top = routes.shape[0]
    chosen = [
        jnp.sum(jnp.where(routes[k : k + 1, :] == expert, logits, 0.0), axis=0, keepdims=True)
        for k in range(top)
    ]
    peak = functools.reduce(jnp.maximum, chosen)
    grown = [jnp.exp(value - peak) for value in chosen]
    whole = functools.reduce(jnp.add, grown)
    slots = send_out.shape[0]
    slot = lax.broadcasted_iota(jnp.int32, (slots, tok), 0)
    pick = jnp.zeros((slots, tok), F32)
    weight = jnp.zeros((slots, tok), F32)
    for k in range(top):
        gate = grown[k] / whole
        gates_out[k : k + 1, :] = gate
        hot = slot_of[k : k + 1, :] == slot
        pick = jnp.where(hot, 1.0, pick)
        weight = jnp.where(hot, gate * keep[k : k + 1, :], weight)
    pick_out[...] = pick.T.astype(BF)
    pick = pick.astype(BF)
    for t in range(blocks):
        send_out[:, t * col : (t + 1) * col] = dot(pick, mixed_out[t]).astype(BF)
    gate = row_sum(weight)
    first = gate.astype(BF)
    second = (gate - first.astype(F32)).astype(BF)
    third = (gate - first.astype(F32) - second.astype(F32)).astype(BF)
    lane = lax.broadcasted_iota(jnp.int32, (slots, 128), 1)
    facts = jnp.zeros((slots, 128), F32)
    for n, piece in enumerate((first, second, third)):
        facts = jnp.where(lane == n, piece.astype(F32), facts)
    send_out[:, width:] = facts.astype(BF)
    post.finish()


def front_call(x_all, bias, cos_rows, sin_rows, gain1, gain2, q_gain, k_gain, router_t, routes,
               slot_of, keep, weights, slots):
    blocks, tok, col = tiles = x_all.shape
    width = col * blocks
    shape = jax.ShapeDtypeStruct
    vmem = pl.BlockSpec(memory_space=pltpu.VMEM)
    top = routes.shape[0]
    return pl.pallas_call(
        front_kernel,
        out_shape=(
            shape(tiles, F32), shape(tiles, BF), shape((tok, col), F32), shape((tok, col), F32),
            shape((tok, col), BF), shape((tok, col), BF), shape((tok, col), BF),
            shape((tok, col), BF), shape((top, tok), F32), shape((slots, width + 128), BF),
            shape((tok, slots), BF),
        ),
        in_specs=[vmem] * 12 + [pl.BlockSpec(memory_space=pl.ANY)] * 4,
        out_specs=(vmem,) * 11,
        scratch_shapes=[
            pltpu.VMEM((width, col), BF), pltpu.VMEM((width, col), BF), pltpu.VMEM((width, col), BF),
            pltpu.VMEM((col, width), BF),
            pltpu.VMEM(tiles, BF), pltpu.VMEM(tiles, BF),
            pltpu.VMEM((2, tok // 2, col), BF), pltpu.VMEM((2, tok, col), BF), pltpu.VMEM(tiles, BF),
            pltpu.SemaphoreType.DMA((4,)),
            pltpu.SemaphoreType.DMA((8,)), pltpu.SemaphoreType.DMA((8,)),
        ],
        compiler_params=pltpu.CompilerParams(
            collective_id=1, has_side_effects=True, vmem_limit_bytes=56 * 1024 * 1024
        ),
        cost_estimate=SHADOW,
        name="front",
    )(x_all, bias, cos_rows, sin_rows, gain1, gain2, q_gain, k_gain, router_t, routes, slot_of,
      keep, *weights)


def back_kernel(
    pick_t, ret, slot_of, keep, gates, routes, bias, cos_rows, sin_rows, gain2,
    q_gain, k_gain, router, resid, dy_all, mixed, qh, kh, vh,
    q_hbm, k_hbm, wo_hbm,
    d_qkv, dr, d_mine, router_out, small_out,
    q_raw, k_raw, wo, parts, halves, box, total, dm, d_att, dg_mine, dg_box,
    load_sem, send_sem, recv_sem,
):
    me, peers = tensor_peers()
    ready = greet("tensor", peers)
    loads = fetch([(wo_hbm, wo), (q_hbm, q_raw), (k_hbm, k_raw)], load_sem)
    blocks, tok, col = parts.shape
    width = blocks * col
    post = Post("tensor", send_sem, recv_sem)
    for t in range(blocks):
        parts[t] = dot(pick_t[...], ret[:, t * col : (t + 1) * col]).astype(BF)
    ready()
    first = scatter_start(post, parts, halves, me)
    top = routes.shape[0]
    dgate = row_sum(ret[:, width:].astype(F32))
    slot = lax.broadcasted_iota(jnp.int32, (ret.shape[0], tok), 0)
    for k in range(top):
        hot = slot_of[k : k + 1, :] == slot
        dg_mine[k : k + 1, :] = jnp.sum(jnp.where(hot, dgate, 0.0), axis=0, keepdims=True)
    dg_in = [post.push(dg_mine, dg_box.at[d], peer) for d, peer in enumerate(peers)]
    moved = scatter_relay(post, parts, halves, box, me, first)
    total[me] = scatter_total(parts, box, me, moved).astype(BF)
    total_first = gather_start(post, total, me)

    arrive(dg_in)
    d_gates = dg_mine[...]
    for d in range(blocks - 1):
        d_gates = d_gates + dg_box[d]
    d_gates = d_gates * keep[...]
    gate = gates[...]
    d_chosen = gate * (d_gates - jnp.sum(gate * d_gates, axis=0, keepdims=True))
    expert = lax.broadcasted_iota(jnp.int32, (router.shape[1], tok), 0)
    d_logits_t = jnp.zeros(expert.shape, F32)
    for k in range(top):
        hot = routes[k : k + 1, :] == expert
        d_logits_t = jnp.where(hot, d_chosen[k : k + 1, :], d_logits_t)
    d_logits = d_logits_t.T.astype(BF)
    square = jnp.zeros((tok, 1), F32)
    for t in range(blocks):
        rows = slice(t * col, (t + 1) * col)
        dm[t] = dot(d_logits, router[rows, :], 1, 1)
        square = square + row_sum(resid[t] * resid[t])
    r2 = inverse_rms(square, width)
    total_moved = gather_relay(post, total, me, total_first)
    for t in range(blocks):
        rows = slice(t * col, (t + 1) * col)
        router_out[rows, :] = dot(mixed[t].T, d_logits).astype(BF)
    arrive(total_moved)
    cross = jnp.zeros((tok, 1), F32)
    for t in range(blocks):
        dm[t] = dm[t] + total[t].astype(F32)
        cross = cross + row_sum(resid[t] * gain2[t : t + 1, :] * dm[t])
    cross = cross * (1.0 / width) * r2 * r2 * r2
    small_out[...] = jnp.zeros_like(small_out)
    for t in range(blocks):
        d_mixed = dm[t]
        small_out[t : t + 1, :] = jnp.sum(d_mixed * resid[t] * r2, axis=0, keepdims=True)
        d_resid = dy_all[t].astype(F32) + r2 * gain2[t : t + 1, :] * d_mixed - resid[t] * cross
        dm[t] = d_resid
        dr[t] = d_resid.astype(BF)
    d_mine[...] = dm[me]
    for copy in loads:
        copy.wait()
    value = dot(dr[0], wo[:, 0:col], 1, 1)
    for t in range(1, blocks):
        value = value + dot(dr[t], wo[:, t * col : (t + 1) * col], 1, 1)
    d_att[...] = value.astype(BF)

    head = q_gain.shape[1]
    scale = 1.0 / math.sqrt(head)
    q_part = jnp.zeros((1, head), F32)
    k_part = jnp.zeros((1, head), F32)

    def unturn(grown, raw, gain):
        d_unit = grown * cos_rows[...] - pltpu.roll(grown, head // 2, 1) * sin_rows[...]
        inverse = inverse_rms(row_sum(raw * raw), head)
        unit = raw * inverse
        gain_part = jnp.sum(d_unit * unit, axis=0, keepdims=True)
        d_unit = d_unit * gain[...]
        d_raw = inverse * (d_unit - unit * (row_sum(unit * d_unit) * (1.0 / head)))
        return d_raw.astype(BF), gain_part

    for h in range(col // head):
        lanes = slice(h * head, (h + 1) * head)
        probs = softmax_rows(qh[:, lanes], kh[:, lanes], bias[...], scale)
        d_head = d_att[:, lanes]
        d_probs = dot(d_head, vh[:, lanes], 1, 1)
        d_scores = probs * (d_probs - row_sum(probs * d_probs))
        d_qkv[:, 2 * col + h * head : 2 * col + (h + 1) * head] = dot(
            probs.T.astype(BF), d_head
        ).astype(BF)
        d_q, part = unturn(dot(d_scores.astype(BF), kh[:, lanes]) * scale, q_raw[:, lanes], q_gain)
        q_part = q_part + part
        d_qkv[:, lanes] = d_q
        d_k, part = unturn(dot(d_scores.T.astype(BF), qh[:, lanes]) * scale, k_raw[:, lanes], k_gain)
        k_part = k_part + part
        d_qkv[:, col + h * head : col + (h + 1) * head] = d_k
    small_out[blocks : blocks + 1, :head] = q_part
    small_out[blocks : blocks + 1, head : 2 * head] = k_part
    post.finish()


def back_call(pick_t, ret, slot_of, keep, gates, routes, bias, cos_rows, sin_rows,
              gain2, q_gain, k_gain, router, resid, dy_all, mixed, qh, kh, vh, q_raw, k_raw, wo):
    blocks, tok, col = dy_all.shape
    width = blocks * col
    tiles = (blocks, tok, col)
    shape = jax.ShapeDtypeStruct
    vmem = pl.BlockSpec(memory_space=pltpu.VMEM)
    top = routes.shape[0]
    count = 8 + blocks - 1
    return pl.pallas_call(
        back_kernel,
        out_shape=(
            shape((tok, 3 * col), BF), shape(tiles, BF), shape((tok, col), F32),
            shape((width, 128), BF), shape((8, col), F32),
        ),
        in_specs=[vmem] * 19 + [pl.BlockSpec(memory_space=pl.ANY)] * 3,
        out_specs=(vmem,) * 5,
        scratch_shapes=[
            pltpu.VMEM((tok, col), F32), pltpu.VMEM((tok, col), F32), pltpu.VMEM((col, width), BF),
            pltpu.VMEM(tiles, BF), pltpu.VMEM((2, tok // 2, col), BF), pltpu.VMEM((2, tok, col), BF),
            pltpu.VMEM(tiles, BF), pltpu.VMEM(tiles, F32), pltpu.VMEM((tok, col), BF),
            pltpu.VMEM((top, tok), F32), pltpu.VMEM((blocks - 1, top, tok), F32),
            pltpu.SemaphoreType.DMA((3,)),
            pltpu.SemaphoreType.DMA((count,)), pltpu.SemaphoreType.DMA((count,)),
        ],
        compiler_params=pltpu.CompilerParams(
            collective_id=2, has_side_effects=True, vmem_limit_bytes=48 * 1024 * 1024
        ),
        cost_estimate=pl.CostEstimate(
            flops=20_000_000_000, bytes_accessed=1, transcendentals=0
        ),
        name="back",
    )(pick_t, ret, slot_of, keep, gates, routes, bias, cos_rows, sin_rows, gain2,
      q_gain, k_gain, router, resid, dy_all, mixed, qh, kh, vh, q_raw, k_raw, wo)


def octet():
    me = lax.axis_index("expert")
    core = me % 2
    return me - core, core, lax.axis_index("tensor")


def octet_others(base, core, rank):
    count = lax.axis_size("tensor")
    others = [{"expert": base + core, "tensor": (rank + d) % count} for d in range(1, count)]
    return others + [
        {"expert": base + 1 - core, "tensor": (rank + d) % count} for d in range(count)
    ]


def meet(others):
    barrier = pltpu.get_barrier_semaphore()
    for other in others:
        pl.semaphore_signal(barrier, inc=1, device_id=other, device_id_type=MESH)
    return lambda: pl.semaphore_wait(barrier, len(others))


def remote(source, target, send_sem, recv_sem, device):
    return pltpu.make_async_remote_copy(
        src_ref=source, dst_ref=target, send_sem=send_sem, recv_sem=recv_sem, device_id=device,
        device_id_type=MESH,
    )


def weights_kernel(w, first, second, out, local_sem, near_sem, send_sem, recv_sem, pass_send, pass_recv):
    base, core, rank = octet()
    ready = meet(octet_others(base, core, rank))
    ranks = out.shape[0]
    half = out.shape[2] // 2
    sibling = {"expert": base + 1 - core, "tensor": rank}

    def part(ref, index, side):
        return ref.at[index, :, pl.ds(side * half, half), :]

    offsets = (3 - 2 * core, 1 + 2 * core)
    kept = []
    for n, source in enumerate((first, second)):
        place = part(out, (rank + offsets[n]) % ranks, core)
        kept.append(pltpu.make_async_copy(source, place, near_sem.at[n]))
        kept[-1].start()
    ready()
    side = rank % 2
    target = 2 * core + side
    sends = []
    for k in range(2):
        here = (target == rank) & (core == k)
        source, place = part(w, side, k), part(out, rank, k)
        local = pltpu.make_async_copy(source, place, local_sem)
        away = remote(
            source, place, send_sem.at[k], recv_sem.at[rank], {"expert": base + k, "tensor": target}
        )
        pl.when(here)(local.start)
        pl.when(jnp.logical_not(here))(away.start)
        sends.append((here, away))
    passed = []
    for n, source in enumerate((first, second)):
        d = offsets[n]
        place = part(out, (rank + d) % ranks, core)
        passed.append(remote(source, place, pass_send.at[d], pass_recv.at[d], sibling))
        passed[-1].start()
    for d in (0, 2):
        quarter = (rank + d) % ranks
        mine = part(out, quarter, core)
        arrival = remote(mine, mine, send_sem.at[0], recv_sem.at[quarter], sibling)
        here = (rank // 2 == core) & (d == 0)
        pl.when(here)(pltpu.make_async_copy(part(w, 0, 0), mine, local_sem).wait)
        pl.when(jnp.logical_not(here))(arrival.wait_recv)
        passed.append(remote(mine, mine, pass_send.at[d], pass_recv.at[d], sibling))
        passed[-1].start()
    for copy in passed:
        copy.wait_send()
    for d in range(ranks):
        theirs = part(out, (rank + d) % ranks, 1 - core)
        remote(theirs, theirs, pass_send.at[d], pass_recv.at[d], sibling).wait_recv()
    for here, away in sends:
        pl.when(jnp.logical_not(here))(away.wait_send)
    for copy in kept:
        copy.wait()


def weights_call(w, first, second):
    _, three, width, hidden = w.shape
    hbm = pl.BlockSpec(memory_space=pl.ANY)
    pairs, sems = pltpu.SemaphoreType.DMA((2,)), pltpu.SemaphoreType.DMA((4,))
    return pl.pallas_call(
        weights_kernel,
        out_shape=jax.ShapeDtypeStruct((4, three, width, hidden), BF),
        in_specs=[hbm] * 3,
        out_specs=hbm,
        scratch_shapes=[pltpu.SemaphoreType.DMA, pairs, pairs, sems, sems, sems],
        compiler_params=pltpu.CompilerParams(
            collective_id=4, has_side_effects=True, vmem_limit_bytes=60 * 1024 * 1024
        ),
        cost_estimate=SHADOW,
        name="weights",
    )(w, first, second)


def near_weights(w):
    ranks = lax.axis_size("tensor")
    places = lax.axis_size("expert")
    half = w.shape[2] // 2
    core, rank = lax.axis_index("expert") % 2, lax.axis_index("tensor")
    side = 1 - rank % 2
    leftward = jnp.where(2 * core + side == (rank + 1) % ranks, 0, 1)
    come = []
    for turn_over in range(2):
        pairs = []
        for place in range(places):
            for t in range(ranks):
                target = 2 * (place % 2) + 1 - t % 2
                to_core = (0 if target == (t + 1) % ranks else 1) ^ turn_over
                pairs.append((place * ranks + t, (place - place % 2 + to_core) * ranks + target))
        to_core = jnp.where(turn_over == 0, leftward, 1 - leftward)
        piece = lax.dynamic_slice(w, (side, 0, to_core * half, 0), (1,) + w.shape[1:2] + (half,) + w.shape[3:])
        come.append(lax.ppermute(piece[0], ("expert", "tensor"), pairs))
    return come


def home_kernel(grads, out, far_out, own, got, load_sem, local_sem, swap_send, swap_recv, send_sem, recv_sem):
    base, core, rank = octet()
    ready = meet(octet_others(base, core, rank))
    ranks, three, half, hidden = own.shape
    sibling = {"expert": base + 1 - core, "tensor": rank}
    order = (1, 3, 0, 2)
    loads, swaps = [], []
    for d in order:
        quarter = (rank + d) % ranks
        source = grads.at[quarter, :, pl.ds(core * half, half), :]
        loads.append(pltpu.make_async_copy(source, own.at[d], load_sem.at[d]))
        loads[-1].start()
    ready()
    for d in order:
        quarter = (rank + d) % ranks
        source = grads.at[quarter, :, pl.ds((1 - core) * half, half), :]
        swaps.append(remote(source, got.at[d], swap_send.at[d], swap_recv.at[d], sibling))
        swaps[-1].start()
    owner = rank // 2
    side = rank - 2 * owner
    rows = 64
    place = out.at[side, :, pl.ds(core * half, half), :]
    stays = owner == core
    sends = []
    for n, d in enumerate(order):
        loads[n].wait()
        swaps[n].wait_recv()

        def one(i, _, d=d):
            c, at = i // (half // rows), i % (half // rows) * rows
            here = pl.ds(pl.multiple_of(at, rows), rows)
            value = own[d, c, here, :].astype(F32) + got[d, c, here, :].astype(F32)
            own[d, c, here, :] = value.astype(BF)
            return 0

        lax.fori_loop(0, three * (half // rows), one, 0)
        if d == 2:
            far = pltpu.make_async_copy(own.at[d], far_out, load_sem.at[d])
            far.start()
            continue
        away = remote(
            own.at[d], place, send_sem.at[d], recv_sem.at[2 * side + core],
            {"expert": base + owner, "tensor": (rank + d) % ranks},
        )
        if d:
            away.start()
        else:
            kept = pltpu.make_async_copy(own.at[d], place, local_sem)
            pl.when(stays)(kept.start)
            pl.when(jnp.logical_not(stays))(away.start)
        sends.append((d, away))
    for s in range(2):
        for k in range(2):
            off = (2 * core + s - rank) % ranks
            mine = out.at[s, :, pl.ds(k * half, half), :]
            arrival = remote(own.at[0], mine, send_sem.at[0], recv_sem.at[2 * s + k], sibling)
            own_chip = off == 0
            comes = (off != 2) & jnp.logical_not(own_chip & (core == k))
            pl.when(comes)(arrival.wait_recv)
    pl.when(stays)(kept.wait)
    for d, away in sends:
        if d:
            away.wait_send()
        else:
            pl.when(jnp.logical_not(stays))(away.wait_send)
    for swap in swaps:
        swap.wait_send()
    far.wait()


def home_call(grads):
    ranks, three, width, hidden = grads.shape
    hbm = pl.BlockSpec(memory_space=pl.ANY)
    sems = pltpu.SemaphoreType.DMA((4,))
    halves = pltpu.VMEM((ranks, three, width // 2, hidden), BF)
    shape = jax.ShapeDtypeStruct
    return pl.pallas_call(
        home_kernel,
        out_shape=(
            shape((2, three, width, hidden), BF), shape((three, width // 2, hidden), BF),
        ),
        in_specs=[hbm],
        out_specs=(hbm, hbm),
        scratch_shapes=[
            halves, halves, sems, pltpu.SemaphoreType.DMA, sems, sems, sems, sems,
        ],
        compiler_params=pltpu.CompilerParams(
            collective_id=5, has_side_effects=True, vmem_limit_bytes=60 * 1024 * 1024
        ),
        cost_estimate=SHADOW,
        name="home",
    )(grads)


def expert_kernel(rows_ref, dys, w_ref, y_ref, dx_ref, grad_ref, rows_t, dys_t, y_acc, dx_acc, gate_of, dgate):
    step = pl.program_id(0)
    width = y_acc.shape[1]
    rows = rows_ref.at[:, :width]

    @pl.when(step == 0)
    def _():
        gate_of[...] = row_sum(rows_ref[:, width:].astype(F32))
        rows_t[...] = rows[...].T
        dys_t[...] = (dys[...].astype(F32) * gate_of[...]).astype(BF).T
        dgate[...] = jnp.zeros_like(dgate)
        y_acc[...] = jnp.zeros_like(y_acc)
        dx_acc[...] = jnp.zeros_like(dx_acc)

    w_gate, w_up, w_down = w_ref[0, 0], w_ref[0, 1], w_ref[0, 2]
    gate = dot(rows[...], w_gate)
    up = dot(rows[...], w_up)
    d_raw = dot(dys[...], w_down)
    d_act = d_raw * gate_of[...]
    sig = 1.0 / (1.0 + jnp.exp(-gate))
    silu = gate * sig
    act = (silu * up).astype(BF)
    dgate[...] += row_sum(act.astype(F32) * d_raw)
    d_gate = (d_act * up * sig * (1.0 + gate * (1.0 - sig))).astype(BF)
    d_up = (d_act * silu).astype(BF)
    y_acc[...] += dot(act, w_down, 1, 1)
    dx_acc[...] += dot(d_gate, w_gate, 1, 1) + dot(d_up, w_up, 1, 1)
    grad_ref[0, 0] = dot(rows_t[...], d_gate).astype(BF)
    grad_ref[0, 1] = dot(rows_t[...], d_up).astype(BF)
    grad_ref[0, 2] = dot(dys_t[...], act).astype(BF)

    @pl.when(step == pl.num_programs(0) - 1)
    def _():
        first = dgate[...].astype(BF).astype(F32)
        lane = lax.broadcasted_iota(jnp.int32, (y_ref.shape[0], 128), 1)
        facts = jnp.where(lane == 0, first, jnp.where(lane == 1, dgate[...] - first, 0.0))
        y_ref[...] = (y_acc[...] * gate_of[...]).astype(BF)
        dx_ref[:, :width] = dx_acc[...].astype(BF)
        dx_ref[:, width:] = facts.astype(BF)


def expert_call(rows, dys, weights):
    quarters, _, width, hidden = weights.shape
    count = rows.shape[0]
    shape = jax.ShapeDtypeStruct

    def whole(value):
        return pl.BlockSpec(value.shape, lambda q: (0, 0), pipeline_mode=pl.Buffered(1))

    block = pl.BlockSpec((1, 3, width, hidden), lambda q: (q, 0, 0, 0))
    outs = [shape((count, width), BF), shape((count, width + 128), BF)]
    return pl.pallas_call(
        expert_kernel,
        grid=(quarters,),
        out_shape=tuple(outs) + (shape(weights.shape, BF),),
        in_specs=[whole(rows), whole(dys), block],
        out_specs=tuple(whole(value) for value in outs) + (block,),
        scratch_shapes=[
            pltpu.VMEM((width, count), BF),
            pltpu.VMEM((width, count), BF),
            pltpu.VMEM((count, width), F32),
            pltpu.VMEM((count, width), F32),
            pltpu.VMEM((count, 1), F32),
            pltpu.VMEM((count, 1), F32),
        ],
        compiler_params=pltpu.CompilerParams(vmem_limit_bytes=62 * 1024 * 1024),
        cost_estimate=COST,
        name="expert",
    )(rows, dys, weights)


def plane():
    me = lax.axis_index("expert")
    core, z, y = me % 2, (me // 2) % 4, me // 8
    return [
        (core, me + 1 - 2 * core),
        ((y + y // 2) % 2, me + 8 * (1 - 2 * (y % 2))),
        (y // 2, me + 8 * (3 - 2 * y)),
        ((z + z // 2) % 2, me + 2 * (1 - 2 * (z % 2))),
        (z // 2, me + 2 * (3 - 2 * z)),
    ]

ORDERS = ((1, 3, 2, 4), (3, 2, 4, 1), (2, 4, 1, 3), (4, 1, 3, 2))

def reduce_kernel(
    d_qkv, dr, d_mine, router_part, small_in, x_all, gain1, ob, pick_y, ret_y,
    far_hbm, resid_hbm, wq_hbm, wk_hbm, wv_hbm,
    q_out, k_out, v_out, router_out, o_out, dx_out, out_out, small_out, far_out,
    wq, wk, wv, resid, parts, y_parts, halves, box_x, note, buf, box, got,
    load_sem, out_sem, x_send, x_recv, send_sem, recv_sem, far_send, far_recv,
):
    me, peers = tensor_peers()
    dims = plane()
    base, core, _ = octet()
    ready = meet(octet_others(base, core, me) + [{"expert": partner} for _, partner in dims[1:]])
    loads = fetch(
        [(wq_hbm, wq), (wk_hbm, wk), (wv_hbm, wv), (resid_hbm.at[me], resid)], load_sem
    )
    blocks, tok, col = x_all.shape
    width = blocks * col
    head = col // blocks
    square = jnp.zeros((tok, 1), F32)
    for t in range(blocks):
        value = x_all[t].astype(F32)
        square = square + row_sum(value * value)
    r1 = inverse_rms(square, width)
    post_x = Post("tensor", x_send, x_recv)
    post = Post("expert", send_sem, recv_sem)
    x_halves, x_box = halves.at[pl.ds(0, 2)], box_x.at[pl.ds(0, 2)]
    y_halves, y_box = halves.at[pl.ds(2, 2)], box_x.at[pl.ds(2, 2)]
    chunks = buf.shape[0] // blocks
    rows_chunk = buf.shape[1]

    def products(t):
        here = pl.ds(t * chunks, chunks)
        normed = (x_all[t].astype(F32) * r1 * gain1[pl.ds(t, 1), :]).T.astype(BF)
        for n in range(3):
            lanes = slice(n * col, (n + 1) * col)
            value = dot(normed, d_qkv[:, lanes]).astype(BF)
            buf[here, :, lanes] = value.reshape(chunks, rows_chunk, col)
        value = dot(dr[t].T, ob[...]).astype(BF)
        buf[here, :, 3 * col : 4 * col] = value.reshape(chunks, rows_chunk, col)
        value = router_part[pl.ds(t * col, col), :]
        buf[here, :, 4 * col :] = value.reshape(chunks, rows_chunk, value.shape[1])

    def add(target, place, first, count):
        def one(i, _):
            total = buf[place + i].astype(F32) + box[first + i].astype(F32)
            target[place + i] = total.astype(BF)
            return 0

        lax.fori_loop(0, count, one, 0)

    half = far_hbm.shape[1]
    owner = me // 2

    def far_copy(n, side, device):
        return remote(
            far_hbm.at[n], far_out.at[n, pl.ds(side * half, half), :],
            far_send.at[n], far_recv.at[n, side], device,
        )

    far_copies = [
        far_copy(n, core, {"expert": base + owner, "tensor": (me + 2) % blocks}) for n in range(3)
    ]
    copies = []
    ready()
    for n in range(2):
        products(2 * (1 - core) + n)
        for s in range(2 * n, 2 * n + 2):
            source = buf.at[pl.ds((1 - core) * 64 + s * 16, 16)]
            copies.append(post.push(source, box.at[pl.ds(31 * s, 16)], dims[0][1]))
    for copy in loads:
        copy.wait()
    for t in range(blocks):
        rows = slice(t * col, (t + 1) * col)
        parts[t] = (
            dot(d_qkv[:, 0:col], wq[rows, :], 1, 1)
            + dot(d_qkv[:, col : 2 * col], wk[rows, :], 1, 1)
            + dot(d_qkv[:, 2 * col : 3 * col], wv[rows, :], 1, 1)
        ).astype(BF)
    x_first = scatter_start(post_x, parts, x_halves, me)
    far_copies[0].start()
    for n in range(2):
        products(2 * core + n)
    x_moved = scatter_relay(post_x, parts, x_halves, x_box, me, x_first)
    far_copies[1].start()
    place = [core * 64 + s * 16 for s in range(4)]
    size, first = 16, 0

    def halve(k):
        for s in range(4):
            copies[s].wait_recv()
            add(buf, place[s], 31 * s + first, size)
            bit, partner = dims[ORDERS[s][k]]
            half = size // 2
            copies[s] = post.push(
                buf.at[pl.ds(place[s] + (1 - bit) * half, half)],
                box.at[pl.ds(31 * s + first + size, half)],
                partner,
            )
            place[s] = place[s] + bit * half

    halve(0)
    first, size = first + size, size // 2

    for t in range(blocks):
        y_parts[t] = dot(pick_y[...], ret_y[:, t * col : (t + 1) * col]).astype(BF)
    y_first = scatter_start(post_x, y_parts, y_halves, me)
    d_an = scatter_total(parts, x_box, me, x_moved)
    x_mine = x_all[me].astype(F32)
    grown = gain1[pl.ds(me, 1), :] * d_an
    mean_part = row_sum(x_mine * grown)
    note[me, 0:8, :] = jnp.broadcast_to(
        jnp.sum(d_an * x_mine * r1, axis=0, keepdims=True), (8, col)
    )
    note[me, 8:16, 0:tok] = jnp.broadcast_to(mean_part, (tok, 128)).T[0:8, :]
    note[me, 8:16, tok:] = jnp.broadcast_to(small_in[blocks : blocks + 1, : 2 * head], (8, 2 * head))
    note_in = [post_x.push(note.at[me], note.at[me], peer) for peer in peers]

    halve(1)
    first, size = first + size, size // 2
    y_moved = scatter_relay(post_x, y_parts, y_halves, y_box, me, y_first)
    far_copies[2].start()
    halve(2)
    first, size = first + size, size // 2
    halve(3)
    first, size = first + size, size // 2
    for s in range(4):
        copies[s].wait_recv()
        add(got, place[s], 31 * s + first, 1)
        here = got.at[pl.ds(place[s], 1)]
        copies[s] = post.push(here, here, dims[ORDERS[s][3]][1])

    arrive(note_in)
    facts = note[0, 8:16, :]
    for t in range(1, blocks):
        facts = facts + note[t, 8:16, :]
    for t in range(blocks):
        small_out[t : t + 1, :] = note[t, 0:1, :]
        small_out[blocks + t : blocks + t + 1, :] = small_in[t : t + 1, :]
    small_out[2 * blocks :, :] = facts
    mean = jnp.broadcast_to(facts[0:1, 0:tok], (128, tok)).T[:, 0:1] * (1.0 / width)
    dx_out[...] = (d_mine[...] + r1 * grown - x_mine * (r1 * r1 * r1 * mean)).astype(BF)

    size = 1
    stores = []

    def keep(n, at):
        here = pl.ds(at, 16)
        outs = (q_out, k_out, v_out, None, router_out)
        for m, target in enumerate(outs):
            lanes = pl.ds(m * col, target.shape[2] if m != 3 else col)
            if m == 3:
                turned = got[here, :, lanes].reshape(16 * rows_chunk, col).T
                o_out[:, pl.ds(pl.multiple_of(at * rows_chunk, 128), 16 * rows_chunk)] = turned
                continue
            stores.append(
                pltpu.make_async_copy(got.at[here, :, lanes], target.at[here], out_sem.at[n, m])
            )
            stores[-1].start()

    for k in range(3, -1, -1):
        for s in range(4):
            copies[s].wait_recv()
            bit, _ = dims[ORDERS[s][k]]
            place[s] = place[s] - bit * size
            partner = dims[ORDERS[s][k - 1]][1] if k else dims[0][1]
            here = got.at[pl.ds(place[s], 2 * size)]
            copies[s] = post.push(here, here, partner)
            if not k:
                keep(s, place[s])
        size *= 2
        if k == 2:
            out_out[...] = (resid[...] + scatter_total(y_parts, y_box, me, y_moved)).astype(BF)
    for s in range(4):
        copies[s].wait_recv()
        keep(4 + s, (1 - core) * 64 + s * 16)
    post.finish()
    post_x.finish()
    for store in stores:
        store.wait()
    comes = (me + 2) % blocks // 2 == core
    for n in range(3):
        for side in range(2):
            pl.when(comes)(far_copy(n, side, {"expert": base + core, "tensor": (me + 2) % blocks}).wait_recv)
        far_copies[n].wait_send()


def reduce_call(d_qkv, dr, d_mine, router_part, small, x_all, gain1, ob, pick_y, ret_y, far, resid,
                weights):
    blocks, tok, col = x_all.shape
    width = blocks * col
    tiles = (blocks, tok, col)
    wide = (128, 16, 4 * col + 128)
    shape = jax.ShapeDtypeStruct
    vmem = pl.BlockSpec(memory_space=pltpu.VMEM)
    hbm = pl.BlockSpec(memory_space=pl.ANY)
    count = 8 + blocks - 1
    return pl.pallas_call(
        reduce_kernel,
        out_shape=(
            shape(wide[:2] + (col,), BF), shape(wide[:2] + (col,), BF), shape(wide[:2] + (col,), BF),
            shape(wide[:2] + (128,), BF), shape((col, width), BF),
            shape((tok, col), BF), shape((tok, col), BF), shape((16, col), F32),
            shape((far.shape[0], 2 * far.shape[1], far.shape[2]), BF),
        ),
        in_specs=[vmem] * 10 + [hbm] * 5,
        out_specs=(hbm,) * 4 + (vmem,) * 4 + (hbm,),
        scratch_shapes=[
            pltpu.VMEM((width, col), BF), pltpu.VMEM((width, col), BF), pltpu.VMEM((width, col), BF),
            pltpu.VMEM((tok, col), F32), pltpu.VMEM(tiles, BF), pltpu.VMEM(tiles, BF),
            pltpu.VMEM((4, tok // 2, col), BF), pltpu.VMEM((4, tok, col), BF),
            pltpu.VMEM((blocks, 16, col), F32),
            pltpu.VMEM(wide, BF), pltpu.VMEM((124,) + wide[1:], BF), pltpu.VMEM(wide, BF),
            pltpu.SemaphoreType.DMA((4,)), pltpu.SemaphoreType.DMA((8, 5)),
            pltpu.SemaphoreType.DMA((count,)), pltpu.SemaphoreType.DMA((count,)),
            pltpu.SemaphoreType.DMA((40,)), pltpu.SemaphoreType.DMA((40,)),
            pltpu.SemaphoreType.DMA((3,)), pltpu.SemaphoreType.DMA((3, 2)),
        ],
        compiler_params=pltpu.CompilerParams(
            collective_id=3, has_side_effects=True, vmem_limit_bytes=60 * 1024 * 1024
        ),
        cost_estimate=COST,
        name="reduce",
    )(d_qkv, dr, d_mine, router_part, small, x_all, gain1, ob, pick_y, ret_y, far, resid, *weights)


def body(
    tokens,
    out_grad,
    seq_lengths,
    dest_index,
    routes,
    pair_order,
    norm1_gain,
    w_query,
    w_key,
    w_value,
    q_gain,
    k_gain,
    w_output,
    norm2_gain,
    w_router,
    expert_w,
):
    groups = lax.axis_size("expert")
    tensor_count = lax.axis_size("tensor")
    group_id = lax.axis_index("expert")
    tensor_id = lax.axis_index("tensor")
    tok_count, col_count = tokens.shape
    width = col_count * tensor_count
    move_rows = tok_count // groups
    expert_count = w_router.shape[1]
    top_count = routes.shape[1]
    local_experts = expert_w.shape[0]

    w_stored = jnp.transpose(expert_w, (0, 2, 1, 3))
    w_near = near_weights(w_stored)

    routes_t = routes.T
    order_t = pair_order[0].reshape(tok_count, top_count).T
    pair_expert = routes_t.reshape(-1)
    pair_total = tok_count * top_count
    base = pair_expert * pair_total
    keyed = base + order_t.reshape(-1)
    before = (keyed[None, :] < keyed[:, None]) & (keyed[None, :] >= base[:, None])
    ranks = jnp.sum(before.astype(jnp.int32), axis=1).reshape(top_count, tok_count)
    expert_axis = jnp.arange(expert_count, dtype=jnp.int32)
    route_hot = routes_t[:, None, :] == expert_axis[None, :, None]
    counts = jnp.sum(route_hot.astype(F32), axis=(0, 2))

    places = jnp.arange(tok_count, dtype=jnp.int32)
    arrival_rank = jnp.sum((dest_index[None, :] < dest_index[:, None]).astype(jnp.int32), axis=1)
    by_rank = (arrival_rank[None, :] == places[:, None]).astype(BF)
    inner = jnp.broadcast_to((dest_index % tok_count).astype(BF)[:, None], (tok_count, 64))
    facts = jnp.broadcast_to(counts.astype(BF)[None, :], (tok_count, expert_count))
    outgoing = dot(by_rank, jnp.concatenate([tokens, out_grad, inner, facts], axis=1)).astype(BF)
    got = exchange(outgoing.reshape(groups, move_rows, -1), "expert")
    all_counts = got[:, 0, 2 * col_count + 64 :].astype(jnp.int32)
    lower = jnp.arange(groups, dtype=jnp.int32) < group_id
    offsets = jnp.sum(jnp.where(lower[:, None], all_counts, 0), axis=0)
    mine = got[:, :, 2 * col_count].astype(jnp.int32).reshape(-1)
    put = (mine[None, :] == places[:, None]).astype(BF)
    local = dot(put, got.reshape(tok_count, -1)[:, : 2 * col_count]).astype(BF)
    capacity = 5 * tok_count * groups * top_count // (4 * expert_count)
    most_rows = 3 * tok_count * top_count // (2 * expert_count)
    per = most_rows // 2
    slots = groups * per
    slot_global = jnp.sum(jnp.where(route_hot, offsets[None, :, None], 0), axis=1) + ranks
    kept = slot_global < capacity
    keep_mask = kept.astype(F32)
    here = kept & (routes_t % tensor_count == tensor_id)
    owner = routes_t // tensor_count * 2 + ranks % 2
    slot_of = jnp.where(here, owner * per + ranks // 2, -1)

    seq_ids, positions = sequence_layout(seq_lengths[0], tok_count)
    bias = jnp.where(seq_ids[:, None] == seq_ids[None, :], 0.0, mask_fill)
    cos_tab, sin_tab = rope_tables(positions, q_gain.shape[0])
    cos_rows = jnp.concatenate([cos_tab, cos_tab], axis=1)
    sin_rows = jnp.concatenate([-sin_tab, sin_tab], axis=1)
    gain1 = norm1_gain.astype(F32).reshape(tensor_count, col_count)
    gain2 = norm2_gain.astype(F32).reshape(tensor_count, col_count)
    head_gains = (q_gain.astype(F32)[None], k_gain.astype(F32)[None])
    router = jnp.pad(w_router, ((0, 0), (0, 128 - expert_count)))
    weights = (w_query, w_key, w_value, w_output)
    def homeward(value):
        return exchange(value.reshape(groups, -1, value.shape[1]), "expert").reshape(value.shape)

    x_all, dy_all, send_dy = pre_call(local, slot_of, tensor_count, slots)
    send_dy, x_all = lax.optimization_barrier((send_dy, x_all))
    recv_dy = homeward(send_dy)
    (
        resid, mixed, q_raw, k_raw, qh, kh, vh, attended, gates, send_rows, pick_t,
    ) = front_call(
        x_all, bias, cos_rows, sin_rows, gain1, gain2, *head_gains, router.T, routes_t, slot_of,
        keep_mask, weights, slots,
    )
    send_rows, w_stored, recv_dy = lax.optimization_barrier((send_rows, w_stored, recv_dy))
    recv_rows = homeward(send_rows)
    y_rows, d_rows, partial = expert_call(recv_rows, recv_dy, weights_call(w_stored, *w_near))
    ret_rows = homeward(d_rows)
    near, far = home_call(partial)
    ret_rows, near, far, y_rows = lax.optimization_barrier((ret_rows, near, far, y_rows))
    ret_y = homeward(y_rows)
    d_qkv, dr, d_mine, router_part, small = back_call(
        pick_t, ret_rows, slot_of, keep_mask, gates, routes_t, bias, cos_rows,
        sin_rows, gain2, *head_gains, router, resid, dy_all, mixed, qh, kh, vh, q_raw, k_raw,
        w_output,
    )
    *wide, router_sum, out_proj, dx_slice, out_slice, small, far = reduce_call(
        d_qkv, dr, d_mine, router_part, small, x_all, gain1, attended, pick_t, ret_y, far, resid,
        weights[:3],
    )

    going = dot(put, jnp.concatenate([out_slice, dx_slice], axis=1), 0, 0).astype(BF)
    small = small[:9].astype(BF).reshape(move_rows, -1)
    small = jnp.pad(small, ((0, 0), (0, -small.shape[1] % 128)))
    small = jnp.broadcast_to(small[None], (groups,) + small.shape)
    back = exchange(jnp.concatenate([going.reshape(groups, move_rows, -1), small], axis=2), "expert")
    small = jnp.sum(back[:, :, 2 * col_count :].astype(F32), axis=0)[:, : 9 * col_count // move_rows]
    small = small.reshape(-1)
    back = dot(by_rank, back.reshape(tok_count, -1)[:, : 2 * col_count], 0, 0).astype(BF)
    opposite = (tensor_id + 2) % tensor_count - 2 * (group_id % 2)
    is_far = jnp.arange(local_experts) == opposite
    expert_grad = jnp.where(is_far[:, None, None, None], far[None], near).astype(F32)
    expert_grad = jnp.transpose(expert_grad, (0, 2, 1, 3))
    wide = [value.reshape(width, -1) for value in wide]
    gain_at = 2 * width + tok_count
    head = q_gain.shape[0]
    return (
        back[:, :col_count],
        back[:, col_count:],
        small[:width],
        wide[0].astype(F32),
        wide[1].astype(F32),
        wide[2].astype(F32),
        small[gain_at : gain_at + head],
        small[gain_at + head : gain_at + 2 * head],
        out_proj.astype(F32),
        small[width : 2 * width],
        router_sum.reshape(width, -1)[:, :expert_count].astype(F32),
        expert_grad,
    )


def solution(mesh):
    in_specs = (
        P("expert", "tensor"),
        P("expert", "tensor"),
        P("expert", None),
        P("expert"),
        P("expert", None),
        P("expert", None),
        P(),
        P(None, "tensor"),
        P(None, "tensor"),
        P(None, "tensor"),
        P(),
        P(),
        P("tensor", None),
        P(),
        P(),
        P("expert", None, None, "tensor"),
    )
    out_specs = (
        P("expert", "tensor"),
        P("expert", "tensor"),
        P(),
        P(None, "tensor"),
        P(None, "tensor"),
        P(None, "tensor"),
        P(),
        P(),
        P("tensor", None),
        P(),
        P(),
        P("expert", None, None, "tensor"),
    )
    return jax.shard_map(body, mesh=mesh, in_specs=in_specs, out_specs=out_specs, check_vma=False)
```

```python
import functools
import math

import jax
import jax.numpy as jnp
from jax import lax
from jax.experimental import pallas as pl
from jax.experimental.pallas import tpu as pltpu
from jax.sharding import PartitionSpec as P

norm_eps = 1e-06
rope_base = 10000.0
mask_fill = -1e30


def rope_tables(positions, width):
    half_width = width // 2
    steps_idx = jnp.arange(half_width, dtype=jnp.float32)
    freqs = jnp.exp(steps_idx * (-2.0 * math.log(rope_base) / width))
    angles = positions.astype(jnp.float32)[:, None] * freqs[None, :]
    return (jnp.cos(angles), jnp.sin(angles))


def sequence_layout(lengths_row, count):
    seq_ends = jnp.cumsum(lengths_row)
    places = jnp.arange(count, dtype=jnp.int32)
    passed = (places[:, None] >= seq_ends[None, :]).astype(jnp.int32)
    seq_ids = jnp.sum(passed, axis=1)
    starts = jnp.sum(passed * lengths_row[None, :], axis=1)
    return (seq_ids, places - starts)


BF = jnp.bfloat16
F32 = jnp.float32
SHADOW = pl.CostEstimate(flops=40_000_000_000, bytes_accessed=1, transcendentals=0)
COST = pl.CostEstimate(flops=1, bytes_accessed=1, transcendentals=0)


def dot(left, right, left_dim=1, right_dim=0):
    return lax.dot_general(
        left, right, (((left_dim,), (right_dim,)), ((), ())), preferred_element_type=F32
    )


def exchange(value, axis):
    return lax.all_to_all(value, axis, split_axis=0, concat_axis=0, tiled=True)


def gather_blocks(value, axis):
    return exchange(jnp.broadcast_to(value[None], (lax.axis_size(axis),) + value.shape), axis)


def column_blocks(value, count):
    return jnp.stack(jnp.split(value, count, axis=1))


MESH = pl.DeviceIdType.MESH


def tensor_peers():
    me = lax.axis_index("tensor")
    count = lax.axis_size("tensor")
    return me, [(me + d) % count for d in range(1, count)]


def greet(axis, peers):
    barrier = pltpu.get_barrier_semaphore()
    for peer in peers:
        pl.semaphore_signal(barrier, inc=1, device_id={axis: peer}, device_id_type=MESH)
    return lambda: pl.semaphore_wait(barrier, len(peers))


class Post:
    def __init__(self, axis, send_sem, recv_sem):
        self.axis, self.send_sem, self.recv_sem = axis, send_sem, recv_sem
        self.started = []
        self.used = 0

    def push(self, source, target, peer):
        slot = self.used
        self.used += 1
        copy = pltpu.make_async_remote_copy(
            src_ref=source,
            dst_ref=target,
            send_sem=self.send_sem.at[slot],
            recv_sem=self.recv_sem.at[slot],
            device_id={self.axis: peer},
            device_id_type=MESH,
        )
        copy.start()
        self.started.append(copy)
        return copy

    def finish(self):
        for copy in self.started:
            copy.wait_send()
        self.started = []


def arrive(copies):
    for copy in copies:
        copy.wait_recv()


def ring(me):
    count = lax.axis_size("tensor")
    return (me + 1) % count, (me + count - 1) % count


def gather_start(post, ref, me):
    right, left = ring(me)
    return [post.push(ref.at[me], ref.at[me], peer) for peer in (right, left)]


def gather_relay(post, ref, me, first):
    right, left = ring(me)
    half = ref.shape[1] // 2
    first[0].wait_recv()
    here = ref.at[left, pl.ds(0, half)]
    one = post.push(here, here, right)
    first[1].wait_recv()
    here = ref.at[right, pl.ds(half, half)]
    return [one, post.push(here, here, left)]


def scatter_start(post, parts, halves, me):
    right, left = ring(me)
    far = ring(right)[0]
    half = parts.shape[1] // 2
    return [
        post.push(parts.at[far, pl.ds(0, half)], halves.at[0], right),
        post.push(parts.at[far, pl.ds(half, half)], halves.at[1], left),
    ]


def scatter_relay(post, parts, halves, box, me, first):
    right, left = ring(me)
    half = parts.shape[1] // 2
    copies = []
    for n, (peer, rows) in enumerate(((right, pl.ds(0, half)), (left, pl.ds(half, half)))):
        first[n].wait_recv()
        parts[peer, rows, :] = (parts[peer, rows, :].astype(F32) + halves[n].astype(F32)).astype(BF)
        copies.append(post.push(parts.at[peer], box.at[n], peer))
    return copies


def scatter_total(parts, box, me, copies):
    arrive(copies)
    return parts[me].astype(F32) + box[0].astype(F32) + box[1].astype(F32)


def fetch(pairs, sem):
    copies = [
        pltpu.make_async_copy(source, target, sem.at[n]) for n, (source, target) in enumerate(pairs)
    ]
    for copy in copies:
        copy.start()
    return copies


def turn(value, cos_rows, sin_rows):
    return value * cos_rows + pltpu.roll(value, value.shape[-1] // 2, 1) * sin_rows


def inverse_rms(total, width):
    return lax.rsqrt(total * (1.0 / width) + norm_eps)


def row_sum(value):
    return jnp.sum(value, axis=1, keepdims=True)


def softmax_rows(query, key, bias, scale):
    scores = dot(query, key, 1, 1) * scale + bias
    grown = jnp.exp(scores - jnp.max(scores, axis=1, keepdims=True))
    return grown / row_sum(grown)


def select_slots(slot_of, slots):
    top, tok = slot_of.shape
    slot = lax.broadcasted_iota(jnp.int32, (slots, tok), 0)
    pick = jnp.zeros((slots, tok), F32)
    for k in range(top):
        pick = jnp.where(slot_of[k : k + 1, :] == slot, 1.0, pick)
    return pick


def pre_kernel(local, slot_of, x_out, dy_out, send_out, x_all, dy_all, send_sem, recv_sem):
    me = lax.axis_index("tensor")
    ready = greet("tensor", ring(me))
    blocks, _, col = x_all.shape
    x_all[me] = local[:, :col]
    dy_all[me] = local[:, col:]
    ready()
    post = Post("tensor", send_sem, recv_sem)
    dy_in = gather_start(post, dy_all, me)
    x_in = gather_start(post, x_all, me)
    pick = select_slots(slot_of, send_out.shape[0]).astype(BF)
    dy_in = gather_relay(post, dy_all, me, dy_in)
    x_in = gather_relay(post, x_all, me, x_in)
    arrive(dy_in)
    dy_out[...] = dy_all[...]
    for t in range(blocks):
        send_out[:, t * col : (t + 1) * col] = dot(pick, dy_all[t]).astype(BF)
    arrive(x_in)
    x_out[...] = x_all[...]
    post.finish()


def pre_call(local, slot_of, blocks, slots):
    tok, both = local.shape
    col = both // 2
    tiles = (blocks, tok, col)
    shape = jax.ShapeDtypeStruct
    vmem = pl.BlockSpec(memory_space=pltpu.VMEM)
    return pl.pallas_call(
        pre_kernel,
        out_shape=(shape(tiles, BF), shape(tiles, BF), shape((slots, col * blocks), BF)),
        in_specs=[vmem] * 2,
        out_specs=(vmem,) * 3,
        scratch_shapes=[
            pltpu.VMEM(tiles, BF), pltpu.VMEM(tiles, BF),
            pltpu.SemaphoreType.DMA((8,)), pltpu.SemaphoreType.DMA((8,)),
        ],
        compiler_params=pltpu.CompilerParams(
            collective_id=6, has_side_effects=True, vmem_limit_bytes=48 * 1024 * 1024
        ),
        cost_estimate=COST,
        name="pre",
    )(local, slot_of)


def front_kernel(
    x_all, bias, cos_rows, sin_rows, gain1, gain2, q_gain, k_gain, router_t, routes, slot_of, keep,
    wq_hbm, wk_hbm, wv_hbm, wo_hbm,
    resid_out, mixed_out, q_out, k_out, qh_out, kh_out, vh_out, ob_out,
    gates_out, send_out, pick_out,
    wq, wk, wv, wo, an, parts, halves, box, total, load_sem, send_sem, recv_sem,
):
    me = lax.axis_index("tensor")
    ready = greet("tensor", ring(me))
    loads = fetch([(wq_hbm, wq), (wk_hbm, wk), (wv_hbm, wv), (wo_hbm, wo)], load_sem)
    blocks, tok, col = x_all.shape
    width = blocks * col
    post = Post("tensor", send_sem, recv_sem)
    square = jnp.zeros((tok, 1), F32)
    for t in range(blocks):
        value = x_all[t].astype(F32)
        square = square + row_sum(value * value)
    r1 = inverse_rms(square, width)
    for t in range(blocks):
        an[t] = (x_all[t].astype(F32) * r1 * gain1[t : t + 1, :]).astype(BF)

    for copy in loads:
        copy.wait()

    def project(weight):
        value = dot(an[0], weight[0:col, :])
        for t in range(1, blocks):
            value = value + dot(an[t], weight[t * col : (t + 1) * col, :])
        return value

    q_out[...] = project(wq)
    k_out[...] = project(wk)
    vh_out[...] = project(wv).astype(BF)
    head = q_gain.shape[1]
    scale = 1.0 / math.sqrt(head)
    for h in range(col // head):
        lanes = slice(h * head, (h + 1) * head)
        for raw, gain, rotated in ((q_out, q_gain, qh_out), (k_out, k_gain, kh_out)):
            value = raw[:, lanes]
            value = value * inverse_rms(row_sum(value * value), head) * gain[...]
            rotated[:, lanes] = turn(value, cos_rows[...], sin_rows[...]).astype(BF)
        probs = softmax_rows(qh_out[:, lanes], kh_out[:, lanes], bias[...], scale).astype(BF)
        ob_out[:, lanes] = dot(probs, vh_out[:, lanes]).astype(BF)
    for t in range(blocks):
        parts[t] = dot(ob_out[...], wo[:, t * col : (t + 1) * col]).astype(BF)
    ready()
    first = scatter_start(post, parts, halves, me)
    moved = scatter_relay(post, parts, halves, box, me, first)
    total[me] = scatter_total(parts, box, me, moved).astype(BF)
    arrive(gather_relay(post, total, me, gather_start(post, total, me)))
    square = jnp.zeros((tok, 1), F32)
    for t in range(blocks):
        value = x_all[t].astype(F32) + total[t].astype(F32)
        resid_out[t] = value
        square = square + row_sum(value * value)
    r2 = inverse_rms(square, width)
    logits = jnp.zeros((router_t.shape[0], tok), F32)
    for t in range(blocks):
        mixed_out[t] = (resid_out[t] * r2 * gain2[t : t + 1, :]).astype(BF)
        logits = logits + dot(router_t[:, t * col : (t + 1) * col], mixed_out[t], 1, 1)
    expert = lax.broadcasted_iota(jnp.int32, logits.shape, 0)
    top = routes.shape[0]
    chosen = [
        jnp.sum(jnp.where(routes[k : k + 1, :] == expert, logits, 0.0), axis=0, keepdims=True)
        for k in range(top)
    ]
    peak = functools.reduce(jnp.maximum, chosen)
    grown = [jnp.exp(value - peak) for value in chosen]
    whole = functools.reduce(jnp.add, grown)
    slots = send_out.shape[0]
    slot = lax.broadcasted_iota(jnp.int32, (slots, tok), 0)
    pick = jnp.zeros((slots, tok), F32)
    weight = jnp.zeros((slots, tok), F32)
    for k in range(top):
        gate = grown[k] / whole
        gates_out[k : k + 1, :] = gate
        hot = slot_of[k : k + 1, :] == slot
        pick = jnp.where(hot, 1.0, pick)
        weight = jnp.where(hot, gate * keep[k : k + 1, :], weight)
    pick_out[...] = pick.T.astype(BF)
    pick = pick.astype(BF)
    for t in range(blocks):
        send_out[:, t * col : (t + 1) * col] = dot(pick, mixed_out[t]).astype(BF)
    gate = row_sum(weight)
    first = gate.astype(BF)
    second = (gate - first.astype(F32)).astype(BF)
    third = (gate - first.astype(F32) - second.astype(F32)).astype(BF)
    lane = lax.broadcasted_iota(jnp.int32, (slots, 128), 1)
    facts = jnp.zeros((slots, 128), F32)
    for n, piece in enumerate((first, second, third)):
        facts = jnp.where(lane == n, piece.astype(F32), facts)
    send_out[:, width:] = facts.astype(BF)
    post.finish()


def front_call(x_all, bias, cos_rows, sin_rows, gain1, gain2, q_gain, k_gain, router_t, routes,
               slot_of, keep, weights, slots):
    blocks, tok, col = tiles = x_all.shape
    width = col * blocks
    shape = jax.ShapeDtypeStruct
    vmem = pl.BlockSpec(memory_space=pltpu.VMEM)
    top = routes.shape[0]
    return pl.pallas_call(
        front_kernel,
        out_shape=(
            shape(tiles, F32), shape(tiles, BF), shape((tok, col), F32), shape((tok, col), F32),
            shape((tok, col), BF), shape((tok, col), BF), shape((tok, col), BF),
            shape((tok, col), BF), shape((top, tok), F32), shape((slots, width + 128), BF),
            shape((tok, slots), BF),
        ),
        in_specs=[vmem] * 12 + [pl.BlockSpec(memory_space=pl.ANY)] * 4,
        out_specs=(vmem,) * 11,
        scratch_shapes=[
            pltpu.VMEM((width, col), BF), pltpu.VMEM((width, col), BF), pltpu.VMEM((width, col), BF),
            pltpu.VMEM((col, width), BF),
            pltpu.VMEM(tiles, BF), pltpu.VMEM(tiles, BF),
            pltpu.VMEM((2, tok // 2, col), BF), pltpu.VMEM((2, tok, col), BF), pltpu.VMEM(tiles, BF),
            pltpu.SemaphoreType.DMA((4,)),
            pltpu.SemaphoreType.DMA((8,)), pltpu.SemaphoreType.DMA((8,)),
        ],
        compiler_params=pltpu.CompilerParams(
            collective_id=1, has_side_effects=True, vmem_limit_bytes=56 * 1024 * 1024
        ),
        cost_estimate=SHADOW,
        name="front",
    )(x_all, bias, cos_rows, sin_rows, gain1, gain2, q_gain, k_gain, router_t, routes, slot_of,
      keep, *weights)


def back_kernel(
    pick_t, ret, slot_of, keep, gates, routes, bias, cos_rows, sin_rows, gain2,
    q_gain, k_gain, router, resid, dy_all, mixed, qh, kh, vh,
    q_hbm, k_hbm, wo_hbm,
    d_qkv, dr, d_mine, router_out, small_out,
    q_raw, k_raw, wo, parts, halves, box, total, dm, d_att, dg_mine, dg_box,
    load_sem, send_sem, recv_sem,
):
    me, peers = tensor_peers()
    ready = greet("tensor", peers)
    loads = fetch([(wo_hbm, wo), (q_hbm, q_raw), (k_hbm, k_raw)], load_sem)
    blocks, tok, col = parts.shape
    width = blocks * col
    post = Post("tensor", send_sem, recv_sem)
    for t in range(blocks):
        parts[t] = dot(pick_t[...], ret[:, t * col : (t + 1) * col]).astype(BF)
    ready()
    first = scatter_start(post, parts, halves, me)
    top = routes.shape[0]
    dgate = row_sum(ret[:, width:].astype(F32))
    slot = lax.broadcasted_iota(jnp.int32, (ret.shape[0], tok), 0)
    for k in range(top):
        hot = slot_of[k : k + 1, :] == slot
        dg_mine[k : k + 1, :] = jnp.sum(jnp.where(hot, dgate, 0.0), axis=0, keepdims=True)
    dg_in = [post.push(dg_mine, dg_box.at[d], peer) for d, peer in enumerate(peers)]
    moved = scatter_relay(post, parts, halves, box, me, first)
    total[me] = scatter_total(parts, box, me, moved).astype(BF)
    total_first = gather_start(post, total, me)

    arrive(dg_in)
    d_gates = dg_mine[...]
    for d in range(blocks - 1):
        d_gates = d_gates + dg_box[d]
    d_gates = d_gates * keep[...]
    gate = gates[...]
    d_chosen = gate * (d_gates - jnp.sum(gate * d_gates, axis=0, keepdims=True))
    expert = lax.broadcasted_iota(jnp.int32, (router.shape[1], tok), 0)
    d_logits_t = jnp.zeros(expert.shape, F32)
    for k in range(top):
        hot = routes[k : k + 1, :] == expert
        d_logits_t = jnp.where(hot, d_chosen[k : k + 1, :], d_logits_t)
    d_logits = d_logits_t.T.astype(BF)
    square = jnp.zeros((tok, 1), F32)
    for t in range(blocks):
        rows = slice(t * col, (t + 1) * col)
        dm[t] = dot(d_logits, router[rows, :], 1, 1)
        square = square + row_sum(resid[t] * resid[t])
    r2 = inverse_rms(square, width)
    total_moved = gather_relay(post, total, me, total_first)
    for t in range(blocks):
        rows = slice(t * col, (t + 1) * col)
        router_out[rows, :] = dot(mixed[t].T, d_logits).astype(BF)
    arrive(total_moved)
    cross = jnp.zeros((tok, 1), F32)
    for t in range(blocks):
        dm[t] = dm[t] + total[t].astype(F32)
        cross = cross + row_sum(resid[t] * gain2[t : t + 1, :] * dm[t])
    cross = cross * (1.0 / width) * r2 * r2 * r2
    small_out[...] = jnp.zeros_like(small_out)
    for t in range(blocks):
        d_mixed = dm[t]
        small_out[t : t + 1, :] = jnp.sum(d_mixed * resid[t] * r2, axis=0, keepdims=True)
        d_resid = dy_all[t].astype(F32) + r2 * gain2[t : t + 1, :] * d_mixed - resid[t] * cross
        dm[t] = d_resid
        dr[t] = d_resid.astype(BF)
    d_mine[...] = dm[me]
    for copy in loads:
        copy.wait()
    value = dot(dr[0], wo[:, 0:col], 1, 1)
    for t in range(1, blocks):
        value = value + dot(dr[t], wo[:, t * col : (t + 1) * col], 1, 1)
    d_att[...] = value.astype(BF)

    head = q_gain.shape[1]
    scale = 1.0 / math.sqrt(head)
    q_part = jnp.zeros((1, head), F32)
    k_part = jnp.zeros((1, head), F32)

    def unturn(grown, raw, gain):
        d_unit = grown * cos_rows[...] - pltpu.roll(grown, head // 2, 1) * sin_rows[...]
        inverse = inverse_rms(row_sum(raw * raw), head)
        unit = raw * inverse
        gain_part = jnp.sum(d_unit * unit, axis=0, keepdims=True)
        d_unit = d_unit * gain[...]
        d_raw = inverse * (d_unit - unit * (row_sum(unit * d_unit) * (1.0 / head)))
        return d_raw.astype(BF), gain_part

    for h in range(col // head):
        lanes = slice(h * head, (h + 1) * head)
        probs = softmax_rows(qh[:, lanes], kh[:, lanes], bias[...], scale)
        d_head = d_att[:, lanes]
        d_probs = dot(d_head, vh[:, lanes], 1, 1)
        d_scores = probs * (d_probs - row_sum(probs * d_probs))
        d_qkv[:, 2 * col + h * head : 2 * col + (h + 1) * head] = dot(
            probs.T.astype(BF), d_head
        ).astype(BF)
        d_q, part = unturn(dot(d_scores.astype(BF), kh[:, lanes]) * scale, q_raw[:, lanes], q_gain)
        q_part = q_part + part
        d_qkv[:, lanes] = d_q
        d_k, part = unturn(dot(d_scores.T.astype(BF), qh[:, lanes]) * scale, k_raw[:, lanes], k_gain)
        k_part = k_part + part
        d_qkv[:, col + h * head : col + (h + 1) * head] = d_k
    small_out[blocks : blocks + 1, :head] = q_part
    small_out[blocks : blocks + 1, head : 2 * head] = k_part
    post.finish()


def back_call(pick_t, ret, slot_of, keep, gates, routes, bias, cos_rows, sin_rows,
              gain2, q_gain, k_gain, router, resid, dy_all, mixed, qh, kh, vh, q_raw, k_raw, wo):
    blocks, tok, col = dy_all.shape
    width = blocks * col
    tiles = (blocks, tok, col)
    shape = jax.ShapeDtypeStruct
    vmem = pl.BlockSpec(memory_space=pltpu.VMEM)
    top = routes.shape[0]
    count = 8 + blocks - 1
    return pl.pallas_call(
        back_kernel,
        out_shape=(
            shape((tok, 3 * col), BF), shape(tiles, BF), shape((tok, col), F32),
            shape((width, 128), BF), shape((8, col), F32),
        ),
        in_specs=[vmem] * 19 + [pl.BlockSpec(memory_space=pl.ANY)] * 3,
        out_specs=(vmem,) * 5,
        scratch_shapes=[
            pltpu.VMEM((tok, col), F32), pltpu.VMEM((tok, col), F32), pltpu.VMEM((col, width), BF),
            pltpu.VMEM(tiles, BF), pltpu.VMEM((2, tok // 2, col), BF), pltpu.VMEM((2, tok, col), BF),
            pltpu.VMEM(tiles, BF), pltpu.VMEM(tiles, F32), pltpu.VMEM((tok, col), BF),
            pltpu.VMEM((top, tok), F32), pltpu.VMEM((blocks - 1, top, tok), F32),
            pltpu.SemaphoreType.DMA((3,)),
            pltpu.SemaphoreType.DMA((count,)), pltpu.SemaphoreType.DMA((count,)),
        ],
        compiler_params=pltpu.CompilerParams(
            collective_id=2, has_side_effects=True, vmem_limit_bytes=48 * 1024 * 1024
        ),
        cost_estimate=pl.CostEstimate(
            flops=20_000_000_000, bytes_accessed=1, transcendentals=0
        ),
        name="back",
    )(pick_t, ret, slot_of, keep, gates, routes, bias, cos_rows, sin_rows, gain2,
      q_gain, k_gain, router, resid, dy_all, mixed, qh, kh, vh, q_raw, k_raw, wo)


def octet():
    me = lax.axis_index("expert")
    core = me % 2
    return me - core, core, lax.axis_index("tensor")


def octet_others(base, core, rank):
    count = lax.axis_size("tensor")
    others = [{"expert": base + core, "tensor": (rank + d) % count} for d in range(1, count)]
    return others + [
        {"expert": base + 1 - core, "tensor": (rank + d) % count} for d in range(count)
    ]


def meet(others):
    barrier = pltpu.get_barrier_semaphore()
    for other in others:
        pl.semaphore_signal(barrier, inc=1, device_id=other, device_id_type=MESH)
    return lambda: pl.semaphore_wait(barrier, len(others))


def remote(source, target, send_sem, recv_sem, device):
    return pltpu.make_async_remote_copy(
        src_ref=source, dst_ref=target, send_sem=send_sem, recv_sem=recv_sem, device_id=device,
        device_id_type=MESH,
    )


def weights_kernel(
    w, first, out, near, own, load_sem, near_sem, send_sem, recv_sem, pass_send, pass_recv
):
    base, core, rank = octet()
    ready = meet(octet_others(base, core, rank))
    ranks = out.shape[0]
    half = out.shape[2] // 2
    sibling = {"expert": base + 1 - core, "tensor": rank}
    side = rank % 2
    target = 2 * core + side
    own_chip = target == rank

    def part(ref, index, which):
        return ref.at[index, :, pl.ds(which * half, half), :]

    mine = 1 - (rank // 2 + core) % 2
    loads = fetch([(first, near)], load_sem)
    own_loads, own_stores = [], []
    for k in range(2):
        own_loads.append(pltpu.make_async_copy(part(w, side, k), own.at[k], load_sem.at[2 + k]))
        own_stores.append(pltpu.make_async_copy(own.at[k], part(out, rank, k), near_sem.at[2 + k]))
        pl.when(own_chip)(own_loads[k].start)
    ready()
    sends = []
    for k in range(2):
        device = {"expert": base + mine * (1 - core) + (1 - mine) * k, "tensor": target}
        arrives = recv_sem.at[1 - mine, mine * k]
        sends.append(remote(part(w, side, k), part(out, rank, k), send_sem.at[k], arrives, device))
        sends[k].start()
    other = 1 - side
    beside = 2 * core + other
    to_core = 1 - ((beside - rank) % ranks - 1) // 2
    sends.append(
        remote(
            part(w, other, to_core), part(out, rank, to_core), send_sem.at[2], recv_sem.at[1, 1],
            {"expert": base + to_core, "tensor": beside},
        )
    )
    sends[2].start()
    come, coming = 3 - 2 * core, 1 + 2 * core
    place = part(out, (rank + come) % ranks, core)
    loads[0].wait()
    passed = [remote(near, place, pass_send.at[come], pass_recv.at[come], sibling)]
    passed[0].start()
    stores = [pltpu.make_async_copy(near, place, near_sem.at[0])]
    stores[0].start()

    @pl.when(own_chip)
    def _():
        for k in range(2):
            own_loads[k].wait()
            own_stores[k].start()

    place = part(out, (rank + coming) % ranks, core)
    remote(place, place, send_sem.at[2], recv_sem.at[1, 1], sibling).wait_recv()
    passed.append(remote(place, place, pass_send.at[coming], pass_recv.at[coming], sibling))
    passed[-1].start()
    far = part(out, (rank + 2) % ranks, core)
    remote(far, far, send_sem.at[0], recv_sem.at[1, 0], sibling).wait_recv()
    passed.append(remote(far, far, pass_send.at[2], pass_recv.at[2], sibling))
    passed[-1].start()
    for k in range(2):
        theirs = part(out, rank, k)
        arrival = remote(theirs, theirs, send_sem.at[k], recv_sem.at[0, k], sibling)
        pl.when(jnp.logical_not(own_chip))(arrival.wait_recv)
        pl.when(own_chip)(own_stores[k].wait)
    for d in range(1, ranks):
        theirs = part(out, (rank + d) % ranks, 1 - core)
        remote(theirs, theirs, pass_send.at[d], pass_recv.at[d], sibling).wait_recv()
    for copy in passed + sends:
        copy.wait_send()
    for copy in stores:
        copy.wait()


def weights_call(w, first):
    _, three, width, hidden = w.shape
    hbm = pl.BlockSpec(memory_space=pl.ANY)
    sems = pltpu.SemaphoreType.DMA((4,))
    halves = pltpu.VMEM((2, three, width // 2, hidden), BF)
    return pl.pallas_call(
        weights_kernel,
        out_shape=jax.ShapeDtypeStruct((4, three, width, hidden), BF),
        in_specs=[hbm] * 2,
        out_specs=hbm,
        scratch_shapes=[
            pltpu.VMEM((three, width // 2, hidden), BF), halves, sems, sems,
            pltpu.SemaphoreType.DMA((3,)),
            pltpu.SemaphoreType.DMA((2, 2)), sems, sems,
        ],
        compiler_params=pltpu.CompilerParams(
            collective_id=4, has_side_effects=True, vmem_limit_bytes=60 * 1024 * 1024
        ),
        cost_estimate=SHADOW,
        name="weights",
    )(w, first)


def near_weights(w):
    ranks, places = lax.axis_size("tensor"), lax.axis_size("expert")
    half = w.shape[2] // 2
    core, rank = lax.axis_index("expert") % 2, lax.axis_index("tensor")
    side = 1 - rank % 2
    leftward = jnp.where(2 * core + side == (rank + 1) % ranks, 0, 1)
    piece = lax.dynamic_slice(w, (side, 0, leftward * half, 0), (1, w.shape[1], half, w.shape[3]))
    pairs = []
    for place in range(places):
        for t in range(ranks):
            target = 2 * (place % 2) + 1 - t % 2
            to_core = 0 if target == (t + 1) % ranks else 1
            pairs.append((place * ranks + t, (place - place % 2 + to_core) * ranks + target))
    return lax.ppermute(piece[0], ("expert", "tensor"), pairs)


def home_kernel(grads, out, far_out, own, got, load_sem, local_sem, swap_send, swap_recv, send_sem, recv_sem):
    base, core, rank = octet()
    ready = meet(octet_others(base, core, rank))
    ranks, three, half, hidden = own.shape
    sibling = {"expert": base + 1 - core, "tensor": rank}
    order = (1, 3, 0, 2)
    loads, swaps = [], []
    for d in order:
        quarter = (rank + d) % ranks
        source = grads.at[quarter, :, pl.ds(core * half, half), :]
        loads.append(pltpu.make_async_copy(source, own.at[d], load_sem.at[d]))
        loads[-1].start()
    ready()
    for d in order:
        quarter = (rank + d) % ranks
        source = grads.at[quarter, :, pl.ds((1 - core) * half, half), :]
        swaps.append(remote(source, got.at[d], swap_send.at[d], swap_recv.at[d], sibling))
        swaps[-1].start()
    owner = rank // 2
    side = rank - 2 * owner
    rows = 64
    place = out.at[side, :, pl.ds(core * half, half), :]
    stays = owner == core
    sends = []
    for n, d in enumerate(order):
        loads[n].wait()
        swaps[n].wait_recv()

        def one(i, _, d=d):
            c, at = i // (half // rows), i % (half // rows) * rows
            here = pl.ds(pl.multiple_of(at, rows), rows)
            value = own[d, c, here, :].astype(F32) + got[d, c, here, :].astype(F32)
            own[d, c, here, :] = value.astype(BF)
            return 0

        lax.fori_loop(0, three * (half // rows), one, 0)
        if d == 2:
            far = pltpu.make_async_copy(own.at[d], far_out, load_sem.at[d])
            far.start()
            continue
        away = remote(
            own.at[d], place, send_sem.at[d], recv_sem.at[2 * side + core],
            {"expert": base + owner, "tensor": (rank + d) % ranks},
        )
        if d:
            away.start()
        else:
            kept = pltpu.make_async_copy(own.at[d], place, local_sem)
            pl.when(stays)(kept.start)
            pl.when(jnp.logical_not(stays))(away.start)
        sends.append((d, away))
    for s in range(2):
        for k in range(2):
            off = (2 * core + s - rank) % ranks
            mine = out.at[s, :, pl.ds(k * half, half), :]
            arrival = remote(own.at[0], mine, send_sem.at[0], recv_sem.at[2 * s + k], sibling)
            own_chip = off == 0
            comes = (off != 2) & jnp.logical_not(own_chip & (core == k))
            pl.when(comes)(arrival.wait_recv)
    pl.when(stays)(kept.wait)
    for d, away in sends:
        if d:
            away.wait_send()
        else:
            pl.when(jnp.logical_not(stays))(away.wait_send)
    for swap in swaps:
        swap.wait_send()
    far.wait()


def home_call(grads):
    ranks, three, width, hidden = grads.shape
    hbm = pl.BlockSpec(memory_space=pl.ANY)
    sems = pltpu.SemaphoreType.DMA((4,))
    halves = pltpu.VMEM((ranks, three, width // 2, hidden), BF)
    shape = jax.ShapeDtypeStruct
    return pl.pallas_call(
        home_kernel,
        out_shape=(
            shape((2, three, width, hidden), BF), shape((three, width // 2, hidden), BF),
        ),
        in_specs=[hbm],
        out_specs=(hbm, hbm),
        scratch_shapes=[
            halves, halves, sems, pltpu.SemaphoreType.DMA, sems, sems, sems, sems,
        ],
        compiler_params=pltpu.CompilerParams(
            collective_id=5, has_side_effects=True, vmem_limit_bytes=60 * 1024 * 1024
        ),
        cost_estimate=SHADOW,
        name="home",
    )(grads)


def expert_kernel(rows_ref, dys, w_ref, y_ref, dx_ref, grad_ref, rows_t, dys_t, y_acc, dx_acc, gate_of, dgate):
    step = pl.program_id(0)
    width = y_acc.shape[1]
    rows = rows_ref.at[:, :width]

    @pl.when(step == 0)
    def _():
        gate_of[...] = row_sum(rows_ref[:, width:].astype(F32))
        rows_t[...] = rows[...].T
        dys_t[...] = (dys[...].astype(F32) * gate_of[...]).astype(BF).T
        dgate[...] = jnp.zeros_like(dgate)
        y_acc[...] = jnp.zeros_like(y_acc)
        dx_acc[...] = jnp.zeros_like(dx_acc)

    w_gate, w_up, w_down = w_ref[0, 0], w_ref[0, 1], w_ref[0, 2]
    gate = dot(rows[...], w_gate)
    up = dot(rows[...], w_up)
    d_raw = dot(dys[...], w_down)
    d_act = d_raw * gate_of[...]
    sig = 1.0 / (1.0 + jnp.exp(-gate))
    silu = gate * sig
    act = (silu * up).astype(BF)
    dgate[...] += row_sum(act.astype(F32) * d_raw)
    d_gate = (d_act * up * sig * (1.0 + gate * (1.0 - sig))).astype(BF)
    d_up = (d_act * silu).astype(BF)
    y_acc[...] += dot(act, w_down, 1, 1)
    dx_acc[...] += dot(d_gate, w_gate, 1, 1) + dot(d_up, w_up, 1, 1)
    grad_ref[0, 0] = dot(rows_t[...], d_gate).astype(BF)
    grad_ref[0, 1] = dot(rows_t[...], d_up).astype(BF)
    grad_ref[0, 2] = dot(dys_t[...], act).astype(BF)

    @pl.when(step == pl.num_programs(0) - 1)
    def _():
        first = dgate[...].astype(BF).astype(F32)
        lane = lax.broadcasted_iota(jnp.int32, (y_ref.shape[0], 128), 1)
        facts = jnp.where(lane == 0, first, jnp.where(lane == 1, dgate[...] - first, 0.0))
        y_ref[...] = (y_acc[...] * gate_of[...]).astype(BF)
        dx_ref[:, :width] = dx_acc[...].astype(BF)
        dx_ref[:, width:] = facts.astype(BF)


def expert_call(rows, dys, weights):
    quarters, _, width, hidden = weights.shape
    count = rows.shape[0]
    shape = jax.ShapeDtypeStruct

    def whole(value):
        return pl.BlockSpec(value.shape, lambda q: (0, 0), pipeline_mode=pl.Buffered(1))

    block = pl.BlockSpec((1, 3, width, hidden), lambda q: (q, 0, 0, 0))
    outs = [shape((count, width), BF), shape((count, width + 128), BF)]
    return pl.pallas_call(
        expert_kernel,
        grid=(quarters,),
        out_shape=tuple(outs) + (shape(weights.shape, BF),),
        in_specs=[whole(rows), whole(dys), block],
        out_specs=tuple(whole(value) for value in outs) + (block,),
        scratch_shapes=[
            pltpu.VMEM((width, count), BF),
            pltpu.VMEM((width, count), BF),
            pltpu.VMEM((count, width), F32),
            pltpu.VMEM((count, width), F32),
            pltpu.VMEM((count, 1), F32),
            pltpu.VMEM((count, 1), F32),
        ],
        compiler_params=pltpu.CompilerParams(vmem_limit_bytes=62 * 1024 * 1024),
        cost_estimate=COST,
        name="expert",
    )(rows, dys, weights)


def plane():
    me = lax.axis_index("expert")
    core, z, y = me % 2, (me // 2) % 4, me // 8
    return [
        (core, me + 1 - 2 * core),
        ((y + y // 2) % 2, me + 8 * (1 - 2 * (y % 2))),
        (y // 2, me + 8 * (3 - 2 * y)),
        ((z + z // 2) % 2, me + 2 * (1 - 2 * (z % 2))),
        (z // 2, me + 2 * (3 - 2 * z)),
    ]

ORDERS = ((1, 3, 2, 4), (3, 2, 4, 1), (2, 4, 1, 3), (4, 1, 3, 2))

def reduce_kernel(
    d_qkv, dr, d_mine, router_part, small_in, x_all, gain1, ob, pick_y, ret_y,
    far_hbm, resid_hbm, wq_hbm, wk_hbm, wv_hbm,
    q_out, k_out, v_out, router_out, o_out, dx_out, out_out, small_out, far_out,
    wq, wk, wv, resid, parts, y_parts, halves, box_x, note, buf, box, got,
    load_sem, out_sem, x_send, x_recv, send_sem, recv_sem, far_send, far_recv,
):
    me, peers = tensor_peers()
    dims = plane()
    base, core, _ = octet()
    ready = meet(octet_others(base, core, me) + [{"expert": partner} for _, partner in dims[1:]])
    loads = fetch(
        [(wq_hbm, wq), (wk_hbm, wk), (wv_hbm, wv), (resid_hbm.at[me], resid)], load_sem
    )
    blocks, tok, col = x_all.shape
    width = blocks * col
    head = col // blocks
    square = jnp.zeros((tok, 1), F32)
    for t in range(blocks):
        value = x_all[t].astype(F32)
        square = square + row_sum(value * value)
    r1 = inverse_rms(square, width)
    post_x = Post("tensor", x_send, x_recv)
    post = Post("expert", send_sem, recv_sem)
    x_halves, x_box = halves.at[pl.ds(0, 2)], box_x.at[pl.ds(0, 2)]
    y_halves, y_box = halves.at[pl.ds(2, 2)], box_x.at[pl.ds(2, 2)]
    chunks = buf.shape[0] // blocks
    rows_chunk = buf.shape[1]

    def products(t):
        here = pl.ds(t * chunks, chunks)
        normed = (x_all[t].astype(F32) * r1 * gain1[pl.ds(t, 1), :]).T.astype(BF)
        for n in range(3):
            lanes = slice(n * col, (n + 1) * col)
            value = dot(normed, d_qkv[:, lanes]).astype(BF)
            buf[here, :, lanes] = value.reshape(chunks, rows_chunk, col)
        value = dot(dr[t].T, ob[...]).astype(BF)
        buf[here, :, 3 * col : 4 * col] = value.reshape(chunks, rows_chunk, col)
        value = router_part[pl.ds(t * col, col), :]
        buf[here, :, 4 * col :] = value.reshape(chunks, rows_chunk, value.shape[1])

    def add(target, place, first, count):
        def one(i, _):
            total = buf[place + i].astype(F32) + box[first + i].astype(F32)
            target[place + i] = total.astype(BF)
            return 0

        lax.fori_loop(0, count, one, 0)

    half = far_hbm.shape[1]
    owner = me // 2

    def far_copy(n, side, device):
        return remote(
            far_hbm.at[n], far_out.at[n, pl.ds(side * half, half), :],
            far_send.at[n], far_recv.at[n, side], device,
        )

    far_copies = [
        far_copy(n, core, {"expert": base + owner, "tensor": (me + 2) % blocks}) for n in range(3)
    ]
    copies = []
    ready()
    for n in range(2):
        products(2 * (1 - core) + n)
        for s in range(2 * n, 2 * n + 2):
            source = buf.at[pl.ds((1 - core) * 64 + s * 16, 16)]
            copies.append(post.push(source, box.at[pl.ds(31 * s, 16)], dims[0][1]))
    for copy in loads:
        copy.wait()
    for t in range(blocks):
        rows = slice(t * col, (t + 1) * col)
        parts[t] = (
            dot(d_qkv[:, 0:col], wq[rows, :], 1, 1)
            + dot(d_qkv[:, col : 2 * col], wk[rows, :], 1, 1)
            + dot(d_qkv[:, 2 * col : 3 * col], wv[rows, :], 1, 1)
        ).astype(BF)
    x_first = scatter_start(post_x, parts, x_halves, me)
    far_copies[0].start()
    for n in range(2):
        products(2 * core + n)
    x_moved = scatter_relay(post_x, parts, x_halves, x_box, me, x_first)
    far_copies[1].start()
    place = [core * 64 + s * 16 for s in range(4)]
    size, first = 16, 0

    def halve(k):
        for s in range(4):
            copies[s].wait_recv()
            add(buf, place[s], 31 * s + first, size)
            bit, partner = dims[ORDERS[s][k]]
            half = size // 2
            copies[s] = post.push(
                buf.at[pl.ds(place[s] + (1 - bit) * half, half)],
                box.at[pl.ds(31 * s + first + size, half)],
                partner,
            )
            place[s] = place[s] + bit * half

    halve(0)
    first, size = first + size, size // 2

    for t in range(blocks):
        y_parts[t] = dot(pick_y[...], ret_y[:, t * col : (t + 1) * col]).astype(BF)
    y_first = scatter_start(post_x, y_parts, y_halves, me)
    d_an = scatter_total(parts, x_box, me, x_moved)
    x_mine = x_all[me].astype(F32)
    grown = gain1[pl.ds(me, 1), :] * d_an
    mean_part = row_sum(x_mine * grown)
    note[me, 0:8, :] = jnp.broadcast_to(
        jnp.sum(d_an * x_mine * r1, axis=0, keepdims=True), (8, col)
    )
    note[me, 8:16, 0:tok] = jnp.broadcast_to(mean_part, (tok, 128)).T[0:8, :]
    note[me, 8:16, tok:] = jnp.broadcast_to(small_in[blocks : blocks + 1, : 2 * head], (8, 2 * head))
    note_in = [post_x.push(note.at[me], note.at[me], peer) for peer in peers]

    halve(1)
    first, size = first + size, size // 2
    y_moved = scatter_relay(post_x, y_parts, y_halves, y_box, me, y_first)
    far_copies[2].start()
    halve(2)
    first, size = first + size, size // 2
    halve(3)
    first, size = first + size, size // 2
    for s in range(4):
        copies[s].wait_recv()
        add(got, place[s], 31 * s + first, 1)
        here = got.at[pl.ds(place[s], 1)]
        copies[s] = post.push(here, here, dims[ORDERS[s][3]][1])

    arrive(note_in)
    facts = note[0, 8:16, :]
    for t in range(1, blocks):
        facts = facts + note[t, 8:16, :]
    for t in range(blocks):
        small_out[t : t + 1, :] = note[t, 0:1, :]
        small_out[blocks + t : blocks + t + 1, :] = small_in[t : t + 1, :]
    small_out[2 * blocks :, :] = facts
    mean = jnp.broadcast_to(facts[0:1, 0:tok], (128, tok)).T[:, 0:1] * (1.0 / width)
    dx_out[...] = (d_mine[...] + r1 * grown - x_mine * (r1 * r1 * r1 * mean)).astype(BF)

    size = 1
    stores = []

    def keep(n, at):
        here = pl.ds(at, 16)
        outs = (q_out, k_out, v_out, None, router_out)
        for m, target in enumerate(outs):
            lanes = pl.ds(m * col, target.shape[2] if m != 3 else col)
            if m == 3:
                turned = got[here, :, lanes].reshape(16 * rows_chunk, col).T
                o_out[:, pl.ds(pl.multiple_of(at * rows_chunk, 128), 16 * rows_chunk)] = turned
                continue
            stores.append(
                pltpu.make_async_copy(got.at[here, :, lanes], target.at[here], out_sem.at[n, m])
            )
            stores[-1].start()

    for k in range(3, -1, -1):
        for s in range(4):
            copies[s].wait_recv()
            bit, _ = dims[ORDERS[s][k]]
            place[s] = place[s] - bit * size
            partner = dims[ORDERS[s][k - 1]][1] if k else dims[0][1]
            here = got.at[pl.ds(place[s], 2 * size)]
            copies[s] = post.push(here, here, partner)
            if not k:
                keep(s, place[s])
        size *= 2
        if k == 2:
            out_out[...] = (resid[...] + scatter_total(y_parts, y_box, me, y_moved)).astype(BF)
    for s in range(4):
        copies[s].wait_recv()
        keep(4 + s, (1 - core) * 64 + s * 16)
    post.finish()
    post_x.finish()
    for store in stores:
        store.wait()
    comes = (me + 2) % blocks // 2 == core
    for n in range(3):
        for side in range(2):
            pl.when(comes)(far_copy(n, side, {"expert": base + core, "tensor": (me + 2) % blocks}).wait_recv)
        far_copies[n].wait_send()


def reduce_call(d_qkv, dr, d_mine, router_part, small, x_all, gain1, ob, pick_y, ret_y, far, resid,
                weights):
    blocks, tok, col = x_all.shape
    width = blocks * col
    tiles = (blocks, tok, col)
    wide = (128, 16, 4 * col + 128)
    shape = jax.ShapeDtypeStruct
    vmem = pl.BlockSpec(memory_space=pltpu.VMEM)
    hbm = pl.BlockSpec(memory_space=pl.ANY)
    count = 8 + blocks - 1
    return pl.pallas_call(
        reduce_kernel,
        out_shape=(
            shape(wide[:2] + (col,), BF), shape(wide[:2] + (col,), BF), shape(wide[:2] + (col,), BF),
            shape(wide[:2] + (128,), BF), shape((col, width), BF),
            shape((tok, col), BF), shape((tok, col), BF), shape((16, col), F32),
            shape((far.shape[0], 2 * far.shape[1], far.shape[2]), BF),
        ),
        in_specs=[vmem] * 10 + [hbm] * 5,
        out_specs=(hbm,) * 4 + (vmem,) * 4 + (hbm,),
        scratch_shapes=[
            pltpu.VMEM((width, col), BF), pltpu.VMEM((width, col), BF), pltpu.VMEM((width, col), BF),
            pltpu.VMEM((tok, col), F32), pltpu.VMEM(tiles, BF), pltpu.VMEM(tiles, BF),
            pltpu.VMEM((4, tok // 2, col), BF), pltpu.VMEM((4, tok, col), BF),
            pltpu.VMEM((blocks, 16, col), F32),
            pltpu.VMEM(wide, BF), pltpu.VMEM((124,) + wide[1:], BF), pltpu.VMEM(wide, BF),
            pltpu.SemaphoreType.DMA((4,)), pltpu.SemaphoreType.DMA((8, 5)),
            pltpu.SemaphoreType.DMA((count,)), pltpu.SemaphoreType.DMA((count,)),
            pltpu.SemaphoreType.DMA((40,)), pltpu.SemaphoreType.DMA((40,)),
            pltpu.SemaphoreType.DMA((3,)), pltpu.SemaphoreType.DMA((3, 2)),
        ],
        compiler_params=pltpu.CompilerParams(
            collective_id=3, has_side_effects=True, vmem_limit_bytes=60 * 1024 * 1024
        ),
        cost_estimate=COST,
        name="reduce",
    )(d_qkv, dr, d_mine, router_part, small, x_all, gain1, ob, pick_y, ret_y, far, resid, *weights)


def body(
    tokens,
    out_grad,
    seq_lengths,
    dest_index,
    routes,
    pair_order,
    norm1_gain,
    w_query,
    w_key,
    w_value,
    q_gain,
    k_gain,
    w_output,
    norm2_gain,
    w_router,
    expert_w,
):
    groups = lax.axis_size("expert")
    tensor_count = lax.axis_size("tensor")
    group_id = lax.axis_index("expert")
    tensor_id = lax.axis_index("tensor")
    tok_count, col_count = tokens.shape
    width = col_count * tensor_count
    move_rows = tok_count // groups
    expert_count = w_router.shape[1]
    top_count = routes.shape[1]
    local_experts = expert_w.shape[0]

    w_stored = jnp.transpose(expert_w, (0, 2, 1, 3))
    w_near = near_weights(w_stored)

    routes_t = routes.T
    order_t = pair_order[0].reshape(tok_count, top_count).T
    pair_expert = routes_t.reshape(-1)
    pair_total = tok_count * top_count
    base = pair_expert * pair_total
    keyed = base + order_t.reshape(-1)
    before = (keyed[None, :] < keyed[:, None]) & (keyed[None, :] >= base[:, None])
    ranks = jnp.sum(before.astype(jnp.int32), axis=1).reshape(top_count, tok_count)
    expert_axis = jnp.arange(expert_count, dtype=jnp.int32)
    route_hot = routes_t[:, None, :] == expert_axis[None, :, None]
    counts = jnp.sum(route_hot.astype(F32), axis=(0, 2))

    places = jnp.arange(tok_count, dtype=jnp.int32)
    arrival_rank = jnp.sum((dest_index[None, :] < dest_index[:, None]).astype(jnp.int32), axis=1)
    by_rank = (arrival_rank[None, :] == places[:, None]).astype(BF)
    inner = jnp.broadcast_to((dest_index % tok_count).astype(BF)[:, None], (tok_count, 64))
    facts = jnp.broadcast_to(counts.astype(BF)[None, :], (tok_count, expert_count))
    outgoing = dot(by_rank, jnp.concatenate([tokens, out_grad, inner, facts], axis=1)).astype(BF)
    got = exchange(outgoing.reshape(groups, move_rows, -1), "expert")
    all_counts = got[:, 0, 2 * col_count + 64 :].astype(jnp.int32)
    lower = jnp.arange(groups, dtype=jnp.int32) < group_id
    offsets = jnp.sum(jnp.where(lower[:, None], all_counts, 0), axis=0)
    mine = got[:, :, 2 * col_count].astype(jnp.int32).reshape(-1)
    put = (mine[None, :] == places[:, None]).astype(BF)
    local = dot(put, got.reshape(tok_count, -1)[:, : 2 * col_count]).astype(BF)
    capacity = 5 * tok_count * groups * top_count // (4 * expert_count)
    most_rows = 3 * tok_count * top_count // (2 * expert_count)
    per = most_rows // 2
    slots = groups * per
    slot_global = jnp.sum(jnp.where(route_hot, offsets[None, :, None], 0), axis=1) + ranks
    kept = slot_global < capacity
    keep_mask = kept.astype(F32)
    here = kept & (routes_t % tensor_count == tensor_id)
    owner = routes_t // tensor_count * 2 + ranks % 2
    slot_of = jnp.where(here, owner * per + ranks // 2, -1)

    seq_ids, positions = sequence_layout(seq_lengths[0], tok_count)
    bias = jnp.where(seq_ids[:, None] == seq_ids[None, :], 0.0, mask_fill)
    cos_tab, sin_tab = rope_tables(positions, q_gain.shape[0])
    cos_rows = jnp.concatenate([cos_tab, cos_tab], axis=1)
    sin_rows = jnp.concatenate([-sin_tab, sin_tab], axis=1)
    gain1 = norm1_gain.astype(F32).reshape(tensor_count, col_count)
    gain2 = norm2_gain.astype(F32).reshape(tensor_count, col_count)
    head_gains = (q_gain.astype(F32)[None], k_gain.astype(F32)[None])
    router = jnp.pad(w_router, ((0, 0), (0, 128 - expert_count)))
    weights = (w_query, w_key, w_value, w_output)
    def homeward(value):
        return exchange(value.reshape(groups, -1, value.shape[1]), "expert").reshape(value.shape)

    x_all, dy_all, send_dy = pre_call(local, slot_of, tensor_count, slots)
    send_dy, x_all = lax.optimization_barrier((send_dy, x_all))
    recv_dy = homeward(send_dy)
    (
        resid, mixed, q_raw, k_raw, qh, kh, vh, attended, gates, send_rows, pick_t,
    ) = front_call(
        x_all, bias, cos_rows, sin_rows, gain1, gain2, *head_gains, router.T, routes_t, slot_of,
        keep_mask, weights, slots,
    )
    send_rows, w_stored, recv_dy = lax.optimization_barrier((send_rows, w_stored, recv_dy))
    recv_rows = homeward(send_rows)
    y_rows, d_rows, partial = expert_call(recv_rows, recv_dy, weights_call(w_stored, w_near))
    ret_rows = homeward(d_rows)
    near, far = home_call(partial)
    ret_rows, near, far, y_rows = lax.optimization_barrier((ret_rows, near, far, y_rows))
    ret_y = homeward(y_rows)
    d_qkv, dr, d_mine, router_part, small = back_call(
        pick_t, ret_rows, slot_of, keep_mask, gates, routes_t, bias, cos_rows,
        sin_rows, gain2, *head_gains, router, resid, dy_all, mixed, qh, kh, vh, q_raw, k_raw,
        w_output,
    )
    *wide, router_sum, out_proj, dx_slice, out_slice, small, far = reduce_call(
        d_qkv, dr, d_mine, router_part, small, x_all, gain1, attended, pick_t, ret_y, far, resid,
        weights[:3],
    )

    going = dot(put, jnp.concatenate([out_slice, dx_slice], axis=1), 0, 0).astype(BF)
    small = small[:9].astype(BF).reshape(move_rows, -1)
    small = jnp.pad(small, ((0, 0), (0, -small.shape[1] % 128)))
    small = jnp.broadcast_to(small[None], (groups,) + small.shape)
    back = exchange(jnp.concatenate([going.reshape(groups, move_rows, -1), small], axis=2), "expert")
    small = jnp.sum(back[:, :, 2 * col_count :].astype(F32), axis=0)[:, : 9 * col_count // move_rows]
    small = small.reshape(-1)
    back = dot(by_rank, back.reshape(tok_count, -1)[:, : 2 * col_count], 0, 0).astype(BF)
    opposite = (tensor_id + 2) % tensor_count - 2 * (group_id % 2)
    is_far = jnp.arange(local_experts) == opposite
    expert_grad = jnp.where(is_far[:, None, None, None], far[None], near).astype(F32)
    expert_grad = jnp.transpose(expert_grad, (0, 2, 1, 3))
    wide = [value.reshape(width, -1) for value in wide]
    gain_at = 2 * width + tok_count
    head = q_gain.shape[0]
    return (
        back[:, :col_count],
        back[:, col_count:],
        small[:width],
        wide[0].astype(F32),
        wide[1].astype(F32),
        wide[2].astype(F32),
        small[gain_at : gain_at + head],
        small[gain_at + head : gain_at + 2 * head],
        out_proj.astype(F32),
        small[width : 2 * width],
        router_sum.reshape(width, -1)[:, :expert_count].astype(F32),
        expert_grad,
    )


def solution(mesh):
    in_specs = (
        P("expert", "tensor"),
        P("expert", "tensor"),
        P("expert", None),
        P("expert"),
        P("expert", None),
        P("expert", None),
        P(),
        P(None, "tensor"),
        P(None, "tensor"),
        P(None, "tensor"),
        P(),
        P(),
        P("tensor", None),
        P(),
        P(),
        P("expert", None, None, "tensor"),
    )
    out_specs = (
        P("expert", "tensor"),
        P("expert", "tensor"),
        P(),
        P(None, "tensor"),
        P(None, "tensor"),
        P(None, "tensor"),
        P(),
        P(),
        P("tensor", None),
        P(),
        P(),
        P("expert", None, None, "tensor"),
    )
    return jax.shard_map(body, mesh=mesh, in_specs=in_specs, out_specs=out_specs, check_vma=False)
```

```python
import functools
import math

import jax
import jax.numpy as jnp
from jax import lax
from jax.experimental import pallas as pl
from jax.experimental.pallas import tpu as pltpu
from jax.sharding import PartitionSpec as P

norm_eps = 1e-06
rope_base = 10000.0
mask_fill = -1e30


def rope_tables(positions, width):
    half_width = width // 2
    steps_idx = jnp.arange(half_width, dtype=jnp.float32)
    freqs = jnp.exp(steps_idx * (-2.0 * math.log(rope_base) / width))
    angles = positions.astype(jnp.float32)[:, None] * freqs[None, :]
    return (jnp.cos(angles), jnp.sin(angles))


def sequence_layout(lengths_row, count):
    seq_ends = jnp.cumsum(lengths_row)
    places = jnp.arange(count, dtype=jnp.int32)
    passed = (places[:, None] >= seq_ends[None, :]).astype(jnp.int32)
    seq_ids = jnp.sum(passed, axis=1)
    starts = jnp.sum(passed * lengths_row[None, :], axis=1)
    return (seq_ids, places - starts)


BF = jnp.bfloat16
F32 = jnp.float32
SHADOW = pl.CostEstimate(flops=40_000_000_000, bytes_accessed=1, transcendentals=0)
COST = pl.CostEstimate(flops=1, bytes_accessed=1, transcendentals=0)


def dot(left, right, left_dim=1, right_dim=0):
    return lax.dot_general(
        left, right, (((left_dim,), (right_dim,)), ((), ())), preferred_element_type=F32
    )


def exchange(value, axis):
    return lax.all_to_all(value, axis, split_axis=0, concat_axis=0, tiled=True)


def gather_blocks(value, axis):
    return exchange(jnp.broadcast_to(value[None], (lax.axis_size(axis),) + value.shape), axis)


def column_blocks(value, count):
    return jnp.stack(jnp.split(value, count, axis=1))


MESH = pl.DeviceIdType.MESH


def tensor_peers():
    me = lax.axis_index("tensor")
    count = lax.axis_size("tensor")
    return me, [(me + d) % count for d in range(1, count)]


def greet(axis, peers):
    barrier = pltpu.get_barrier_semaphore()
    for peer in peers:
        pl.semaphore_signal(barrier, inc=1, device_id={axis: peer}, device_id_type=MESH)
    return lambda: pl.semaphore_wait(barrier, len(peers))


class Post:
    def __init__(self, axis, send_sem, recv_sem):
        self.axis, self.send_sem, self.recv_sem = axis, send_sem, recv_sem
        self.started = []
        self.used = 0

    def push(self, source, target, peer):
        slot = self.used
        self.used += 1
        copy = pltpu.make_async_remote_copy(
            src_ref=source,
            dst_ref=target,
            send_sem=self.send_sem.at[slot],
            recv_sem=self.recv_sem.at[slot],
            device_id={self.axis: peer},
            device_id_type=MESH,
        )
        copy.start()
        self.started.append(copy)
        return copy

    def finish(self):
        for copy in self.started:
            copy.wait_send()
        self.started = []


def arrive(copies):
    for copy in copies:
        copy.wait_recv()


def ring(me):
    count = lax.axis_size("tensor")
    return (me + 1) % count, (me + count - 1) % count


def gather_start(post, ref, me):
    right, left = ring(me)
    return [post.push(ref.at[me], ref.at[me], peer) for peer in (right, left)]


def gather_relay(post, ref, me, first):
    right, left = ring(me)
    half = ref.shape[1] // 2
    first[0].wait_recv()
    here = ref.at[left, pl.ds(0, half)]
    one = post.push(here, here, right)
    first[1].wait_recv()
    here = ref.at[right, pl.ds(half, half)]
    return [one, post.push(here, here, left)]


def scatter_start(post, parts, halves, me):
    right, left = ring(me)
    far = ring(right)[0]
    half = parts.shape[1] // 2
    return [
        post.push(parts.at[far, pl.ds(0, half)], halves.at[0], right),
        post.push(parts.at[far, pl.ds(half, half)], halves.at[1], left),
    ]


def scatter_relay(post, parts, halves, box, me, first):
    right, left = ring(me)
    half = parts.shape[1] // 2
    copies = []
    for n, (peer, rows) in enumerate(((right, pl.ds(0, half)), (left, pl.ds(half, half)))):
        first[n].wait_recv()
        parts[peer, rows, :] = (parts[peer, rows, :].astype(F32) + halves[n].astype(F32)).astype(BF)
        copies.append(post.push(parts.at[peer], box.at[n], peer))
    return copies


def scatter_total(parts, box, me, copies):
    arrive(copies)
    return parts[me].astype(F32) + box[0].astype(F32) + box[1].astype(F32)


def fetch(pairs, sem):
    copies = [
        pltpu.make_async_copy(source, target, sem.at[n]) for n, (source, target) in enumerate(pairs)
    ]
    for copy in copies:
        copy.start()
    return copies


def turn(value, cos_rows, sin_rows):
    return value * cos_rows + pltpu.roll(value, value.shape[-1] // 2, 1) * sin_rows


def inverse_rms(total, width):
    return lax.rsqrt(total * (1.0 / width) + norm_eps)


def row_sum(value):
    return jnp.sum(value, axis=1, keepdims=True)


def softmax_rows(query, key, bias, scale):
    scores = dot(query, key, 1, 1) * scale + bias
    grown = jnp.exp(scores - jnp.max(scores, axis=1, keepdims=True))
    return grown / row_sum(grown)


def select_slots(slot_of, slots):
    top, tok = slot_of.shape
    slot = lax.broadcasted_iota(jnp.int32, (slots, tok), 0)
    pick = jnp.zeros((slots, tok), F32)
    for k in range(top):
        pick = jnp.where(slot_of[k : k + 1, :] == slot, 1.0, pick)
    return pick


def pre_kernel(local, slot_of, x_out, dy_out, send_out, x_all, dy_all, send_sem, recv_sem):
    me = lax.axis_index("tensor")
    ready = greet("tensor", ring(me))
    blocks, _, col = x_all.shape
    x_all[me] = local[:, :col]
    dy_all[me] = local[:, col:]
    ready()
    post = Post("tensor", send_sem, recv_sem)
    dy_in = gather_start(post, dy_all, me)
    x_in = gather_start(post, x_all, me)
    pick = select_slots(slot_of, send_out.shape[0]).astype(BF)
    dy_in = gather_relay(post, dy_all, me, dy_in)
    x_in = gather_relay(post, x_all, me, x_in)
    arrive(dy_in)
    dy_out[...] = dy_all[...]
    for t in range(blocks):
        send_out[:, t * col : (t + 1) * col] = dot(pick, dy_all[t]).astype(BF)
    arrive(x_in)
    x_out[...] = x_all[...]
    post.finish()


def pre_call(local, slot_of, blocks, slots):
    tok, both = local.shape
    col = both // 2
    tiles = (blocks, tok, col)
    shape = jax.ShapeDtypeStruct
    vmem = pl.BlockSpec(memory_space=pltpu.VMEM)
    return pl.pallas_call(
        pre_kernel,
        out_shape=(shape(tiles, BF), shape(tiles, BF), shape((slots, col * blocks), BF)),
        in_specs=[vmem] * 2,
        out_specs=(vmem,) * 3,
        scratch_shapes=[
            pltpu.VMEM(tiles, BF), pltpu.VMEM(tiles, BF),
            pltpu.SemaphoreType.DMA((8,)), pltpu.SemaphoreType.DMA((8,)),
        ],
        compiler_params=pltpu.CompilerParams(
            collective_id=6, has_side_effects=True, vmem_limit_bytes=48 * 1024 * 1024
        ),
        cost_estimate=COST,
        name="pre",
    )(local, slot_of)


def front_kernel(
    x_all, bias, cos_rows, sin_rows, gain1, gain2, q_gain, k_gain, router_t, routes, slot_of, keep,
    wq_hbm, wk_hbm, wv_hbm, wo_hbm,
    resid_out, mixed_out, q_out, k_out, qh_out, kh_out, vh_out, ob_out,
    gates_out, send_out, pick_out,
    wq, wk, wv, wo, an, parts, halves, box, total, load_sem, send_sem, recv_sem,
):
    me = lax.axis_index("tensor")
    ready = greet("tensor", ring(me))
    loads = fetch([(wq_hbm, wq), (wk_hbm, wk), (wv_hbm, wv), (wo_hbm, wo)], load_sem)
    blocks, tok, col = x_all.shape
    width = blocks * col
    post = Post("tensor", send_sem, recv_sem)
    square = jnp.zeros((tok, 1), F32)
    for t in range(blocks):
        value = x_all[t].astype(F32)
        square = square + row_sum(value * value)
    r1 = inverse_rms(square, width)
    for t in range(blocks):
        an[t] = (x_all[t].astype(F32) * r1 * gain1[t : t + 1, :]).astype(BF)

    for copy in loads:
        copy.wait()

    def project(weight):
        value = dot(an[0], weight[0:col, :])
        for t in range(1, blocks):
            value = value + dot(an[t], weight[t * col : (t + 1) * col, :])
        return value

    q_out[...] = project(wq)
    k_out[...] = project(wk)
    vh_out[...] = project(wv).astype(BF)
    head = q_gain.shape[1]
    scale = 1.0 / math.sqrt(head)
    for h in range(col // head):
        lanes = slice(h * head, (h + 1) * head)
        for raw, gain, rotated in ((q_out, q_gain, qh_out), (k_out, k_gain, kh_out)):
            value = raw[:, lanes]
            value = value * inverse_rms(row_sum(value * value), head) * gain[...]
            rotated[:, lanes] = turn(value, cos_rows[...], sin_rows[...]).astype(BF)
        probs = softmax_rows(qh_out[:, lanes], kh_out[:, lanes], bias[...], scale).astype(BF)
        ob_out[:, lanes] = dot(probs, vh_out[:, lanes]).astype(BF)
    for t in range(blocks):
        parts[t] = dot(ob_out[...], wo[:, t * col : (t + 1) * col]).astype(BF)
    ready()
    first = scatter_start(post, parts, halves, me)
    moved = scatter_relay(post, parts, halves, box, me, first)
    total[me] = scatter_total(parts, box, me, moved).astype(BF)
    arrive(gather_relay(post, total, me, gather_start(post, total, me)))
    square = jnp.zeros((tok, 1), F32)
    for t in range(blocks):
        value = x_all[t].astype(F32) + total[t].astype(F32)
        resid_out[t] = value
        square = square + row_sum(value * value)
    r2 = inverse_rms(square, width)
    logits = jnp.zeros((router_t.shape[0], tok), F32)
    for t in range(blocks):
        mixed_out[t] = (resid_out[t] * r2 * gain2[t : t + 1, :]).astype(BF)
        logits = logits + dot(router_t[:, t * col : (t + 1) * col], mixed_out[t], 1, 1)
    expert = lax.broadcasted_iota(jnp.int32, logits.shape, 0)
    top = routes.shape[0]
    chosen = [
        jnp.sum(jnp.where(routes[k : k + 1, :] == expert, logits, 0.0), axis=0, keepdims=True)
        for k in range(top)
    ]
    peak = functools.reduce(jnp.maximum, chosen)
    grown = [jnp.exp(value - peak) for value in chosen]
    whole = functools.reduce(jnp.add, grown)
    slots = send_out.shape[0]
    slot = lax.broadcasted_iota(jnp.int32, (slots, tok), 0)
    pick = jnp.zeros((slots, tok), F32)
    weight = jnp.zeros((slots, tok), F32)
    for k in range(top):
        gate = grown[k] / whole
        gates_out[k : k + 1, :] = gate
        hot = slot_of[k : k + 1, :] == slot
        pick = jnp.where(hot, 1.0, pick)
        weight = jnp.where(hot, gate * keep[k : k + 1, :], weight)
    pick_out[...] = pick.T.astype(BF)
    pick = pick.astype(BF)
    for t in range(blocks):
        send_out[:, t * col : (t + 1) * col] = dot(pick, mixed_out[t]).astype(BF)
    gate = row_sum(weight)
    first = gate.astype(BF)
    second = (gate - first.astype(F32)).astype(BF)
    third = (gate - first.astype(F32) - second.astype(F32)).astype(BF)
    lane = lax.broadcasted_iota(jnp.int32, (slots, 128), 1)
    facts = jnp.zeros((slots, 128), F32)
    for n, piece in enumerate((first, second, third)):
        facts = jnp.where(lane == n, piece.astype(F32), facts)
    send_out[:, width:] = facts.astype(BF)
    post.finish()


def front_call(x_all, bias, cos_rows, sin_rows, gain1, gain2, q_gain, k_gain, router_t, routes,
               slot_of, keep, weights, slots):
    blocks, tok, col = tiles = x_all.shape
    width = col * blocks
    shape = jax.ShapeDtypeStruct
    vmem = pl.BlockSpec(memory_space=pltpu.VMEM)
    top = routes.shape[0]
    return pl.pallas_call(
        front_kernel,
        out_shape=(
            shape(tiles, F32), shape(tiles, BF), shape((tok, col), F32), shape((tok, col), F32),
            shape((tok, col), BF), shape((tok, col), BF), shape((tok, col), BF),
            shape((tok, col), BF), shape((top, tok), F32), shape((slots, width + 128), BF),
            shape((tok, slots), BF),
        ),
        in_specs=[vmem] * 12 + [pl.BlockSpec(memory_space=pl.ANY)] * 4,
        out_specs=(vmem,) * 11,
        scratch_shapes=[
            pltpu.VMEM((width, col), BF), pltpu.VMEM((width, col), BF), pltpu.VMEM((width, col), BF),
            pltpu.VMEM((col, width), BF),
            pltpu.VMEM(tiles, BF), pltpu.VMEM(tiles, BF),
            pltpu.VMEM((2, tok // 2, col), BF), pltpu.VMEM((2, tok, col), BF), pltpu.VMEM(tiles, BF),
            pltpu.SemaphoreType.DMA((4,)),
            pltpu.SemaphoreType.DMA((8,)), pltpu.SemaphoreType.DMA((8,)),
        ],
        compiler_params=pltpu.CompilerParams(
            collective_id=1, has_side_effects=True, vmem_limit_bytes=56 * 1024 * 1024
        ),
        cost_estimate=SHADOW,
        name="front",
    )(x_all, bias, cos_rows, sin_rows, gain1, gain2, q_gain, k_gain, router_t, routes, slot_of,
      keep, *weights)


def back_kernel(
    pick_t, ret, slot_of, keep, gates, routes, bias, cos_rows, sin_rows, gain2,
    q_gain, k_gain, router, resid, dy_all, mixed, qh, kh, vh,
    q_hbm, k_hbm, wo_hbm,
    d_qkv, dr, d_mine, router_out, small_out,
    q_raw, k_raw, wo, parts, halves, box, total, dm, d_att, dg_mine, dg_box,
    load_sem, send_sem, recv_sem,
):
    me, peers = tensor_peers()
    ready = greet("tensor", peers)
    loads = fetch([(wo_hbm, wo), (q_hbm, q_raw), (k_hbm, k_raw)], load_sem)
    blocks, tok, col = parts.shape
    width = blocks * col
    post = Post("tensor", send_sem, recv_sem)
    for t in range(blocks):
        parts[t] = dot(pick_t[...], ret[:, t * col : (t + 1) * col]).astype(BF)
    ready()
    first = scatter_start(post, parts, halves, me)
    top = routes.shape[0]
    dgate = row_sum(ret[:, width:].astype(F32))
    slot = lax.broadcasted_iota(jnp.int32, (ret.shape[0], tok), 0)
    for k in range(top):
        hot = slot_of[k : k + 1, :] == slot
        dg_mine[k : k + 1, :] = jnp.sum(jnp.where(hot, dgate, 0.0), axis=0, keepdims=True)
    dg_in = [post.push(dg_mine, dg_box.at[d], peer) for d, peer in enumerate(peers)]
    moved = scatter_relay(post, parts, halves, box, me, first)
    total[me] = scatter_total(parts, box, me, moved).astype(BF)
    total_first = gather_start(post, total, me)

    arrive(dg_in)
    d_gates = dg_mine[...]
    for d in range(blocks - 1):
        d_gates = d_gates + dg_box[d]
    d_gates = d_gates * keep[...]
    gate = gates[...]
    d_chosen = gate * (d_gates - jnp.sum(gate * d_gates, axis=0, keepdims=True))
    expert = lax.broadcasted_iota(jnp.int32, (router.shape[1], tok), 0)
    d_logits_t = jnp.zeros(expert.shape, F32)
    for k in range(top):
        hot = routes[k : k + 1, :] == expert
        d_logits_t = jnp.where(hot, d_chosen[k : k + 1, :], d_logits_t)
    d_logits = d_logits_t.T.astype(BF)
    square = jnp.zeros((tok, 1), F32)
    for t in range(blocks):
        rows = slice(t * col, (t + 1) * col)
        dm[t] = dot(d_logits, router[rows, :], 1, 1)
        square = square + row_sum(resid[t] * resid[t])
    r2 = inverse_rms(square, width)
    total_moved = gather_relay(post, total, me, total_first)
    for t in range(blocks):
        rows = slice(t * col, (t + 1) * col)
        router_out[rows, :] = dot(mixed[t].T, d_logits).astype(BF)
    arrive(total_moved)
    cross = jnp.zeros((tok, 1), F32)
    for t in range(blocks):
        dm[t] = dm[t] + total[t].astype(F32)
        cross = cross + row_sum(resid[t] * gain2[t : t + 1, :] * dm[t])
    cross = cross * (1.0 / width) * r2 * r2 * r2
    small_out[...] = jnp.zeros_like(small_out)
    for t in range(blocks):
        d_mixed = dm[t]
        small_out[t : t + 1, :] = jnp.sum(d_mixed * resid[t] * r2, axis=0, keepdims=True)
        d_resid = dy_all[t].astype(F32) + r2 * gain2[t : t + 1, :] * d_mixed - resid[t] * cross
        dm[t] = d_resid
        dr[t] = d_resid.astype(BF)
    d_mine[...] = dm[me]
    for copy in loads:
        copy.wait()
    value = dot(dr[0], wo[:, 0:col], 1, 1)
    for t in range(1, blocks):
        value = value + dot(dr[t], wo[:, t * col : (t + 1) * col], 1, 1)
    d_att[...] = value.astype(BF)

    head = q_gain.shape[1]
    scale = 1.0 / math.sqrt(head)
    q_part = jnp.zeros((1, head), F32)
    k_part = jnp.zeros((1, head), F32)

    def unturn(grown, raw, gain):
        d_unit = grown * cos_rows[...] - pltpu.roll(grown, head // 2, 1) * sin_rows[...]
        inverse = inverse_rms(row_sum(raw * raw), head)
        unit = raw * inverse
        gain_part = jnp.sum(d_unit * unit, axis=0, keepdims=True)
        d_unit = d_unit * gain[...]
        d_raw = inverse * (d_unit - unit * (row_sum(unit * d_unit) * (1.0 / head)))
        return d_raw.astype(BF), gain_part

    for h in range(col // head):
        lanes = slice(h * head, (h + 1) * head)
        probs = softmax_rows(qh[:, lanes], kh[:, lanes], bias[...], scale)
        d_head = d_att[:, lanes]
        d_probs = dot(d_head, vh[:, lanes], 1, 1)
        d_scores = probs * (d_probs - row_sum(probs * d_probs))
        d_qkv[:, 2 * col + h * head : 2 * col + (h + 1) * head] = dot(
            probs.T.astype(BF), d_head
        ).astype(BF)
        d_q, part = unturn(dot(d_scores.astype(BF), kh[:, lanes]) * scale, q_raw[:, lanes], q_gain)
        q_part = q_part + part
        d_qkv[:, lanes] = d_q
        d_k, part = unturn(dot(d_scores.T.astype(BF), qh[:, lanes]) * scale, k_raw[:, lanes], k_gain)
        k_part = k_part + part
        d_qkv[:, col + h * head : col + (h + 1) * head] = d_k
    small_out[blocks : blocks + 1, :head] = q_part
    small_out[blocks : blocks + 1, head : 2 * head] = k_part
    post.finish()


def back_call(pick_t, ret, slot_of, keep, gates, routes, bias, cos_rows, sin_rows,
              gain2, q_gain, k_gain, router, resid, dy_all, mixed, qh, kh, vh, q_raw, k_raw, wo):
    blocks, tok, col = dy_all.shape
    width = blocks * col
    tiles = (blocks, tok, col)
    shape = jax.ShapeDtypeStruct
    vmem = pl.BlockSpec(memory_space=pltpu.VMEM)
    top = routes.shape[0]
    count = 8 + blocks - 1
    return pl.pallas_call(
        back_kernel,
        out_shape=(
            shape((tok, 3 * col), BF), shape(tiles, BF), shape((tok, col), F32),
            shape((width, 128), BF), shape((8, col), F32),
        ),
        in_specs=[vmem] * 19 + [pl.BlockSpec(memory_space=pl.ANY)] * 3,
        out_specs=(vmem,) * 5,
        scratch_shapes=[
            pltpu.VMEM((tok, col), F32), pltpu.VMEM((tok, col), F32), pltpu.VMEM((col, width), BF),
            pltpu.VMEM(tiles, BF), pltpu.VMEM((2, tok // 2, col), BF), pltpu.VMEM((2, tok, col), BF),
            pltpu.VMEM(tiles, BF), pltpu.VMEM(tiles, F32), pltpu.VMEM((tok, col), BF),
            pltpu.VMEM((top, tok), F32), pltpu.VMEM((blocks - 1, top, tok), F32),
            pltpu.SemaphoreType.DMA((3,)),
            pltpu.SemaphoreType.DMA((count,)), pltpu.SemaphoreType.DMA((count,)),
        ],
        compiler_params=pltpu.CompilerParams(
            collective_id=2, has_side_effects=True, vmem_limit_bytes=48 * 1024 * 1024
        ),
        cost_estimate=pl.CostEstimate(
            flops=20_000_000_000, bytes_accessed=1, transcendentals=0
        ),
        name="back",
    )(pick_t, ret, slot_of, keep, gates, routes, bias, cos_rows, sin_rows, gain2,
      q_gain, k_gain, router, resid, dy_all, mixed, qh, kh, vh, q_raw, k_raw, wo)


def octet():
    me = lax.axis_index("expert")
    core = me % 2
    return me - core, core, lax.axis_index("tensor")


def octet_others(base, core, rank):
    count = lax.axis_size("tensor")
    others = [{"expert": base + core, "tensor": (rank + d) % count} for d in range(1, count)]
    return others + [
        {"expert": base + 1 - core, "tensor": (rank + d) % count} for d in range(count)
    ]


def meet(others):
    barrier = pltpu.get_barrier_semaphore()
    for other in others:
        pl.semaphore_signal(barrier, inc=1, device_id=other, device_id_type=MESH)
    return lambda: pl.semaphore_wait(barrier, len(others))


def remote(source, target, send_sem, recv_sem, device):
    return pltpu.make_async_remote_copy(
        src_ref=source, dst_ref=target, send_sem=send_sem, recv_sem=recv_sem, device_id=device,
        device_id_type=MESH,
    )


def weights_kernel(
    w, first, second, out, near, own, load_sem, near_sem, send_sem, recv_sem, pass_send, pass_recv
):
    base, core, rank = octet()
    ready = meet(octet_others(base, core, rank))
    ranks = out.shape[0]
    half = out.shape[2] // 2
    sibling = {"expert": base + 1 - core, "tensor": rank}
    side = rank % 2
    target = 2 * core + side
    own_chip = target == rank

    def part(ref, index, which):
        return ref.at[index, :, pl.ds(which * half, half), :]

    mine = 1 - (rank // 2 + core) % 2
    loads = fetch([(first, near.at[0]), (second, near.at[1])], load_sem)
    own_loads, own_stores = [], []
    for k in range(2):
        own_loads.append(pltpu.make_async_copy(part(w, side, k), own.at[k], load_sem.at[2 + k]))
        own_stores.append(pltpu.make_async_copy(own.at[k], part(out, rank, k), near_sem.at[2 + k]))
        pl.when(own_chip)(own_loads[k].start)
    ready()
    sends = []
    for k in range(2):
        device = {"expert": base + mine * (1 - core) + (1 - mine) * k, "tensor": target}
        arrives = recv_sem.at[1 - mine, mine * k]
        sends.append(remote(part(w, side, k), part(out, rank, k), send_sem.at[k], arrives, device))
        sends[k].start()
    offsets = (3 - 2 * core, 1 + 2 * core)
    stores, passed = [], []
    for n in range(2):
        d = offsets[n]
        place = part(out, (rank + d) % ranks, core)
        loads[n].wait()
        passed.append(remote(near.at[n], place, pass_send.at[d], pass_recv.at[d], sibling))
        passed[-1].start()
        stores.append(pltpu.make_async_copy(near.at[n], place, near_sem.at[n]))
        stores[-1].start()

    @pl.when(own_chip)
    def _():
        for k in range(2):
            own_loads[k].wait()
            own_stores[k].start()

    far = part(out, (rank + 2) % ranks, core)
    remote(far, far, send_sem.at[0], recv_sem.at[1, 0], sibling).wait_recv()
    passed.append(remote(far, far, pass_send.at[2], pass_recv.at[2], sibling))
    passed[-1].start()
    for k in range(2):
        theirs = part(out, rank, k)
        arrival = remote(theirs, theirs, send_sem.at[k], recv_sem.at[0, k], sibling)
        pl.when(jnp.logical_not(own_chip))(arrival.wait_recv)
        pl.when(own_chip)(own_stores[k].wait)
    for d in range(1, ranks):
        theirs = part(out, (rank + d) % ranks, 1 - core)
        remote(theirs, theirs, pass_send.at[d], pass_recv.at[d], sibling).wait_recv()
    for copy in passed + sends:
        copy.wait_send()
    for copy in stores:
        copy.wait()


def weights_call(w, first, second):
    _, three, width, hidden = w.shape
    hbm = pl.BlockSpec(memory_space=pl.ANY)
    sems = pltpu.SemaphoreType.DMA((4,))
    halves = pltpu.VMEM((2, three, width // 2, hidden), BF)
    return pl.pallas_call(
        weights_kernel,
        out_shape=jax.ShapeDtypeStruct((4, three, width, hidden), BF),
        in_specs=[hbm] * 3,
        out_specs=hbm,
        scratch_shapes=[
            halves, halves, sems, sems, pltpu.SemaphoreType.DMA((2,)),
            pltpu.SemaphoreType.DMA((2, 2)), sems, sems,
        ],
        compiler_params=pltpu.CompilerParams(
            collective_id=4, has_side_effects=True, vmem_limit_bytes=60 * 1024 * 1024
        ),
        cost_estimate=SHADOW,
        name="weights",
    )(w, first, second)


def near_weights(w, turn_over):
    ranks, places = lax.axis_size("tensor"), lax.axis_size("expert")
    half = w.shape[2] // 2
    core, rank = lax.axis_index("expert") % 2, lax.axis_index("tensor")
    side = 1 - rank % 2
    to_core = jnp.where(2 * core + side == (rank + 1) % ranks, turn_over, 1 - turn_over)
    piece = lax.dynamic_slice(w, (side, 0, to_core * half, 0), (1, w.shape[1], half, w.shape[3]))
    pairs = []
    for place in range(places):
        for t in range(ranks):
            target = 2 * (place % 2) + 1 - t % 2
            core_of = (0 if target == (t + 1) % ranks else 1) ^ turn_over
            pairs.append((place * ranks + t, (place - place % 2 + core_of) * ranks + target))
    return lax.ppermute(piece[0], ("expert", "tensor"), pairs)


def home_kernel(grads, out, far_out, own, got, load_sem, local_sem, swap_send, swap_recv, send_sem, recv_sem):
    base, core, rank = octet()
    ready = meet(octet_others(base, core, rank))
    ranks, three, half, hidden = own.shape
    sibling = {"expert": base + 1 - core, "tensor": rank}
    order = (1, 3, 0, 2)
    loads, swaps = [], []
    for d in order:
        quarter = (rank + d) % ranks
        source = grads.at[quarter, :, pl.ds(core * half, half), :]
        loads.append(pltpu.make_async_copy(source, own.at[d], load_sem.at[d]))
        loads[-1].start()
    ready()
    for d in order:
        quarter = (rank + d) % ranks
        source = grads.at[quarter, :, pl.ds((1 - core) * half, half), :]
        swaps.append(remote(source, got.at[d], swap_send.at[d], swap_recv.at[d], sibling))
        swaps[-1].start()
    owner = rank // 2
    side = rank - 2 * owner
    rows = 64
    place = out.at[side, :, pl.ds(core * half, half), :]
    stays = owner == core
    sends = []
    for n, d in enumerate(order):
        loads[n].wait()
        swaps[n].wait_recv()

        def one(i, _, d=d):
            c, at = i // (half // rows), i % (half // rows) * rows
            here = pl.ds(pl.multiple_of(at, rows), rows)
            value = own[d, c, here, :].astype(F32) + got[d, c, here, :].astype(F32)
            own[d, c, here, :] = value.astype(BF)
            return 0

        lax.fori_loop(0, three * (half // rows), one, 0)
        if d == 2:
            far = pltpu.make_async_copy(own.at[d], far_out, load_sem.at[d])
            far.start()
            continue
        away = remote(
            own.at[d], place, send_sem.at[d], recv_sem.at[2 * side + core],
            {"expert": base + owner, "tensor": (rank + d) % ranks},
        )
        if d:
            away.start()
        else:
            kept = pltpu.make_async_copy(own.at[d], place, local_sem)
            pl.when(stays)(kept.start)
            pl.when(jnp.logical_not(stays))(away.start)
        sends.append((d, away))
    for s in range(2):
        for k in range(2):
            off = (2 * core + s - rank) % ranks
            mine = out.at[s, :, pl.ds(k * half, half), :]
            arrival = remote(own.at[0], mine, send_sem.at[0], recv_sem.at[2 * s + k], sibling)
            own_chip = off == 0
            comes = (off != 2) & jnp.logical_not(own_chip & (core == k))
            pl.when(comes)(arrival.wait_recv)
    pl.when(stays)(kept.wait)
    for d, away in sends:
        if d:
            away.wait_send()
        else:
            pl.when(jnp.logical_not(stays))(away.wait_send)
    for swap in swaps:
        swap.wait_send()
    far.wait()


def home_call(grads):
    ranks, three, width, hidden = grads.shape
    hbm = pl.BlockSpec(memory_space=pl.ANY)
    sems = pltpu.SemaphoreType.DMA((4,))
    halves = pltpu.VMEM((ranks, three, width // 2, hidden), BF)
    shape = jax.ShapeDtypeStruct
    return pl.pallas_call(
        home_kernel,
        out_shape=(
            shape((2, three, width, hidden), BF), shape((three, width // 2, hidden), BF),
        ),
        in_specs=[hbm],
        out_specs=(hbm, hbm),
        scratch_shapes=[
            halves, halves, sems, pltpu.SemaphoreType.DMA, sems, sems, sems, sems,
        ],
        compiler_params=pltpu.CompilerParams(
            collective_id=5, has_side_effects=True, vmem_limit_bytes=60 * 1024 * 1024
        ),
        cost_estimate=SHADOW,
        name="home",
    )(grads)


def expert_kernel(rows_ref, dys, w_ref, y_ref, dx_ref, grad_ref, rows_t, dys_t, y_acc, dx_acc, gate_of, dgate):
    step = pl.program_id(0)
    width = y_acc.shape[1]
    rows = rows_ref.at[:, :width]

    @pl.when(step == 0)
    def _():
        gate_of[...] = row_sum(rows_ref[:, width:].astype(F32))
        rows_t[...] = rows[...].T
        dys_t[...] = (dys[...].astype(F32) * gate_of[...]).astype(BF).T
        dgate[...] = jnp.zeros_like(dgate)
        y_acc[...] = jnp.zeros_like(y_acc)
        dx_acc[...] = jnp.zeros_like(dx_acc)

    w_gate, w_up, w_down = w_ref[0, 0], w_ref[0, 1], w_ref[0, 2]
    gate = dot(rows[...], w_gate)
    up = dot(rows[...], w_up)
    d_raw = dot(dys[...], w_down)
    d_act = d_raw * gate_of[...]
    sig = 1.0 / (1.0 + jnp.exp(-gate))
    silu = gate * sig
    act = (silu * up).astype(BF)
    dgate[...] += row_sum(act.astype(F32) * d_raw)
    d_gate = (d_act * up * sig * (1.0 + gate * (1.0 - sig))).astype(BF)
    d_up = (d_act * silu).astype(BF)
    y_acc[...] += dot(act, w_down, 1, 1)
    dx_acc[...] += dot(d_gate, w_gate, 1, 1) + dot(d_up, w_up, 1, 1)
    grad_ref[0, 0] = dot(rows_t[...], d_gate).astype(BF)
    grad_ref[0, 1] = dot(rows_t[...], d_up).astype(BF)
    grad_ref[0, 2] = dot(dys_t[...], act).astype(BF)

    @pl.when(step == pl.num_programs(0) - 1)
    def _():
        first = dgate[...].astype(BF).astype(F32)
        lane = lax.broadcasted_iota(jnp.int32, (y_ref.shape[0], 128), 1)
        facts = jnp.where(lane == 0, first, jnp.where(lane == 1, dgate[...] - first, 0.0))
        y_ref[...] = (y_acc[...] * gate_of[...]).astype(BF)
        dx_ref[:, :width] = dx_acc[...].astype(BF)
        dx_ref[:, width:] = facts.astype(BF)


def expert_call(rows, dys, weights):
    quarters, _, width, hidden = weights.shape
    count = rows.shape[0]
    shape = jax.ShapeDtypeStruct

    def whole(value):
        return pl.BlockSpec(value.shape, lambda q: (0, 0), pipeline_mode=pl.Buffered(1))

    block = pl.BlockSpec((1, 3, width, hidden), lambda q: (q, 0, 0, 0))
    outs = [shape((count, width), BF), shape((count, width + 128), BF)]
    return pl.pallas_call(
        expert_kernel,
        grid=(quarters,),
        out_shape=tuple(outs) + (shape(weights.shape, BF),),
        in_specs=[whole(rows), whole(dys), block],
        out_specs=tuple(whole(value) for value in outs) + (block,),
        scratch_shapes=[
            pltpu.VMEM((width, count), BF),
            pltpu.VMEM((width, count), BF),
            pltpu.VMEM((count, width), F32),
            pltpu.VMEM((count, width), F32),
            pltpu.VMEM((count, 1), F32),
            pltpu.VMEM((count, 1), F32),
        ],
        compiler_params=pltpu.CompilerParams(vmem_limit_bytes=62 * 1024 * 1024),
        cost_estimate=COST,
        name="expert",
    )(rows, dys, weights)


def plane():
    me = lax.axis_index("expert")
    core, z, y = me % 2, (me // 2) % 4, me // 8
    return [
        (core, me + 1 - 2 * core),
        ((y + y // 2) % 2, me + 8 * (1 - 2 * (y % 2))),
        (y // 2, me + 8 * (3 - 2 * y)),
        ((z + z // 2) % 2, me + 2 * (1 - 2 * (z % 2))),
        (z // 2, me + 2 * (3 - 2 * z)),
    ]

ORDERS = ((1, 3, 2, 4), (3, 2, 4, 1), (2, 4, 1, 3), (4, 1, 3, 2))

def reduce_kernel(
    d_qkv, dr, d_mine, router_part, small_in, x_all, gain1, ob, pick_y, ret_y,
    far_hbm, resid_hbm, wq_hbm, wk_hbm, wv_hbm,
    q_out, k_out, v_out, router_out, o_out, dx_out, out_out, small_out, far_out,
    wq, wk, wv, resid, parts, y_parts, halves, box_x, note, buf, box, got,
    load_sem, out_sem, x_send, x_recv, send_sem, recv_sem, far_send, far_recv,
):
    me, peers = tensor_peers()
    dims = plane()
    base, core, _ = octet()
    ready = meet(octet_others(base, core, me) + [{"expert": partner} for _, partner in dims[1:]])
    loads = fetch(
        [(wq_hbm, wq), (wk_hbm, wk), (wv_hbm, wv), (resid_hbm.at[me], resid)], load_sem
    )
    blocks, tok, col = x_all.shape
    width = blocks * col
    head = col // blocks
    square = jnp.zeros((tok, 1), F32)
    for t in range(blocks):
        value = x_all[t].astype(F32)
        square = square + row_sum(value * value)
    r1 = inverse_rms(square, width)
    post_x = Post("tensor", x_send, x_recv)
    post = Post("expert", send_sem, recv_sem)
    x_halves, x_box = halves.at[pl.ds(0, 2)], box_x.at[pl.ds(0, 2)]
    y_halves, y_box = halves.at[pl.ds(2, 2)], box_x.at[pl.ds(2, 2)]
    chunks = buf.shape[0] // blocks
    rows_chunk = buf.shape[1]

    def products(t):
        here = pl.ds(t * chunks, chunks)
        normed = (x_all[t].astype(F32) * r1 * gain1[pl.ds(t, 1), :]).T.astype(BF)
        for n in range(3):
            lanes = slice(n * col, (n + 1) * col)
            value = dot(normed, d_qkv[:, lanes]).astype(BF)
            buf[here, :, lanes] = value.reshape(chunks, rows_chunk, col)
        value = dot(dr[t].T, ob[...]).astype(BF)
        buf[here, :, 3 * col : 4 * col] = value.reshape(chunks, rows_chunk, col)
        value = router_part[pl.ds(t * col, col), :]
        buf[here, :, 4 * col :] = value.reshape(chunks, rows_chunk, value.shape[1])

    def add(target, place, first, count):
        def one(i, _):
            total = buf[place + i].astype(F32) + box[first + i].astype(F32)
            target[place + i] = total.astype(BF)
            return 0

        lax.fori_loop(0, count, one, 0)

    half = far_hbm.shape[1]
    owner = me // 2

    def far_copy(n, side, device):
        return remote(
            far_hbm.at[n], far_out.at[n, pl.ds(side * half, half), :],
            far_send.at[n], far_recv.at[n, side], device,
        )

    far_copies = [
        far_copy(n, core, {"expert": base + owner, "tensor": (me + 2) % blocks}) for n in range(3)
    ]
    copies = []
    ready()
    for n in range(2):
        products(2 * (1 - core) + n)
        for s in range(2 * n, 2 * n + 2):
            source = buf.at[pl.ds((1 - core) * 64 + s * 16, 16)]
            copies.append(post.push(source, box.at[pl.ds(31 * s, 16)], dims[0][1]))
    for copy in loads:
        copy.wait()
    for t in range(blocks):
        rows = slice(t * col, (t + 1) * col)
        parts[t] = (
            dot(d_qkv[:, 0:col], wq[rows, :], 1, 1)
            + dot(d_qkv[:, col : 2 * col], wk[rows, :], 1, 1)
            + dot(d_qkv[:, 2 * col : 3 * col], wv[rows, :], 1, 1)
        ).astype(BF)
    x_first = scatter_start(post_x, parts, x_halves, me)
    far_copies[0].start()
    for n in range(2):
        products(2 * core + n)
    x_moved = scatter_relay(post_x, parts, x_halves, x_box, me, x_first)
    far_copies[1].start()
    place = [core * 64 + s * 16 for s in range(4)]
    size, first = 16, 0

    def halve(k):
        for s in range(4):
            copies[s].wait_recv()
            add(buf, place[s], 31 * s + first, size)
            bit, partner = dims[ORDERS[s][k]]
            half = size // 2
            copies[s] = post.push(
                buf.at[pl.ds(place[s] + (1 - bit) * half, half)],
                box.at[pl.ds(31 * s + first + size, half)],
                partner,
            )
            place[s] = place[s] + bit * half

    halve(0)
    first, size = first + size, size // 2

    for t in range(blocks):
        y_parts[t] = dot(pick_y[...], ret_y[:, t * col : (t + 1) * col]).astype(BF)
    y_first = scatter_start(post_x, y_parts, y_halves, me)
    d_an = scatter_total(parts, x_box, me, x_moved)
    x_mine = x_all[me].astype(F32)
    grown = gain1[pl.ds(me, 1), :] * d_an
    mean_part = row_sum(x_mine * grown)
    note[me, 0:8, :] = jnp.broadcast_to(
        jnp.sum(d_an * x_mine * r1, axis=0, keepdims=True), (8, col)
    )
    note[me, 8:16, 0:tok] = jnp.broadcast_to(mean_part, (tok, 128)).T[0:8, :]
    note[me, 8:16, tok:] = jnp.broadcast_to(small_in[blocks : blocks + 1, : 2 * head], (8, 2 * head))
    note_in = [post_x.push(note.at[me], note.at[me], peer) for peer in peers]

    halve(1)
    first, size = first + size, size // 2
    y_moved = scatter_relay(post_x, y_parts, y_halves, y_box, me, y_first)
    far_copies[2].start()
    halve(2)
    first, size = first + size, size // 2
    halve(3)
    first, size = first + size, size // 2
    shared = [[] for _ in range(4)]
    for s in range(4):
        copies[s].wait_recv()
        add(got, place[s], 31 * s + first, 1)
        here = got.at[pl.ds(place[s], 1)]
        copies[s] = post.push(here, here, dims[ORDERS[s][3]][1])
        shared[s].append(post.push(here, here, dims[0][1]))

    arrive(note_in)
    facts = note[0, 8:16, :]
    for t in range(1, blocks):
        facts = facts + note[t, 8:16, :]
    for t in range(blocks):
        small_out[t : t + 1, :] = note[t, 0:1, :]
        small_out[blocks + t : blocks + t + 1, :] = small_in[t : t + 1, :]
    small_out[2 * blocks :, :] = facts
    mean = jnp.broadcast_to(facts[0:1, 0:tok], (128, tok)).T[:, 0:1] * (1.0 / width)
    dx_out[...] = (d_mine[...] + r1 * grown - x_mine * (r1 * r1 * r1 * mean)).astype(BF)

    size = 1
    stores = []

    def keep(n, at):
        here = pl.ds(at, 16)
        outs = (q_out, k_out, v_out, None, router_out)
        for m, target in enumerate(outs):
            lanes = pl.ds(m * col, target.shape[2] if m != 3 else col)
            if m == 3:
                turned = got[here, :, lanes].reshape(16 * rows_chunk, col).T
                o_out[:, pl.ds(pl.multiple_of(at * rows_chunk, 128), 16 * rows_chunk)] = turned
                continue
            stores.append(
                pltpu.make_async_copy(got.at[here, :, lanes], target.at[here], out_sem.at[n, m])
            )
            stores[-1].start()

    for k in range(3, -1, -1):
        for s in range(4):
            copies[s].wait_recv()
            bit, _ = dims[ORDERS[s][k]]
            come = got.at[pl.ds(place[s] + (1 - 2 * bit) * size, size)]
            place[s] = place[s] - bit * size
            if k:
                here = got.at[pl.ds(place[s], 2 * size)]
                copies[s] = post.push(here, here, dims[ORDERS[s][k - 1]][1])
            shared[s].append(post.push(come, come, dims[0][1]))
            if not k:
                keep(s, place[s])
        size *= 2
        if k == 2:
            out_out[...] = (resid[...] + scatter_total(y_parts, y_box, me, y_moved)).astype(BF)
    for s in range(4):
        arrive(shared[s])
        keep(4 + s, (1 - core) * 64 + s * 16)
    post.finish()
    post_x.finish()
    for store in stores:
        store.wait()
    comes = (me + 2) % blocks // 2 == core
    for n in range(3):
        for side in range(2):
            pl.when(comes)(far_copy(n, side, {"expert": base + core, "tensor": (me + 2) % blocks}).wait_recv)
        far_copies[n].wait_send()


def reduce_call(d_qkv, dr, d_mine, router_part, small, x_all, gain1, ob, pick_y, ret_y, far, resid,
                weights):
    blocks, tok, col = x_all.shape
    width = blocks * col
    tiles = (blocks, tok, col)
    wide = (128, 16, 4 * col + 128)
    shape = jax.ShapeDtypeStruct
    vmem = pl.BlockSpec(memory_space=pltpu.VMEM)
    hbm = pl.BlockSpec(memory_space=pl.ANY)
    count = 8 + blocks - 1
    return pl.pallas_call(
        reduce_kernel,
        out_shape=(
            shape(wide[:2] + (col,), BF), shape(wide[:2] + (col,), BF), shape(wide[:2] + (col,), BF),
            shape(wide[:2] + (128,), BF), shape((col, width), BF),
            shape((tok, col), BF), shape((tok, col), BF), shape((16, col), F32),
            shape((far.shape[0], 2 * far.shape[1], far.shape[2]), BF),
        ),
        in_specs=[vmem] * 10 + [hbm] * 5,
        out_specs=(hbm,) * 4 + (vmem,) * 4 + (hbm,),
        scratch_shapes=[
            pltpu.VMEM((width, col), BF), pltpu.VMEM((width, col), BF), pltpu.VMEM((width, col), BF),
            pltpu.VMEM((tok, col), F32), pltpu.VMEM(tiles, BF), pltpu.VMEM(tiles, BF),
            pltpu.VMEM((4, tok // 2, col), BF), pltpu.VMEM((4, tok, col), BF),
            pltpu.VMEM((blocks, 16, col), F32),
            pltpu.VMEM(wide, BF), pltpu.VMEM((124,) + wide[1:], BF), pltpu.VMEM(wide, BF),
            pltpu.SemaphoreType.DMA((4,)), pltpu.SemaphoreType.DMA((8, 5)),
            pltpu.SemaphoreType.DMA((count,)), pltpu.SemaphoreType.DMA((count,)),
            pltpu.SemaphoreType.DMA((56,)), pltpu.SemaphoreType.DMA((56,)),
            pltpu.SemaphoreType.DMA((3,)), pltpu.SemaphoreType.DMA((3, 2)),
        ],
        compiler_params=pltpu.CompilerParams(
            collective_id=3, has_side_effects=True, vmem_limit_bytes=60 * 1024 * 1024
        ),
        cost_estimate=COST,
        name="reduce",
    )(d_qkv, dr, d_mine, router_part, small, x_all, gain1, ob, pick_y, ret_y, far, resid, *weights)


def body(
    tokens,
    out_grad,
    seq_lengths,
    dest_index,
    routes,
    pair_order,
    norm1_gain,
    w_query,
    w_key,
    w_value,
    q_gain,
    k_gain,
    w_output,
    norm2_gain,
    w_router,
    expert_w,
):
    groups = lax.axis_size("expert")
    tensor_count = lax.axis_size("tensor")
    group_id = lax.axis_index("expert")
    tensor_id = lax.axis_index("tensor")
    tok_count, col_count = tokens.shape
    width = col_count * tensor_count
    move_rows = tok_count // groups
    expert_count = w_router.shape[1]
    top_count = routes.shape[1]
    local_experts = expert_w.shape[0]

    w_stored = jnp.transpose(expert_w, (0, 2, 1, 3))
    w_first = near_weights(w_stored, 0)

    routes_t = routes.T
    order_t = pair_order[0].reshape(tok_count, top_count).T
    pair_expert = routes_t.reshape(-1)
    pair_total = tok_count * top_count
    base = pair_expert * pair_total
    keyed = base + order_t.reshape(-1)
    before = (keyed[None, :] < keyed[:, None]) & (keyed[None, :] >= base[:, None])
    ranks = jnp.sum(before.astype(jnp.int32), axis=1).reshape(top_count, tok_count)
    expert_axis = jnp.arange(expert_count, dtype=jnp.int32)
    route_hot = routes_t[:, None, :] == expert_axis[None, :, None]
    counts = jnp.sum(route_hot.astype(F32), axis=(0, 2))

    places = jnp.arange(tok_count, dtype=jnp.int32)
    arrival_rank = jnp.sum((dest_index[None, :] < dest_index[:, None]).astype(jnp.int32), axis=1)
    by_rank = (arrival_rank[None, :] == places[:, None]).astype(BF)
    inner = jnp.broadcast_to((dest_index % tok_count).astype(BF)[:, None], (tok_count, 64))
    facts = jnp.broadcast_to(counts.astype(BF)[None, :], (tok_count, expert_count))
    outgoing = dot(by_rank, jnp.concatenate([tokens, out_grad, inner, facts], axis=1)).astype(BF)
    got = exchange(outgoing.reshape(groups, move_rows, -1), "expert")
    all_counts = got[:, 0, 2 * col_count + 64 :].astype(jnp.int32)
    lower = jnp.arange(groups, dtype=jnp.int32) < group_id
    offsets = jnp.sum(jnp.where(lower[:, None], all_counts, 0), axis=0)
    mine = got[:, :, 2 * col_count].astype(jnp.int32).reshape(-1)
    put = (mine[None, :] == places[:, None]).astype(BF)
    local = dot(put, got.reshape(tok_count, -1)[:, : 2 * col_count]).astype(BF)
    capacity = 5 * tok_count * groups * top_count // (4 * expert_count)
    most_rows = 3 * tok_count * top_count // (2 * expert_count)
    per = most_rows // 2
    slots = groups * per
    slot_global = jnp.sum(jnp.where(route_hot, offsets[None, :, None], 0), axis=1) + ranks
    kept = slot_global < capacity
    keep_mask = kept.astype(F32)
    here = kept & (routes_t % tensor_count == tensor_id)
    owner = routes_t // tensor_count * 2 + ranks % 2
    slot_of = jnp.where(here, owner * per + ranks // 2, -1)

    seq_ids, positions = sequence_layout(seq_lengths[0], tok_count)
    bias = jnp.where(seq_ids[:, None] == seq_ids[None, :], 0.0, mask_fill)
    cos_tab, sin_tab = rope_tables(positions, q_gain.shape[0])
    cos_rows = jnp.concatenate([cos_tab, cos_tab], axis=1)
    sin_rows = jnp.concatenate([-sin_tab, sin_tab], axis=1)
    gain1 = norm1_gain.astype(F32).reshape(tensor_count, col_count)
    gain2 = norm2_gain.astype(F32).reshape(tensor_count, col_count)
    head_gains = (q_gain.astype(F32)[None], k_gain.astype(F32)[None])
    router = jnp.pad(w_router, ((0, 0), (0, 128 - expert_count)))
    weights = (w_query, w_key, w_value, w_output)
    def homeward(value):
        return exchange(value.reshape(groups, -1, value.shape[1]), "expert").reshape(value.shape)

    x_all, dy_all, send_dy = pre_call(local, slot_of, tensor_count, slots)
    send_dy, x_all, w_stored = lax.optimization_barrier((send_dy, x_all, w_stored))
    w_second = near_weights(w_stored, 1)
    recv_dy = homeward(send_dy)
    (
        resid, mixed, q_raw, k_raw, qh, kh, vh, attended, gates, send_rows, pick_t,
    ) = front_call(
        x_all, bias, cos_rows, sin_rows, gain1, gain2, *head_gains, router.T, routes_t, slot_of,
        keep_mask, weights, slots,
    )
    send_rows, w_stored, recv_dy = lax.optimization_barrier((send_rows, w_stored, recv_dy))
    recv_rows = homeward(send_rows)
    y_rows, d_rows, partial = expert_call(recv_rows, recv_dy, weights_call(w_stored, w_first, w_second))
    ret_rows = homeward(d_rows)
    near, far = home_call(partial)
    ret_rows, near, far, y_rows = lax.optimization_barrier((ret_rows, near, far, y_rows))
    ret_y = homeward(y_rows)
    d_qkv, dr, d_mine, router_part, small = back_call(
        pick_t, ret_rows, slot_of, keep_mask, gates, routes_t, bias, cos_rows,
        sin_rows, gain2, *head_gains, router, resid, dy_all, mixed, qh, kh, vh, q_raw, k_raw,
        w_output,
    )
    *wide, router_sum, out_proj, dx_slice, out_slice, small, far = reduce_call(
        d_qkv, dr, d_mine, router_part, small, x_all, gain1, attended, pick_t, ret_y, far, resid,
        weights[:3],
    )

    going = dot(put, jnp.concatenate([out_slice, dx_slice], axis=1), 0, 0).astype(BF)
    small = small[:9].astype(BF).reshape(move_rows, -1)
    small = jnp.pad(small, ((0, 0), (0, -small.shape[1] % 128)))
    small = jnp.broadcast_to(small[None], (groups,) + small.shape)
    back = exchange(jnp.concatenate([going.reshape(groups, move_rows, -1), small], axis=2), "expert")
    small = jnp.sum(back[:, :, 2 * col_count :].astype(F32), axis=0)[:, : 9 * col_count // move_rows]
    small = small.reshape(-1)
    back = dot(by_rank, back.reshape(tok_count, -1)[:, : 2 * col_count], 0, 0).astype(BF)
    opposite = (tensor_id + 2) % tensor_count - 2 * (group_id % 2)
    is_far = jnp.arange(local_experts) == opposite
    expert_grad = jnp.where(is_far[:, None, None, None], far[None], near).astype(F32)
    expert_grad = jnp.transpose(expert_grad, (0, 2, 1, 3))
    wide = [value.reshape(width, -1) for value in wide]
    gain_at = 2 * width + tok_count
    head = q_gain.shape[0]
    return (
        back[:, :col_count],
        back[:, col_count:],
        small[:width],
        wide[0].astype(F32),
        wide[1].astype(F32),
        wide[2].astype(F32),
        small[gain_at : gain_at + head],
        small[gain_at + head : gain_at + 2 * head],
        out_proj.astype(F32),
        small[width : 2 * width],
        router_sum.reshape(width, -1)[:, :expert_count].astype(F32),
        expert_grad,
    )


def solution(mesh):
    in_specs = (
        P("expert", "tensor"),
        P("expert", "tensor"),
        P("expert", None),
        P("expert"),
        P("expert", None),
        P("expert", None),
        P(),
        P(None, "tensor"),
        P(None, "tensor"),
        P(None, "tensor"),
        P(),
        P(),
        P("tensor", None),
        P(),
        P(),
        P("expert", None, None, "tensor"),
    )
    out_specs = (
        P("expert", "tensor"),
        P("expert", "tensor"),
        P(),
        P(None, "tensor"),
        P(None, "tensor"),
        P(None, "tensor"),
        P(),
        P(),
        P("tensor", None),
        P(),
        P(),
        P("expert", None, None, "tensor"),
    )
    return jax.shard_map(body, mesh=mesh, in_specs=in_specs, out_specs=out_specs, check_vma=False)
```

```python
import functools
import math

import jax
import jax.numpy as jnp
from jax import lax
from jax.experimental import pallas as pl
from jax.experimental.pallas import tpu as pltpu
from jax.sharding import PartitionSpec as P

norm_eps = 1e-06
rope_base = 10000.0
mask_fill = -1e30


def rope_tables(positions, width):
    half_width = width // 2
    steps_idx = jnp.arange(half_width, dtype=jnp.float32)
    freqs = jnp.exp(steps_idx * (-2.0 * math.log(rope_base) / width))
    angles = positions.astype(jnp.float32)[:, None] * freqs[None, :]
    return (jnp.cos(angles), jnp.sin(angles))


def sequence_layout(lengths_row, count):
    seq_ends = jnp.cumsum(lengths_row)
    places = jnp.arange(count, dtype=jnp.int32)
    passed = (places[:, None] >= seq_ends[None, :]).astype(jnp.int32)
    seq_ids = jnp.sum(passed, axis=1)
    starts = jnp.sum(passed * lengths_row[None, :], axis=1)
    return (seq_ids, places - starts)


BF = jnp.bfloat16
F32 = jnp.float32
SHADOW = pl.CostEstimate(flops=40_000_000_000, bytes_accessed=1, transcendentals=0)
COST = pl.CostEstimate(flops=1, bytes_accessed=1, transcendentals=0)


def dot(left, right, left_dim=1, right_dim=0):
    return lax.dot_general(
        left, right, (((left_dim,), (right_dim,)), ((), ())), preferred_element_type=F32
    )


def exchange(value, axis):
    return lax.all_to_all(value, axis, split_axis=0, concat_axis=0, tiled=True)


def gather_blocks(value, axis):
    return exchange(jnp.broadcast_to(value[None], (lax.axis_size(axis),) + value.shape), axis)


def column_blocks(value, count):
    return jnp.stack(jnp.split(value, count, axis=1))


MESH = pl.DeviceIdType.MESH


def tensor_peers():
    me = lax.axis_index("tensor")
    count = lax.axis_size("tensor")
    return me, [(me + d) % count for d in range(1, count)]


def greet(axis, peers):
    barrier = pltpu.get_barrier_semaphore()
    for peer in peers:
        pl.semaphore_signal(barrier, inc=1, device_id={axis: peer}, device_id_type=MESH)
    return lambda: pl.semaphore_wait(barrier, len(peers))


class Post:
    def __init__(self, axis, send_sem, recv_sem):
        self.axis, self.send_sem, self.recv_sem = axis, send_sem, recv_sem
        self.started = []
        self.used = 0

    def push(self, source, target, peer):
        slot = self.used
        self.used += 1
        copy = pltpu.make_async_remote_copy(
            src_ref=source,
            dst_ref=target,
            send_sem=self.send_sem.at[slot],
            recv_sem=self.recv_sem.at[slot],
            device_id={self.axis: peer},
            device_id_type=MESH,
        )
        copy.start()
        self.started.append(copy)
        return copy

    def finish(self):
        for copy in self.started:
            copy.wait_send()
        self.started = []


def arrive(copies):
    for copy in copies:
        copy.wait_recv()


def ring(me):
    count = lax.axis_size("tensor")
    return (me + 1) % count, (me + count - 1) % count


def gather_start(post, ref, me):
    right, left = ring(me)
    return [post.push(ref.at[me], ref.at[me], peer) for peer in (right, left)]


def gather_relay(post, ref, me, first):
    right, left = ring(me)
    half = ref.shape[1] // 2
    first[0].wait_recv()
    here = ref.at[left, pl.ds(0, half)]
    one = post.push(here, here, right)
    first[1].wait_recv()
    here = ref.at[right, pl.ds(half, half)]
    return [one, post.push(here, here, left)]


def scatter_start(post, parts, halves, me):
    right, left = ring(me)
    far = ring(right)[0]
    half = parts.shape[1] // 2
    return [
        post.push(parts.at[far, pl.ds(0, half)], halves.at[0], right),
        post.push(parts.at[far, pl.ds(half, half)], halves.at[1], left),
    ]


def scatter_relay(post, parts, halves, box, me, first):
    right, left = ring(me)
    half = parts.shape[1] // 2
    copies = []
    for n, (peer, rows) in enumerate(((right, pl.ds(0, half)), (left, pl.ds(half, half)))):
        first[n].wait_recv()
        parts[peer, rows, :] = (parts[peer, rows, :].astype(F32) + halves[n].astype(F32)).astype(BF)
        copies.append(post.push(parts.at[peer], box.at[n], peer))
    return copies


def scatter_total(parts, box, me, copies):
    arrive(copies)
    return parts[me].astype(F32) + box[0].astype(F32) + box[1].astype(F32)


def fetch(pairs, sem):
    copies = [
        pltpu.make_async_copy(source, target, sem.at[n]) for n, (source, target) in enumerate(pairs)
    ]
    for copy in copies:
        copy.start()
    return copies


def turn(value, cos_rows, sin_rows):
    return value * cos_rows + pltpu.roll(value, value.shape[-1] // 2, 1) * sin_rows


def inverse_rms(total, width):
    return lax.rsqrt(total * (1.0 / width) + norm_eps)


def row_sum(value):
    return jnp.sum(value, axis=1, keepdims=True)


def softmax_rows(query, key, bias, scale):
    scores = dot(query, key, 1, 1) * scale + bias
    grown = jnp.exp(scores - jnp.max(scores, axis=1, keepdims=True))
    return grown / row_sum(grown)


def select_slots(slot_of, slots):
    top, tok = slot_of.shape
    slot = lax.broadcasted_iota(jnp.int32, (slots, tok), 0)
    pick = jnp.zeros((slots, tok), F32)
    for k in range(top):
        pick = jnp.where(slot_of[k : k + 1, :] == slot, 1.0, pick)
    return pick


def pre_kernel(local, slot_of, x_out, dy_out, send_out, x_all, dy_all, send_sem, recv_sem):
    me = lax.axis_index("tensor")
    ready = greet("tensor", ring(me))
    blocks, _, col = x_all.shape
    x_all[me] = local[:, :col]
    dy_all[me] = local[:, col:]
    ready()
    post = Post("tensor", send_sem, recv_sem)
    dy_in = gather_start(post, dy_all, me)
    x_in = gather_start(post, x_all, me)
    pick = select_slots(slot_of, send_out.shape[0]).astype(BF)
    dy_in = gather_relay(post, dy_all, me, dy_in)
    x_in = gather_relay(post, x_all, me, x_in)
    arrive(dy_in)
    dy_out[...] = dy_all[...]
    for t in range(blocks):
        send_out[:, t * col : (t + 1) * col] = dot(pick, dy_all[t]).astype(BF)
    arrive(x_in)
    x_out[...] = x_all[...]
    post.finish()


def pre_call(local, slot_of, blocks, slots):
    tok, both = local.shape
    col = both // 2
    tiles = (blocks, tok, col)
    shape = jax.ShapeDtypeStruct
    vmem = pl.BlockSpec(memory_space=pltpu.VMEM)
    return pl.pallas_call(
        pre_kernel,
        out_shape=(shape(tiles, BF), shape(tiles, BF), shape((slots, col * blocks), BF)),
        in_specs=[vmem] * 2,
        out_specs=(vmem,) * 3,
        scratch_shapes=[
            pltpu.VMEM(tiles, BF), pltpu.VMEM(tiles, BF),
            pltpu.SemaphoreType.DMA((8,)), pltpu.SemaphoreType.DMA((8,)),
        ],
        compiler_params=pltpu.CompilerParams(
            collective_id=6, has_side_effects=True, vmem_limit_bytes=63 * 1024 * 1024
        ),
        cost_estimate=COST,
        name="pre",
    )(local, slot_of)


def front_kernel(
    x_all, bias, cos_rows, sin_rows, gain1, gain2, q_gain, k_gain, router_t, routes, slot_of, keep,
    wq_hbm, wk_hbm, wv_hbm, wo_hbm,
    resid_out, mixed_out, q_out, k_out, qh_out, kh_out, vh_out, ob_out,
    gates_out, send_out, pick_out,
    wq, wk, wv, wo, an, parts, halves, box, total, load_sem, send_sem, recv_sem,
):
    me = lax.axis_index("tensor")
    ready = greet("tensor", ring(me))
    loads = fetch([(wq_hbm, wq), (wk_hbm, wk), (wv_hbm, wv), (wo_hbm, wo)], load_sem)
    blocks, tok, col = x_all.shape
    width = blocks * col
    post = Post("tensor", send_sem, recv_sem)
    square = jnp.zeros((tok, 1), F32)
    for t in range(blocks):
        value = x_all[t].astype(F32)
        square = square + row_sum(value * value)
    r1 = inverse_rms(square, width)
    for t in range(blocks):
        an[t] = (x_all[t].astype(F32) * r1 * gain1[t : t + 1, :]).astype(BF)

    for copy in loads:
        copy.wait()

    def project(weight):
        value = dot(an[0], weight[0:col, :])
        for t in range(1, blocks):
            value = value + dot(an[t], weight[t * col : (t + 1) * col, :])
        return value

    q_out[...] = project(wq)
    k_out[...] = project(wk)
    vh_out[...] = project(wv).astype(BF)
    head = q_gain.shape[1]
    scale = 1.0 / math.sqrt(head)
    for h in range(col // head):
        lanes = slice(h * head, (h + 1) * head)
        for raw, gain, rotated in ((q_out, q_gain, qh_out), (k_out, k_gain, kh_out)):
            value = raw[:, lanes]
            value = value * inverse_rms(row_sum(value * value), head) * gain[...]
            rotated[:, lanes] = turn(value, cos_rows[...], sin_rows[...]).astype(BF)
        probs = softmax_rows(qh_out[:, lanes], kh_out[:, lanes], bias[...], scale).astype(BF)
        ob_out[:, lanes] = dot(probs, vh_out[:, lanes]).astype(BF)
    for t in range(blocks):
        parts[t] = dot(ob_out[...], wo[:, t * col : (t + 1) * col]).astype(BF)
    ready()
    first = scatter_start(post, parts, halves, me)
    moved = scatter_relay(post, parts, halves, box, me, first)
    total[me] = scatter_total(parts, box, me, moved).astype(BF)
    arrive(gather_relay(post, total, me, gather_start(post, total, me)))
    square = jnp.zeros((tok, 1), F32)
    for t in range(blocks):
        value = x_all[t].astype(F32) + total[t].astype(F32)
        resid_out[t] = value
        square = square + row_sum(value * value)
    r2 = inverse_rms(square, width)
    logits = jnp.zeros((router_t.shape[0], tok), F32)
    for t in range(blocks):
        mixed_out[t] = (resid_out[t] * r2 * gain2[t : t + 1, :]).astype(BF)
        logits = logits + dot(router_t[:, t * col : (t + 1) * col], mixed_out[t], 1, 1)
    expert = lax.broadcasted_iota(jnp.int32, logits.shape, 0)
    top = routes.shape[0]
    chosen = [
        jnp.sum(jnp.where(routes[k : k + 1, :] == expert, logits, 0.0), axis=0, keepdims=True)
        for k in range(top)
    ]
    peak = functools.reduce(jnp.maximum, chosen)
    grown = [jnp.exp(value - peak) for value in chosen]
    whole = functools.reduce(jnp.add, grown)
    slots = send_out.shape[0]
    slot = lax.broadcasted_iota(jnp.int32, (slots, tok), 0)
    pick = jnp.zeros((slots, tok), F32)
    weight = jnp.zeros((slots, tok), F32)
    for k in range(top):
        gate = grown[k] / whole
        gates_out[k : k + 1, :] = gate
        hot = slot_of[k : k + 1, :] == slot
        pick = jnp.where(hot, 1.0, pick)
        weight = jnp.where(hot, gate * keep[k : k + 1, :], weight)
    pick_out[...] = pick.T.astype(BF)
    pick = pick.astype(BF)
    for t in range(blocks):
        send_out[:, t * col : (t + 1) * col] = dot(pick, mixed_out[t]).astype(BF)
    gate = row_sum(weight)
    first = gate.astype(BF)
    second = (gate - first.astype(F32)).astype(BF)
    third = (gate - first.astype(F32) - second.astype(F32)).astype(BF)
    lane = lax.broadcasted_iota(jnp.int32, (slots, 128), 1)
    facts = jnp.zeros((slots, 128), F32)
    for n, piece in enumerate((first, second, third)):
        facts = jnp.where(lane == n, piece.astype(F32), facts)
    send_out[:, width:] = facts.astype(BF)
    post.finish()


def front_call(x_all, bias, cos_rows, sin_rows, gain1, gain2, q_gain, k_gain, router_t, routes,
               slot_of, keep, weights, slots):
    blocks, tok, col = tiles = x_all.shape
    width = col * blocks
    shape = jax.ShapeDtypeStruct
    vmem = pl.BlockSpec(memory_space=pltpu.VMEM)
    top = routes.shape[0]
    return pl.pallas_call(
        front_kernel,
        out_shape=(
            shape(tiles, F32), shape(tiles, BF), shape((tok, col), F32), shape((tok, col), F32),
            shape((tok, col), BF), shape((tok, col), BF), shape((tok, col), BF),
            shape((tok, col), BF), shape((top, tok), F32), shape((slots, width + 128), BF),
            shape((tok, slots), BF),
        ),
        in_specs=[vmem] * 12 + [pl.BlockSpec(memory_space=pl.ANY)] * 4,
        out_specs=(vmem,) * 11,
        scratch_shapes=[
            pltpu.VMEM((width, col), BF), pltpu.VMEM((width, col), BF), pltpu.VMEM((width, col), BF),
            pltpu.VMEM((col, width), BF),
            pltpu.VMEM(tiles, BF), pltpu.VMEM(tiles, BF),
            pltpu.VMEM((2, tok // 2, col), BF), pltpu.VMEM((2, tok, col), BF), pltpu.VMEM(tiles, BF),
            pltpu.SemaphoreType.DMA((4,)),
            pltpu.SemaphoreType.DMA((8,)), pltpu.SemaphoreType.DMA((8,)),
        ],
        compiler_params=pltpu.CompilerParams(
            collective_id=1, has_side_effects=True, vmem_limit_bytes=56 * 1024 * 1024
        ),
        cost_estimate=SHADOW,
        name="front",
    )(x_all, bias, cos_rows, sin_rows, gain1, gain2, q_gain, k_gain, router_t, routes, slot_of,
      keep, *weights)


def back_kernel(
    pick_t, ret, slot_of, keep, gates, routes, bias, cos_rows, sin_rows, gain2,
    q_gain, k_gain, router, resid, dy_all, mixed, qh, kh, vh,
    q_hbm, k_hbm, wo_hbm,
    d_qkv, dr, d_mine, router_out, small_out,
    q_raw, k_raw, wo, parts, halves, box, total, dm, d_att, dg_mine, dg_box,
    load_sem, send_sem, recv_sem,
):
    me, peers = tensor_peers()
    ready = greet("tensor", peers)
    loads = fetch([(wo_hbm, wo), (q_hbm, q_raw), (k_hbm, k_raw)], load_sem)
    blocks, tok, col = parts.shape
    width = blocks * col
    post = Post("tensor", send_sem, recv_sem)
    for t in range(blocks):
        parts[t] = dot(pick_t[...], ret[:, t * col : (t + 1) * col]).astype(BF)
    ready()
    first = scatter_start(post, parts, halves, me)
    top = routes.shape[0]
    dgate = row_sum(ret[:, width:].astype(F32))
    slot = lax.broadcasted_iota(jnp.int32, (ret.shape[0], tok), 0)
    for k in range(top):
        hot = slot_of[k : k + 1, :] == slot
        dg_mine[k : k + 1, :] = jnp.sum(jnp.where(hot, dgate, 0.0), axis=0, keepdims=True)
    dg_in = [post.push(dg_mine, dg_box.at[d], peer) for d, peer in enumerate(peers)]
    moved = scatter_relay(post, parts, halves, box, me, first)
    total[me] = scatter_total(parts, box, me, moved).astype(BF)
    total_first = gather_start(post, total, me)

    arrive(dg_in)
    d_gates = dg_mine[...]
    for d in range(blocks - 1):
        d_gates = d_gates + dg_box[d]
    d_gates = d_gates * keep[...]
    gate = gates[...]
    d_chosen = gate * (d_gates - jnp.sum(gate * d_gates, axis=0, keepdims=True))
    expert = lax.broadcasted_iota(jnp.int32, (router.shape[1], tok), 0)
    d_logits_t = jnp.zeros(expert.shape, F32)
    for k in range(top):
        hot = routes[k : k + 1, :] == expert
        d_logits_t = jnp.where(hot, d_chosen[k : k + 1, :], d_logits_t)
    d_logits = d_logits_t.T.astype(BF)
    square = jnp.zeros((tok, 1), F32)
    for t in range(blocks):
        rows = slice(t * col, (t + 1) * col)
        dm[t] = dot(d_logits, router[rows, :], 1, 1)
        square = square + row_sum(resid[t] * resid[t])
    r2 = inverse_rms(square, width)
    total_moved = gather_relay(post, total, me, total_first)
    for t in range(blocks):
        rows = slice(t * col, (t + 1) * col)
        router_out[rows, :] = dot(mixed[t].T, d_logits).astype(BF)
    arrive(total_moved)
    cross = jnp.zeros((tok, 1), F32)
    for t in range(blocks):
        dm[t] = dm[t] + total[t].astype(F32)
        cross = cross + row_sum(resid[t] * gain2[t : t + 1, :] * dm[t])
    cross = cross * (1.0 / width) * r2 * r2 * r2
    small_out[...] = jnp.zeros_like(small_out)
    for t in range(blocks):
        d_mixed = dm[t]
        small_out[t : t + 1, :] = jnp.sum(d_mixed * resid[t] * r2, axis=0, keepdims=True)
        d_resid = dy_all[t].astype(F32) + r2 * gain2[t : t + 1, :] * d_mixed - resid[t] * cross
        dm[t] = d_resid
        dr[t] = d_resid.astype(BF)
    d_mine[...] = dm[me]
    for copy in loads:
        copy.wait()
    value = dot(dr[0], wo[:, 0:col], 1, 1)
    for t in range(1, blocks):
        value = value + dot(dr[t], wo[:, t * col : (t + 1) * col], 1, 1)
    d_att[...] = value.astype(BF)

    head = q_gain.shape[1]
    scale = 1.0 / math.sqrt(head)
    q_part = jnp.zeros((1, head), F32)
    k_part = jnp.zeros((1, head), F32)

    def unturn(grown, raw, gain):
        d_unit = grown * cos_rows[...] - pltpu.roll(grown, head // 2, 1) * sin_rows[...]
        inverse = inverse_rms(row_sum(raw * raw), head)
        unit = raw * inverse
        gain_part = jnp.sum(d_unit * unit, axis=0, keepdims=True)
        d_unit = d_unit * gain[...]
        d_raw = inverse * (d_unit - unit * (row_sum(unit * d_unit) * (1.0 / head)))
        return d_raw.astype(BF), gain_part

    for h in range(col // head):
        lanes = slice(h * head, (h + 1) * head)
        probs = softmax_rows(qh[:, lanes], kh[:, lanes], bias[...], scale)
        d_head = d_att[:, lanes]
        d_probs = dot(d_head, vh[:, lanes], 1, 1)
        d_scores = probs * (d_probs - row_sum(probs * d_probs))
        d_qkv[:, 2 * col + h * head : 2 * col + (h + 1) * head] = dot(
            probs.T.astype(BF), d_head
        ).astype(BF)
        d_q, part = unturn(dot(d_scores.astype(BF), kh[:, lanes]) * scale, q_raw[:, lanes], q_gain)
        q_part = q_part + part
        d_qkv[:, lanes] = d_q
        d_k, part = unturn(dot(d_scores.T.astype(BF), qh[:, lanes]) * scale, k_raw[:, lanes], k_gain)
        k_part = k_part + part
        d_qkv[:, col + h * head : col + (h + 1) * head] = d_k
    small_out[blocks : blocks + 1, :head] = q_part
    small_out[blocks : blocks + 1, head : 2 * head] = k_part
    post.finish()


def back_call(pick_t, ret, slot_of, keep, gates, routes, bias, cos_rows, sin_rows,
              gain2, q_gain, k_gain, router, resid, dy_all, mixed, qh, kh, vh, q_raw, k_raw, wo):
    blocks, tok, col = dy_all.shape
    width = blocks * col
    tiles = (blocks, tok, col)
    shape = jax.ShapeDtypeStruct
    vmem = pl.BlockSpec(memory_space=pltpu.VMEM)
    top = routes.shape[0]
    count = 8 + blocks - 1
    return pl.pallas_call(
        back_kernel,
        out_shape=(
            shape((tok, 3 * col), BF), shape(tiles, BF), shape((tok, col), F32),
            shape((width, 128), BF), shape((8, col), F32),
        ),
        in_specs=[vmem] * 19 + [pl.BlockSpec(memory_space=pl.ANY)] * 3,
        out_specs=(vmem,) * 5,
        scratch_shapes=[
            pltpu.VMEM((tok, col), F32), pltpu.VMEM((tok, col), F32), pltpu.VMEM((col, width), BF),
            pltpu.VMEM(tiles, BF), pltpu.VMEM((2, tok // 2, col), BF), pltpu.VMEM((2, tok, col), BF),
            pltpu.VMEM(tiles, BF), pltpu.VMEM(tiles, F32), pltpu.VMEM((tok, col), BF),
            pltpu.VMEM((top, tok), F32), pltpu.VMEM((blocks - 1, top, tok), F32),
            pltpu.SemaphoreType.DMA((3,)),
            pltpu.SemaphoreType.DMA((count,)), pltpu.SemaphoreType.DMA((count,)),
        ],
        compiler_params=pltpu.CompilerParams(
            collective_id=2, has_side_effects=True, vmem_limit_bytes=63 * 1024 * 1024
        ),
        cost_estimate=pl.CostEstimate(
            flops=20_000_000_000, bytes_accessed=1, transcendentals=0
        ),
        name="back",
    )(pick_t, ret, slot_of, keep, gates, routes, bias, cos_rows, sin_rows, gain2,
      q_gain, k_gain, router, resid, dy_all, mixed, qh, kh, vh, q_raw, k_raw, wo)


def octet():
    me = lax.axis_index("expert")
    core = me % 2
    return me - core, core, lax.axis_index("tensor")


def octet_others(base, core, rank):
    count = lax.axis_size("tensor")
    others = [{"expert": base + core, "tensor": (rank + d) % count} for d in range(1, count)]
    return others + [
        {"expert": base + 1 - core, "tensor": (rank + d) % count} for d in range(count)
    ]


def meet(others):
    barrier = pltpu.get_barrier_semaphore()
    for other in others:
        pl.semaphore_signal(barrier, inc=1, device_id=other, device_id_type=MESH)
    return lambda: pl.semaphore_wait(barrier, len(others))


def remote(source, target, send_sem, recv_sem, device):
    return pltpu.make_async_remote_copy(
        src_ref=source, dst_ref=target, send_sem=send_sem, recv_sem=recv_sem, device_id=device,
        device_id_type=MESH,
    )


def weights_kernel(
    w, first, second, out, near, own, load_sem, near_sem, send_sem, recv_sem, pass_send, pass_recv
):
    base, core, rank = octet()
    ready = meet(octet_others(base, core, rank))
    ranks = out.shape[0]
    half = out.shape[2] // 2
    sibling = {"expert": base + 1 - core, "tensor": rank}
    side = rank % 2
    target = 2 * core + side
    own_chip = target == rank

    def part(ref, index, which):
        return ref.at[index, :, pl.ds(which * half, half), :]

    mine = 1 - (rank // 2 + core) % 2
    loads = fetch([(first, near.at[0]), (second, near.at[1])], load_sem)
    own_loads, own_stores = [], []
    for k in range(2):
        own_loads.append(pltpu.make_async_copy(part(w, side, k), own.at[k], load_sem.at[2 + k]))
        own_stores.append(pltpu.make_async_copy(own.at[k], part(out, rank, k), near_sem.at[2 + k]))
        pl.when(own_chip)(own_loads[k].start)
    ready()
    sends = []
    for k in range(2):
        device = {"expert": base + mine * (1 - core) + (1 - mine) * k, "tensor": target}
        arrives = recv_sem.at[1 - mine, mine * k]
        sends.append(remote(part(w, side, k), part(out, rank, k), send_sem.at[k], arrives, device))
        sends[k].start()
    offsets = (3 - 2 * core, 1 + 2 * core)
    stores, passed = [], []
    for n in range(2):
        d = offsets[n]
        place = part(out, (rank + d) % ranks, core)
        loads[n].wait()
        passed.append(remote(near.at[n], place, pass_send.at[d], pass_recv.at[d], sibling))
        passed[-1].start()
        stores.append(pltpu.make_async_copy(near.at[n], place, near_sem.at[n]))
        stores[-1].start()

    @pl.when(own_chip)
    def _():
        for k in range(2):
            own_loads[k].wait()
            own_stores[k].start()

    far = part(out, (rank + 2) % ranks, core)
    remote(far, far, send_sem.at[0], recv_sem.at[1, 0], sibling).wait_recv()
    passed.append(remote(far, far, pass_send.at[2], pass_recv.at[2], sibling))
    passed[-1].start()
    for k in range(2):
        theirs = part(out, rank, k)
        arrival = remote(theirs, theirs, send_sem.at[k], recv_sem.at[0, k], sibling)
        pl.when(jnp.logical_not(own_chip))(arrival.wait_recv)
        pl.when(own_chip)(own_stores[k].wait)
    for d in range(1, ranks):
        theirs = part(out, (rank + d) % ranks, 1 - core)
        remote(theirs, theirs, pass_send.at[d], pass_recv.at[d], sibling).wait_recv()
    for copy in passed + sends:
        copy.wait_send()
    for copy in stores:
        copy.wait()


def weights_call(w, first, second):
    _, three, width, hidden = w.shape
    hbm = pl.BlockSpec(memory_space=pl.ANY)
    sems = pltpu.SemaphoreType.DMA((4,))
    halves = pltpu.VMEM((2, three, width // 2, hidden), BF)
    return pl.pallas_call(
        weights_kernel,
        out_shape=jax.ShapeDtypeStruct((4, three, width, hidden), BF),
        in_specs=[hbm] * 3,
        out_specs=hbm,
        scratch_shapes=[
            halves, halves, sems, sems, pltpu.SemaphoreType.DMA((2,)),
            pltpu.SemaphoreType.DMA((2, 2)), sems, sems,
        ],
        compiler_params=pltpu.CompilerParams(
            collective_id=4, has_side_effects=True, vmem_limit_bytes=60 * 1024 * 1024
        ),
        cost_estimate=SHADOW,
        name="weights",
    )(w, first, second)


def near_weights(w, turn_over):
    ranks, places = lax.axis_size("tensor"), lax.axis_size("expert")
    half = w.shape[2] // 2
    core, rank = lax.axis_index("expert") % 2, lax.axis_index("tensor")
    side = 1 - rank % 2
    to_core = jnp.where(2 * core + side == (rank + 1) % ranks, turn_over, 1 - turn_over)
    piece = lax.dynamic_slice(w, (side, 0, to_core * half, 0), (1, w.shape[1], half, w.shape[3]))
    pairs = []
    for place in range(places):
        for t in range(ranks):
            target = 2 * (place % 2) + 1 - t % 2
            core_of = (0 if target == (t + 1) % ranks else 1) ^ turn_over
            pairs.append((place * ranks + t, (place - place % 2 + core_of) * ranks + target))
    return lax.ppermute(piece[0], ("expert", "tensor"), pairs)


def home_kernel(grads, out, far_out, own, got, load_sem, local_sem, swap_send, swap_recv, send_sem, recv_sem):
    base, core, rank = octet()
    ready = meet(octet_others(base, core, rank))
    ranks, three, half, hidden = own.shape
    sibling = {"expert": base + 1 - core, "tensor": rank}
    order = (1, 3, 0, 2)
    loads, swaps = [], []
    for d in order:
        quarter = (rank + d) % ranks
        source = grads.at[quarter, :, pl.ds(core * half, half), :]
        loads.append(pltpu.make_async_copy(source, own.at[d], load_sem.at[d]))
        loads[-1].start()
    ready()
    for d in order:
        quarter = (rank + d) % ranks
        source = grads.at[quarter, :, pl.ds((1 - core) * half, half), :]
        swaps.append(remote(source, got.at[d], swap_send.at[d], swap_recv.at[d], sibling))
        swaps[-1].start()
    owner = rank // 2
    side = rank - 2 * owner
    rows = 64
    place = out.at[side, :, pl.ds(core * half, half), :]
    stays = owner == core
    sends = []
    for n, d in enumerate(order):
        loads[n].wait()
        swaps[n].wait_recv()

        def one(i, _, d=d):
            c, at = i // (half // rows), i % (half // rows) * rows
            here = pl.ds(pl.multiple_of(at, rows), rows)
            value = own[d, c, here, :].astype(F32) + got[d, c, here, :].astype(F32)
            own[d, c, here, :] = value.astype(BF)
            return 0

        lax.fori_loop(0, three * (half // rows), one, 0)
        if d == 2:
            far = pltpu.make_async_copy(own.at[d], far_out, load_sem.at[d])
            far.start()
            continue
        away = remote(
            own.at[d], place, send_sem.at[d], recv_sem.at[2 * side + core],
            {"expert": base + owner, "tensor": (rank + d) % ranks},
        )
        if d:
            away.start()
        else:
            kept = pltpu.make_async_copy(own.at[d], place, local_sem)
            pl.when(stays)(kept.start)
            pl.when(jnp.logical_not(stays))(away.start)
        sends.append((d, away))
    for s in range(2):
        for k in range(2):
            off = (2 * core + s - rank) % ranks
            mine = out.at[s, :, pl.ds(k * half, half), :]
            arrival = remote(own.at[0], mine, send_sem.at[0], recv_sem.at[2 * s + k], sibling)
            own_chip = off == 0
            comes = (off != 2) & jnp.logical_not(own_chip & (core == k))
            pl.when(comes)(arrival.wait_recv)
    pl.when(stays)(kept.wait)
    for d, away in sends:
        if d:
            away.wait_send()
        else:
            pl.when(jnp.logical_not(stays))(away.wait_send)
    for swap in swaps:
        swap.wait_send()
    far.wait()


def home_call(grads):
    ranks, three, width, hidden = grads.shape
    hbm = pl.BlockSpec(memory_space=pl.ANY)
    sems = pltpu.SemaphoreType.DMA((4,))
    halves = pltpu.VMEM((ranks, three, width // 2, hidden), BF)
    shape = jax.ShapeDtypeStruct
    return pl.pallas_call(
        home_kernel,
        out_shape=(
            shape((2, three, width, hidden), BF), shape((three, width // 2, hidden), BF),
        ),
        in_specs=[hbm],
        out_specs=(hbm, hbm),
        scratch_shapes=[
            halves, halves, sems, pltpu.SemaphoreType.DMA, sems, sems, sems, sems,
        ],
        compiler_params=pltpu.CompilerParams(
            collective_id=5, has_side_effects=True, vmem_limit_bytes=60 * 1024 * 1024
        ),
        cost_estimate=SHADOW,
        name="home",
    )(grads)


def expert_kernel(rows_ref, dys, w_ref, y_ref, dx_ref, grad_ref, rows_t, dys_t, y_acc, dx_acc, gate_of, dgate):
    step = pl.program_id(0)
    width = y_acc.shape[1]
    rows = rows_ref.at[:, :width]

    @pl.when(step == 0)
    def _():
        gate_of[...] = row_sum(rows_ref[:, width:].astype(F32))
        rows_t[...] = rows[...].T
        dys_t[...] = (dys[...].astype(F32) * gate_of[...]).astype(BF).T
        dgate[...] = jnp.zeros_like(dgate)
        y_acc[...] = jnp.zeros_like(y_acc)
        dx_acc[...] = jnp.zeros_like(dx_acc)

    w_gate, w_up, w_down = w_ref[0, 0], w_ref[0, 1], w_ref[0, 2]
    gate = dot(rows[...], w_gate)
    up = dot(rows[...], w_up)
    d_raw = dot(dys[...], w_down)
    d_act = d_raw * gate_of[...]
    sig = 1.0 / (1.0 + jnp.exp(-gate))
    silu = gate * sig
    act = (silu * up).astype(BF)
    dgate[...] += row_sum(act.astype(F32) * d_raw)
    d_gate = (d_act * up * sig * (1.0 + gate * (1.0 - sig))).astype(BF)
    d_up = (d_act * silu).astype(BF)
    y_acc[...] += dot(act, w_down, 1, 1)
    dx_acc[...] += dot(d_gate, w_gate, 1, 1) + dot(d_up, w_up, 1, 1)
    grad_ref[0, 0] = dot(rows_t[...], d_gate).astype(BF)
    grad_ref[0, 1] = dot(rows_t[...], d_up).astype(BF)
    grad_ref[0, 2] = dot(dys_t[...], act).astype(BF)

    @pl.when(step == pl.num_programs(0) - 1)
    def _():
        first = dgate[...].astype(BF).astype(F32)
        lane = lax.broadcasted_iota(jnp.int32, (y_ref.shape[0], 128), 1)
        facts = jnp.where(lane == 0, first, jnp.where(lane == 1, dgate[...] - first, 0.0))
        y_ref[...] = (y_acc[...] * gate_of[...]).astype(BF)
        dx_ref[:, :width] = dx_acc[...].astype(BF)
        dx_ref[:, width:] = facts.astype(BF)


def expert_call(rows, dys, weights):
    quarters, _, width, hidden = weights.shape
    count = rows.shape[0]
    shape = jax.ShapeDtypeStruct

    def whole(value):
        return pl.BlockSpec(value.shape, lambda q: (0, 0), pipeline_mode=pl.Buffered(1))

    block = pl.BlockSpec((1, 3, width, hidden), lambda q: (q, 0, 0, 0))
    outs = [shape((count, width), BF), shape((count, width + 128), BF)]
    return pl.pallas_call(
        expert_kernel,
        grid=(quarters,),
        out_shape=tuple(outs) + (shape(weights.shape, BF),),
        in_specs=[whole(rows), whole(dys), block],
        out_specs=tuple(whole(value) for value in outs) + (block,),
        scratch_shapes=[
            pltpu.VMEM((width, count), BF),
            pltpu.VMEM((width, count), BF),
            pltpu.VMEM((count, width), F32),
            pltpu.VMEM((count, width), F32),
            pltpu.VMEM((count, 1), F32),
            pltpu.VMEM((count, 1), F32),
        ],
        compiler_params=pltpu.CompilerParams(vmem_limit_bytes=62 * 1024 * 1024),
        cost_estimate=COST,
        name="expert",
    )(rows, dys, weights)


def plane():
    me = lax.axis_index("expert")
    core, z, y = me % 2, (me // 2) % 4, me // 8
    return [
        (core, me + 1 - 2 * core),
        ((y + y // 2) % 2, me + 8 * (1 - 2 * (y % 2))),
        (y // 2, me + 8 * (3 - 2 * y)),
        ((z + z // 2) % 2, me + 2 * (1 - 2 * (z % 2))),
        (z // 2, me + 2 * (3 - 2 * z)),
    ]

ORDERS = ((1, 3, 2, 4), (3, 2, 4, 1), (2, 4, 1, 3), (4, 1, 3, 2))

def reduce_kernel(
    d_qkv, dr, d_mine, router_part, small_in, x_all, gain1, ob, pick_y, ret_y,
    far_hbm, resid_hbm, wq_hbm, wk_hbm, wv_hbm,
    q_out, k_out, v_out, o_out, dx_out, out_out, small_out, far_out,
    wq, wk, wv, resid, parts, y_parts, halves, box_x, note, buf, box, got,
    load_sem, out_sem, x_send, x_recv, send_sem, recv_sem, far_send, far_recv,
):
    me, peers = tensor_peers()
    dims = plane()
    base, core, _ = octet()
    ready = meet(octet_others(base, core, me) + [{"expert": partner} for _, partner in dims[1:]])
    loads = fetch(
        [(wq_hbm, wq), (wk_hbm, wk), (wv_hbm, wv), (resid_hbm.at[me], resid)], load_sem
    )
    blocks, tok, col = x_all.shape
    width = blocks * col
    head = col // blocks
    square = jnp.zeros((tok, 1), F32)
    for t in range(blocks):
        value = x_all[t].astype(F32)
        square = square + row_sum(value * value)
    r1 = inverse_rms(square, width)
    post_x = Post("tensor", x_send, x_recv)
    post = Post("expert", send_sem, recv_sem)
    x_halves, x_box = halves.at[pl.ds(0, 2)], box_x.at[pl.ds(0, 2)]
    y_halves, y_box = halves.at[pl.ds(2, 2)], box_x.at[pl.ds(2, 2)]
    chunks = buf.shape[0] // blocks
    rows_chunk = buf.shape[1]

    def products(t):
        here = pl.ds(t * chunks, chunks)
        normed = (x_all[t].astype(F32) * r1 * gain1[pl.ds(t, 1), :]).T.astype(BF)
        for n in range(3):
            lanes = slice(n * col, (n + 1) * col)
            value = dot(normed, d_qkv[:, lanes]).astype(BF)
            buf[here, :, lanes] = value.reshape(chunks, rows_chunk, col)
        value = dot(dr[t].T, ob[...]).astype(BF)
        buf[here, :, 3 * col : 4 * col] = value.reshape(chunks, rows_chunk, col)
        value = router_part[pl.ds(t * col, col), :]
        buf[here, :, 4 * col :] = value.reshape(chunks, rows_chunk, value.shape[1])

    def add(target, place, first, count):
        def one(i, _):
            total = buf[place + i].astype(F32) + box[first + i].astype(F32)
            target[place + i] = total.astype(BF)
            return 0

        lax.fori_loop(0, count, one, 0)

    half = far_hbm.shape[1]
    owner = me // 2

    def far_copy(n, side, device):
        return remote(
            far_hbm.at[n], far_out.at[n, pl.ds(side * half, half), :],
            far_send.at[n], far_recv.at[n, side], device,
        )

    far_copies = [
        far_copy(n, core, {"expert": base + owner, "tensor": (me + 2) % blocks}) for n in range(3)
    ]
    copies = []
    ready()
    for n in range(2):
        products(2 * (1 - core) + n)
        for s in range(2 * n, 2 * n + 2):
            source = buf.at[pl.ds((1 - core) * 64 + s * 16, 16)]
            copies.append(post.push(source, box.at[pl.ds(31 * s, 16)], dims[0][1]))
    for copy in loads:
        copy.wait()
    for t in range(blocks):
        rows = slice(t * col, (t + 1) * col)
        parts[t] = (
            dot(d_qkv[:, 0:col], wq[rows, :], 1, 1)
            + dot(d_qkv[:, col : 2 * col], wk[rows, :], 1, 1)
            + dot(d_qkv[:, 2 * col : 3 * col], wv[rows, :], 1, 1)
        ).astype(BF)
    x_first = scatter_start(post_x, parts, x_halves, me)
    for n in range(2):
        products(2 * core + n)
    x_moved = scatter_relay(post_x, parts, x_halves, x_box, me, x_first)
    place = [core * 64 + s * 16 for s in range(4)]
    size, first = 16, 0

    def halve(k):
        for s in range(4):
            copies[s].wait_recv()
            add(buf, place[s], 31 * s + first, size)
            bit, partner = dims[ORDERS[s][k]]
            half = size // 2
            copies[s] = post.push(
                buf.at[pl.ds(place[s] + (1 - bit) * half, half)],
                box.at[pl.ds(31 * s + first + size, half)],
                partner,
            )
            place[s] = place[s] + bit * half

    halve(0)
    first, size = first + size, size // 2

    for t in range(blocks):
        y_parts[t] = dot(pick_y[...], ret_y[:, t * col : (t + 1) * col]).astype(BF)
    y_first = scatter_start(post_x, y_parts, y_halves, me)
    d_an = scatter_total(parts, x_box, me, x_moved)
    x_mine = x_all[me].astype(F32)
    grown = gain1[pl.ds(me, 1), :] * d_an
    mean_part = row_sum(x_mine * grown)
    note[me, 0:8, :] = jnp.broadcast_to(
        jnp.sum(d_an * x_mine * r1, axis=0, keepdims=True), (8, col)
    )
    note[me, 8:16, 0:tok] = jnp.broadcast_to(mean_part, (tok, 128)).T[0:8, :]
    note[me, 8:16, tok:] = jnp.broadcast_to(small_in[blocks : blocks + 1, : 2 * head], (8, 2 * head))
    note_in = [post_x.push(note.at[me], note.at[me], peer) for peer in peers]

    halve(1)
    far_copies[0].start()
    first, size = first + size, size // 2
    y_moved = scatter_relay(post_x, y_parts, y_halves, y_box, me, y_first)
    halve(2)
    first, size = first + size, size // 2
    halve(3)
    far_copies[1].start()
    first, size = first + size, size // 2
    shared = [[] for _ in range(4)]
    for s in range(4):
        copies[s].wait_recv()
        add(got, place[s], 31 * s + first, 1)
        here = got.at[pl.ds(place[s], 1)]
        copies[s] = post.push(here, here, dims[ORDERS[s][3]][1])
        shared[s].append(post.push(here, here, dims[0][1]))

    arrive(note_in)
    facts = note[0, 8:16, :]
    for t in range(1, blocks):
        facts = facts + note[t, 8:16, :]
    for t in range(blocks):
        small_out[t : t + 1, :] = note[t, 0:1, :]
        small_out[blocks + t : blocks + t + 1, :] = small_in[t : t + 1, :]
    small_out[2 * blocks :, :] = facts
    mean = jnp.broadcast_to(facts[0:1, 0:tok], (128, tok)).T[:, 0:1] * (1.0 / width)
    dx_out[...] = (d_mine[...] + r1 * grown - x_mine * (r1 * r1 * r1 * mean)).astype(BF)

    size = 1
    stores = []

    def keep(n, at):
        here = pl.ds(at, 16)
        for m, target in enumerate((q_out, k_out, v_out)):
            stores.append(
                pltpu.make_async_copy(
                    got.at[here, :, pl.ds(m * col, col)], target.at[here], out_sem.at[n, m]
                )
            )
            stores[-1].start()
        count = 16 * rows_chunk
        turned = got[here, :, 3 * col :].reshape(count, o_out.shape[0]).T
        o_out[:, pl.ds(pl.multiple_of(at * rows_chunk, 128), count)] = turned

    for k in range(3, -1, -1):
        for s in range(4):
            copies[s].wait_recv()
            bit, _ = dims[ORDERS[s][k]]
            come = got.at[pl.ds(place[s] + (1 - 2 * bit) * size, size)]
            place[s] = place[s] - bit * size
            if k:
                here = got.at[pl.ds(place[s], 2 * size)]
                copies[s] = post.push(here, here, dims[ORDERS[s][k - 1]][1])
            shared[s].append(post.push(come, come, dims[0][1]))
            if not k:
                keep(s, place[s])
        size *= 2
        if k == 3:
            far_copies[2].start()
        if k == 2:
            out_out[...] = (resid[...] + scatter_total(y_parts, y_box, me, y_moved)).astype(BF)
    for s in range(4):
        arrive(shared[s])
        keep(4 + s, (1 - core) * 64 + s * 16)
    post.finish()
    post_x.finish()
    for store in stores:
        store.wait()
    comes = (me + 2) % blocks // 2 == core
    for n in range(3):
        for side in range(2):
            pl.when(comes)(far_copy(n, side, {"expert": base + core, "tensor": (me + 2) % blocks}).wait_recv)
        far_copies[n].wait_send()


def reduce_call(d_qkv, dr, d_mine, router_part, small, x_all, gain1, ob, pick_y, ret_y, far, resid,
                weights):
    blocks, tok, col = x_all.shape
    width = blocks * col
    tiles = (blocks, tok, col)
    wide = (128, 16, 4 * col + 128)
    shape = jax.ShapeDtypeStruct
    vmem = pl.BlockSpec(memory_space=pltpu.VMEM)
    hbm = pl.BlockSpec(memory_space=pl.ANY)
    count = 8 + blocks - 1
    return pl.pallas_call(
        reduce_kernel,
        out_shape=(
            shape(wide[:2] + (col,), BF), shape(wide[:2] + (col,), BF), shape(wide[:2] + (col,), BF),
            shape((col + 128, width), BF),
            shape((tok, col), BF), shape((tok, col), BF), shape((16, col), F32),
            shape((far.shape[0], 2 * far.shape[1], far.shape[2]), BF),
        ),
        in_specs=[vmem] * 10 + [hbm] * 5,
        out_specs=(hbm,) * 3 + (vmem,) * 4 + (hbm,),
        scratch_shapes=[
            pltpu.VMEM((width, col), BF), pltpu.VMEM((width, col), BF), pltpu.VMEM((width, col), BF),
            pltpu.VMEM((tok, col), F32), pltpu.VMEM(tiles, BF), pltpu.VMEM(tiles, BF),
            pltpu.VMEM((4, tok // 2, col), BF), pltpu.VMEM((4, tok, col), BF),
            pltpu.VMEM((blocks, 16, col), F32),
            pltpu.VMEM(wide, BF), pltpu.VMEM((124,) + wide[1:], BF), pltpu.VMEM(wide, BF),
            pltpu.SemaphoreType.DMA((4,)), pltpu.SemaphoreType.DMA((8, 3)),
            pltpu.SemaphoreType.DMA((count,)), pltpu.SemaphoreType.DMA((count,)),
            pltpu.SemaphoreType.DMA((56,)), pltpu.SemaphoreType.DMA((56,)),
            pltpu.SemaphoreType.DMA((3,)), pltpu.SemaphoreType.DMA((3, 2)),
        ],
        compiler_params=pltpu.CompilerParams(
            collective_id=3, has_side_effects=True, vmem_limit_bytes=60 * 1024 * 1024
        ),
        cost_estimate=COST,
        name="reduce",
    )(d_qkv, dr, d_mine, router_part, small, x_all, gain1, ob, pick_y, ret_y, far, resid, *weights)


def body(
    tokens,
    out_grad,
    seq_lengths,
    dest_index,
    routes,
    pair_order,
    norm1_gain,
    w_query,
    w_key,
    w_value,
    q_gain,
    k_gain,
    w_output,
    norm2_gain,
    w_router,
    expert_w,
):
    groups = lax.axis_size("expert")
    tensor_count = lax.axis_size("tensor")
    group_id = lax.axis_index("expert")
    tensor_id = lax.axis_index("tensor")
    tok_count, col_count = tokens.shape
    width = col_count * tensor_count
    move_rows = tok_count // groups
    expert_count = w_router.shape[1]
    top_count = routes.shape[1]
    local_experts = expert_w.shape[0]

    w_stored = jnp.transpose(expert_w, (0, 2, 1, 3))
    w_first = near_weights(w_stored, 0)

    routes_t = routes.T
    order_t = pair_order[0].reshape(tok_count, top_count).T
    pair_expert = routes_t.reshape(-1)
    pair_total = tok_count * top_count
    base = pair_expert * pair_total
    keyed = base + order_t.reshape(-1)
    before = (keyed[None, :] < keyed[:, None]) & (keyed[None, :] >= base[:, None])
    ranks = jnp.sum(before.astype(jnp.int32), axis=1).reshape(top_count, tok_count)
    expert_axis = jnp.arange(expert_count, dtype=jnp.int32)
    route_hot = routes_t[:, None, :] == expert_axis[None, :, None]
    counts = jnp.sum(route_hot.astype(F32), axis=(0, 2))

    places = jnp.arange(tok_count, dtype=jnp.int32)
    arrival_rank = jnp.sum((dest_index[None, :] < dest_index[:, None]).astype(jnp.int32), axis=1)
    by_rank = (arrival_rank[None, :] == places[:, None]).astype(BF)
    inner = jnp.broadcast_to((dest_index % tok_count).astype(BF)[:, None], (tok_count, 64))
    facts = jnp.broadcast_to(counts.astype(BF)[None, :], (tok_count, expert_count))
    outgoing = dot(by_rank, jnp.concatenate([tokens, out_grad, inner, facts], axis=1)).astype(BF)
    got = exchange(outgoing.reshape(groups, move_rows, -1), "expert")
    all_counts = got[:, 0, 2 * col_count + 64 :].astype(jnp.int32)
    lower = jnp.arange(groups, dtype=jnp.int32) < group_id
    offsets = jnp.sum(jnp.where(lower[:, None], all_counts, 0), axis=0)
    mine = got[:, :, 2 * col_count].astype(jnp.int32).reshape(-1)
    put = (mine[None, :] == places[:, None]).astype(BF)
    local = dot(put, got.reshape(tok_count, -1)[:, : 2 * col_count]).astype(BF)
    capacity = 5 * tok_count * groups * top_count // (4 * expert_count)
    most_rows = 3 * tok_count * top_count // (2 * expert_count)
    per = most_rows // 2
    slots = groups * per
    slot_global = jnp.sum(jnp.where(route_hot, offsets[None, :, None], 0), axis=1) + ranks
    kept = slot_global < capacity
    keep_mask = kept.astype(F32)
    here = kept & (routes_t % tensor_count == tensor_id)
    owner = routes_t // tensor_count * 2 + ranks % 2
    slot_of = jnp.where(here, owner * per + ranks // 2, -1)

    seq_ids, positions = sequence_layout(seq_lengths[0], tok_count)
    bias = jnp.where(seq_ids[:, None] == seq_ids[None, :], 0.0, mask_fill)
    cos_tab, sin_tab = rope_tables(positions, q_gain.shape[0])
    cos_rows = jnp.concatenate([cos_tab, cos_tab], axis=1)
    sin_rows = jnp.concatenate([-sin_tab, sin_tab], axis=1)
    gain1 = norm1_gain.astype(F32).reshape(tensor_count, col_count)
    gain2 = norm2_gain.astype(F32).reshape(tensor_count, col_count)
    head_gains = (q_gain.astype(F32)[None], k_gain.astype(F32)[None])
    router = jnp.pad(w_router, ((0, 0), (0, 128 - expert_count)))
    weights = (w_query, w_key, w_value, w_output)
    def homeward(value):
        return exchange(value.reshape(groups, -1, value.shape[1]), "expert").reshape(value.shape)

    x_all, dy_all, send_dy = pre_call(local, slot_of, tensor_count, slots)
    send_dy, x_all, w_stored = lax.optimization_barrier((send_dy, x_all, w_stored))
    w_second = near_weights(w_stored, 1)
    recv_dy = homeward(send_dy)
    (
        resid, mixed, q_raw, k_raw, qh, kh, vh, attended, gates, send_rows, pick_t,
    ) = front_call(
        x_all, bias, cos_rows, sin_rows, gain1, gain2, *head_gains, router.T, routes_t, slot_of,
        keep_mask, weights, slots,
    )
    send_rows, w_stored, recv_dy = lax.optimization_barrier((send_rows, w_stored, recv_dy))
    recv_rows = homeward(send_rows)
    y_rows, d_rows, partial = expert_call(recv_rows, recv_dy, weights_call(w_stored, w_first, w_second))
    ret_rows = homeward(d_rows)
    near, far = home_call(partial)
    ret_rows, near, far, y_rows = lax.optimization_barrier((ret_rows, near, far, y_rows))
    ret_y = homeward(y_rows)
    d_qkv, dr, d_mine, router_part, small = back_call(
        pick_t, ret_rows, slot_of, keep_mask, gates, routes_t, bias, cos_rows,
        sin_rows, gain2, *head_gains, router, resid, dy_all, mixed, qh, kh, vh, q_raw, k_raw,
        w_output,
    )
    *wide, turned, dx_slice, out_slice, small, far = reduce_call(
        d_qkv, dr, d_mine, router_part, small, x_all, gain1, attended, pick_t, ret_y, far, resid,
        weights[:3],
    )

    going = dot(put, jnp.concatenate([out_slice, dx_slice], axis=1), 0, 0).astype(BF)
    small = small[:9].astype(BF).reshape(move_rows, -1)
    small = jnp.pad(small, ((0, 0), (0, -small.shape[1] % 128)))
    small = jnp.broadcast_to(small[None], (groups,) + small.shape)
    back = exchange(jnp.concatenate([going.reshape(groups, move_rows, -1), small], axis=2), "expert")
    small = jnp.sum(back[:, :, 2 * col_count :].astype(F32), axis=0)[:, : 9 * col_count // move_rows]
    small = small.reshape(-1)
    back = dot(by_rank, back.reshape(tok_count, -1)[:, : 2 * col_count], 0, 0).astype(BF)
    opposite = (tensor_id + 2) % tensor_count - 2 * (group_id % 2)
    is_far = jnp.arange(local_experts) == opposite
    expert_grad = jnp.where(is_far[:, None, None, None], far[None], near).astype(F32)
    expert_grad = jnp.transpose(expert_grad, (0, 2, 1, 3))
    wide = [value.reshape(width, -1) for value in wide]
    gain_at = 2 * width + tok_count
    head = q_gain.shape[0]
    return (
        back[:, :col_count],
        back[:, col_count:],
        small[:width],
        wide[0].astype(F32),
        wide[1].astype(F32),
        wide[2].astype(F32),
        small[gain_at : gain_at + head],
        small[gain_at + head : gain_at + 2 * head],
        turned[:col_count].astype(F32),
        small[width : 2 * width],
        turned[col_count : col_count + expert_count].astype(F32).T,
        expert_grad,
    )


def solution(mesh):
    in_specs = (
        P("expert", "tensor"),
        P("expert", "tensor"),
        P("expert", None),
        P("expert"),
        P("expert", None),
        P("expert", None),
        P(),
        P(None, "tensor"),
        P(None, "tensor"),
        P(None, "tensor"),
        P(),
        P(),
        P("tensor", None),
        P(),
        P(),
        P("expert", None, None, "tensor"),
    )
    out_specs = (
        P("expert", "tensor"),
        P("expert", "tensor"),
        P(),
        P(None, "tensor"),
        P(None, "tensor"),
        P(None, "tensor"),
        P(),
        P(),
        P("tensor", None),
        P(),
        P(),
        P("expert", None, None, "tensor"),
    )
    return jax.shard_map(body, mesh=mesh, in_specs=in_specs, out_specs=out_specs, check_vma=False)
```

```python
import functools
import math

import jax
import jax.numpy as jnp
from jax import lax
from jax.experimental import pallas as pl
from jax.experimental.pallas import tpu as pltpu
from jax.sharding import PartitionSpec as P

norm_eps = 1e-06
rope_base = 10000.0
mask_fill = -1e30


def rope_tables(positions, width):
    half_width = width // 2
    steps_idx = jnp.arange(half_width, dtype=jnp.float32)
    freqs = jnp.exp(steps_idx * (-2.0 * math.log(rope_base) / width))
    angles = positions.astype(jnp.float32)[:, None] * freqs[None, :]
    return (jnp.cos(angles), jnp.sin(angles))


def sequence_layout(lengths_row, count):
    seq_ends = jnp.cumsum(lengths_row)
    places = jnp.arange(count, dtype=jnp.int32)
    passed = (places[:, None] >= seq_ends[None, :]).astype(jnp.int32)
    seq_ids = jnp.sum(passed, axis=1)
    starts = jnp.sum(passed * lengths_row[None, :], axis=1)
    return (seq_ids, places - starts)


BF = jnp.bfloat16
F32 = jnp.float32
SHADOW = pl.CostEstimate(flops=40_000_000_000, bytes_accessed=1, transcendentals=0)
COST = pl.CostEstimate(flops=1, bytes_accessed=1, transcendentals=0)


def dot(left, right, left_dim=1, right_dim=0):
    return lax.dot_general(
        left, right, (((left_dim,), (right_dim,)), ((), ())), preferred_element_type=F32
    )


def exchange(value, axis):
    return lax.all_to_all(value, axis, split_axis=0, concat_axis=0, tiled=True)


def gather_blocks(value, axis):
    return exchange(jnp.broadcast_to(value[None], (lax.axis_size(axis),) + value.shape), axis)


def column_blocks(value, count):
    return jnp.stack(jnp.split(value, count, axis=1))


MESH = pl.DeviceIdType.MESH


def tensor_peers():
    me = lax.axis_index("tensor")
    count = lax.axis_size("tensor")
    return me, [(me + d) % count for d in range(1, count)]


def greet(axis, peers):
    barrier = pltpu.get_barrier_semaphore()
    for peer in peers:
        pl.semaphore_signal(barrier, inc=1, device_id={axis: peer}, device_id_type=MESH)
    return lambda: pl.semaphore_wait(barrier, len(peers))


class Post:
    def __init__(self, axis, send_sem, recv_sem):
        self.axis, self.send_sem, self.recv_sem = axis, send_sem, recv_sem
        self.started = []
        self.used = 0

    def push(self, source, target, peer):
        slot = self.used
        self.used += 1
        copy = pltpu.make_async_remote_copy(
            src_ref=source,
            dst_ref=target,
            send_sem=self.send_sem.at[slot],
            recv_sem=self.recv_sem.at[slot],
            device_id={self.axis: peer},
            device_id_type=MESH,
        )
        copy.start()
        self.started.append(copy)
        return copy

    def finish(self):
        for copy in self.started:
            copy.wait_send()
        self.started = []


def arrive(copies):
    for copy in copies:
        copy.wait_recv()


def ring(me):
    count = lax.axis_size("tensor")
    return (me + 1) % count, (me + count - 1) % count


def gather_start(post, ref, me):
    right, left = ring(me)
    return [post.push(ref.at[me], ref.at[me], peer) for peer in (right, left)]


def gather_relay(post, ref, me, first):
    right, left = ring(me)
    half = ref.shape[1] // 2
    first[0].wait_recv()
    here = ref.at[left, pl.ds(0, half)]
    one = post.push(here, here, right)
    first[1].wait_recv()
    here = ref.at[right, pl.ds(half, half)]
    return [one, post.push(here, here, left)]


def scatter_start(post, parts, halves, me):
    right, left = ring(me)
    far = ring(right)[0]
    half = parts.shape[1] // 2
    return [
        post.push(parts.at[far, pl.ds(0, half)], halves.at[0], right),
        post.push(parts.at[far, pl.ds(half, half)], halves.at[1], left),
    ]


def scatter_relay(post, parts, halves, box, me, first):
    right, left = ring(me)
    half = parts.shape[1] // 2
    copies = []
    for n, (peer, rows) in enumerate(((right, pl.ds(0, half)), (left, pl.ds(half, half)))):
        first[n].wait_recv()
        parts[peer, rows, :] = (parts[peer, rows, :].astype(F32) + halves[n].astype(F32)).astype(BF)
        copies.append(post.push(parts.at[peer], box.at[n], peer))
    return copies


def scatter_total(parts, box, me, copies):
    arrive(copies)
    return parts[me].astype(F32) + box[0].astype(F32) + box[1].astype(F32)


def fetch(pairs, sem):
    copies = [
        pltpu.make_async_copy(source, target, sem.at[n]) for n, (source, target) in enumerate(pairs)
    ]
    for copy in copies:
        copy.start()
    return copies


def turn(value, cos_rows, sin_rows):
    return value * cos_rows + pltpu.roll(value, value.shape[-1] // 2, 1) * sin_rows


def inverse_rms(total, width):
    return lax.rsqrt(total * (1.0 / width) + norm_eps)


def row_sum(value):
    return jnp.sum(value, axis=1, keepdims=True)


def softmax_rows(query, key, bias, scale):
    scores = dot(query, key, 1, 1) * scale + bias
    grown = jnp.exp(scores - jnp.max(scores, axis=1, keepdims=True))
    return grown / row_sum(grown)


def select_slots(slot_of, slots):
    top, tok = slot_of.shape
    slot = lax.broadcasted_iota(jnp.int32, (slots, tok), 0)
    pick = jnp.zeros((slots, tok), F32)
    for k in range(top):
        pick = jnp.where(slot_of[k : k + 1, :] == slot, 1.0, pick)
    return pick


def pre_kernel(local, slot_of, x_out, dy_out, send_out, x_all, dy_all, send_sem, recv_sem):
    me = lax.axis_index("tensor")
    ready = greet("tensor", ring(me))
    blocks, _, col = x_all.shape
    x_all[me] = local[:, :col]
    dy_all[me] = local[:, col:]
    ready()
    post = Post("tensor", send_sem, recv_sem)
    dy_in = gather_start(post, dy_all, me)
    x_in = gather_start(post, x_all, me)
    pick = select_slots(slot_of, send_out.shape[0]).astype(BF)
    dy_in = gather_relay(post, dy_all, me, dy_in)
    x_in = gather_relay(post, x_all, me, x_in)
    arrive(dy_in)
    dy_out[...] = dy_all[...]
    for t in range(blocks):
        send_out[:, t * col : (t + 1) * col] = dot(pick, dy_all[t]).astype(BF)
    arrive(x_in)
    x_out[...] = x_all[...]
    post.finish()


def pre_call(local, slot_of, blocks, slots):
    tok, both = local.shape
    col = both // 2
    tiles = (blocks, tok, col)
    shape = jax.ShapeDtypeStruct
    vmem = pl.BlockSpec(memory_space=pltpu.VMEM)
    return pl.pallas_call(
        pre_kernel,
        out_shape=(shape(tiles, BF), shape(tiles, BF), shape((slots, col * blocks), BF)),
        in_specs=[vmem] * 2,
        out_specs=(vmem,) * 3,
        scratch_shapes=[
            pltpu.VMEM(tiles, BF), pltpu.VMEM(tiles, BF),
            pltpu.SemaphoreType.DMA((8,)), pltpu.SemaphoreType.DMA((8,)),
        ],
        compiler_params=pltpu.CompilerParams(
            collective_id=6, has_side_effects=True, vmem_limit_bytes=63 * 1024 * 1024
        ),
        cost_estimate=COST,
        name="pre",
    )(local, slot_of)


def front_kernel(
    x_all, bias, cos_rows, sin_rows, gain1, gain2, q_gain, k_gain, router_t, routes, slot_of, keep,
    wq_hbm, wk_hbm, wv_hbm, wo_hbm,
    resid_out, mixed_out, q_out, k_out, qh_out, kh_out, vh_out, ob_out,
    gates_out, send_out, pick_out,
    wq, wk, wv, wo, an, parts, halves, box, total, load_sem, send_sem, recv_sem,
):
    me = lax.axis_index("tensor")
    ready = greet("tensor", ring(me))
    loads = fetch([(wq_hbm, wq), (wk_hbm, wk), (wv_hbm, wv), (wo_hbm, wo)], load_sem)
    blocks, tok, col = x_all.shape
    width = blocks * col
    post = Post("tensor", send_sem, recv_sem)
    square = jnp.zeros((tok, 1), F32)
    for t in range(blocks):
        value = x_all[t].astype(F32)
        square = square + row_sum(value * value)
    r1 = inverse_rms(square, width)
    for t in range(blocks):
        an[t] = (x_all[t].astype(F32) * r1 * gain1[t : t + 1, :]).astype(BF)

    for copy in loads:
        copy.wait()

    def project(weight):
        value = dot(an[0], weight[0:col, :])
        for t in range(1, blocks):
            value = value + dot(an[t], weight[t * col : (t + 1) * col, :])
        return value

    q_out[...] = project(wq)
    k_out[...] = project(wk)
    vh_out[...] = project(wv).astype(BF)
    head = q_gain.shape[1]
    scale = 1.0 / math.sqrt(head)
    for h in range(col // head):
        lanes = slice(h * head, (h + 1) * head)
        for raw, gain, rotated in ((q_out, q_gain, qh_out), (k_out, k_gain, kh_out)):
            value = raw[:, lanes]
            value = value * inverse_rms(row_sum(value * value), head) * gain[...]
            rotated[:, lanes] = turn(value, cos_rows[...], sin_rows[...]).astype(BF)
        probs = softmax_rows(qh_out[:, lanes], kh_out[:, lanes], bias[...], scale).astype(BF)
        ob_out[:, lanes] = dot(probs, vh_out[:, lanes]).astype(BF)
    for t in range(blocks):
        parts[t] = dot(ob_out[...], wo[:, t * col : (t + 1) * col]).astype(BF)
    ready()
    first = scatter_start(post, parts, halves, me)
    moved = scatter_relay(post, parts, halves, box, me, first)
    total[me] = scatter_total(parts, box, me, moved).astype(BF)
    arrive(gather_relay(post, total, me, gather_start(post, total, me)))
    square = jnp.zeros((tok, 1), F32)
    for t in range(blocks):
        value = x_all[t].astype(F32) + total[t].astype(F32)
        resid_out[t] = value
        square = square + row_sum(value * value)
    r2 = inverse_rms(square, width)
    logits = jnp.zeros((router_t.shape[0], tok), F32)
    for t in range(blocks):
        mixed_out[t] = (resid_out[t] * r2 * gain2[t : t + 1, :]).astype(BF)
        logits = logits + dot(router_t[:, t * col : (t + 1) * col], mixed_out[t], 1, 1)
    expert = lax.broadcasted_iota(jnp.int32, logits.shape, 0)
    top = routes.shape[0]
    chosen = [
        jnp.sum(jnp.where(routes[k : k + 1, :] == expert, logits, 0.0), axis=0, keepdims=True)
        for k in range(top)
    ]
    peak = functools.reduce(jnp.maximum, chosen)
    grown = [jnp.exp(value - peak) for value in chosen]
    whole = functools.reduce(jnp.add, grown)
    slots = send_out.shape[0]
    slot = lax.broadcasted_iota(jnp.int32, (slots, tok), 0)
    pick = jnp.zeros((slots, tok), F32)
    weight = jnp.zeros((slots, tok), F32)
    for k in range(top):
        gate = grown[k] / whole
        gates_out[k : k + 1, :] = gate
        hot = slot_of[k : k + 1, :] == slot
        pick = jnp.where(hot, 1.0, pick)
        weight = jnp.where(hot, gate * keep[k : k + 1, :], weight)
    pick_out[...] = pick.T.astype(BF)
    pick = pick.astype(BF)
    for t in range(blocks):
        send_out[:, t * col : (t + 1) * col] = dot(pick, mixed_out[t]).astype(BF)
    gate = row_sum(weight)
    first = gate.astype(BF)
    second = (gate - first.astype(F32)).astype(BF)
    third = (gate - first.astype(F32) - second.astype(F32)).astype(BF)
    lane = lax.broadcasted_iota(jnp.int32, (slots, 128), 1)
    facts = jnp.zeros((slots, 128), F32)
    for n, piece in enumerate((first, second, third)):
        facts = jnp.where(lane == n, piece.astype(F32), facts)
    send_out[:, width:] = facts.astype(BF)
    post.finish()


def front_call(x_all, bias, cos_rows, sin_rows, gain1, gain2, q_gain, k_gain, router_t, routes,
               slot_of, keep, weights, slots):
    blocks, tok, col = tiles = x_all.shape
    width = col * blocks
    shape = jax.ShapeDtypeStruct
    vmem = pl.BlockSpec(memory_space=pltpu.VMEM)
    top = routes.shape[0]
    return pl.pallas_call(
        front_kernel,
        out_shape=(
            shape(tiles, F32), shape(tiles, BF), shape((tok, col), F32), shape((tok, col), F32),
            shape((tok, col), BF), shape((tok, col), BF), shape((tok, col), BF),
            shape((tok, col), BF), shape((top, tok), F32), shape((slots, width + 128), BF),
            shape((tok, slots), BF),
        ),
        in_specs=[vmem] * 12 + [pl.BlockSpec(memory_space=pl.ANY)] * 4,
        out_specs=(vmem,) * 11,
        scratch_shapes=[
            pltpu.VMEM((width, col), BF), pltpu.VMEM((width, col), BF), pltpu.VMEM((width, col), BF),
            pltpu.VMEM((col, width), BF),
            pltpu.VMEM(tiles, BF), pltpu.VMEM(tiles, BF),
            pltpu.VMEM((2, tok // 2, col), BF), pltpu.VMEM((2, tok, col), BF), pltpu.VMEM(tiles, BF),
            pltpu.SemaphoreType.DMA((4,)),
            pltpu.SemaphoreType.DMA((8,)), pltpu.SemaphoreType.DMA((8,)),
        ],
        compiler_params=pltpu.CompilerParams(
            collective_id=1, has_side_effects=True, vmem_limit_bytes=63 * 1024 * 1024
        ),
        cost_estimate=SHADOW,
        name="front",
    )(x_all, bias, cos_rows, sin_rows, gain1, gain2, q_gain, k_gain, router_t, routes, slot_of,
      keep, *weights)


def back_kernel(
    pick_t, ret, slot_of, keep, gates, routes, bias, cos_rows, sin_rows, gain2,
    q_gain, k_gain, router, resid, dy_all, mixed, qh, kh, vh,
    q_hbm, k_hbm, wo_hbm,
    d_qkv, dr, d_mine, router_out, small_out,
    q_raw, k_raw, wo, parts, halves, box, total, dm, d_att, dg_mine, dg_box,
    load_sem, send_sem, recv_sem,
):
    me, peers = tensor_peers()
    ready = greet("tensor", peers)
    loads = fetch([(wo_hbm, wo), (q_hbm, q_raw), (k_hbm, k_raw)], load_sem)
    blocks, tok, col = parts.shape
    width = blocks * col
    post = Post("tensor", send_sem, recv_sem)
    for t in range(blocks):
        parts[t] = dot(pick_t[...], ret[:, t * col : (t + 1) * col]).astype(BF)
    ready()
    first = scatter_start(post, parts, halves, me)
    top = routes.shape[0]
    dgate = row_sum(ret[:, width:].astype(F32))
    slot = lax.broadcasted_iota(jnp.int32, (ret.shape[0], tok), 0)
    for k in range(top):
        hot = slot_of[k : k + 1, :] == slot
        dg_mine[k : k + 1, :] = jnp.sum(jnp.where(hot, dgate, 0.0), axis=0, keepdims=True)
    dg_in = [post.push(dg_mine, dg_box.at[d], peer) for d, peer in enumerate(peers)]
    moved = scatter_relay(post, parts, halves, box, me, first)
    total[me] = scatter_total(parts, box, me, moved).astype(BF)
    total_first = gather_start(post, total, me)

    arrive(dg_in)
    d_gates = dg_mine[...]
    for d in range(blocks - 1):
        d_gates = d_gates + dg_box[d]
    d_gates = d_gates * keep[...]
    gate = gates[...]
    d_chosen = gate * (d_gates - jnp.sum(gate * d_gates, axis=0, keepdims=True))
    expert = lax.broadcasted_iota(jnp.int32, (router.shape[1], tok), 0)
    d_logits_t = jnp.zeros(expert.shape, F32)
    for k in range(top):
        hot = routes[k : k + 1, :] == expert
        d_logits_t = jnp.where(hot, d_chosen[k : k + 1, :], d_logits_t)
    d_logits = d_logits_t.T.astype(BF)
    square = jnp.zeros((tok, 1), F32)
    for t in range(blocks):
        rows = slice(t * col, (t + 1) * col)
        dm[t] = dot(d_logits, router[rows, :], 1, 1)
        square = square + row_sum(resid[t] * resid[t])
    r2 = inverse_rms(square, width)
    total_moved = gather_relay(post, total, me, total_first)
    for t in range(blocks):
        rows = slice(t * col, (t + 1) * col)
        router_out[rows, :] = dot(mixed[t].T, d_logits).astype(BF)
    arrive(total_moved)
    cross = jnp.zeros((tok, 1), F32)
    for t in range(blocks):
        dm[t] = dm[t] + total[t].astype(F32)
        cross = cross + row_sum(resid[t] * gain2[t : t + 1, :] * dm[t])
    cross = cross * (1.0 / width) * r2 * r2 * r2
    small_out[...] = jnp.zeros_like(small_out)
    for t in range(blocks):
        d_mixed = dm[t]
        small_out[t : t + 1, :] = jnp.sum(d_mixed * resid[t] * r2, axis=0, keepdims=True)
        d_resid = dy_all[t].astype(F32) + r2 * gain2[t : t + 1, :] * d_mixed - resid[t] * cross
        dm[t] = d_resid
        dr[t] = d_resid.astype(BF)
    d_mine[...] = dm[me]
    for copy in loads:
        copy.wait()
    value = dot(dr[0], wo[:, 0:col], 1, 1)
    for t in range(1, blocks):
        value = value + dot(dr[t], wo[:, t * col : (t + 1) * col], 1, 1)
    d_att[...] = value.astype(BF)

    head = q_gain.shape[1]
    scale = 1.0 / math.sqrt(head)
    q_part = jnp.zeros((1, head), F32)
    k_part = jnp.zeros((1, head), F32)

    def unturn(grown, raw, gain):
        d_unit = grown * cos_rows[...] - pltpu.roll(grown, head // 2, 1) * sin_rows[...]
        inverse = inverse_rms(row_sum(raw * raw), head)
        unit = raw * inverse
        gain_part = jnp.sum(d_unit * unit, axis=0, keepdims=True)
        d_unit = d_unit * gain[...]
        d_raw = inverse * (d_unit - unit * (row_sum(unit * d_unit) * (1.0 / head)))
        return d_raw.astype(BF), gain_part

    for h in range(col // head):
        lanes = slice(h * head, (h + 1) * head)
        probs = softmax_rows(qh[:, lanes], kh[:, lanes], bias[...], scale)
        d_head = d_att[:, lanes]
        d_probs = dot(d_head, vh[:, lanes], 1, 1)
        d_scores = probs * (d_probs - row_sum(probs * d_probs))
        d_qkv[:, 2 * col + h * head : 2 * col + (h + 1) * head] = dot(
            probs.T.astype(BF), d_head
        ).astype(BF)
        d_q, part = unturn(dot(d_scores.astype(BF), kh[:, lanes]) * scale, q_raw[:, lanes], q_gain)
        q_part = q_part + part
        d_qkv[:, lanes] = d_q
        d_k, part = unturn(dot(d_scores.T.astype(BF), qh[:, lanes]) * scale, k_raw[:, lanes], k_gain)
        k_part = k_part + part
        d_qkv[:, col + h * head : col + (h + 1) * head] = d_k
    small_out[blocks : blocks + 1, :head] = q_part
    small_out[blocks : blocks + 1, head : 2 * head] = k_part
    post.finish()


def back_call(pick_t, ret, slot_of, keep, gates, routes, bias, cos_rows, sin_rows,
              gain2, q_gain, k_gain, router, resid, dy_all, mixed, qh, kh, vh, q_raw, k_raw, wo):
    blocks, tok, col = dy_all.shape
    width = blocks * col
    tiles = (blocks, tok, col)
    shape = jax.ShapeDtypeStruct
    vmem = pl.BlockSpec(memory_space=pltpu.VMEM)
    top = routes.shape[0]
    count = 8 + blocks - 1
    return pl.pallas_call(
        back_kernel,
        out_shape=(
            shape((tok, 3 * col), BF), shape(tiles, BF), shape((tok, col), F32),
            shape((width, 128), BF), shape((8, col), F32),
        ),
        in_specs=[vmem] * 19 + [pl.BlockSpec(memory_space=pl.ANY)] * 3,
        out_specs=(vmem,) * 5,
        scratch_shapes=[
            pltpu.VMEM((tok, col), F32), pltpu.VMEM((tok, col), F32), pltpu.VMEM((col, width), BF),
            pltpu.VMEM(tiles, BF), pltpu.VMEM((2, tok // 2, col), BF), pltpu.VMEM((2, tok, col), BF),
            pltpu.VMEM(tiles, BF), pltpu.VMEM(tiles, F32), pltpu.VMEM((tok, col), BF),
            pltpu.VMEM((top, tok), F32), pltpu.VMEM((blocks - 1, top, tok), F32),
            pltpu.SemaphoreType.DMA((3,)),
            pltpu.SemaphoreType.DMA((count,)), pltpu.SemaphoreType.DMA((count,)),
        ],
        compiler_params=pltpu.CompilerParams(
            collective_id=2, has_side_effects=True, vmem_limit_bytes=63 * 1024 * 1024
        ),
        cost_estimate=pl.CostEstimate(
            flops=20_000_000_000, bytes_accessed=1, transcendentals=0
        ),
        name="back",
    )(pick_t, ret, slot_of, keep, gates, routes, bias, cos_rows, sin_rows, gain2,
      q_gain, k_gain, router, resid, dy_all, mixed, qh, kh, vh, q_raw, k_raw, wo)


def octet():
    me = lax.axis_index("expert")
    core = me % 2
    return me - core, core, lax.axis_index("tensor")


def octet_others(base, core, rank):
    count = lax.axis_size("tensor")
    others = [{"expert": base + core, "tensor": (rank + d) % count} for d in range(1, count)]
    return others + [
        {"expert": base + 1 - core, "tensor": (rank + d) % count} for d in range(count)
    ]


def meet(others):
    barrier = pltpu.get_barrier_semaphore()
    for other in others:
        pl.semaphore_signal(barrier, inc=1, device_id=other, device_id_type=MESH)
    return lambda: pl.semaphore_wait(barrier, len(others))


def remote(source, target, send_sem, recv_sem, device):
    return pltpu.make_async_remote_copy(
        src_ref=source, dst_ref=target, send_sem=send_sem, recv_sem=recv_sem, device_id=device,
        device_id_type=MESH,
    )


def weights_kernel(
    w, first, second, out, near, own, load_sem, near_sem, send_sem, recv_sem, pass_send, pass_recv
):
    base, core, rank = octet()
    ready = meet(octet_others(base, core, rank))
    ranks = out.shape[0]
    half = out.shape[2] // 2
    sibling = {"expert": base + 1 - core, "tensor": rank}
    side = rank % 2
    target = 2 * core + side
    own_chip = target == rank

    def part(ref, index, which):
        return ref.at[index, :, pl.ds(which * half, half), :]

    mine = 1 - (rank // 2 + core) % 2
    loads = fetch([(first, near.at[0]), (second, near.at[1])], load_sem)
    own_loads, own_stores = [], []
    for k in range(2):
        own_loads.append(pltpu.make_async_copy(part(w, side, k), own.at[k], load_sem.at[2 + k]))
        own_stores.append(pltpu.make_async_copy(own.at[k], part(out, rank, k), near_sem.at[2 + k]))
        pl.when(own_chip)(own_loads[k].start)
    ready()
    sends = []
    for k in range(2):
        device = {"expert": base + mine * (1 - core) + (1 - mine) * k, "tensor": target}
        arrives = recv_sem.at[1 - mine, mine * k]
        sends.append(remote(part(w, side, k), part(out, rank, k), send_sem.at[k], arrives, device))
        sends[k].start()
    offsets = (3 - 2 * core, 1 + 2 * core)
    stores, passed = [], []
    for n in range(2):
        d = offsets[n]
        place = part(out, (rank + d) % ranks, core)
        loads[n].wait()
        passed.append(remote(near.at[n], place, pass_send.at[d], pass_recv.at[d], sibling))
        passed[-1].start()
        stores.append(pltpu.make_async_copy(near.at[n], place, near_sem.at[n]))
        stores[-1].start()

    @pl.when(own_chip)
    def _():
        for k in range(2):
            own_loads[k].wait()
            own_stores[k].start()

    far = part(out, (rank + 2) % ranks, core)
    remote(far, far, send_sem.at[0], recv_sem.at[1, 0], sibling).wait_recv()
    passed.append(remote(far, far, pass_send.at[2], pass_recv.at[2], sibling))
    passed[-1].start()
    for k in range(2):
        theirs = part(out, rank, k)
        arrival = remote(theirs, theirs, send_sem.at[k], recv_sem.at[0, k], sibling)
        pl.when(jnp.logical_not(own_chip))(arrival.wait_recv)
        pl.when(own_chip)(own_stores[k].wait)
    for d in range(1, ranks):
        theirs = part(out, (rank + d) % ranks, 1 - core)
        remote(theirs, theirs, pass_send.at[d], pass_recv.at[d], sibling).wait_recv()
    for copy in passed + sends:
        copy.wait_send()
    for copy in stores:
        copy.wait()


def weights_call(w, first, second):
    _, three, width, hidden = w.shape
    hbm = pl.BlockSpec(memory_space=pl.ANY)
    sems = pltpu.SemaphoreType.DMA((4,))
    halves = pltpu.VMEM((2, three, width // 2, hidden), BF)
    return pl.pallas_call(
        weights_kernel,
        out_shape=jax.ShapeDtypeStruct((4, three, width, hidden), BF),
        in_specs=[hbm] * 3,
        out_specs=hbm,
        scratch_shapes=[
            halves, halves, sems, sems, pltpu.SemaphoreType.DMA((2,)),
            pltpu.SemaphoreType.DMA((2, 2)), sems, sems,
        ],
        compiler_params=pltpu.CompilerParams(
            collective_id=4, has_side_effects=True, vmem_limit_bytes=63 * 1024 * 1024
        ),
        cost_estimate=SHADOW,
        name="weights",
    )(w, first, second)


def near_weights(w, turn_over):
    ranks, places = lax.axis_size("tensor"), lax.axis_size("expert")
    half = w.shape[2] // 2
    core, rank = lax.axis_index("expert") % 2, lax.axis_index("tensor")
    side = 1 - rank % 2
    to_core = jnp.where(2 * core + side == (rank + 1) % ranks, turn_over, 1 - turn_over)
    piece = lax.dynamic_slice(w, (side, 0, to_core * half, 0), (1, w.shape[1], half, w.shape[3]))
    pairs = []
    for place in range(places):
        for t in range(ranks):
            target = 2 * (place % 2) + 1 - t % 2
            core_of = (0 if target == (t + 1) % ranks else 1) ^ turn_over
            pairs.append((place * ranks + t, (place - place % 2 + core_of) * ranks + target))
    return lax.ppermute(piece[0], ("expert", "tensor"), pairs)


def home_kernel(grads, out, far_out, own, got, load_sem, local_sem, swap_send, swap_recv, send_sem, recv_sem):
    base, core, rank = octet()
    ready = meet(octet_others(base, core, rank))
    ranks, three, half, hidden = own.shape
    sibling = {"expert": base + 1 - core, "tensor": rank}
    order = (1, 3, 0, 2)
    loads, swaps = [], []
    for d in order:
        quarter = (rank + d) % ranks
        source = grads.at[quarter, :, pl.ds(core * half, half), :]
        loads.append(pltpu.make_async_copy(source, own.at[d], load_sem.at[d]))
        loads[-1].start()
    ready()
    for d in order:
        quarter = (rank + d) % ranks
        source = grads.at[quarter, :, pl.ds((1 - core) * half, half), :]
        swaps.append(remote(source, got.at[d], swap_send.at[d], swap_recv.at[d], sibling))
        swaps[-1].start()
    owner = rank // 2
    side = rank - 2 * owner
    rows = 64
    place = out.at[side, :, pl.ds(core * half, half), :]
    stays = owner == core
    sends = []
    for n, d in enumerate(order):
        loads[n].wait()
        swaps[n].wait_recv()

        def one(i, _, d=d):
            c, at = i // (half // rows), i % (half // rows) * rows
            here = pl.ds(pl.multiple_of(at, rows), rows)
            value = own[d, c, here, :].astype(F32) + got[d, c, here, :].astype(F32)
            own[d, c, here, :] = value.astype(BF)
            return 0

        lax.fori_loop(0, three * (half // rows), one, 0)
        if d == 2:
            far = pltpu.make_async_copy(own.at[d], far_out, load_sem.at[d])
            far.start()
            continue
        away = remote(
            own.at[d], place, send_sem.at[d], recv_sem.at[2 * side + core],
            {"expert": base + owner, "tensor": (rank + d) % ranks},
        )
        if d:
            away.start()
        else:
            kept = pltpu.make_async_copy(own.at[d], place, local_sem)
            pl.when(stays)(kept.start)
            pl.when(jnp.logical_not(stays))(away.start)
        sends.append((d, away))
    for s in range(2):
        for k in range(2):
            off = (2 * core + s - rank) % ranks
            mine = out.at[s, :, pl.ds(k * half, half), :]
            arrival = remote(own.at[0], mine, send_sem.at[0], recv_sem.at[2 * s + k], sibling)
            own_chip = off == 0
            comes = (off != 2) & jnp.logical_not(own_chip & (core == k))
            pl.when(comes)(arrival.wait_recv)
    pl.when(stays)(kept.wait)
    for d, away in sends:
        if d:
            away.wait_send()
        else:
            pl.when(jnp.logical_not(stays))(away.wait_send)
    for swap in swaps:
        swap.wait_send()
    far.wait()


def home_call(grads):
    ranks, three, width, hidden = grads.shape
    hbm = pl.BlockSpec(memory_space=pl.ANY)
    sems = pltpu.SemaphoreType.DMA((4,))
    halves = pltpu.VMEM((ranks, three, width // 2, hidden), BF)
    shape = jax.ShapeDtypeStruct
    return pl.pallas_call(
        home_kernel,
        out_shape=(
            shape((2, three, width, hidden), BF), shape((three, width // 2, hidden), BF),
        ),
        in_specs=[hbm],
        out_specs=(hbm, hbm),
        scratch_shapes=[
            halves, halves, sems, pltpu.SemaphoreType.DMA, sems, sems, sems, sems,
        ],
        compiler_params=pltpu.CompilerParams(
            collective_id=5, has_side_effects=True, vmem_limit_bytes=63 * 1024 * 1024
        ),
        cost_estimate=SHADOW,
        name="home",
    )(grads)


def expert_kernel(rows_ref, dys, w_ref, y_ref, dx_ref, grad_ref, rows_t, dys_t, y_acc, dx_acc, gate_of, dgate):
    step = pl.program_id(0)
    width = y_acc.shape[1]
    rows = rows_ref.at[:, :width]

    @pl.when(step == 0)
    def _():
        gate_of[...] = row_sum(rows_ref[:, width:].astype(F32))
        rows_t[...] = rows[...].T
        dys_t[...] = (dys[...].astype(F32) * gate_of[...]).astype(BF).T
        dgate[...] = jnp.zeros_like(dgate)
        y_acc[...] = jnp.zeros_like(y_acc)
        dx_acc[...] = jnp.zeros_like(dx_acc)

    w_gate, w_up, w_down = w_ref[0, 0], w_ref[0, 1], w_ref[0, 2]
    gate = dot(rows[...], w_gate)
    up = dot(rows[...], w_up)
    d_raw = dot(dys[...], w_down)
    d_act = d_raw * gate_of[...]
    sig = 1.0 / (1.0 + jnp.exp(-gate))
    silu = gate * sig
    act = (silu * up).astype(BF)
    dgate[...] += row_sum(act.astype(F32) * d_raw)
    d_gate = (d_act * up * sig * (1.0 + gate * (1.0 - sig))).astype(BF)
    d_up = (d_act * silu).astype(BF)
    y_acc[...] += dot(act, w_down, 1, 1)
    dx_acc[...] += dot(d_gate, w_gate, 1, 1) + dot(d_up, w_up, 1, 1)
    grad_ref[0, 0] = dot(rows_t[...], d_gate).astype(BF)
    grad_ref[0, 1] = dot(rows_t[...], d_up).astype(BF)
    grad_ref[0, 2] = dot(dys_t[...], act).astype(BF)

    @pl.when(step == pl.num_programs(0) - 1)
    def _():
        first = dgate[...].astype(BF).astype(F32)
        lane = lax.broadcasted_iota(jnp.int32, (y_ref.shape[0], 128), 1)
        facts = jnp.where(lane == 0, first, jnp.where(lane == 1, dgate[...] - first, 0.0))
        y_ref[...] = (y_acc[...] * gate_of[...]).astype(BF)
        dx_ref[:, :width] = dx_acc[...].astype(BF)
        dx_ref[:, width:] = facts.astype(BF)


def expert_call(rows, dys, weights):
    quarters, _, width, hidden = weights.shape
    count = rows.shape[0]
    shape = jax.ShapeDtypeStruct

    def whole(value):
        return pl.BlockSpec(value.shape, lambda q: (0, 0), pipeline_mode=pl.Buffered(1))

    block = pl.BlockSpec((1, 3, width, hidden), lambda q: (q, 0, 0, 0))
    outs = [shape((count, width), BF), shape((count, width + 128), BF)]
    return pl.pallas_call(
        expert_kernel,
        grid=(quarters,),
        out_shape=tuple(outs) + (shape(weights.shape, BF),),
        in_specs=[whole(rows), whole(dys), block],
        out_specs=tuple(whole(value) for value in outs) + (block,),
        scratch_shapes=[
            pltpu.VMEM((width, count), BF),
            pltpu.VMEM((width, count), BF),
            pltpu.VMEM((count, width), F32),
            pltpu.VMEM((count, width), F32),
            pltpu.VMEM((count, 1), F32),
            pltpu.VMEM((count, 1), F32),
        ],
        compiler_params=pltpu.CompilerParams(vmem_limit_bytes=63 * 1024 * 1024),
        cost_estimate=COST,
        name="expert",
    )(rows, dys, weights)


def plane():
    me = lax.axis_index("expert")
    core, z, y = me % 2, (me // 2) % 4, me // 8
    return [
        (core, me + 1 - 2 * core),
        ((y + y // 2) % 2, me + 8 * (1 - 2 * (y % 2))),
        (y // 2, me + 8 * (3 - 2 * y)),
        ((z + z // 2) % 2, me + 2 * (1 - 2 * (z % 2))),
        (z // 2, me + 2 * (3 - 2 * z)),
    ]

ORDERS = ((1, 3, 2, 4), (3, 2, 4, 1), (2, 4, 1, 3), (4, 1, 3, 2))

def reduce_kernel(
    d_qkv, dr, d_mine, router_part, small_in, x_all, gain1, ob, pick_y, ret_y,
    far_hbm, resid_hbm, wq_hbm, wk_hbm, wv_hbm,
    q_out, k_out, v_out, o_out, dx_out, out_out, small_out, far_out,
    wq, wk, wv, resid, parts, y_parts, halves, box_x, note, buf, box, got,
    load_sem, out_sem, x_send, x_recv, send_sem, recv_sem, far_send, far_recv,
):
    me, peers = tensor_peers()
    dims = plane()
    base, core, _ = octet()
    ready = meet(octet_others(base, core, me) + [{"expert": partner} for _, partner in dims[1:]])
    loads = fetch(
        [(wq_hbm, wq), (wk_hbm, wk), (wv_hbm, wv), (resid_hbm.at[me], resid)], load_sem
    )
    blocks, tok, col = x_all.shape
    width = blocks * col
    head = col // blocks
    square = jnp.zeros((tok, 1), F32)
    for t in range(blocks):
        value = x_all[t].astype(F32)
        square = square + row_sum(value * value)
    r1 = inverse_rms(square, width)
    post_x = Post("tensor", x_send, x_recv)
    post = Post("expert", send_sem, recv_sem)
    x_halves, x_box = halves.at[pl.ds(0, 2)], box_x.at[pl.ds(0, 2)]
    y_halves, y_box = halves.at[pl.ds(2, 2)], box_x.at[pl.ds(2, 2)]
    chunks = buf.shape[0] // blocks
    rows_chunk = buf.shape[1]

    def products(t):
        here = pl.ds(t * chunks, chunks)
        normed = (x_all[t].astype(F32) * r1 * gain1[pl.ds(t, 1), :]).T.astype(BF)
        for n in range(3):
            lanes = slice(n * col, (n + 1) * col)
            value = dot(normed, d_qkv[:, lanes]).astype(BF)
            buf[here, :, lanes] = value.reshape(chunks, rows_chunk, col)
        value = dot(dr[t].T, ob[...]).astype(BF)
        buf[here, :, 3 * col : 4 * col] = value.reshape(chunks, rows_chunk, col)
        value = router_part[pl.ds(t * col, col), :]
        buf[here, :, 4 * col :] = value.reshape(chunks, rows_chunk, value.shape[1])

    def add(target, place, first, count):
        def one(i, _):
            total = buf[place + i].astype(F32) + box[first + i].astype(F32)
            target[place + i] = total.astype(BF)
            return 0

        lax.fori_loop(0, count, one, 0)

    half = far_hbm.shape[1]
    owner = me // 2

    def far_copy(n, side, device):
        return remote(
            far_hbm.at[n], far_out.at[n, pl.ds(side * half, half), :],
            far_send.at[n], far_recv.at[n, side], device,
        )

    far_copies = [
        far_copy(n, core, {"expert": base + owner, "tensor": (me + 2) % blocks}) for n in range(3)
    ]
    copies = []
    ready()
    for n in range(2):
        products(2 * (1 - core) + n)
        for s in range(2 * n, 2 * n + 2):
            source = buf.at[pl.ds((1 - core) * 64 + s * 16, 16)]
            copies.append(post.push(source, box.at[pl.ds(31 * s, 16)], dims[0][1]))
    for copy in loads:
        copy.wait()
    for t in range(blocks):
        rows = slice(t * col, (t + 1) * col)
        parts[t] = (
            dot(d_qkv[:, 0:col], wq[rows, :], 1, 1)
            + dot(d_qkv[:, col : 2 * col], wk[rows, :], 1, 1)
            + dot(d_qkv[:, 2 * col : 3 * col], wv[rows, :], 1, 1)
        ).astype(BF)
    x_first = scatter_start(post_x, parts, x_halves, me)
    for n in range(2):
        products(2 * core + n)
    x_moved = scatter_relay(post_x, parts, x_halves, x_box, me, x_first)
    place = [core * 64 + s * 16 for s in range(4)]
    size, first = 16, 0

    def halve(k):
        for s in range(4):
            copies[s].wait_recv()
            add(buf, place[s], 31 * s + first, size)
            bit, partner = dims[ORDERS[s][k]]
            half = size // 2
            copies[s] = post.push(
                buf.at[pl.ds(place[s] + (1 - bit) * half, half)],
                box.at[pl.ds(31 * s + first + size, half)],
                partner,
            )
            place[s] = place[s] + bit * half

    halve(0)
    first, size = first + size, size // 2

    for t in range(blocks):
        y_parts[t] = dot(pick_y[...], ret_y[:, t * col : (t + 1) * col]).astype(BF)
    y_first = scatter_start(post_x, y_parts, y_halves, me)
    d_an = scatter_total(parts, x_box, me, x_moved)
    x_mine = x_all[me].astype(F32)
    grown = gain1[pl.ds(me, 1), :] * d_an
    mean_part = row_sum(x_mine * grown)
    note[me, 0:8, :] = jnp.broadcast_to(
        jnp.sum(d_an * x_mine * r1, axis=0, keepdims=True), (8, col)
    )
    note[me, 8:16, 0:tok] = jnp.broadcast_to(mean_part, (tok, 128)).T[0:8, :]
    note[me, 8:16, tok:] = jnp.broadcast_to(small_in[blocks : blocks + 1, : 2 * head], (8, 2 * head))
    note_in = [post_x.push(note.at[me], note.at[me], peer) for peer in peers]

    halve(1)
    far_copies[0].start()
    first, size = first + size, size // 2
    y_moved = scatter_relay(post_x, y_parts, y_halves, y_box, me, y_first)
    halve(2)
    first, size = first + size, size // 2
    halve(3)
    far_copies[1].start()
    first, size = first + size, size // 2
    shared = [[] for _ in range(4)]
    for s in range(4):
        copies[s].wait_recv()
        add(got, place[s], 31 * s + first, 1)
        here = got.at[pl.ds(place[s], 1)]
        copies[s] = post.push(here, here, dims[ORDERS[s][3]][1])
        shared[s].append(post.push(here, here, dims[0][1]))

    arrive(note_in)
    facts = note[0, 8:16, :]
    for t in range(1, blocks):
        facts = facts + note[t, 8:16, :]
    for t in range(blocks):
        small_out[t : t + 1, :] = note[t, 0:1, :]
        small_out[blocks + t : blocks + t + 1, :] = small_in[t : t + 1, :]
    small_out[2 * blocks :, :] = facts
    mean = jnp.broadcast_to(facts[0:1, 0:tok], (128, tok)).T[:, 0:1] * (1.0 / width)
    dx_out[...] = (d_mine[...] + r1 * grown - x_mine * (r1 * r1 * r1 * mean)).astype(BF)

    size = 1
    stores = []

    def keep(n, at):
        here = pl.ds(at, 16)
        for m, target in enumerate((q_out, k_out, v_out)):
            stores.append(
                pltpu.make_async_copy(
                    got.at[here, :, pl.ds(m * col, col)], target.at[here], out_sem.at[n, m]
                )
            )
            stores[-1].start()
        count = 16 * rows_chunk
        turned = got[here, :, 3 * col :].reshape(count, o_out.shape[0]).T
        o_out[:, pl.ds(pl.multiple_of(at * rows_chunk, 128), count)] = turned

    for k in range(3, -1, -1):
        for s in range(4):
            copies[s].wait_recv()
            bit, _ = dims[ORDERS[s][k]]
            come = got.at[pl.ds(place[s] + (1 - 2 * bit) * size, size)]
            place[s] = place[s] - bit * size
            if k:
                here = got.at[pl.ds(place[s], 2 * size)]
                copies[s] = post.push(here, here, dims[ORDERS[s][k - 1]][1])
            shared[s].append(post.push(come, come, dims[0][1]))
            if not k:
                keep(s, place[s])
        size *= 2
        if k == 3:
            far_copies[2].start()
        if k == 2:
            out_out[...] = (resid[...] + scatter_total(y_parts, y_box, me, y_moved)).astype(BF)
    for s in range(4):
        arrive(shared[s])
        keep(4 + s, (1 - core) * 64 + s * 16)
    post.finish()
    post_x.finish()
    for store in stores:
        store.wait()
    comes = (me + 2) % blocks // 2 == core
    for n in range(3):
        for side in range(2):
            pl.when(comes)(far_copy(n, side, {"expert": base + core, "tensor": (me + 2) % blocks}).wait_recv)
        far_copies[n].wait_send()


def reduce_call(d_qkv, dr, d_mine, router_part, small, x_all, gain1, ob, pick_y, ret_y, far, resid,
                weights):
    blocks, tok, col = x_all.shape
    width = blocks * col
    tiles = (blocks, tok, col)
    wide = (128, 16, 4 * col + 128)
    shape = jax.ShapeDtypeStruct
    vmem = pl.BlockSpec(memory_space=pltpu.VMEM)
    hbm = pl.BlockSpec(memory_space=pl.ANY)
    count = 8 + blocks - 1
    return pl.pallas_call(
        reduce_kernel,
        out_shape=(
            shape(wide[:2] + (col,), BF), shape(wide[:2] + (col,), BF), shape(wide[:2] + (col,), BF),
            shape((col + 128, width), BF),
            shape((tok, col), BF), shape((tok, col), BF), shape((16, col), F32),
            shape((far.shape[0], 2 * far.shape[1], far.shape[2]), BF),
        ),
        in_specs=[vmem] * 10 + [hbm] * 5,
        out_specs=(hbm,) * 3 + (vmem,) * 4 + (hbm,),
        scratch_shapes=[
            pltpu.VMEM((width, col), BF), pltpu.VMEM((width, col), BF), pltpu.VMEM((width, col), BF),
            pltpu.VMEM((tok, col), F32), pltpu.VMEM(tiles, BF), pltpu.VMEM(tiles, BF),
            pltpu.VMEM((4, tok // 2, col), BF), pltpu.VMEM((4, tok, col), BF),
            pltpu.VMEM((blocks, 16, col), F32),
            pltpu.VMEM(wide, BF), pltpu.VMEM((124,) + wide[1:], BF), pltpu.VMEM(wide, BF),
            pltpu.SemaphoreType.DMA((4,)), pltpu.SemaphoreType.DMA((8, 3)),
            pltpu.SemaphoreType.DMA((count,)), pltpu.SemaphoreType.DMA((count,)),
            pltpu.SemaphoreType.DMA((56,)), pltpu.SemaphoreType.DMA((56,)),
            pltpu.SemaphoreType.DMA((3,)), pltpu.SemaphoreType.DMA((3, 2)),
        ],
        compiler_params=pltpu.CompilerParams(
            collective_id=3, has_side_effects=True, vmem_limit_bytes=63 * 1024 * 1024
        ),
        cost_estimate=COST,
        name="reduce",
    )(d_qkv, dr, d_mine, router_part, small, x_all, gain1, ob, pick_y, ret_y, far, resid, *weights)


def body(
    tokens,
    out_grad,
    seq_lengths,
    dest_index,
    routes,
    pair_order,
    norm1_gain,
    w_query,
    w_key,
    w_value,
    q_gain,
    k_gain,
    w_output,
    norm2_gain,
    w_router,
    expert_w,
):
    groups = lax.axis_size("expert")
    tensor_count = lax.axis_size("tensor")
    group_id = lax.axis_index("expert")
    tensor_id = lax.axis_index("tensor")
    tok_count, col_count = tokens.shape
    width = col_count * tensor_count
    move_rows = tok_count // groups
    expert_count = w_router.shape[1]
    top_count = routes.shape[1]
    local_experts = expert_w.shape[0]

    w_stored = jnp.transpose(expert_w, (0, 2, 1, 3))
    w_first = near_weights(w_stored, 0)

    routes_t = routes.T
    order_t = pair_order[0].reshape(tok_count, top_count).T
    pair_expert = routes_t.reshape(-1)
    pair_total = tok_count * top_count
    base = pair_expert * pair_total
    keyed = base + order_t.reshape(-1)
    before = (keyed[None, :] < keyed[:, None]) & (keyed[None, :] >= base[:, None])
    ranks = jnp.sum(before.astype(jnp.int32), axis=1).reshape(top_count, tok_count)
    expert_axis = jnp.arange(expert_count, dtype=jnp.int32)
    route_hot = routes_t[:, None, :] == expert_axis[None, :, None]
    counts = jnp.sum(route_hot.astype(F32), axis=(0, 2))

    places = jnp.arange(tok_count, dtype=jnp.int32)
    arrival_rank = jnp.sum((dest_index[None, :] < dest_index[:, None]).astype(jnp.int32), axis=1)
    by_rank = (arrival_rank[None, :] == places[:, None]).astype(BF)
    inner = jnp.broadcast_to((dest_index % tok_count).astype(BF)[:, None], (tok_count, 64))
    facts = jnp.broadcast_to(counts.astype(BF)[None, :], (tok_count, expert_count))
    outgoing = dot(by_rank, jnp.concatenate([tokens, out_grad, inner, facts], axis=1)).astype(BF)
    got = exchange(outgoing.reshape(groups, move_rows, -1), "expert")
    all_counts = got[:, 0, 2 * col_count + 64 :].astype(jnp.int32)
    lower = jnp.arange(groups, dtype=jnp.int32) < group_id
    offsets = jnp.sum(jnp.where(lower[:, None], all_counts, 0), axis=0)
    mine = got[:, :, 2 * col_count].astype(jnp.int32).reshape(-1)
    put = (mine[None, :] == places[:, None]).astype(BF)
    local = dot(put, got.reshape(tok_count, -1)[:, : 2 * col_count]).astype(BF)
    capacity = 5 * tok_count * groups * top_count // (4 * expert_count)
    most_rows = 3 * tok_count * top_count // (2 * expert_count)
    per = most_rows // 2
    slots = groups * per
    slot_global = jnp.sum(jnp.where(route_hot, offsets[None, :, None], 0), axis=1) + ranks
    kept = slot_global < capacity
    keep_mask = kept.astype(F32)
    here = kept & (routes_t % tensor_count == tensor_id)
    owner = routes_t // tensor_count * 2 + ranks % 2
    slot_of = jnp.where(here, owner * per + ranks // 2, -1)

    seq_ids, positions = sequence_layout(seq_lengths[0], tok_count)
    bias = jnp.where(seq_ids[:, None] == seq_ids[None, :], 0.0, mask_fill)
    cos_tab, sin_tab = rope_tables(positions, q_gain.shape[0])
    cos_rows = jnp.concatenate([cos_tab, cos_tab], axis=1)
    sin_rows = jnp.concatenate([-sin_tab, sin_tab], axis=1)
    gain1 = norm1_gain.astype(F32).reshape(tensor_count, col_count)
    gain2 = norm2_gain.astype(F32).reshape(tensor_count, col_count)
    head_gains = (q_gain.astype(F32)[None], k_gain.astype(F32)[None])
    router = jnp.pad(w_router, ((0, 0), (0, 128 - expert_count)))
    weights = (w_query, w_key, w_value, w_output)
    def homeward(value):
        return exchange(value.reshape(groups, -1, value.shape[1]), "expert").reshape(value.shape)

    x_all, dy_all, send_dy = pre_call(local, slot_of, tensor_count, slots)
    send_dy, x_all, w_stored = lax.optimization_barrier((send_dy, x_all, w_stored))
    w_second = near_weights(w_stored, 1)
    recv_dy = homeward(send_dy)
    (
        resid, mixed, q_raw, k_raw, qh, kh, vh, attended, gates, send_rows, pick_t,
    ) = front_call(
        x_all, bias, cos_rows, sin_rows, gain1, gain2, *head_gains, router.T, routes_t, slot_of,
        keep_mask, weights, slots,
    )
    send_rows, w_stored, recv_dy = lax.optimization_barrier((send_rows, w_stored, recv_dy))
    recv_rows = homeward(send_rows)
    y_rows, d_rows, partial = expert_call(recv_rows, recv_dy, weights_call(w_stored, w_first, w_second))
    ret_rows = homeward(d_rows)
    near, far = home_call(partial)
    ret_rows, near, far, y_rows = lax.optimization_barrier((ret_rows, near, far, y_rows))
    ret_y = homeward(y_rows)
    d_qkv, dr, d_mine, router_part, small = back_call(
        pick_t, ret_rows, slot_of, keep_mask, gates, routes_t, bias, cos_rows,
        sin_rows, gain2, *head_gains, router, resid, dy_all, mixed, qh, kh, vh, q_raw, k_raw,
        w_output,
    )
    *wide, turned, dx_slice, out_slice, small, far = reduce_call(
        d_qkv, dr, d_mine, router_part, small, x_all, gain1, attended, pick_t, ret_y, far, resid,
        weights[:3],
    )

    going = dot(put, jnp.concatenate([out_slice, dx_slice], axis=1), 0, 0).astype(BF)
    small = small[:9].astype(BF).reshape(move_rows, -1)
    small = jnp.pad(small, ((0, 0), (0, -small.shape[1] % 128)))
    small = jnp.broadcast_to(small[None], (groups,) + small.shape)
    back = exchange(jnp.concatenate([going.reshape(groups, move_rows, -1), small], axis=2), "expert")
    small = jnp.sum(back[:, :, 2 * col_count :].astype(F32), axis=0)[:, : 9 * col_count // move_rows]
    small = small.reshape(-1)
    back = dot(by_rank, back.reshape(tok_count, -1)[:, : 2 * col_count], 0, 0).astype(BF)
    opposite = (tensor_id + 2) % tensor_count - 2 * (group_id % 2)
    is_far = jnp.arange(local_experts) == opposite
    expert_grad = jnp.where(is_far[:, None, None, None], far[None], near).astype(F32)
    expert_grad = jnp.transpose(expert_grad, (0, 2, 1, 3))
    wide = [value.reshape(width, -1) for value in wide]
    gain_at = 2 * width + tok_count
    head = q_gain.shape[0]
    return (
        back[:, :col_count],
        back[:, col_count:],
        small[:width],
        wide[0].astype(F32),
        wide[1].astype(F32),
        wide[2].astype(F32),
        small[gain_at : gain_at + head],
        small[gain_at + head : gain_at + 2 * head],
        turned[:col_count].astype(F32),
        small[width : 2 * width],
        turned[col_count : col_count + expert_count].astype(F32).T,
        expert_grad,
    )


def solution(mesh):
    in_specs = (
        P("expert", "tensor"),
        P("expert", "tensor"),
        P("expert", None),
        P("expert"),
        P("expert", None),
        P("expert", None),
        P(),
        P(None, "tensor"),
        P(None, "tensor"),
        P(None, "tensor"),
        P(),
        P(),
        P("tensor", None),
        P(),
        P(),
        P("expert", None, None, "tensor"),
    )
    out_specs = (
        P("expert", "tensor"),
        P("expert", "tensor"),
        P(),
        P(None, "tensor"),
        P(None, "tensor"),
        P(None, "tensor"),
        P(),
        P(),
        P("tensor", None),
        P(),
        P(),
        P("expert", None, None, "tensor"),
    )
    return jax.shard_map(body, mesh=mesh, in_specs=in_specs, out_specs=out_specs, check_vma=False)
```

```python
import functools
import math

import jax
import jax.numpy as jnp
from jax import lax
from jax.experimental import pallas as pl
from jax.experimental.pallas import tpu as pltpu
from jax.sharding import PartitionSpec as P

norm_eps = 1e-06
rope_base = 10000.0
mask_fill = -1e30


def rope_tables(positions, width):
    half_width = width // 2
    steps_idx = jnp.arange(half_width, dtype=jnp.float32)
    freqs = jnp.exp(steps_idx * (-2.0 * math.log(rope_base) / width))
    angles = positions.astype(jnp.float32)[:, None] * freqs[None, :]
    return (jnp.cos(angles), jnp.sin(angles))


def sequence_layout(lengths_row, count):
    seq_ends = jnp.cumsum(lengths_row)
    places = jnp.arange(count, dtype=jnp.int32)
    passed = (places[:, None] >= seq_ends[None, :]).astype(jnp.int32)
    seq_ids = jnp.sum(passed, axis=1)
    starts = jnp.sum(passed * lengths_row[None, :], axis=1)
    return (seq_ids, places - starts)


BF = jnp.bfloat16
F32 = jnp.float32
SHADOW = pl.CostEstimate(flops=40_000_000_000, bytes_accessed=1, transcendentals=0)
COST = pl.CostEstimate(flops=1, bytes_accessed=1, transcendentals=0)


def dot(left, right, left_dim=1, right_dim=0):
    return lax.dot_general(
        left, right, (((left_dim,), (right_dim,)), ((), ())), preferred_element_type=F32
    )


def exchange(value, axis):
    return lax.all_to_all(value, axis, split_axis=0, concat_axis=0, tiled=True)


def gather_blocks(value, axis):
    return exchange(jnp.broadcast_to(value[None], (lax.axis_size(axis),) + value.shape), axis)


def column_blocks(value, count):
    return jnp.stack(jnp.split(value, count, axis=1))


MESH = pl.DeviceIdType.MESH


def tensor_peers():
    me = lax.axis_index("tensor")
    count = lax.axis_size("tensor")
    return me, [(me + d) % count for d in range(1, count)]


def greet(axis, peers):
    barrier = pltpu.get_barrier_semaphore()
    for peer in peers:
        pl.semaphore_signal(barrier, inc=1, device_id={axis: peer}, device_id_type=MESH)
    return lambda: pl.semaphore_wait(barrier, len(peers))


class Post:
    def __init__(self, axis, send_sem, recv_sem):
        self.axis, self.send_sem, self.recv_sem = axis, send_sem, recv_sem
        self.started = []
        self.used = 0

    def push(self, source, target, peer):
        slot = self.used
        self.used += 1
        copy = pltpu.make_async_remote_copy(
            src_ref=source,
            dst_ref=target,
            send_sem=self.send_sem.at[slot],
            recv_sem=self.recv_sem.at[slot],
            device_id={self.axis: peer},
            device_id_type=MESH,
        )
        copy.start()
        self.started.append(copy)
        return copy

    def finish(self):
        for copy in self.started:
            copy.wait_send()
        self.started = []


def arrive(copies):
    for copy in copies:
        copy.wait_recv()


def ring(me):
    count = lax.axis_size("tensor")
    return (me + 1) % count, (me + count - 1) % count


def gather_start(post, ref, me):
    right, left = ring(me)
    return [post.push(ref.at[me], ref.at[me], peer) for peer in (right, left)]


def gather_relay(post, ref, me, first):
    right, left = ring(me)
    half = ref.shape[1] // 2
    first[0].wait_recv()
    here = ref.at[left, pl.ds(0, half)]
    one = post.push(here, here, right)
    first[1].wait_recv()
    here = ref.at[right, pl.ds(half, half)]
    return [one, post.push(here, here, left)]


def scatter_start(post, parts, halves, me):
    right, left = ring(me)
    far = ring(right)[0]
    half = parts.shape[1] // 2
    return [
        post.push(parts.at[far, pl.ds(0, half)], halves.at[0], right),
        post.push(parts.at[far, pl.ds(half, half)], halves.at[1], left),
    ]


def scatter_relay(post, parts, halves, box, me, first):
    right, left = ring(me)
    half = parts.shape[1] // 2
    copies = []
    for n, (peer, rows) in enumerate(((right, pl.ds(0, half)), (left, pl.ds(half, half)))):
        first[n].wait_recv()
        parts[peer, rows, :] = (parts[peer, rows, :].astype(F32) + halves[n].astype(F32)).astype(BF)
        copies.append(post.push(parts.at[peer], box.at[n], peer))
    return copies


def scatter_total(parts, box, me, copies):
    arrive(copies)
    return parts[me].astype(F32) + box[0].astype(F32) + box[1].astype(F32)


def fetch(pairs, sem):
    copies = [
        pltpu.make_async_copy(source, target, sem.at[n]) for n, (source, target) in enumerate(pairs)
    ]
    for copy in copies:
        copy.start()
    return copies


def turn(value, cos_rows, sin_rows):
    return value * cos_rows + pltpu.roll(value, value.shape[-1] // 2, 1) * sin_rows


def inverse_rms(total, width):
    return lax.rsqrt(total * (1.0 / width) + norm_eps)


def row_sum(value):
    return jnp.sum(value, axis=1, keepdims=True)


def softmax_rows(query, key, bias, scale):
    scores = dot(query, key, 1, 1) * scale + bias
    grown = jnp.exp(scores - jnp.max(scores, axis=1, keepdims=True))
    return grown / row_sum(grown)


def select_slots(slot_of, slots):
    top, tok = slot_of.shape
    slot = lax.broadcasted_iota(jnp.int32, (slots, tok), 0)
    pick = jnp.zeros((slots, tok), F32)
    for k in range(top):
        pick = jnp.where(slot_of[k : k + 1, :] == slot, 1.0, pick)
    return pick


def pre_kernel(local, slot_of, x_out, dy_out, send_out, x_all, dy_all, send_sem, recv_sem):
    me = lax.axis_index("tensor")
    ready = greet("tensor", ring(me))
    blocks, _, col = x_all.shape
    x_all[me] = local[:, :col]
    dy_all[me] = local[:, col:]
    ready()
    post = Post("tensor", send_sem, recv_sem)
    dy_in = gather_start(post, dy_all, me)
    x_in = gather_start(post, x_all, me)
    pick = select_slots(slot_of, send_out.shape[0]).astype(BF)
    dy_in = gather_relay(post, dy_all, me, dy_in)
    x_in = gather_relay(post, x_all, me, x_in)
    arrive(dy_in)
    dy_out[...] = dy_all[...]
    for t in range(blocks):
        send_out[:, t * col : (t + 1) * col] = dot(pick, dy_all[t]).astype(BF)
    arrive(x_in)
    x_out[...] = x_all[...]
    post.finish()


def pre_call(local, slot_of, blocks, slots):
    tok, both = local.shape
    col = both // 2
    tiles = (blocks, tok, col)
    shape = jax.ShapeDtypeStruct
    vmem = pl.BlockSpec(memory_space=pltpu.VMEM)
    return pl.pallas_call(
        pre_kernel,
        out_shape=(shape(tiles, BF), shape(tiles, BF), shape((slots, col * blocks), BF)),
        in_specs=[vmem] * 2,
        out_specs=(vmem,) * 3,
        scratch_shapes=[
            pltpu.VMEM(tiles, BF), pltpu.VMEM(tiles, BF),
            pltpu.SemaphoreType.DMA((8,)), pltpu.SemaphoreType.DMA((8,)),
        ],
        compiler_params=pltpu.CompilerParams(
            collective_id=6, has_side_effects=True, vmem_limit_bytes=63 * 1024 * 1024
        ),
        cost_estimate=COST,
        name="pre",
    )(local, slot_of)


def front_kernel(
    x_all, bias, cos_rows, sin_rows, gain1, gain2, q_gain, k_gain, router, routes, slot_of, keep,
    wq_hbm, wk_hbm, wv_hbm, wo_hbm,
    resid_out, mixed_out, q_out, k_out, qh_out, kh_out, vh_out, ob_out,
    gates_out, send_out, pick_out,
    wq, wk, wv, wo, an, parts, halves, box, total, load_sem, send_sem, recv_sem,
):
    me = lax.axis_index("tensor")
    ready = greet("tensor", ring(me))
    loads = fetch([(wq_hbm, wq), (wk_hbm, wk), (wv_hbm, wv), (wo_hbm, wo)], load_sem)
    blocks, tok, col = x_all.shape
    width = blocks * col
    post = Post("tensor", send_sem, recv_sem)
    square = jnp.zeros((tok, 1), F32)
    for t in range(blocks):
        value = x_all[t].astype(F32)
        square = square + row_sum(value * value)
    r1 = inverse_rms(square, width)
    for t in range(blocks):
        an[t] = (x_all[t].astype(F32) * r1 * gain1[t : t + 1, :]).astype(BF)

    for copy in loads:
        copy.wait()

    def project(weight):
        value = dot(an[0], weight[0:col, :])
        for t in range(1, blocks):
            value = value + dot(an[t], weight[t * col : (t + 1) * col, :])
        return value

    q_out[...] = project(wq)
    k_out[...] = project(wk)
    vh_out[...] = project(wv).astype(BF)
    head = q_gain.shape[1]
    scale = 1.0 / math.sqrt(head)
    for h in range(col // head):
        lanes = slice(h * head, (h + 1) * head)
        for raw, gain, rotated in ((q_out, q_gain, qh_out), (k_out, k_gain, kh_out)):
            value = raw[:, lanes]
            value = value * inverse_rms(row_sum(value * value), head) * gain[...]
            rotated[:, lanes] = turn(value, cos_rows[...], sin_rows[...]).astype(BF)
        probs = softmax_rows(qh_out[:, lanes], kh_out[:, lanes], bias[...], scale).astype(BF)
        ob_out[:, lanes] = dot(probs, vh_out[:, lanes]).astype(BF)
    for t in range(blocks):
        parts[t] = dot(ob_out[...], wo[:, t * col : (t + 1) * col]).astype(BF)
    ready()
    first = scatter_start(post, parts, halves, me)
    moved = scatter_relay(post, parts, halves, box, me, first)
    total[me] = scatter_total(parts, box, me, moved).astype(BF)
    arrive(gather_relay(post, total, me, gather_start(post, total, me)))
    square = jnp.zeros((tok, 1), F32)
    for t in range(blocks):
        value = x_all[t].astype(F32) + total[t].astype(F32)
        resid_out[t] = value
        square = square + row_sum(value * value)
    r2 = inverse_rms(square, width)
    logits = jnp.zeros((router.shape[1], tok), F32)
    for t in range(blocks):
        mixed_out[t] = (resid_out[t] * r2 * gain2[t : t + 1, :]).astype(BF)
        logits = logits + dot(router[t * col : (t + 1) * col, :].T, mixed_out[t], 1, 1)
    expert = lax.broadcasted_iota(jnp.int32, logits.shape, 0)
    top = routes.shape[0]
    chosen = [
        jnp.sum(jnp.where(routes[k : k + 1, :] == expert, logits, 0.0), axis=0, keepdims=True)
        for k in range(top)
    ]
    peak = functools.reduce(jnp.maximum, chosen)
    grown = [jnp.exp(value - peak) for value in chosen]
    whole = functools.reduce(jnp.add, grown)
    slots = send_out.shape[0]
    slot = lax.broadcasted_iota(jnp.int32, (slots, tok), 0)
    pick = jnp.zeros((slots, tok), F32)
    weight = jnp.zeros((slots, tok), F32)
    for k in range(top):
        gate = grown[k] / whole
        gates_out[k : k + 1, :] = gate
        hot = slot_of[k : k + 1, :] == slot
        pick = jnp.where(hot, 1.0, pick)
        weight = jnp.where(hot, gate * keep[k : k + 1, :], weight)
    pick_out[...] = pick.T.astype(BF)
    pick = pick.astype(BF)
    for t in range(blocks):
        send_out[:, t * col : (t + 1) * col] = dot(pick, mixed_out[t]).astype(BF)
    gate = row_sum(weight)
    first = gate.astype(BF)
    second = (gate - first.astype(F32)).astype(BF)
    third = (gate - first.astype(F32) - second.astype(F32)).astype(BF)
    lane = lax.broadcasted_iota(jnp.int32, (slots, 128), 1)
    facts = jnp.zeros((slots, 128), F32)
    for n, piece in enumerate((first, second, third)):
        facts = jnp.where(lane == n, piece.astype(F32), facts)
    send_out[:, width:] = facts.astype(BF)
    post.finish()


def front_call(x_all, bias, cos_rows, sin_rows, gain1, gain2, q_gain, k_gain, router, routes,
               slot_of, keep, weights, slots):
    blocks, tok, col = tiles = x_all.shape
    width = col * blocks
    shape = jax.ShapeDtypeStruct
    vmem = pl.BlockSpec(memory_space=pltpu.VMEM)
    top = routes.shape[0]
    return pl.pallas_call(
        front_kernel,
        out_shape=(
            shape(tiles, F32), shape(tiles, BF), shape((tok, col), F32), shape((tok, col), F32),
            shape((tok, col), BF), shape((tok, col), BF), shape((tok, col), BF),
            shape((tok, col), BF), shape((top, tok), F32), shape((slots, width + 128), BF),
            shape((tok, slots), BF),
        ),
        in_specs=[vmem] * 12 + [pl.BlockSpec(memory_space=pl.ANY)] * 4,
        out_specs=(vmem,) * 11,
        scratch_shapes=[
            pltpu.VMEM((width, col), BF), pltpu.VMEM((width, col), BF), pltpu.VMEM((width, col), BF),
            pltpu.VMEM((col, width), BF),
            pltpu.VMEM(tiles, BF), pltpu.VMEM(tiles, BF),
            pltpu.VMEM((2, tok // 2, col), BF), pltpu.VMEM((2, tok, col), BF), pltpu.VMEM(tiles, BF),
            pltpu.SemaphoreType.DMA((4,)),
            pltpu.SemaphoreType.DMA((8,)), pltpu.SemaphoreType.DMA((8,)),
        ],
        compiler_params=pltpu.CompilerParams(
            collective_id=1, has_side_effects=True, vmem_limit_bytes=63 * 1024 * 1024
        ),
        cost_estimate=SHADOW,
        name="front",
    )(x_all, bias, cos_rows, sin_rows, gain1, gain2, q_gain, k_gain, router, routes, slot_of,
      keep, *weights)


def back_kernel(
    pick_t, ret, slot_of, keep, gates, routes, bias, cos_rows, sin_rows, gain2,
    q_gain, k_gain, router, resid, dy_all, mixed, qh, kh, vh,
    q_hbm, k_hbm, wo_hbm,
    d_qkv, dr, d_mine, router_out, small_out,
    q_raw, k_raw, wo, parts, halves, box, total, dm, d_att, dg_mine, dg_box,
    load_sem, send_sem, recv_sem,
):
    me, peers = tensor_peers()
    ready = greet("tensor", peers)
    loads = fetch([(wo_hbm, wo), (q_hbm, q_raw), (k_hbm, k_raw)], load_sem)
    blocks, tok, col = parts.shape
    width = blocks * col
    post = Post("tensor", send_sem, recv_sem)
    for t in range(blocks):
        parts[t] = dot(pick_t[...], ret[:, t * col : (t + 1) * col]).astype(BF)
    ready()
    first = scatter_start(post, parts, halves, me)
    top = routes.shape[0]
    dgate = row_sum(ret[:, width:].astype(F32))
    slot = lax.broadcasted_iota(jnp.int32, (ret.shape[0], tok), 0)
    for k in range(top):
        hot = slot_of[k : k + 1, :] == slot
        dg_mine[k : k + 1, :] = jnp.sum(jnp.where(hot, dgate, 0.0), axis=0, keepdims=True)
    dg_in = [post.push(dg_mine, dg_box.at[d], peer) for d, peer in enumerate(peers)]
    moved = scatter_relay(post, parts, halves, box, me, first)
    total[me] = scatter_total(parts, box, me, moved).astype(BF)
    total_first = gather_start(post, total, me)

    arrive(dg_in)
    d_gates = dg_mine[...]
    for d in range(blocks - 1):
        d_gates = d_gates + dg_box[d]
    d_gates = d_gates * keep[...]
    gate = gates[...]
    d_chosen = gate * (d_gates - jnp.sum(gate * d_gates, axis=0, keepdims=True))
    expert = lax.broadcasted_iota(jnp.int32, (router.shape[1], tok), 0)
    d_logits_t = jnp.zeros(expert.shape, F32)
    for k in range(top):
        hot = routes[k : k + 1, :] == expert
        d_logits_t = jnp.where(hot, d_chosen[k : k + 1, :], d_logits_t)
    d_logits = d_logits_t.T.astype(BF)
    square = jnp.zeros((tok, 1), F32)
    for t in range(blocks):
        rows = slice(t * col, (t + 1) * col)
        dm[t] = dot(d_logits, router[rows, :], 1, 1)
        square = square + row_sum(resid[t] * resid[t])
    r2 = inverse_rms(square, width)
    total_moved = gather_relay(post, total, me, total_first)
    for t in range(blocks):
        rows = slice(t * col, (t + 1) * col)
        router_out[rows, :] = dot(mixed[t].T, d_logits).astype(BF)
    arrive(total_moved)
    cross = jnp.zeros((tok, 1), F32)
    for t in range(blocks):
        dm[t] = dm[t] + total[t].astype(F32)
        cross = cross + row_sum(resid[t] * gain2[t : t + 1, :] * dm[t])
    cross = cross * (1.0 / width) * r2 * r2 * r2
    small_out[...] = jnp.zeros_like(small_out)
    for t in range(blocks):
        d_mixed = dm[t]
        small_out[t : t + 1, :] = jnp.sum(d_mixed * resid[t] * r2, axis=0, keepdims=True)
        d_resid = dy_all[t].astype(F32) + r2 * gain2[t : t + 1, :] * d_mixed - resid[t] * cross
        dm[t] = d_resid
        dr[t] = d_resid.astype(BF)
    d_mine[...] = dm[me]
    for copy in loads:
        copy.wait()
    value = dot(dr[0], wo[:, 0:col], 1, 1)
    for t in range(1, blocks):
        value = value + dot(dr[t], wo[:, t * col : (t + 1) * col], 1, 1)
    d_att[...] = value.astype(BF)

    head = q_gain.shape[1]
    scale = 1.0 / math.sqrt(head)
    q_part = jnp.zeros((1, head), F32)
    k_part = jnp.zeros((1, head), F32)

    def unturn(grown, raw, gain):
        d_unit = grown * cos_rows[...] - pltpu.roll(grown, head // 2, 1) * sin_rows[...]
        inverse = inverse_rms(row_sum(raw * raw), head)
        unit = raw * inverse
        gain_part = jnp.sum(d_unit * unit, axis=0, keepdims=True)
        d_unit = d_unit * gain[...]
        d_raw = inverse * (d_unit - unit * (row_sum(unit * d_unit) * (1.0 / head)))
        return d_raw.astype(BF), gain_part

    for h in range(col // head):
        lanes = slice(h * head, (h + 1) * head)
        probs = softmax_rows(qh[:, lanes], kh[:, lanes], bias[...], scale)
        d_head = d_att[:, lanes]
        d_probs = dot(d_head, vh[:, lanes], 1, 1)
        d_scores = probs * (d_probs - row_sum(probs * d_probs))
        d_qkv[:, 2 * col + h * head : 2 * col + (h + 1) * head] = dot(
            probs.T.astype(BF), d_head
        ).astype(BF)
        d_q, part = unturn(dot(d_scores.astype(BF), kh[:, lanes]) * scale, q_raw[:, lanes], q_gain)
        q_part = q_part + part
        d_qkv[:, lanes] = d_q
        d_k, part = unturn(dot(d_scores.T.astype(BF), qh[:, lanes]) * scale, k_raw[:, lanes], k_gain)
        k_part = k_part + part
        d_qkv[:, col + h * head : col + (h + 1) * head] = d_k
    small_out[blocks : blocks + 1, :head] = q_part
    small_out[blocks : blocks + 1, head : 2 * head] = k_part
    post.finish()


def back_call(pick_t, ret, slot_of, keep, gates, routes, bias, cos_rows, sin_rows,
              gain2, q_gain, k_gain, router, resid, dy_all, mixed, qh, kh, vh, q_raw, k_raw, wo):
    blocks, tok, col = dy_all.shape
    width = blocks * col
    tiles = (blocks, tok, col)
    shape = jax.ShapeDtypeStruct
    vmem = pl.BlockSpec(memory_space=pltpu.VMEM)
    top = routes.shape[0]
    count = 8 + blocks - 1
    return pl.pallas_call(
        back_kernel,
        out_shape=(
            shape((tok, 3 * col), BF), shape(tiles, BF), shape((tok, col), F32),
            shape((width, 128), BF), shape((8, col), F32),
        ),
        in_specs=[vmem] * 19 + [pl.BlockSpec(memory_space=pl.ANY)] * 3,
        out_specs=(vmem,) * 5,
        scratch_shapes=[
            pltpu.VMEM((tok, col), F32), pltpu.VMEM((tok, col), F32), pltpu.VMEM((col, width), BF),
            pltpu.VMEM(tiles, BF), pltpu.VMEM((2, tok // 2, col), BF), pltpu.VMEM((2, tok, col), BF),
            pltpu.VMEM(tiles, BF), pltpu.VMEM(tiles, F32), pltpu.VMEM((tok, col), BF),
            pltpu.VMEM((top, tok), F32), pltpu.VMEM((blocks - 1, top, tok), F32),
            pltpu.SemaphoreType.DMA((3,)),
            pltpu.SemaphoreType.DMA((count,)), pltpu.SemaphoreType.DMA((count,)),
        ],
        compiler_params=pltpu.CompilerParams(
            collective_id=2, has_side_effects=True, vmem_limit_bytes=63 * 1024 * 1024
        ),
        cost_estimate=pl.CostEstimate(
            flops=20_000_000_000, bytes_accessed=1, transcendentals=0
        ),
        name="back",
    )(pick_t, ret, slot_of, keep, gates, routes, bias, cos_rows, sin_rows, gain2,
      q_gain, k_gain, router, resid, dy_all, mixed, qh, kh, vh, q_raw, k_raw, wo)


def octet():
    me = lax.axis_index("expert")
    core = me % 2
    return me - core, core, lax.axis_index("tensor")


def octet_others(base, core, rank):
    count = lax.axis_size("tensor")
    others = [{"expert": base + core, "tensor": (rank + d) % count} for d in range(1, count)]
    return others + [
        {"expert": base + 1 - core, "tensor": (rank + d) % count} for d in range(count)
    ]


def meet(others):
    barrier = pltpu.get_barrier_semaphore()
    for other in others:
        pl.semaphore_signal(barrier, inc=1, device_id=other, device_id_type=MESH)
    return lambda: pl.semaphore_wait(barrier, len(others))


def remote(source, target, send_sem, recv_sem, device):
    return pltpu.make_async_remote_copy(
        src_ref=source, dst_ref=target, send_sem=send_sem, recv_sem=recv_sem, device_id=device,
        device_id_type=MESH,
    )


def weights_kernel(
    w, first, second, out, near, own, load_sem, near_sem, send_sem, recv_sem, pass_send, pass_recv
):
    base, core, rank = octet()
    ready = meet(octet_others(base, core, rank))
    ranks = out.shape[0]
    half = out.shape[2] // 2
    sibling = {"expert": base + 1 - core, "tensor": rank}
    side = rank % 2
    target = 2 * core + side
    own_chip = target == rank

    def part(ref, index, which):
        return ref.at[index, :, pl.ds(which * half, half), :]

    mine = 1 - (rank // 2 + core) % 2
    loads = fetch([(first, near.at[0]), (second, near.at[1])], load_sem)
    own_loads, own_stores = [], []
    for k in range(2):
        own_loads.append(pltpu.make_async_copy(part(w, side, k), own.at[k], load_sem.at[2 + k]))
        own_stores.append(pltpu.make_async_copy(own.at[k], part(out, rank, k), near_sem.at[2 + k]))
        pl.when(own_chip)(own_loads[k].start)
    ready()
    sends = []
    for k in range(2):
        device = {"expert": base + mine * (1 - core) + (1 - mine) * k, "tensor": target}
        arrives = recv_sem.at[1 - mine, mine * k]
        sends.append(remote(part(w, side, k), part(out, rank, k), send_sem.at[k], arrives, device))
        sends[k].start()
    offsets = (3 - 2 * core, 1 + 2 * core)
    stores, passed = [], []
    for n in range(2):
        d = offsets[n]
        place = part(out, (rank + d) % ranks, core)
        loads[n].wait()
        passed.append(remote(near.at[n], place, pass_send.at[d], pass_recv.at[d], sibling))
        passed[-1].start()
        stores.append(pltpu.make_async_copy(near.at[n], place, near_sem.at[n]))
        stores[-1].start()

    @pl.when(own_chip)
    def _():
        for k in range(2):
            own_loads[k].wait()
            own_stores[k].start()

    far = part(out, (rank + 2) % ranks, core)
    remote(far, far, send_sem.at[0], recv_sem.at[1, 0], sibling).wait_recv()
    passed.append(remote(far, far, pass_send.at[2], pass_recv.at[2], sibling))
    passed[-1].start()
    for k in range(2):
        theirs = part(out, rank, k)
        arrival = remote(theirs, theirs, send_sem.at[k], recv_sem.at[0, k], sibling)
        pl.when(jnp.logical_not(own_chip))(arrival.wait_recv)
        pl.when(own_chip)(own_stores[k].wait)
    for d in range(1, ranks):
        theirs = part(out, (rank + d) % ranks, 1 - core)
        remote(theirs, theirs, pass_send.at[d], pass_recv.at[d], sibling).wait_recv()
    for copy in passed + sends:
        copy.wait_send()
    for copy in stores:
        copy.wait()


def weights_call(w, first, second):
    _, three, width, hidden = w.shape
    hbm = pl.BlockSpec(memory_space=pl.ANY)
    sems = pltpu.SemaphoreType.DMA((4,))
    halves = pltpu.VMEM((2, three, width // 2, hidden), BF)
    return pl.pallas_call(
        weights_kernel,
        out_shape=jax.ShapeDtypeStruct((4, three, width, hidden), BF),
        in_specs=[hbm] * 3,
        out_specs=hbm,
        scratch_shapes=[
            halves, halves, sems, sems, pltpu.SemaphoreType.DMA((2,)),
            pltpu.SemaphoreType.DMA((2, 2)), sems, sems,
        ],
        compiler_params=pltpu.CompilerParams(
            collective_id=4, has_side_effects=True, vmem_limit_bytes=63 * 1024 * 1024
        ),
        cost_estimate=SHADOW,
        name="weights",
    )(w, first, second)


def near_weights(w, turn_over):
    ranks, places = lax.axis_size("tensor"), lax.axis_size("expert")
    half = w.shape[2] // 2
    core, rank = lax.axis_index("expert") % 2, lax.axis_index("tensor")
    side = 1 - rank % 2
    to_core = jnp.where(2 * core + side == (rank + 1) % ranks, turn_over, 1 - turn_over)
    piece = lax.dynamic_slice(w, (side, 0, to_core * half, 0), (1, w.shape[1], half, w.shape[3]))
    pairs = []
    for place in range(places):
        for t in range(ranks):
            target = 2 * (place % 2) + 1 - t % 2
            core_of = (0 if target == (t + 1) % ranks else 1) ^ turn_over
            pairs.append((place * ranks + t, (place - place % 2 + core_of) * ranks + target))
    return lax.ppermute(piece[0], ("expert", "tensor"), pairs)


def home_kernel(grads, out, far_out, own, got, load_sem, local_sem, swap_send, swap_recv, send_sem, recv_sem):
    base, core, rank = octet()
    ready = meet(octet_others(base, core, rank))
    ranks, three, half, hidden = own.shape
    sibling = {"expert": base + 1 - core, "tensor": rank}
    order = (1, 3, 0, 2)
    loads, swaps = [], []
    for d in order:
        quarter = (rank + d) % ranks
        source = grads.at[quarter, :, pl.ds(core * half, half), :]
        loads.append(pltpu.make_async_copy(source, own.at[d], load_sem.at[d]))
        loads[-1].start()
    ready()
    for d in order:
        quarter = (rank + d) % ranks
        source = grads.at[quarter, :, pl.ds((1 - core) * half, half), :]
        swaps.append(remote(source, got.at[d], swap_send.at[d], swap_recv.at[d], sibling))
        swaps[-1].start()
    owner = rank // 2
    side = rank - 2 * owner
    rows = 64
    place = out.at[side, :, pl.ds(core * half, half), :]
    stays = owner == core
    sends = []
    for n, d in enumerate(order):
        loads[n].wait()
        swaps[n].wait_recv()

        def one(i, _, d=d):
            c, at = i // (half // rows), i % (half // rows) * rows
            here = pl.ds(pl.multiple_of(at, rows), rows)
            value = own[d, c, here, :].astype(F32) + got[d, c, here, :].astype(F32)
            own[d, c, here, :] = value.astype(BF)
            return 0

        lax.fori_loop(0, three * (half // rows), one, 0)
        if d == 2:
            far = pltpu.make_async_copy(own.at[d], far_out, load_sem.at[d])
            far.start()
            continue
        away = remote(
            own.at[d], place, send_sem.at[d], recv_sem.at[2 * side + core],
            {"expert": base + owner, "tensor": (rank + d) % ranks},
        )
        if d:
            away.start()
        else:
            kept = pltpu.make_async_copy(own.at[d], place, local_sem)
            pl.when(stays)(kept.start)
            pl.when(jnp.logical_not(stays))(away.start)
        sends.append((d, away))
    for s in range(2):
        for k in range(2):
            off = (2 * core + s - rank) % ranks
            mine = out.at[s, :, pl.ds(k * half, half), :]
            arrival = remote(own.at[0], mine, send_sem.at[0], recv_sem.at[2 * s + k], sibling)
            own_chip = off == 0
            comes = (off != 2) & jnp.logical_not(own_chip & (core == k))
            pl.when(comes)(arrival.wait_recv)
    pl.when(stays)(kept.wait)
    for d, away in sends:
        if d:
            away.wait_send()
        else:
            pl.when(jnp.logical_not(stays))(away.wait_send)
    for swap in swaps:
        swap.wait_send()
    far.wait()


def home_call(grads):
    ranks, three, width, hidden = grads.shape
    hbm = pl.BlockSpec(memory_space=pl.ANY)
    sems = pltpu.SemaphoreType.DMA((4,))
    halves = pltpu.VMEM((ranks, three, width // 2, hidden), BF)
    shape = jax.ShapeDtypeStruct
    return pl.pallas_call(
        home_kernel,
        out_shape=(
            shape((2, three, width, hidden), BF), shape((three, width // 2, hidden), BF),
        ),
        in_specs=[hbm],
        out_specs=(hbm, hbm),
        scratch_shapes=[
            halves, halves, sems, pltpu.SemaphoreType.DMA, sems, sems, sems, sems,
        ],
        compiler_params=pltpu.CompilerParams(
            collective_id=5, has_side_effects=True, vmem_limit_bytes=63 * 1024 * 1024
        ),
        cost_estimate=SHADOW,
        name="home",
    )(grads)


def expert_kernel(rows_ref, dys, w_ref, y_ref, dx_ref, grad_ref, rows_t, dys_t, y_acc, dx_acc, gate_of, dgate):
    step = pl.program_id(0)
    width = y_acc.shape[1]
    rows = rows_ref.at[:, :width]

    @pl.when(step == 0)
    def _():
        gate_of[...] = row_sum(rows_ref[:, width:].astype(F32))
        rows_t[...] = rows[...].T
        dys_t[...] = (dys[...].astype(F32) * gate_of[...]).astype(BF).T
        dgate[...] = jnp.zeros_like(dgate)
        y_acc[...] = jnp.zeros_like(y_acc)
        dx_acc[...] = jnp.zeros_like(dx_acc)

    w_gate, w_up, w_down = w_ref[0, 0], w_ref[0, 1], w_ref[0, 2]
    gate = dot(rows[...], w_gate)
    up = dot(rows[...], w_up)
    d_raw = dot(dys[...], w_down)
    d_act = d_raw * gate_of[...]
    sig = 1.0 / (1.0 + jnp.exp(-gate))
    silu = gate * sig
    act = (silu * up).astype(BF)
    dgate[...] += row_sum(act.astype(F32) * d_raw)
    d_gate = (d_act * up * sig * (1.0 + gate * (1.0 - sig))).astype(BF)
    d_up = (d_act * silu).astype(BF)
    y_acc[...] += dot(act, w_down, 1, 1)
    dx_acc[...] += dot(d_gate, w_gate, 1, 1) + dot(d_up, w_up, 1, 1)
    grad_ref[0, 0] = dot(rows_t[...], d_gate).astype(BF)
    grad_ref[0, 1] = dot(rows_t[...], d_up).astype(BF)
    grad_ref[0, 2] = dot(dys_t[...], act).astype(BF)

    @pl.when(step == pl.num_programs(0) - 1)
    def _():
        first = dgate[...].astype(BF).astype(F32)
        lane = lax.broadcasted_iota(jnp.int32, (y_ref.shape[0], 128), 1)
        facts = jnp.where(lane == 0, first, jnp.where(lane == 1, dgate[...] - first, 0.0))
        y_ref[...] = (y_acc[...] * gate_of[...]).astype(BF)
        dx_ref[:, :width] = dx_acc[...].astype(BF)
        dx_ref[:, width:] = facts.astype(BF)


def expert_call(rows, dys, weights):
    quarters, _, width, hidden = weights.shape
    count = rows.shape[0]
    shape = jax.ShapeDtypeStruct

    def whole(value):
        return pl.BlockSpec(value.shape, lambda q: (0, 0), pipeline_mode=pl.Buffered(1))

    block = pl.BlockSpec((1, 3, width, hidden), lambda q: (q, 0, 0, 0))
    outs = [shape((count, width), BF), shape((count, width + 128), BF)]
    return pl.pallas_call(
        expert_kernel,
        grid=(quarters,),
        out_shape=tuple(outs) + (shape(weights.shape, BF),),
        in_specs=[whole(rows), whole(dys), block],
        out_specs=tuple(whole(value) for value in outs) + (block,),
        scratch_shapes=[
            pltpu.VMEM((width, count), BF),
            pltpu.VMEM((width, count), BF),
            pltpu.VMEM((count, width), F32),
            pltpu.VMEM((count, width), F32),
            pltpu.VMEM((count, 1), F32),
            pltpu.VMEM((count, 1), F32),
        ],
        compiler_params=pltpu.CompilerParams(vmem_limit_bytes=63 * 1024 * 1024),
        cost_estimate=COST,
        name="expert",
    )(rows, dys, weights)


def plane():
    me = lax.axis_index("expert")
    core, z, y = me % 2, (me // 2) % 4, me // 8
    return [
        (core, me + 1 - 2 * core),
        ((y + y // 2) % 2, me + 8 * (1 - 2 * (y % 2))),
        (y // 2, me + 8 * (3 - 2 * y)),
        ((z + z // 2) % 2, me + 2 * (1 - 2 * (z % 2))),
        (z // 2, me + 2 * (3 - 2 * z)),
    ]

ORDERS = ((1, 3, 2, 4), (3, 2, 4, 1), (2, 4, 1, 3), (4, 1, 3, 2))

def reduce_kernel(
    d_qkv, dr, d_mine, router_part, small_in, x_all, gain1, ob, pick_y, ret_y,
    far_hbm, resid_hbm, wq_hbm, wk_hbm, wv_hbm,
    q_out, k_out, v_out, o_out, router_out, dx_out, out_out, small_out, far_out,
    wq, wk, wv, resid, parts, y_parts, halves, box_x, note, buf, box, got,
    load_sem, out_sem, x_send, x_recv, send_sem, recv_sem, far_send, far_recv,
):
    me, peers = tensor_peers()
    dims = plane()
    base, core, _ = octet()
    ready = meet(octet_others(base, core, me) + [{"expert": partner} for _, partner in dims[1:]])
    loads = fetch(
        [(wq_hbm, wq), (wk_hbm, wk), (wv_hbm, wv), (resid_hbm.at[me], resid)], load_sem
    )
    blocks, tok, col = x_all.shape
    width = blocks * col
    head = col // blocks
    square = jnp.zeros((tok, 1), F32)
    for t in range(blocks):
        value = x_all[t].astype(F32)
        square = square + row_sum(value * value)
    r1 = inverse_rms(square, width)
    post_x = Post("tensor", x_send, x_recv)
    post = Post("expert", send_sem, recv_sem)
    x_halves, x_box = halves.at[pl.ds(0, 2)], box_x.at[pl.ds(0, 2)]
    y_halves, y_box = halves.at[pl.ds(2, 2)], box_x.at[pl.ds(2, 2)]
    chunks = buf.shape[0] // blocks
    rows_chunk = buf.shape[1]

    def products(t):
        here = pl.ds(t * chunks, chunks)
        normed = (x_all[t].astype(F32) * r1 * gain1[pl.ds(t, 1), :]).T.astype(BF)
        for n in range(3):
            lanes = slice(n * col, (n + 1) * col)
            value = dot(normed, d_qkv[:, lanes]).astype(BF)
            buf[here, :, lanes] = value.reshape(chunks, rows_chunk, col)
        value = dot(dr[t].T, ob[...]).astype(BF)
        buf[here, :, 3 * col : 4 * col] = value.reshape(chunks, rows_chunk, col)
        value = router_part[pl.ds(t * col, col), :]
        buf[here, :, 4 * col :] = value.reshape(chunks, rows_chunk, value.shape[1])

    def add(target, place, first, count):
        def one(i, _):
            total = buf[place + i].astype(F32) + box[first + i].astype(F32)
            target[place + i] = total.astype(BF)
            return 0

        lax.fori_loop(0, count, one, 0)

    half = far_hbm.shape[1]
    owner = me // 2

    def far_copy(n, side, device):
        return remote(
            far_hbm.at[n], far_out.at[n, pl.ds(side * half, half), :],
            far_send.at[n], far_recv.at[n, side], device,
        )

    far_copies = [
        far_copy(n, core, {"expert": base + owner, "tensor": (me + 2) % blocks}) for n in range(3)
    ]
    copies = []
    ready()
    for n in range(2):
        products(2 * (1 - core) + n)
        for s in range(2 * n, 2 * n + 2):
            source = buf.at[pl.ds((1 - core) * 64 + s * 16, 16)]
            copies.append(post.push(source, box.at[pl.ds(31 * s, 16)], dims[0][1]))
    for copy in loads:
        copy.wait()
    for t in range(blocks):
        rows = slice(t * col, (t + 1) * col)
        parts[t] = (
            dot(d_qkv[:, 0:col], wq[rows, :], 1, 1)
            + dot(d_qkv[:, col : 2 * col], wk[rows, :], 1, 1)
            + dot(d_qkv[:, 2 * col : 3 * col], wv[rows, :], 1, 1)
        ).astype(BF)
    x_first = scatter_start(post_x, parts, x_halves, me)
    for n in range(2):
        products(2 * core + n)
    x_moved = scatter_relay(post_x, parts, x_halves, x_box, me, x_first)
    place = [core * 64 + s * 16 for s in range(4)]
    size, first = 16, 0

    def halve(k):
        for s in range(4):
            copies[s].wait_recv()
            add(buf, place[s], 31 * s + first, size)
            bit, partner = dims[ORDERS[s][k]]
            half = size // 2
            copies[s] = post.push(
                buf.at[pl.ds(place[s] + (1 - bit) * half, half)],
                box.at[pl.ds(31 * s + first + size, half)],
                partner,
            )
            place[s] = place[s] + bit * half

    halve(0)
    first, size = first + size, size // 2

    for t in range(blocks):
        y_parts[t] = dot(pick_y[...], ret_y[:, t * col : (t + 1) * col]).astype(BF)
    y_first = scatter_start(post_x, y_parts, y_halves, me)
    d_an = scatter_total(parts, x_box, me, x_moved)
    x_mine = x_all[me].astype(F32)
    grown = gain1[pl.ds(me, 1), :] * d_an
    mean_part = row_sum(x_mine * grown)
    note[me, 0:8, :] = jnp.broadcast_to(
        jnp.sum(d_an * x_mine * r1, axis=0, keepdims=True), (8, col)
    )
    note[me, 8:16, 0:tok] = jnp.broadcast_to(mean_part, (tok, 128)).T[0:8, :]
    note[me, 8:16, tok:] = jnp.broadcast_to(small_in[blocks : blocks + 1, : 2 * head], (8, 2 * head))
    note_in = [post_x.push(note.at[me], note.at[me], peer) for peer in peers]

    halve(1)
    far_copies[0].start()
    first, size = first + size, size // 2
    y_moved = scatter_relay(post_x, y_parts, y_halves, y_box, me, y_first)
    halve(2)
    first, size = first + size, size // 2
    halve(3)
    far_copies[1].start()
    first, size = first + size, size // 2
    shared = [[] for _ in range(4)]
    for s in range(4):
        copies[s].wait_recv()
        add(got, place[s], 31 * s + first, 1)
        here = got.at[pl.ds(place[s], 1)]
        copies[s] = post.push(here, here, dims[ORDERS[s][3]][1])
        shared[s].append(post.push(here, here, dims[0][1]))

    arrive(note_in)
    facts = note[0, 8:16, :]
    for t in range(1, blocks):
        facts = facts + note[t, 8:16, :]
    for t in range(blocks):
        small_out[t : t + 1, :] = note[t, 0:1, :]
        small_out[blocks + t : blocks + t + 1, :] = small_in[t : t + 1, :]
    small_out[2 * blocks :, :] = facts
    mean = jnp.broadcast_to(facts[0:1, 0:tok], (128, tok)).T[:, 0:1] * (1.0 / width)
    dx_out[...] = (d_mine[...] + r1 * grown - x_mine * (r1 * r1 * r1 * mean)).astype(BF)

    size = 1
    stores = []

    def keep(n, at):
        here = pl.ds(at, 16)
        for m, target in enumerate((q_out, k_out, v_out)):
            stores.append(
                pltpu.make_async_copy(
                    got.at[here, :, pl.ds(m * col, col)], target.at[here], out_sem.at[n, m]
                )
            )
            stores[-1].start()
        count = 16 * rows_chunk
        there = pl.ds(pl.multiple_of(at * rows_chunk, 128), count)
        o_out[:, there] = got[here, :, 3 * col : 4 * col].reshape(count, col).T
        router_out[:, there] = got[here, :, 4 * col :].reshape(count, router_out.shape[0]).T

    for k in range(3, -1, -1):
        for s in range(4):
            copies[s].wait_recv()
            bit, _ = dims[ORDERS[s][k]]
            come = got.at[pl.ds(place[s] + (1 - 2 * bit) * size, size)]
            place[s] = place[s] - bit * size
            if k:
                here = got.at[pl.ds(place[s], 2 * size)]
                copies[s] = post.push(here, here, dims[ORDERS[s][k - 1]][1])
            shared[s].append(post.push(come, come, dims[0][1]))
            if not k:
                keep(s, place[s])
        size *= 2
        if k == 3:
            far_copies[2].start()
        if k == 2:
            out_out[...] = (resid[...] + scatter_total(y_parts, y_box, me, y_moved)).astype(BF)
    for s in range(4):
        arrive(shared[s])
        keep(4 + s, (1 - core) * 64 + s * 16)
    post.finish()
    post_x.finish()
    for store in stores:
        store.wait()
    comes = (me + 2) % blocks // 2 == core
    for n in range(3):
        for side in range(2):
            pl.when(comes)(far_copy(n, side, {"expert": base + core, "tensor": (me + 2) % blocks}).wait_recv)
        far_copies[n].wait_send()


def reduce_call(d_qkv, dr, d_mine, router_part, small, x_all, gain1, ob, pick_y, ret_y, far, resid,
                weights):
    blocks, tok, col = x_all.shape
    width = blocks * col
    tiles = (blocks, tok, col)
    wide = (128, 16, 4 * col + 128)
    shape = jax.ShapeDtypeStruct
    vmem = pl.BlockSpec(memory_space=pltpu.VMEM)
    hbm = pl.BlockSpec(memory_space=pl.ANY)
    count = 8 + blocks - 1
    return pl.pallas_call(
        reduce_kernel,
        out_shape=(
            shape(wide[:2] + (col,), BF), shape(wide[:2] + (col,), BF), shape(wide[:2] + (col,), BF),
            shape((col, width), BF), shape((128, width), BF),
            shape((tok, col), BF), shape((tok, col), BF), shape((16, col), F32),
            shape((far.shape[0], 2 * far.shape[1], far.shape[2]), BF),
        ),
        in_specs=[vmem] * 10 + [hbm] * 5,
        out_specs=(hbm,) * 3 + (vmem,) * 5 + (hbm,),
        scratch_shapes=[
            pltpu.VMEM((width, col), BF), pltpu.VMEM((width, col), BF), pltpu.VMEM((width, col), BF),
            pltpu.VMEM((tok, col), F32), pltpu.VMEM(tiles, BF), pltpu.VMEM(tiles, BF),
            pltpu.VMEM((4, tok // 2, col), BF), pltpu.VMEM((4, tok, col), BF),
            pltpu.VMEM((blocks, 16, col), F32),
            pltpu.VMEM(wide, BF), pltpu.VMEM((124,) + wide[1:], BF), pltpu.VMEM(wide, BF),
            pltpu.SemaphoreType.DMA((4,)), pltpu.SemaphoreType.DMA((8, 3)),
            pltpu.SemaphoreType.DMA((count,)), pltpu.SemaphoreType.DMA((count,)),
            pltpu.SemaphoreType.DMA((56,)), pltpu.SemaphoreType.DMA((56,)),
            pltpu.SemaphoreType.DMA((3,)), pltpu.SemaphoreType.DMA((3, 2)),
        ],
        compiler_params=pltpu.CompilerParams(
            collective_id=3, has_side_effects=True, vmem_limit_bytes=63 * 1024 * 1024
        ),
        cost_estimate=COST,
        name="reduce",
    )(d_qkv, dr, d_mine, router_part, small, x_all, gain1, ob, pick_y, ret_y, far, resid, *weights)


def body(
    tokens,
    out_grad,
    seq_lengths,
    dest_index,
    routes,
    pair_order,
    norm1_gain,
    w_query,
    w_key,
    w_value,
    q_gain,
    k_gain,
    w_output,
    norm2_gain,
    w_router,
    expert_w,
):
    groups = lax.axis_size("expert")
    tensor_count = lax.axis_size("tensor")
    group_id = lax.axis_index("expert")
    tensor_id = lax.axis_index("tensor")
    tok_count, col_count = tokens.shape
    width = col_count * tensor_count
    move_rows = tok_count // groups
    expert_count = w_router.shape[1]
    top_count = routes.shape[1]
    local_experts = expert_w.shape[0]

    w_stored = jnp.transpose(expert_w, (0, 2, 1, 3))
    w_first = near_weights(w_stored, 0)

    routes_t = routes.T
    order_t = pair_order[0].reshape(tok_count, top_count).T
    pair_expert = routes_t.reshape(-1)
    pair_total = tok_count * top_count
    base = pair_expert * pair_total
    keyed = base + order_t.reshape(-1)
    before = (keyed[None, :] < keyed[:, None]) & (keyed[None, :] >= base[:, None])
    ranks = jnp.sum(before.astype(jnp.int32), axis=1).reshape(top_count, tok_count)
    expert_axis = jnp.arange(expert_count, dtype=jnp.int32)
    route_hot = routes_t[:, None, :] == expert_axis[None, :, None]
    counts = jnp.sum(route_hot.astype(F32), axis=(0, 2))

    places = jnp.arange(tok_count, dtype=jnp.int32)
    arrival_rank = jnp.sum((dest_index[None, :] < dest_index[:, None]).astype(jnp.int32), axis=1)
    by_rank = (arrival_rank[None, :] == places[:, None]).astype(BF)
    inner = jnp.broadcast_to((dest_index % tok_count).astype(BF)[:, None], (tok_count, 64))
    facts = jnp.broadcast_to(counts.astype(BF)[None, :], (tok_count, expert_count))
    outgoing = dot(by_rank, jnp.concatenate([tokens, out_grad, inner, facts], axis=1)).astype(BF)
    got = exchange(outgoing.reshape(groups, move_rows, -1), "expert")
    all_counts = got[:, 0, 2 * col_count + 64 :].astype(jnp.int32)
    lower = jnp.arange(groups, dtype=jnp.int32) < group_id
    offsets = jnp.sum(jnp.where(lower[:, None], all_counts, 0), axis=0)
    mine = got[:, :, 2 * col_count].astype(jnp.int32).reshape(-1)
    put = (mine[None, :] == places[:, None]).astype(BF)
    local = dot(put, got.reshape(tok_count, -1)[:, : 2 * col_count]).astype(BF)
    capacity = 5 * tok_count * groups * top_count // (4 * expert_count)
    most_rows = 3 * tok_count * top_count // (2 * expert_count)
    per = most_rows // 2
    slots = groups * per
    slot_global = jnp.sum(jnp.where(route_hot, offsets[None, :, None], 0), axis=1) + ranks
    kept = slot_global < capacity
    keep_mask = kept.astype(F32)
    here = kept & (routes_t % tensor_count == tensor_id)
    owner = routes_t // tensor_count * 2 + ranks % 2
    slot_of = jnp.where(here, owner * per + ranks // 2, -1)

    seq_ids, positions = sequence_layout(seq_lengths[0], tok_count)
    bias = jnp.where(seq_ids[:, None] == seq_ids[None, :], 0.0, mask_fill)
    cos_tab, sin_tab = rope_tables(positions, q_gain.shape[0])
    cos_rows = jnp.concatenate([cos_tab, cos_tab], axis=1)
    sin_rows = jnp.concatenate([-sin_tab, sin_tab], axis=1)
    gain1 = norm1_gain.astype(F32).reshape(tensor_count, col_count)
    gain2 = norm2_gain.astype(F32).reshape(tensor_count, col_count)
    head_gains = (q_gain.astype(F32)[None], k_gain.astype(F32)[None])
    router = jnp.pad(w_router, ((0, 0), (0, 128 - expert_count)))
    weights = (w_query, w_key, w_value, w_output)
    def homeward(value):
        return exchange(value.reshape(groups, -1, value.shape[1]), "expert").reshape(value.shape)

    x_all, dy_all, send_dy = pre_call(local, slot_of, tensor_count, slots)
    send_dy, x_all, w_stored = lax.optimization_barrier((send_dy, x_all, w_stored))
    w_second = near_weights(w_stored, 1)
    recv_dy = homeward(send_dy)
    (
        resid, mixed, q_raw, k_raw, qh, kh, vh, attended, gates, send_rows, pick_t,
    ) = front_call(
        x_all, bias, cos_rows, sin_rows, gain1, gain2, *head_gains, router, routes_t, slot_of,
        keep_mask, weights, slots,
    )
    send_rows, w_stored, recv_dy = lax.optimization_barrier((send_rows, w_stored, recv_dy))
    recv_rows = homeward(send_rows)
    y_rows, d_rows, partial = expert_call(recv_rows, recv_dy, weights_call(w_stored, w_first, w_second))
    ret_rows = homeward(d_rows)
    near, far = home_call(partial)
    ret_rows, near, far, y_rows = lax.optimization_barrier((ret_rows, near, far, y_rows))
    ret_y = homeward(y_rows)
    d_qkv, dr, d_mine, router_part, small = back_call(
        pick_t, ret_rows, slot_of, keep_mask, gates, routes_t, bias, cos_rows,
        sin_rows, gain2, *head_gains, router, resid, dy_all, mixed, qh, kh, vh, q_raw, k_raw,
        w_output,
    )
    *wide, out_proj, router_sum, dx_slice, out_slice, small, far = reduce_call(
        d_qkv, dr, d_mine, router_part, small, x_all, gain1, attended, pick_t, ret_y, far, resid,
        weights[:3],
    )

    going = dot(put, jnp.concatenate([out_slice, dx_slice], axis=1), 0, 0).astype(BF)
    small = small[:9].astype(BF).reshape(move_rows, -1)
    small = jnp.pad(small, ((0, 0), (0, -small.shape[1] % 128)))
    small = jnp.broadcast_to(small[None], (groups,) + small.shape)
    back = exchange(jnp.concatenate([going.reshape(groups, move_rows, -1), small], axis=2), "expert")
    small = jnp.sum(back[:, :, 2 * col_count :].astype(F32), axis=0)[:, : 9 * col_count // move_rows]
    small = small.reshape(-1)
    back = dot(by_rank, back.reshape(tok_count, -1)[:, : 2 * col_count], 0, 0).astype(BF)
    opposite = (tensor_id + 2) % tensor_count - 2 * (group_id % 2)
    is_far = jnp.arange(local_experts) == opposite
    expert_grad = jnp.where(is_far[:, None, None, None], far[None], near).astype(F32)
    expert_grad = jnp.transpose(expert_grad, (0, 2, 1, 3))
    wide = [value.reshape(width, -1) for value in wide]
    gain_at = 2 * width + tok_count
    head = q_gain.shape[0]
    return (
        back[:, :col_count],
        back[:, col_count:],
        small[:width],
        wide[0].astype(F32),
        wide[1].astype(F32),
        wide[2].astype(F32),
        small[gain_at : gain_at + head],
        small[gain_at + head : gain_at + 2 * head],
        out_proj.astype(F32),
        small[width : 2 * width],
        router_sum[:expert_count].astype(F32).T,
        expert_grad,
    )


def solution(mesh):
    in_specs = (
        P("expert", "tensor"),
        P("expert", "tensor"),
        P("expert", None),
        P("expert"),
        P("expert", None),
        P("expert", None),
        P(),
        P(None, "tensor"),
        P(None, "tensor"),
        P(None, "tensor"),
        P(),
        P(),
        P("tensor", None),
        P(),
        P(),
        P("expert", None, None, "tensor"),
    )
    out_specs = (
        P("expert", "tensor"),
        P("expert", "tensor"),
        P(),
        P(None, "tensor"),
        P(None, "tensor"),
        P(None, "tensor"),
        P(),
        P(),
        P("tensor", None),
        P(),
        P(),
        P("expert", None, None, "tensor"),
    )
    return jax.shard_map(body, mesh=mesh, in_specs=in_specs, out_specs=out_specs, check_vma=False)
```
